32 devices in a mesh: seq: 4 (over y, x), ctx: 8 (over z, core).
Axes of the slice: x: 2, y: 2, z: 4, core: 2. Of those that a mesh axis runs over, the one named last changes fastest.
Arguments:
- block_input: bfloat16 [4096, 1024], P(('ctx', 'seq')), may hold values from -6 to 6
- teacher: bfloat16 [4096, 1024], P(('ctx', 'seq')), may hold values from -6 to 6
- valid_mask: int32 [4096], P(('ctx', 'seq')), may hold values from 0 to 1
- segments: int32 [4096], replicated, may hold values from 0 to 7, never falling along the last dimension, each value on 1 to 2048 neighbouring positions
- mix_proj: bfloat16 [1024, 5120], P(('seq', 'ctx')), may hold values from -0.1875 to 0.1875
- scalar_proj: bfloat16 [1024, 24], P(('seq', 'ctx')), may hold values from -0.1875 to 0.1875
- gate_proj: bfloat16 [1024, 1024], P(('seq', 'ctx')), may hold values from -0.1875 to 0.1875
- out_proj: bfloat16 [1024, 1024], P(('seq', 'ctx')), may hold values from -0.375 to 0.375
- conv_weight: bfloat16 [5120, 4], P(('seq', 'ctx')), may hold values from -2 to 2
- norm_attn: bfloat16 [1024], P(('seq', 'ctx')), may hold values from 0.5 to 1.5
- norm_mlp: bfloat16 [1024], P(('seq', 'ctx')), may hold values from 0.5 to 1.5
- head_gain: bfloat16 [128], replicated, may hold values from 0.5 to 1.5
- a_log: bfloat16 [8], replicated, may hold values from -8 to 1
- dt_bias: bfloat16 [8], replicated, may hold values from -4 to 0.5
- w_gate: bfloat16 [1024, 2816], P(('seq', 'ctx')), may hold values from -0.1875 to 0.1875
- w_up: bfloat16 [1024, 2816], P(('seq', 'ctx')), may hold values from -0.1875 to 0.1875
- w_down: bfloat16 [2816, 1024], P(('seq', 'ctx')), may hold values from -0.109375 to 0.109375
Outputs:
- output: bfloat16 [4096, 1024], P(('ctx', 'seq'))
- mean_loss: float32 [], replicated
- input_grad: float32 [4096, 1024], P(('ctx', 'seq'))
- grad_mix_proj: float32 [1024, 5120], P(('seq', 'ctx'))
- grad_scalar_proj: float32 [1024, 24], P(('seq', 'ctx'))
- grad_gate_proj: float32 [1024, 1024], P(('seq', 'ctx'))
- grad_out_proj: float32 [1024, 1024], P(('seq', 'ctx'))
- grad_conv_weight: float32 [5120, 4], P(('seq', 'ctx'))
- grad_norm_attn: float32 [1024], P(('seq', 'ctx'))
- grad_norm_mlp: float32 [1024], P(('seq', 'ctx'))
- grad_head_gain: float32 [128], replicated
- grad_a_log: float32 [8], replicated
- grad_dt_bias: float32 [8], replicated
- grad_w_gate: float32 [1024, 2816], P(('seq', 'ctx'))
- grad_w_up: float32 [1024, 2816], P(('seq', 'ctx'))
- grad_w_down: float32 [2816, 1024], P(('seq', 'ctx'))
The draws below stay inside these ranges and needn't reach their ends.
Inputs may be any that keep to these rules, and one draw needn't show every extreme that they name: `segments`: segment numbers never fall along the tokens; each document has 1 to 2048 tokens and one has exactly 2048.
All inputs are finite; a program needn't handle non-finite values.
Results may differ from the reference program's by a relative error of at most 0.013.
The reference program's roundings to bfloat16 on the way count: a program that leaves them out, or rounds other values in their place, can miss the bound.
Values may be sent and summed in bfloat16 or wider, within the bound.
A program may use at most 320 MiB of HBM per device.

```python
import math
import jax
import jax.numpy as jnp
import numpy as np
from jax import lax

D = 1024
HEADS = 8
HEAD = 128
NH = 2
FF = 2816
BLOCK_LEN = 64
CONV = 4
TOKENS = 4096
LENGTH = 4096
DOCS = 8
MOST_DOC = 2048


def draw_valid_mask(key, part):
    picks = jax.random.randint(jax.random.fold_in(key, 71), (TOKENS,), 0, 1000)
    places = jnp.arange(TOKENS, dtype=jnp.int32)
    limits = 150 + 750 * places // TOKENS
    return (picks < limits).astype(jnp.int32)


def levels(rng, dims, shards, smallest, high):
    factor_of, own = 1.0, jax.random.fold_in(rng, 6)
    for position, blocks in shards:
        steps = jnp.exp(jax.random.uniform(jax.random.fold_in(own, position), (blocks,), jnp.float32, smallest / len(shards), high / len(shards)))
        factor_of = factor_of * jnp.repeat(steps, dims[position] // blocks).reshape([-1 if axis == position else 1 for axis in range(len(dims))])
    return factor_of


def length_profile(number_of, total, limit, skew):
    portions = [(1 << 20) // math.isqrt(grade ** skew) + 1 for grade in range(2, number_of + 1)]
    rest, given = total - limit - (number_of - 1), [1] * (number_of - 1)
    while rest > 0:
        candidates = [i for i in range(number_of - 1) if given[i] < limit]
        whole, left = sum([portions[i] for i in candidates]), rest
        for i in candidates:
            addition = min(limit - given[i], max(1, left * portions[i] // whole), rest)
            given[i] = given[i] + addition
            rest = rest - addition
    return np.array([limit] + given)


def ragged_sizes(own_key, number_of, total, limit, slope):
    if number_of == 2:
        one = jax.random.randint(own_key, (), max(1, total - limit), min(limit, total - 1) + 1)
        return jnp.stack([one, total - one])
    tallies = jnp.asarray(length_profile(number_of, total, limit, slope), jnp.int32)
    pairs = (number_of - 1) // 2
    giver, taker = tallies[1:1 + 2 * pairs:2], tallies[2:2 + 2 * pairs:2]
    slack = jnp.minimum(giver - 1, limit - taker)
    passed = jax.random.randint(jax.random.fold_in(own_key, 1), (pairs,), 0, 1 << 20) % (slack + 1)
    tallies = tallies.at[1:1 + 2 * pairs:2].set(giver - passed).at[2:2 + 2 * pairs:2].set(taker + passed)
    return tallies[jax.random.permutation(jax.random.fold_in(own_key, 2), number_of)]


def scatter_about(rng, shape, scale, limit, shards=(), kind=jnp.bfloat16):
    drawn = scale * jax.random.normal(rng, shape, jnp.float32)
    if shards:
        drawn = drawn * levels(rng, shape, shards, -0.22, 0.18)
    return jnp.clip(drawn, -limit, limit).astype(kind)


def setup_inputs(seed: int = 0) -> dict:
    keys = jax.random.split(jax.random.key(seed), 18)
    block_input = scatter_about(keys[0], (TOKENS, D), 1.0, 6.0, ((0, 32),))
    teacher = scatter_about(keys[1], (TOKENS, D), 1.0, 6.0, ((0, 32),))
    valid_mask = draw_valid_mask(jax.random.fold_in(keys[17], 71), 0)
    segments = jnp.searchsorted(jnp.cumsum(ragged_sizes(keys[3], DOCS, TOKENS, MOST_DOC, 2)), jnp.arange(TOKENS), side="right").astype(jnp.int32)
    mix_proj = scatter_about(keys[4], (D, (1 + 2 * NH) * HEADS * HEAD), D ** -0.5, 0.1875, ((0, 32),))
    scalar_proj = scatter_about(keys[5], (D, (NH + 1) * HEADS), D ** -0.5, 0.1875, ((0, 32),))
    gate_proj = scatter_about(keys[6], (D, HEADS * HEAD), D ** -0.5, 0.1875, ((0, 32),))
    out_proj = scatter_about(keys[7], (HEADS * HEAD, D), (HEADS * HEAD // 4) ** -0.5, 0.375, ((0, 32),))
    conv_weight = scatter_about(keys[8], ((1 + 2 * NH) * HEADS * HEAD, CONV), 0.5, 2.0, ((0, 32),))
    norm_attn = jnp.clip(1.0 + 0.1 * jax.random.normal(keys[9], (D,), jnp.float32), 0.5, 1.5).astype(jnp.bfloat16)
    norm_mlp = jnp.clip(1.0 + 0.1 * jax.random.normal(keys[10], (D,), jnp.float32), 0.5, 1.5).astype(jnp.bfloat16)
    head_gain = jnp.clip(1.0 + 0.1 * jax.random.normal(keys[11], (HEAD,), jnp.float32), 0.5, 1.5).astype(jnp.bfloat16)
    a_log = jnp.clip(jax.random.uniform(keys[12], (HEADS,), jnp.float32, -8.0, 1.0), -8.0, 1.0).astype(jnp.bfloat16)
    dt_bias = jnp.clip(jax.random.uniform(keys[13], (HEADS,), jnp.float32, -4.0, 0.5), -4.0, 0.5).astype(jnp.bfloat16)
    w_gate = scatter_about(keys[14], (D, FF), D ** -0.5, 0.1875, ((0, 32),))
    w_up = scatter_about(keys[15], (D, FF), D ** -0.5, 0.1875, ((0, 32),))
    w_down = scatter_about(keys[16], (FF, D), FF ** -0.5, 0.109375, ((0, 32),))
    return dict(block_input=block_input, teacher=teacher, valid_mask=valid_mask, segments=segments, mix_proj=mix_proj, scalar_proj=scalar_proj, gate_proj=gate_proj, out_proj=out_proj, conv_weight=conv_weight, norm_attn=norm_attn, norm_mlp=norm_mlp, head_gain=head_gain, a_log=a_log, dt_bias=dt_bias, w_gate=w_gate, w_up=w_up, w_down=w_down)


@jax.custom_vjp
def low(v):
    return lax.optimization_barrier(v.astype(jnp.bfloat16)).astype(jnp.float32)

@jax.custom_vjp
def low_back(v):
    return v

def low_keep(v):
    return (low(v), None)

def low_pass(kept, grad):
    return (grad,)

def back_keep(v):
    return (v, None)

def back_low(kept, grad):
    return (low(grad),)
low.defvjp(low_keep, low_pass)
low_back.defvjp(back_keep, back_low)
NORM_EPS = 1e-06

def dense_product(left_mat, right_mat):
    return jnp.dot(left_mat.astype(jnp.float32), right_mat.astype(jnp.float32), precision=lax.Precision.HIGHEST, preferred_element_type=jnp.float32)

def rms_scale(values, gain_vec):
    return values * lax.rsqrt(lax.optimization_barrier(jnp.mean(values * values, axis=-1, keepdims=True)) + NORM_EPS) * gain_vec

def unit_rows(values):
    return values * lax.rsqrt(lax.optimization_barrier(jnp.sum(values * values, axis=-1, keepdims=True)) + NORM_EPS)

def gated_norm(head_values, gate_values, gain_vec):
    token_count = head_values.shape[0]
    scaled = rms_scale(head_values, gain_vec)
    gated = scaled * jax.nn.silu(gate_values.reshape(head_values.shape))
    return gated.reshape(token_count, -1)

def causal_mix(extended, ext_doc, weight):
    span_rows = extended.shape[0] - (CONV - 1)
    own_doc = ext_doc[CONV - 1:]
    summed = jnp.zeros((span_rows,) + extended.shape[1:], jnp.float32)
    for tap_lag in range(CONV):
        tap_start = CONV - 1 - tap_lag
        linked = (ext_doc[tap_start:tap_start + span_rows] == own_doc).astype(jnp.float32)
        summed = summed + linked[:, None, None] * extended[tap_start:tap_start + span_rows] * weight[:, :, CONV - 1 - tap_lag]
    return summed

def head_inputs(conv_out, scal_rows, a_log, dt_bias):
    row_count = conv_out.shape[0]
    head_count = conv_out.shape[1]
    activated = jax.nn.silu(conv_out).reshape(row_count, head_count, 1 + 2 * NH, HEAD)
    query_vec = unit_rows(activated[:, :, 0]) / math.sqrt(HEAD)
    key_vecs = unit_rows(activated[:, :, 1:1 + NH])
    value_vecs = activated[:, :, 1 + NH:]
    beta_gates = jax.nn.sigmoid(scal_rows[:, :, :NH])
    log_gates = -jnp.exp(a_log)[None, :] * jax.nn.softplus(scal_rows[:, :, NH] + dt_bias[None, :])
    return (query_vec, key_vecs, value_vecs, beta_gates, log_gates)

def block_update(state_matrix, pieces):
    query_vec, key_vecs, value_vecs, beta_gates, log_gates, starts = pieces
    step_count = key_vecs.shape[1]
    row_count = key_vecs.shape[0] * step_count
    flat_keys = key_vecs.reshape(row_count, key_vecs.shape[2])
    flat_values = value_vecs.reshape(row_count, value_vecs.shape[2])
    flat_beta = beta_gates.reshape(row_count)
    first_step = (jnp.arange(step_count) == 0).astype(jnp.float32)
    row_log = ((log_gates * (1.0 - starts))[:, None] * first_step[None, :]).reshape(row_count)
    row_start = (starts[:, None] * first_step[None, :]).reshape(row_count)
    cum_log = jnp.cumsum(row_log)
    cum_start = jnp.cumsum(row_start)
    row_index = jnp.arange(row_count)
    linked = (row_index[:, None] >= row_index[None, :]) & (cum_start[:, None] == cum_start[None, :])
    log_decay_spread = jnp.where(linked, cum_log[:, None] - cum_log[None, :], 0.0)
    decay_mat = jnp.where(linked, jnp.exp(log_decay_spread), 0.0)
    carry_in = jnp.where(cum_start == 0.0, jnp.exp(cum_log), 0.0)
    strict_mask = (row_index[:, None] > row_index[None, :]).astype(jnp.float32)
    system = jnp.eye(row_count, dtype=jnp.float32) + flat_beta[:, None] * strict_mask * decay_mat * dense_product(flat_keys, flat_keys.T)
    right_side = flat_beta[:, None] * jnp.concatenate([flat_values, carry_in[:, None] * flat_keys], axis=1)
    solved = jax.scipy.linalg.solve_triangular(system, right_side, lower=True, unit_diagonal=True)
    value_width = flat_values.shape[1]
    updates = solved[:, :value_width] - dense_product(solved[:, value_width:], state_matrix)
    query_decay = decay_mat[step_count - 1::step_count]
    query_carry = carry_in[step_count - 1::step_count]
    outputs = query_carry[:, None] * dense_product(query_vec, state_matrix) + dense_product(query_decay * dense_product(query_vec, flat_keys.T), updates)
    new_state = carry_in[row_count - 1] * state_matrix + dense_product((decay_mat[row_count - 1][:, None] * flat_keys).T, updates)
    return (new_state, outputs)

def run_head(query_vec, key_vecs, value_vecs, beta_gates, log_gates, initial, starts):
    row_count = query_vec.shape[0]
    block_count = row_count // BLOCK_LEN
    pieces = (query_vec.reshape(block_count, BLOCK_LEN, -1), key_vecs.reshape(block_count, BLOCK_LEN, NH, -1), value_vecs.reshape(block_count, BLOCK_LEN, NH, -1), beta_gates.reshape(block_count, BLOCK_LEN, NH), log_gates.reshape(block_count, BLOCK_LEN), starts.reshape(block_count, BLOCK_LEN))
    final_state, outputs = lax.scan(jax.checkpoint(block_update), initial, pieces)
    return (outputs.reshape(row_count, -1), final_state)

def sequence_forward(inputs_f, weights, teacher_s, mask_s, resets_s, valid_count, token_total):
    mix_proj, scalar_proj, gate_proj, out_proj, conv_weight, norm_attn, norm_mlp, head_gain, a_log, dt_bias, w_gate, w_up, w_down = weights
    row_count = inputs_f.shape[0]
    wide_cols = (1 + 2 * NH) * HEAD
    normed = low(rms_scale(inputs_f, norm_attn))
    proj_rows = low_back(low(dense_product(normed, mix_proj)))
    scal_rows = low_back(low(dense_product(normed, scalar_proj)))
    gate_out = low_back(dense_product(normed, gate_proj))
    doc_ids = jnp.cumsum(resets_s).astype(jnp.int32)
    ext_doc = jnp.concatenate([jnp.full((CONV - 1,), -1, jnp.int32), doc_ids])
    extended = jnp.concatenate([jnp.zeros((CONV - 1, HEADS, wide_cols), jnp.float32), proj_rows.reshape(row_count, HEADS, wide_cols)], axis=0)
    conv_out = causal_mix(extended, ext_doc, conv_weight.reshape(HEADS, wide_cols, CONV))
    query_vec, key_vecs, value_vecs, beta_gates, log_gates = head_inputs(conv_out, scal_rows.reshape(row_count, HEADS, NH + 1), a_log, dt_bias)
    initial = jnp.zeros((HEAD, HEAD), jnp.float32)
    heads_out, finals = jax.vmap(run_head, in_axes=(1, 1, 1, 1, 1, None, None), out_axes=(1, 0))(query_vec, key_vecs, value_vecs, beta_gates, log_gates, initial, resets_s.astype(jnp.float32))
    heads_out = low_back(low(heads_out))
    mixed = low(gated_norm(heads_out, gate_out, head_gain))
    middle = inputs_f + low_back(dense_product(mixed, out_proj))
    second = low(rms_scale(middle, norm_mlp))
    gate_values = low_back(dense_product(second, w_gate))
    up_values = low_back(dense_product(second, w_up))
    hidden = low(jax.nn.silu(gate_values) * up_values)
    final_out = middle + low_back(dense_product(hidden, w_down))
    error_rows = final_out - teacher_s
    objective = token_total / (2.0 * valid_count) * jnp.sum(mask_s[:, None] * error_rows * error_rows)
    return (final_out, objective)

def reference(block_input, teacher, valid_mask, segments, mix_proj, scalar_proj, gate_proj, out_proj, conv_weight, norm_attn, norm_mlp, head_gain, a_log, dt_bias, w_gate, w_up, w_down):
    token_total = block_input.shape[0]
    seq_count = token_total // LENGTH
    positions = jnp.arange(token_total)
    previous = jnp.concatenate([segments[:1], segments[:-1]])
    resets = ((positions % LENGTH == 0) | (segments != previous)).astype(jnp.int32)
    mask_values = valid_mask.astype(jnp.float32)
    valid_count = jnp.maximum(jnp.sum(mask_values), 1.0)
    params = tuple((weight_arr.astype(jnp.float32) for weight_arr in (mix_proj, scalar_proj, gate_proj, out_proj, conv_weight, norm_attn, norm_mlp, head_gain, a_log, dt_bias, w_gate, w_up, w_down)))

    def one_sequence(grad_sums, pieces):
        inputs_s, teacher_s, mask_s, resets_s = pieces

        def forward(inputs_f, weights):
            return sequence_forward(inputs_f, weights, teacher_s, mask_s, resets_s, valid_count, token_total)
        (final_out, objective), back_fn = jax.vjp(forward, inputs_s.astype(jnp.float32), params)
        grad_input, grad_weights = back_fn((jnp.zeros_like(final_out), jnp.ones_like(objective)))
        return (jax.tree.map(jnp.add, grad_sums, grad_weights), (final_out.astype(jnp.bfloat16), objective, grad_input))
    initial = jax.tree.map(jnp.zeros_like, params)
    grad_totals, (outputs, objectives, input_grads) = lax.scan(one_sequence, initial, (block_input.reshape(seq_count, LENGTH, -1), teacher.astype(jnp.float32).reshape(seq_count, LENGTH, -1), mask_values.reshape(seq_count, LENGTH), resets.reshape(seq_count, LENGTH)))
    mean_loss = jnp.sum(objectives) * 2.0 / (token_total * D)
    return (outputs.reshape(token_total, -1), mean_loss, input_grads.reshape(token_total, -1), grad_totals[0], grad_totals[1], grad_totals[2], grad_totals[3], grad_totals[4], grad_totals[5], grad_totals[6], grad_totals[7], grad_totals[8], grad_totals[9], grad_totals[10], grad_totals[11], grad_totals[12])
```

```python
import functools
import math

import jax
import jax.numpy as jnp
from jax import lax
from jax.experimental import pallas as pl
from jax.experimental.pallas import tpu as pltpu
from jax.sharding import PartitionSpec as P

D = 1024
HEADS = 8
HEAD = 128
NH = 2
FF = 2816
BLOCK_LEN = 64
ROWS = BLOCK_LEN * NH
CONV = 4
SEQ_LEN = 32768
WIDE = (1 + 2 * NH) * HEAD
HALO = 16
NORM_EPS = 1e-06
F32 = jnp.float32
BF16 = jnp.bfloat16
BOTH = ("seq", "ctx")


def split_bf16(x):
    if x.dtype == BF16:
        return x, None
    high = x.astype(BF16)
    return high, (x - high.astype(F32)).astype(BF16)


def mm(a, b, ca=1, cb=0, passes=3):
    def one(x, y):
        return lax.dot_general(x, y, (((ca,), (cb,)), ((), ())), preferred_element_type=F32)

    if passes == 1:
        return one(a.astype(BF16), b.astype(BF16))
    ah, al = split_bf16(a)
    bh, bl = split_bf16(b)
    total = one(ah, bh)
    if bl is not None:
        total = total + one(ah, bl)
    if al is not None:
        total = total + one(al, bh)
    return total


def iota(shape, axis):
    return lax.broadcasted_iota(jnp.int32, shape, axis)


def unit_lower_inverse(a):
    n = a.shape[0]
    ri, ci = iota((n, n), 0), iota((n, n), 1)
    own = jnp.where(ri // 8 == ci // 8, a, 0.0)
    pick = (iota((n, 8), 0) % 8 == iota((n, 8), 1)).astype(BF16)
    small = mm(own, pick).reshape(n // 8, 8, 8)
    inv = (ri == ci).astype(F32).reshape(n // 8, 8, n)
    for j in range(7):
        inv = inv - small[:, :, j : j + 1] * inv[:, j : j + 1, :]
    inv = inv.reshape(n, n)
    size = 8
    while size < n:
        off = (ri // (2 * size) == ci // (2 * size)) & (ri // size != ci // size)
        inv = inv - mm(inv, mm(jnp.where(off, a, 0.0), inv))
        size *= 2
    return inv


def decays(rowp, colp, tokp, h):
    cs_row, g_row = rowp[0:1, :], rowp[2 + 2 * h : 3 + 2 * h, :]
    cs_col, g_col = colp[:, 0:1], colp[:, 2 + 2 * h : 3 + 2 * h]
    cs_tok, g_tok = tokp[:, 3:4], tokp[:, 4 + h : 5 + h]
    beta = colp[:, 3 + 2 * h : 4 + 2 * h]
    ri, ci = iota((ROWS, ROWS), 0), iota((ROWS, ROWS), 1)
    strict = (ri > ci) & (cs_col == cs_row)
    decay = jnp.where(strict, jnp.exp(jnp.where(strict, g_col - g_row, 0.0)), 0.0)
    rt, ct = iota((BLOCK_LEN, ROWS), 0), iota((BLOCK_LEN, ROWS), 1)
    seen = (rt * NH + NH - 1 >= ct) & (cs_tok == cs_row)
    qdecay = jnp.where(seen, jnp.exp(jnp.where(seen, g_tok - g_row, 0.0)), 0.0)
    carry = jnp.where(cs_col == 0.0, jnp.exp(g_col), 0.0)
    qcarry = jnp.where(cs_tok == 0.0, jnp.exp(g_tok), 0.0)
    cs_last, g_last = cs_row[:, ROWS - 1 :], g_row[:, ROWS - 1 :]
    same = cs_col == cs_last
    dlast = jnp.where(same, jnp.exp(jnp.where(same, g_last - g_col, 0.0)), 0.0)
    clast = jnp.where(cs_last == 0.0, jnp.exp(g_last), 0.0)
    return beta, decay, qdecay, carry, qcarry, dlast, clast


def lag_rows(ext, lag):
    moved = pltpu.roll(ext, lag, 0) if lag else ext
    return moved[HALO:]


def fwd_kernel(
    heads, proj_ref, w_ref, rowp_ref, colp_ref, tokp_ref,
    oloc_ref, carr_ref, fin_ref, conv_ref, q_ref, k_ref, v_ref, t_ref, kk_ref, at_ref, uw_ref, pl_ref,
    state, weave,
):
    step = pl.program_id(0)
    eye = (iota((HEAD, HEAD), 0) == iota((HEAD, HEAD), 1)).astype(F32)

    @pl.when(step == 0)
    def _():
        for h in range(heads):
            state[h, :, :HEAD] = eye
            state[h, :, HEAD:] = jnp.zeros((HEAD, HEAD), F32)

    base = pl.multiple_of(step * BLOCK_LEN, BLOCK_LEN)
    rowp, colp, tokp = rowp_ref[0], colp_ref[0], tokp_ref[0]
    for h in range(heads):
        cols = slice(h * WIDE, (h + 1) * WIDE)
        ext = proj_ref[pl.ds(base, BLOCK_LEN + HALO), cols].astype(F32)
        conv = ext[HALO:] * w_ref[0:1, cols]
        for lag in range(1, CONV):
            conv = conv + tokp[:, lag - 1 : lag] * lag_rows(ext, lag) * w_ref[lag : lag + 1, cols]
        conv_ref[:, cols] = conv
        act = conv * jax.nn.sigmoid(conv)
        unit = []
        for part in range(1 + NH):
            piece = act[:, part * HEAD : (part + 1) * HEAD]
            unit.append(piece * lax.rsqrt(jnp.sum(piece * piece, axis=1, keepdims=True) + NORM_EPS))
        query = unit[0] * (1.0 / math.sqrt(HEAD))
        for j in range(NH):
            weave[2 * h, pl.ds(j, BLOCK_LEN, NH), :] = unit[1 + j]
            weave[2 * h + 1, pl.ds(j, BLOCK_LEN, NH), :] = act[:, (1 + NH + j) * HEAD : (2 + NH + j) * HEAD]
        keys, values = weave[2 * h], weave[2 * h + 1]
        beta, decay, qdecay, carry, qcarry, dlast, clast = decays(rowp, colp, tokp, h)
        kk = decay * mm(keys, keys, 1, 1)
        inv = unit_lower_inverse(beta * kk)
        uw = mm(inv, jnp.concatenate([beta * values, (beta * carry) * keys], axis=1))
        attn = qdecay * mm(query, keys, 1, 1)
        auw = mm(attn, uw)
        nm = mm(dlast * keys, uw, 0, 0)
        before = state[h]
        out = mm(qcarry * query - auw[:, HEAD:], before)
        hc = slice(h * HEAD, (h + 1) * HEAD)
        carr_ref[:, hc] = out[:, :HEAD]
        oloc_ref[:, hc] = out[:, HEAD:] + auw[:, :HEAD]
        after = mm(clast * eye - nm[:, HEAD:], before)
        state[h, :, :HEAD] = after[:, :HEAD]
        state[h, :, HEAD:] = after[:, HEAD:] + nm[:, :HEAD]
        q_ref[0, h] = query
        k_ref[0, h] = keys
        v_ref[0, h] = values
        t_ref[0, h] = inv
        kk_ref[0, h] = kk
        at_ref[0, h] = attn
        uw_ref[0, h] = uw
        pl_ref[0, h] = before
    fin_ref[...] = state[...]


def recurrence_forward(proj_ext, conv_w, rowp, colp, tokp, heads):
    blocks = rowp.shape[0]
    rows = blocks * BLOCK_LEN
    whole = lambda *dims: pl.BlockSpec(dims, lambda i: (0,) * len(dims))
    by_block = lambda *dims: pl.BlockSpec((1,) + dims, lambda i: (i,) + (0,) * len(dims))
    token = lambda cols: pl.BlockSpec((BLOCK_LEN, cols), lambda i: (i, 0))
    shape = lambda *dims: jax.ShapeDtypeStruct(dims, F32)
    square = (heads, ROWS, HEAD)
    return pl.pallas_call(
        functools.partial(fwd_kernel, heads),
        grid=(blocks,),
        in_specs=[
            whole(*proj_ext.shape), whole(*conv_w.shape),
            by_block(*rowp.shape[1:]), by_block(*colp.shape[1:]), by_block(*tokp.shape[1:]),
        ],
        out_specs=[
            token(heads * HEAD), token(heads * HEAD), whole(heads, HEAD, 2 * HEAD), token(heads * WIDE),
            by_block(heads, BLOCK_LEN, HEAD), by_block(*square), by_block(*square), by_block(*square),
            by_block(*square), by_block(heads, BLOCK_LEN, ROWS), by_block(heads, ROWS, 2 * HEAD),
            by_block(heads, HEAD, 2 * HEAD),
        ],
        out_shape=[
            shape(rows, heads * HEAD), shape(rows, heads * HEAD), shape(heads, HEAD, 2 * HEAD), shape(rows, heads * WIDE),
            shape(blocks, heads, BLOCK_LEN, HEAD), shape(blocks, *square), shape(blocks, *square), shape(blocks, *square),
            shape(blocks, *square), shape(blocks, heads, BLOCK_LEN, ROWS), shape(blocks, heads, ROWS, 2 * HEAD),
            shape(blocks, heads, HEAD, 2 * HEAD),
        ],
        scratch_shapes=[pltpu.VMEM((heads, HEAD, 2 * HEAD), F32), pltpu.VMEM((2 * heads, ROWS, HEAD), F32)],
        compiler_params=pltpu.CompilerParams(vmem_limit_bytes=40 << 20),
        name="recurrence_forward",
    )(proj_ext, conv_w, rowp, colp, tokp)


def state_kernel(heads, index_ref, maps_ref, oloc_ref, carr_ref, gate_ref, gain_ref, heads_ref, mixed_ref, state_ref):
    def hop(k, states):
        return tuple(
            mm(maps_ref[k, h, :, :HEAD], states[h]) + maps_ref[k, h, :, HEAD:].astype(F32) for h in range(heads)
        )

    states = lax.fori_loop(0, index_ref[0], hop, tuple(jnp.zeros((HEAD, HEAD), F32) for _ in range(heads)))
    for h in range(heads):
        hc = slice(h * HEAD, (h + 1) * HEAD)
        state_ref[h] = states[h]
        out = (oloc_ref[:, hc] + mm(carr_ref[:, hc], states[h])).astype(BF16)
        heads_ref[:, hc] = out
        wide = out.astype(F32)
        gate = gate_ref[:, hc]
        scaled = wide * lax.rsqrt(jnp.mean(wide * wide, axis=1, keepdims=True) + NORM_EPS) * gain_ref[...]
        mixed_ref[:, hc] = (scaled * (gate * jax.nn.sigmoid(gate))).astype(BF16)


def state_and_gate(index, maps, oloc, carr, gate_out, gain, heads):
    rows = oloc.shape[0]
    vmem = pl.BlockSpec(memory_space=pltpu.VMEM)
    return pl.pallas_call(
        functools.partial(state_kernel, heads),
        in_specs=[pl.BlockSpec(memory_space=pltpu.SMEM)] + [vmem] * 5,
        out_specs=[vmem] * 3,
        out_shape=[
            jax.ShapeDtypeStruct((rows, heads * HEAD), BF16),
            jax.ShapeDtypeStruct((rows, heads * HEAD), BF16),
            jax.ShapeDtypeStruct((heads, HEAD, HEAD), F32),
        ],
        compiler_params=pltpu.CompilerParams(vmem_limit_bytes=40 << 20),
        name="state_and_gate",
    )(index, maps, oloc, carr, gate_out, gain)


def gate_back_kernel(heads, grad_ref, heads_ref, gate_ref, gain_ref, carr_ref, ghead_ref, ggate_ref, ggain_ref, cot_ref):
    total = jnp.zeros((1, HEAD), F32)
    for h in range(heads):
        hc = slice(h * HEAD, (h + 1) * HEAD)
        x = heads_ref[:, hc].astype(F32)
        gate = gate_ref[:, hc]
        grad = grad_ref[:, hc]
        gain = gain_ref[...]
        inv = lax.rsqrt(jnp.mean(x * x, axis=1, keepdims=True) + NORM_EPS)
        sig = jax.nn.sigmoid(gate)
        silu = gate * sig
        unit = x * inv
        ggate_ref[:, hc] = (grad * unit * gain * (sig * (1.0 + gate * (1.0 - sig)))).astype(BF16)
        weighted = grad * silu
        total = total + jnp.sum(weighted * unit, axis=0, keepdims=True)
        down = weighted * gain
        ghead = (inv * (down - unit * jnp.mean(down * unit, axis=1, keepdims=True))).astype(BF16)
        ghead_ref[:, hc] = ghead
        cot_ref[h] = mm(carr_ref[:, hc], ghead, 0, 0)
    ggain_ref[...] = total


def gate_back(grad_mixed, heads_out, gate_out, gain, carr, heads):
    rows = carr.shape[0]
    vmem = pl.BlockSpec(memory_space=pltpu.VMEM)
    return pl.pallas_call(
        functools.partial(gate_back_kernel, heads),
        in_specs=[vmem] * 5,
        out_specs=[vmem] * 4,
        out_shape=[
            jax.ShapeDtypeStruct((rows, heads * HEAD), BF16),
            jax.ShapeDtypeStruct((rows, heads * HEAD), BF16),
            jax.ShapeDtypeStruct((1, HEAD), F32),
            jax.ShapeDtypeStruct((heads, HEAD, HEAD), F32),
        ],
        compiler_params=pltpu.CompilerParams(vmem_limit_bytes=40 << 20),
        name="gate_back",
    )(grad_mixed, heads_out, gate_out, gain, carr)


def bwd_kernel(
    heads, index_ref, maps_ref, cots_ref, sin_ref, proj_ref, w_ref, rowp_ref, colp_ref, tokp_ref,
    go_ref, conv_ref, q_ref, k_ref, v_ref, t_ref, kk_ref, at_ref, uw_ref, pl_ref,
    gproj_ref, last_ref, spill_ref, gw_ref, gcol_ref, gtok_ref, grow_ref,
    dstate, weave, rim,
):
    step = pl.program_id(0)
    block = pl.num_programs(0) - 1 - step

    @pl.when(step == 0)
    def _():
        pieces = maps_ref.shape[0]

        def hop(i, states):
            k = pieces - 1 - i
            return tuple(
                mm(maps_ref[k, h, :, :HEAD], states[h], 0, 0) + cots_ref[k, h].astype(F32) for h in range(heads)
            )

        found = lax.fori_loop(
            0, pieces - 1 - index_ref[0], hop, tuple(jnp.zeros((HEAD, HEAD), F32) for _ in range(heads))
        )
        for h in range(heads):
            dstate[h] = found[h]
        rim[...] = jnp.zeros_like(rim)
        gw_ref[...] = jnp.zeros_like(gw_ref)

    base = pl.multiple_of(block * BLOCK_LEN, BLOCK_LEN)
    rowp, colp, tokp = rowp_ref[0], colp_ref[0], tokp_ref[0]
    last_row = iota((ROWS, 1), 0) == ROWS - 1
    for h in range(heads):
        cols = slice(h * WIDE, (h + 1) * WIDE)
        hc = slice(h * HEAD, (h + 1) * HEAD)
        beta, decay, qdecay, carry, qcarry, dlast, clast = decays(rowp, colp, tokp, h)
        go = go_ref[:, hc]
        query, keys, values = q_ref[0, h], k_ref[0, h], v_ref[0, h]
        inv, kk, attn, uw = t_ref[0, h], kk_ref[0, h], at_ref[0, h], uw_ref[0, h]
        dnext = dstate[h]
        state = mm(pl_ref[0, h, :, :HEAD], sin_ref[h]) + pl_ref[0, h, :, HEAD:]
        both = mm(jnp.concatenate([keys, uw[:, HEAD:]], axis=0), state)
        ks = both[:ROWS]
        upd = uw[:, :HEAD] - both[ROWS:]
        dupd = mm(attn, go, 0, 0) + dlast * mm(keys, dnext)
        dx = mm(inv, dupd, 0, 0)
        dv = beta * dx
        dy = -(carry * dv)
        go32 = go.astype(F32)
        outer = mm(jnp.concatenate([go32, dx], axis=0), upd, 1, 1)
        dattn, da = outer[:BLOCK_LEN], -outer[BLOCK_LEN:]
        dkd = mm(upd, dnext, 1, 1)
        right = mm(jnp.concatenate([go32, dy], axis=0), state, 1, 1)
        gos = right[:BLOCK_LEN]
        e = beta * da * decay
        f = dattn * qdecay
        ef = jnp.concatenate([f, e], axis=0)
        efk = mm(ef, keys)
        dq = qcarry * gos + efk[:BLOCK_LEN]
        dk = (
            right[BLOCK_LEN:]
            + dlast * dkd
            + efk[BLOCK_LEN:]
            + mm(ef, jnp.concatenate([query, keys], axis=0), 0, 0)
        )
        dstate[h] = clast * dnext + mm(
            jnp.concatenate([qcarry * query, keys], axis=0), jnp.concatenate([go32, dy], axis=0), 0, 0
        )
        dakk = da * kk
        z1 = beta * dakk
        z2 = dattn * attn
        dbeta = jnp.sum(dx * (values - carry * ks), axis=1, keepdims=True) + jnp.sum(dakk, axis=1, keepdims=True)
        dlk = dlast * jnp.sum(dkd * keys, axis=1, keepdims=True)
        tail = jnp.sum(dlk, axis=0, keepdims=True) + clast * jnp.sum(
            jnp.sum(state * dnext, axis=1, keepdims=True), axis=0, keepdims=True
        )
        dgrow = jnp.sum(z1, axis=1, keepdims=True) + jnp.sum(dy * ks, axis=1, keepdims=True) - dlk
        dgrow = dgrow + jnp.where(last_row, tail, 0.0)
        gcol_ref[0, :, 2 * h : 2 * h + 1] = dbeta
        gcol_ref[0, :, 2 * h + 1 : 2 * h + 2] = dgrow
        gtok_ref[0, :, h : h + 1] = jnp.sum(z2, axis=1, keepdims=True) + qcarry * jnp.sum(
            query * gos, axis=1, keepdims=True
        )
        grow_ref[0, h : h + 1, :] = jnp.sum(z1, axis=0, keepdims=True) + jnp.sum(z2, axis=0, keepdims=True)
        weave[2 * h] = dk
        weave[2 * h + 1] = dv
        conv = conv_ref[:, cols]
        sig = jax.nn.sigmoid(conv)
        act = conv * sig
        pieces = []
        for part in range(1 + NH):
            piece = act[:, part * HEAD : (part + 1) * HEAD]
            scale = lax.rsqrt(jnp.sum(piece * piece, axis=1, keepdims=True) + NORM_EPS)
            if part:
                grad = weave[2 * h, pl.ds(part - 1, BLOCK_LEN, NH), :]
            else:
                grad = dq * (1.0 / math.sqrt(HEAD))
            unit = piece * scale
            pieces.append(scale * (grad - unit * jnp.sum(grad * unit, axis=1, keepdims=True)))
        for j in range(NH):
            pieces.append(weave[2 * h + 1, pl.ds(j, BLOCK_LEN, NH), :])
        dconv = jnp.concatenate(pieces, axis=1) * (sig * (1.0 + conv * (1.0 - sig)))
        ext = proj_ref[pl.ds(base, BLOCK_LEN + HALO), cols].astype(F32)
        gw_ref[0:1, cols] += jnp.sum(dconv * ext[HALO:], axis=0, keepdims=True)
        zeros = jnp.zeros((8, WIDE), F32)
        length = BLOCK_LEN + 8
        total = jnp.concatenate([zeros, dconv * w_ref[0:1, cols]], axis=0)
        for lag in range(1, CONV):
            masked = tokp[:, lag - 1 : lag] * dconv
            gw_ref[lag : lag + 1, cols] += jnp.sum(masked * lag_rows(ext, lag), axis=0, keepdims=True)
            total = total + pltpu.roll(
                jnp.concatenate([zeros, masked * w_ref[lag : lag + 1, cols]], axis=0), length - lag, 0
            )
        fixed = total[length - 8 :] + rim[:, cols]
        gproj_ref[:, cols] = jnp.concatenate([total[8 : length - 8], fixed], axis=0).astype(BF16)
        rim[:, cols] = total[:8]
        spill_ref[:, cols] = total[:8]

        @pl.when(step == 0)
        def _():
            last_ref[:, cols] = fixed


def recurrence_backward(index, maps, cots, state_in, proj_ext, conv_w, rowp, colp, tokp, grad_heads, saved, heads):
    blocks = rowp.shape[0]
    rows = blocks * BLOCK_LEN
    whole = lambda *dims: pl.BlockSpec(dims, lambda i: (0,) * len(dims))
    by_block = lambda *dims: pl.BlockSpec((1,) + dims, lambda i: (blocks - 1 - i,) + (0,) * len(dims))
    token = lambda cols: pl.BlockSpec((BLOCK_LEN, cols), lambda i: (blocks - 1 - i, 0))
    shape = lambda *dims: jax.ShapeDtypeStruct(dims, F32)
    square = (heads, ROWS, HEAD)
    return pl.pallas_call(
        functools.partial(bwd_kernel, heads),
        grid=(blocks,),
        in_specs=[
            pl.BlockSpec(memory_space=pltpu.SMEM), whole(*maps.shape), whole(*cots.shape), whole(*state_in.shape),
            whole(*proj_ext.shape), whole(*conv_w.shape),
            by_block(*rowp.shape[1:]), by_block(*colp.shape[1:]), by_block(*tokp.shape[1:]),
            token(heads * HEAD), token(heads * WIDE),
            by_block(heads, BLOCK_LEN, HEAD), by_block(*square), by_block(*square), by_block(*square),
            by_block(*square), by_block(heads, BLOCK_LEN, ROWS), by_block(heads, ROWS, 2 * HEAD),
            by_block(heads, HEAD, 2 * HEAD),
        ],
        out_specs=[
            token(heads * WIDE), whole(8, heads * WIDE), whole(8, heads * WIDE), whole(8, heads * WIDE),
            by_block(ROWS, 2 * heads), by_block(BLOCK_LEN, heads), by_block(heads, ROWS),
        ],
        out_shape=[
            jax.ShapeDtypeStruct((rows, heads * WIDE), BF16), shape(8, heads * WIDE), shape(8, heads * WIDE),
            shape(8, heads * WIDE), shape(blocks, ROWS, 2 * heads), shape(blocks, BLOCK_LEN, heads),
            shape(blocks, heads, ROWS),
        ],
        scratch_shapes=[
            pltpu.VMEM((heads, HEAD, HEAD), F32), pltpu.VMEM((2 * heads, ROWS, HEAD), F32),
            pltpu.VMEM((8, heads * WIDE), F32),
        ],
        compiler_params=pltpu.CompilerParams(vmem_limit_bytes=48 << 20),
        name="recurrence_backward",
    )(index, maps, cots, state_in, proj_ext, conv_w, rowp, colp, tokp, grad_heads, *saved)


def passed_along(x, axis, by):
    devices = lax.axis_size(axis)
    pairs = [(i, i + by) for i in range(devices) if 0 <= i + by < devices]
    return lax.ppermute(x, axis, pairs)


def rms_scale(values, gain_vec):
    return values * lax.rsqrt(jnp.mean(values * values, axis=-1, keepdims=True) + NORM_EPS) * gain_vec


def swiglu_mix(gate_values, up_values):
    return jax.nn.silu(gate_values) * up_values


def scalar_gates(scal, a_log, dt_bias):
    beta = jax.nn.sigmoid(scal[:, :, :NH])
    logs = -jnp.exp(a_log)[None, :] * jax.nn.softplus(scal[:, :, NH] + dt_bias[None, :])
    return beta, logs


def columns_to_rank(w):
    ranks = lax.axis_size("seq")
    rows, cols = w.shape[0], w.shape[1] // ranks
    swapped = lax.all_to_all(w, "seq", split_axis=1, concat_axis=0, tiled=True)
    full = lax.all_gather(swapped.reshape(ranks, rows, cols), "ctx", axis=1, tiled=True)
    return full.reshape(-1, cols)


def rows_of_rank(w):
    return lax.all_gather(w, "ctx", axis=0, tiled=True)


def sum_columns_back(grad):
    ranks, pieces = lax.axis_size("seq"), lax.axis_size("ctx")
    cols = grad.shape[1]
    mine = lax.psum_scatter(
        grad.astype(BF16).reshape(ranks, pieces, -1, cols), "ctx", scatter_dimension=1, tiled=True
    )
    return lax.all_to_all(mine.reshape(-1, cols), "seq", split_axis=0, concat_axis=1, tiled=True).astype(F32)


def sum_rows_back(grad):
    return lax.psum_scatter(grad.astype(BF16), "ctx", scatter_dimension=0, tiled=True).astype(F32)


def gather_tokens(x):
    return lax.all_gather(x, "seq", axis=0, tiled=True)


def sum_tokens(partial):
    ranks = lax.axis_size("seq")
    parts = lax.all_to_all(partial.astype(BF16).reshape(ranks, -1, partial.shape[1]), "seq", 0, 0, tiled=True)
    return jnp.sum(parts.astype(F32), axis=0)


def dot(a, b):
    return jnp.dot(a, b, preferred_element_type=F32)


def dot_t(a, b):
    return jnp.einsum("tc,dc->td", a, b, preferred_element_type=F32)


def t_dot(a, b):
    return jnp.einsum("tr,tc->rc", a, b, preferred_element_type=F32)


def local(
    block_input, teacher, valid_mask, segments, mix_proj, scalar_proj, gate_proj, out_proj, conv_weight,
    norm_attn, norm_mlp, head_gain, a_log, dt_bias, w_gate, w_up, w_down,
):
    seq_size = lax.axis_size("seq")
    heads = HEADS // seq_size
    tok_rows = block_input.shape[0]
    rows = tok_rows * seq_size
    blocks = rows // BLOCK_LEN
    token_total = segments.shape[0]
    seq_length = min(SEQ_LEN, token_total)
    index = lax.axis_index("ctx")
    rank = lax.axis_index("seq")
    head_start = rank * heads

    mix_s = columns_to_rank(mix_proj)
    scal_s = columns_to_rank(scalar_proj)
    gate_s = columns_to_rank(gate_proj)
    wg_s = columns_to_rank(w_gate)
    wu_s = columns_to_rank(w_up)
    out_s = rows_of_rank(out_proj)
    down_s = rows_of_rank(w_down)
    conv_s = rows_of_rank(conv_weight)
    norm_a = lax.all_gather(norm_attn, BOTH, axis=0, tiled=True).astype(F32)
    norm_m = lax.all_gather(norm_mlp, BOTH, axis=0, tiled=True).astype(F32)
    valid_count = jnp.maximum(lax.psum(jnp.sum(valid_mask.astype(F32)), BOTH), 1.0)

    inputs_f = block_input.astype(F32)
    normed_f, norm_in_back = jax.vjp(rms_scale, inputs_f, norm_a)
    normed = gather_tokens(normed_f.astype(BF16))
    proj = dot(normed, mix_s).astype(BF16)
    scal = dot(normed, scal_s).astype(BF16)
    gate_out = dot(normed, gate_s)

    piece_start = index * rows
    window = lax.dynamic_slice_in_dim(jnp.pad(segments, (CONV, 0)), piece_start, rows + CONV)
    place_in = (piece_start + jnp.arange(rows, dtype=jnp.int32)) % seq_length
    own_seg = window[CONV:]
    linked = [
        ((window[CONV - lag : CONV - lag + rows] == own_seg) & (place_in >= lag)).astype(F32) for lag in range(1, CONV)
    ]
    starts = 1.0 - linked[0]
    alog_heads = lax.dynamic_slice_in_dim(a_log.astype(F32), head_start, heads, 0)
    dt_heads = lax.dynamic_slice_in_dim(dt_bias.astype(F32), head_start, heads, 0)
    (beta, logs), gates_back = jax.vjp(
        scalar_gates, scal.astype(F32).reshape(rows, heads, NH + 1), alog_heads, dt_heads
    )
    lower = jnp.tril(jnp.ones((BLOCK_LEN, BLOCK_LEN), F32))
    sums = jnp.einsum(
        "ts,bsh->bth",
        lower,
        jnp.concatenate([starts[:, None], logs * (1.0 - starts)[:, None]], axis=1).reshape(blocks, BLOCK_LEN, heads + 1),
        precision=lax.Precision.HIGHEST,
    )
    tokp = jnp.concatenate([jnp.stack(linked, axis=1).reshape(blocks, BLOCK_LEN, CONV - 1), sums], axis=2)
    sums_rows = jnp.repeat(sums, NH, axis=1)
    beta_rows = jnp.swapaxes(beta, 1, 2).reshape(blocks, ROWS, heads)
    colp = jnp.concatenate(
        [sums_rows[:, :, :1], jnp.zeros_like(sums_rows[:, :, :1])]
        + [x[:, :, h : h + 1] for h in range(heads) for x in (sums_rows[:, :, 1:], beta_rows)],
        axis=2,
    )
    rowp = jnp.swapaxes(colp, 1, 2)
    conv_w = jnp.pad(jnp.flip(conv_s.astype(F32).T, 0), ((0, 8 - CONV), (0, 0)))
    tail = passed_along(proj[rows - HALO :], "ctx", 1)
    proj_ext = jnp.concatenate([tail, proj], axis=0)

    oloc, carr, final, *saved = recurrence_forward(proj_ext, conv_w, rowp, colp, tokp, heads)
    maps = lax.all_gather(final.astype(BF16), "ctx")
    gain = head_gain.astype(F32)[None, :]
    index_arr = index.reshape(1).astype(jnp.int32)
    heads_out, mixed, state_in = state_and_gate(index_arr, maps, oloc, carr, gate_out, gain, heads)

    middle = inputs_f + sum_tokens(dot(mixed, out_s))
    second_f, norm_mlp_back = jax.vjp(rms_scale, middle, norm_m)
    second = gather_tokens(second_f.astype(BF16))
    gate_values = dot(second, wg_s)
    up_values = dot(second, wu_s)
    hidden_f, swiglu_back = jax.vjp(swiglu_mix, gate_values, up_values)
    hidden = hidden_f.astype(BF16)
    final_out = middle + sum_tokens(dot(hidden, down_s))
    mask_values = valid_mask.astype(F32)
    error_rows = final_out - teacher.astype(F32)
    error_sum = jnp.sum(mask_values[:, None] * error_rows * error_rows)
    grad_final = token_total / valid_count * mask_values[:, None] * error_rows

    grad_branch = gather_tokens(grad_final.astype(BF16))
    down_grad = sum_rows_back(t_dot(hidden, grad_branch))
    grad_gate_f, grad_up_f = swiglu_back(dot_t(grad_branch, down_s))
    grad_gate = grad_gate_f.astype(BF16)
    grad_up = grad_up_f.astype(BF16)
    grad_second = sum_tokens(dot_t(grad_gate, wg_s) + dot_t(grad_up, wu_s))
    wg_grad = sum_columns_back(t_dot(second, grad_gate))
    wu_grad = sum_columns_back(t_dot(second, grad_up))
    grad_mid_norm, norm_mlp_term = norm_mlp_back(grad_second)
    grad_middle = grad_final + grad_mid_norm
    grad_mixed_low = gather_tokens(grad_middle.astype(BF16))
    out_grad = sum_rows_back(t_dot(mixed, grad_mixed_low))
    grad_mixed = dot_t(grad_mixed_low, out_s)

    grad_heads, grad_gate_out, gain_term, cot = gate_back(grad_mixed, heads_out, gate_out, gain, carr, heads)
    cots = lax.all_gather(cot.astype(BF16), "ctx")
    grad_proj, last_rows, spill, gw, gcol, gtok, grow = recurrence_backward(
        index_arr, maps, cots, state_in, proj_ext, conv_w, rowp, colp, tokp, grad_heads, saved, heads
    )
    rim_back = passed_along(spill, "ctx", -1)
    grad_proj = lax.dynamic_update_slice_in_dim(grad_proj, (last_rows + rim_back).astype(BF16), rows - 8, 0)
    grad_beta = jnp.swapaxes(gcol[:, :, 0::2].reshape(rows, NH, heads), 1, 2)
    grad_cum = jnp.sum(
        (gcol[:, :, 1::2] - jnp.swapaxes(grow, 1, 2)).reshape(blocks, BLOCK_LEN, NH, heads), axis=2
    ) + gtok
    grad_logs = jnp.einsum("ts,bth->bsh", lower, grad_cum, precision=lax.Precision.HIGHEST).reshape(rows, heads)
    grad_scal_f, grad_alog, grad_dt = gates_back((grad_beta, grad_logs * (1.0 - starts)[:, None]))
    grad_scal = grad_scal_f.reshape(rows, heads * (NH + 1)).astype(BF16)

    grad_normed = sum_tokens(
        dot_t(grad_proj, mix_s) + dot_t(grad_scal, scal_s) + dot_t(grad_gate_out, gate_s)
    )
    grad_in_norm, norm_attn_term = norm_in_back(grad_normed)
    input_grad = grad_middle + grad_in_norm
    mix_grad = sum_columns_back(t_dot(normed, grad_proj))
    scal_grad = sum_columns_back(t_dot(normed, grad_scal))
    gate_grad = sum_columns_back(t_dot(normed, grad_gate_out))
    conv_grad = lax.psum_scatter(jnp.flip(gw[:CONV], 0).T, "ctx", scatter_dimension=0, tiled=True)
    pick = (jnp.arange(HEADS)[None, :] == head_start + jnp.arange(heads)[:, None]).astype(F32)
    small = jnp.concatenate(
        [
            gain_term[0], jnp.sum(grad_alog[:, None] * pick, axis=0), jnp.sum(grad_dt[:, None] * pick, axis=0),
            error_sum[None], norm_attn_term, norm_mlp_term,
        ]
    )
    small = lax.psum(small, BOTH)
    mean_loss = small[HEAD + 2 * HEADS] / (D * valid_count)
    norm_start = HEAD + 2 * HEADS + 1
    own = norm_attn.shape[0]
    place = (rank * lax.axis_size("ctx") + index) * own
    return (
        final_out.astype(BF16),
        mean_loss,
        input_grad,
        mix_grad,
        scal_grad,
        gate_grad,
        out_grad,
        conv_grad,
        lax.dynamic_slice_in_dim(small, norm_start + place, own),
        lax.dynamic_slice_in_dim(small, norm_start + D + place, own),
        small[:HEAD],
        small[HEAD : HEAD + HEADS],
        small[HEAD + HEADS : HEAD + 2 * HEADS],
        wg_grad,
        wu_grad,
        down_grad,
    )


def solution(mesh):
    tokens, vector, matrix = P(("ctx", "seq"), None), P(BOTH), P(BOTH, None)
    in_specs = (
        tokens, tokens, P(("ctx", "seq")), P(), matrix, matrix, matrix, matrix, matrix, vector, vector,
        P(), P(), P(), matrix, matrix, matrix,
    )
    out_specs = (
        tokens, P(), tokens, matrix, matrix, matrix, matrix, matrix, vector, vector, P(), P(), P(),
        matrix, matrix, matrix,
    )
    return jax.shard_map(local, mesh=mesh, in_specs=in_specs, out_specs=out_specs, check_vma=False)
```

```python
import functools
import math

import jax
import jax.numpy as jnp
from jax import lax
from jax.experimental import pallas as pl
from jax.experimental.pallas import tpu as pltpu
from jax.sharding import PartitionSpec as P

D = 1024
HEADS = 8
HEAD = 128
NH = 2
FF = 2816
BLOCK_LEN = 64
ROWS = BLOCK_LEN * NH
CONV = 4
SEQ_LEN = 32768
WIDE = (1 + 2 * NH) * HEAD
HALO = 16
NORM_EPS = 1e-06
F32 = jnp.float32
BF16 = jnp.bfloat16
BOTH = ("seq", "ctx")
MESH = pl.DeviceIdType.MESH


def split_bf16(x):
    if x.dtype == BF16:
        return x, None
    high = x.astype(BF16)
    return high, (x - high.astype(F32)).astype(BF16)


def mm(a, b, ca=1, cb=0, passes=3):
    def one(x, y):
        return lax.dot_general(x, y, (((ca,), (cb,)), ((), ())), preferred_element_type=F32)

    if passes == 1:
        return one(a.astype(BF16), b.astype(BF16))
    ah, al = split_bf16(a)
    bh, bl = split_bf16(b)
    total = one(ah, bh)
    if bl is not None:
        total = total + one(ah, bl)
    if al is not None:
        total = total + one(al, bh)
    return total


def iota(shape, axis):
    return lax.broadcasted_iota(jnp.int32, shape, axis)


def unit_lower_inverse(a):
    n = a.shape[0]
    ri, ci = iota((n, n), 0), iota((n, n), 1)
    own = jnp.where(ri // 8 == ci // 8, a, 0.0)
    pick = (iota((n, 8), 0) % 8 == iota((n, 8), 1)).astype(BF16)
    small = mm(own, pick).reshape(n // 8, 8, 8)
    inv = (ri == ci).astype(F32).reshape(n // 8, 8, n)
    for j in range(7):
        inv = inv - small[:, :, j : j + 1] * inv[:, j : j + 1, :]
    inv = inv.reshape(n, n)
    size = 8
    while size < n:
        off = (ri // (2 * size) == ci // (2 * size)) & (ri // size != ci // size)
        inv = inv - mm(inv, mm(jnp.where(off, a, 0.0), inv))
        size *= 2
    return inv


def decays(rowp, colp, tokp, h):
    cs_row, g_row = rowp[0:1, :], rowp[2 + 2 * h : 3 + 2 * h, :]
    cs_col, g_col = colp[:, 0:1], colp[:, 2 + 2 * h : 3 + 2 * h]
    cs_tok, g_tok = tokp[:, 3:4], tokp[:, 4 + h : 5 + h]
    beta = colp[:, 3 + 2 * h : 4 + 2 * h]
    ri, ci = iota((ROWS, ROWS), 0), iota((ROWS, ROWS), 1)
    strict = (ri > ci) & (cs_col == cs_row)
    decay = jnp.where(strict, jnp.exp(jnp.where(strict, g_col - g_row, 0.0)), 0.0)
    rt, ct = iota((BLOCK_LEN, ROWS), 0), iota((BLOCK_LEN, ROWS), 1)
    seen = (rt * NH + NH - 1 >= ct) & (cs_tok == cs_row)
    qdecay = jnp.where(seen, jnp.exp(jnp.where(seen, g_tok - g_row, 0.0)), 0.0)
    carry = jnp.where(cs_col == 0.0, jnp.exp(g_col), 0.0)
    qcarry = jnp.where(cs_tok == 0.0, jnp.exp(g_tok), 0.0)
    cs_last, g_last = cs_row[:, ROWS - 1 :], g_row[:, ROWS - 1 :]
    same = cs_col == cs_last
    dlast = jnp.where(same, jnp.exp(jnp.where(same, g_last - g_col, 0.0)), 0.0)
    clast = jnp.where(cs_last == 0.0, jnp.exp(g_last), 0.0)
    return beta, decay, qdecay, carry, qcarry, dlast, clast


def lag_rows(ext, lag):
    moved = pltpu.roll(ext, lag, 0) if lag else ext
    return moved[HALO:]


def fwd_kernel(
    heads, proj_ref, w_ref, rowp_ref, colp_ref, tokp_ref,
    oloc_ref, carr_ref, fin_ref, conv_ref, q_ref, k_ref, v_ref, t_ref, kk_ref, at_ref, uw_ref, pl_ref,
    state, weave,
):
    step = pl.program_id(0)
    eye = (iota((HEAD, HEAD), 0) == iota((HEAD, HEAD), 1)).astype(F32)

    @pl.when(step == 0)
    def _():
        for h in range(heads):
            state[h, :, :HEAD] = eye
            state[h, :, HEAD:] = jnp.zeros((HEAD, HEAD), F32)

    base = pl.multiple_of(step * BLOCK_LEN, BLOCK_LEN)
    rowp, colp, tokp = rowp_ref[0], colp_ref[0], tokp_ref[0]
    for h in range(heads):
        cols = slice(h * WIDE, (h + 1) * WIDE)
        ext = proj_ref[pl.ds(base, BLOCK_LEN + HALO), cols].astype(F32)
        conv = ext[HALO:] * w_ref[0:1, cols]
        for lag in range(1, CONV):
            conv = conv + tokp[:, lag - 1 : lag] * lag_rows(ext, lag) * w_ref[lag : lag + 1, cols]
        conv_ref[:, cols] = conv
        act = conv * jax.nn.sigmoid(conv)
        unit = []
        for part in range(1 + NH):
            piece = act[:, part * HEAD : (part + 1) * HEAD]
            unit.append(piece * lax.rsqrt(jnp.sum(piece * piece, axis=1, keepdims=True) + NORM_EPS))
        query = unit[0] * (1.0 / math.sqrt(HEAD))
        for j in range(NH):
            weave[2 * h, pl.ds(j, BLOCK_LEN, NH), :] = unit[1 + j]
            weave[2 * h + 1, pl.ds(j, BLOCK_LEN, NH), :] = act[:, (1 + NH + j) * HEAD : (2 + NH + j) * HEAD]
        keys, values = weave[2 * h], weave[2 * h + 1]
        beta, decay, qdecay, carry, qcarry, dlast, clast = decays(rowp, colp, tokp, h)
        kk = decay * mm(keys, keys, 1, 1)
        inv = unit_lower_inverse(beta * kk)
        uw = mm(inv, jnp.concatenate([beta * values, (beta * carry) * keys], axis=1))
        attn = qdecay * mm(query, keys, 1, 1)
        auw = mm(attn, uw)
        nm = mm(dlast * keys, uw, 0, 0)
        before = state[h]
        out = mm(qcarry * query - auw[:, HEAD:], before)
        hc = slice(h * HEAD, (h + 1) * HEAD)
        carr_ref[:, hc] = out[:, :HEAD]
        oloc_ref[:, hc] = out[:, HEAD:] + auw[:, :HEAD]
        after = mm(clast * eye - nm[:, HEAD:], before)
        state[h, :, :HEAD] = after[:, :HEAD]
        state[h, :, HEAD:] = after[:, HEAD:] + nm[:, :HEAD]
        q_ref[0, h] = query
        k_ref[0, h] = keys
        v_ref[0, h] = values
        t_ref[0, h] = inv
        kk_ref[0, h] = kk
        at_ref[0, h] = attn
        uw_ref[0, h] = uw
        pl_ref[0, h] = before
    fin_ref[...] = state[...]


def recurrence_forward(proj_ext, conv_w, rowp, colp, tokp, heads):
    blocks = rowp.shape[0]
    rows = blocks * BLOCK_LEN
    whole = lambda *dims: pl.BlockSpec(dims, lambda i: (0,) * len(dims))
    by_block = lambda *dims: pl.BlockSpec((1,) + dims, lambda i: (i,) + (0,) * len(dims))
    token = lambda cols: pl.BlockSpec((BLOCK_LEN, cols), lambda i: (i, 0))
    shape = lambda *dims: jax.ShapeDtypeStruct(dims, F32)
    square = (heads, ROWS, HEAD)
    return pl.pallas_call(
        functools.partial(fwd_kernel, heads),
        grid=(blocks,),
        in_specs=[
            whole(*proj_ext.shape), whole(*conv_w.shape),
            by_block(*rowp.shape[1:]), by_block(*colp.shape[1:]), by_block(*tokp.shape[1:]),
        ],
        out_specs=[
            token(heads * HEAD), token(heads * HEAD), whole(heads, HEAD, 2 * HEAD), token(heads * WIDE),
            by_block(heads, BLOCK_LEN, HEAD), by_block(*square), by_block(*square), by_block(*square),
            by_block(*square), by_block(heads, BLOCK_LEN, ROWS), by_block(heads, ROWS, 2 * HEAD),
            by_block(heads, HEAD, 2 * HEAD),
        ],
        out_shape=[
            shape(rows, heads * HEAD), shape(rows, heads * HEAD), shape(heads, HEAD, 2 * HEAD), shape(rows, heads * WIDE),
            shape(blocks, heads, BLOCK_LEN, HEAD), shape(blocks, *square), shape(blocks, *square), shape(blocks, *square),
            shape(blocks, *square), shape(blocks, heads, BLOCK_LEN, ROWS), shape(blocks, heads, ROWS, 2 * HEAD),
            shape(blocks, heads, HEAD, 2 * HEAD),
        ],
        scratch_shapes=[pltpu.VMEM((heads, HEAD, 2 * HEAD), F32), pltpu.VMEM((2 * heads, ROWS, HEAD), F32)],
        compiler_params=pltpu.CompilerParams(vmem_limit_bytes=40 << 20),
        name="recurrence_forward",
    )(proj_ext, conv_w, rowp, colp, tokp)


def state_kernel(heads, index_ref, maps_ref, oloc_ref, carr_ref, gate_ref, gain_ref, heads_ref, mixed_ref, state_ref):
    def hop(k, states):
        return tuple(
            mm(maps_ref[k, h, :, :HEAD], states[h]) + maps_ref[k, h, :, HEAD:].astype(F32) for h in range(heads)
        )

    states = lax.fori_loop(0, index_ref[0], hop, tuple(jnp.zeros((HEAD, HEAD), F32) for _ in range(heads)))
    for h in range(heads):
        hc = slice(h * HEAD, (h + 1) * HEAD)
        state_ref[h] = states[h]
        out = (oloc_ref[:, hc] + mm(carr_ref[:, hc], states[h])).astype(BF16)
        heads_ref[:, hc] = out
        wide = out.astype(F32)
        gate = gate_ref[:, hc]
        scaled = wide * lax.rsqrt(jnp.mean(wide * wide, axis=1, keepdims=True) + NORM_EPS) * gain_ref[...]
        mixed_ref[:, hc] = (scaled * (gate * jax.nn.sigmoid(gate))).astype(BF16)


def state_and_gate(index, maps, oloc, carr, gate_out, gain, heads):
    rows = oloc.shape[0]
    vmem = pl.BlockSpec(memory_space=pltpu.VMEM)
    return pl.pallas_call(
        functools.partial(state_kernel, heads),
        in_specs=[pl.BlockSpec(memory_space=pltpu.SMEM)] + [vmem] * 5,
        out_specs=[vmem] * 3,
        out_shape=[
            jax.ShapeDtypeStruct((rows, heads * HEAD), BF16),
            jax.ShapeDtypeStruct((rows, heads * HEAD), BF16),
            jax.ShapeDtypeStruct((heads, HEAD, HEAD), F32),
        ],
        compiler_params=pltpu.CompilerParams(vmem_limit_bytes=40 << 20),
        name="state_and_gate",
    )(index, maps, oloc, carr, gate_out, gain)


def seq_barrier(size):
    me = lax.axis_index("seq")
    barrier = pltpu.get_barrier_semaphore()

    def greet(i, carry):
        pl.semaphore_signal(barrier, inc=1, device_id={"seq": lax.rem(me + i, size)}, device_id_type=MESH)
        return carry

    lax.fori_loop(1, size, greet, 0)
    pl.semaphore_wait(barrier, size - 1)


def middle_kernel(
    size, heads, scale_ref,
    x_ref, teach_ref, mask_ref, norm_ref, gain_ref, mixed_ref, heads_ref, gate_ref, carr_ref,
    wout_ref, wg_ref, wu_ref, wd_ref,
    final_ref, gmid_ref, ghead_ref, ggate_ref, cot_ref, ggain_ref, gnorm_ref, loss_ref,
    gout_ref, gwg_ref, gwu_ref, gwd_ref,
    second, branch, low, sent, got, own, mid, gfin, gates, ups, hidden, ggates, gups, send_sem, recv_sem,
):
    me = lax.axis_index("seq")
    count = x_ref.shape[0]
    seq_barrier(size)

    def dot(a, b, ca=1, cb=0):
        return lax.dot_general(a, b, (((ca,), (cb,)), ((), ())), preferred_element_type=F32)

    def rows(q):
        return pl.ds(pl.multiple_of(q * count, count), count)

    def part_copy(phase, i):
        return pltpu.make_async_remote_copy(
            sent.at[phase, i - 1], got.at[phase, i - 1], send_sem.at[phase, i - 1], recv_sem.at[phase, i - 1],
            device_id={"seq": lax.rem(me + i, size)}, device_id_type=MESH,
        )

    def block_copy(buffer, phase, i, owner):
        return pltpu.make_async_remote_copy(
            buffer.at[rows(owner)], buffer.at[rows(owner)], send_sem.at[phase, i - 1], recv_sem.at[phase, i - 1],
            device_id={"seq": lax.rem(me + i, size)}, device_id_type=MESH,
        )

    def give_part(phase, i, part):
        @pl.when(i > 0)
        def _():
            sent[phase, i - 1] = part.astype(BF16)
            part_copy(phase, i).start()

        @pl.when(i == 0)
        def _():
            own[...] = part

    def take_parts(phase):
        def add(i, total):
            part_copy(phase, i).wait_recv()
            return total + got[phase, i - 1].astype(F32)

        return lax.fori_loop(1, size, add, own[...])

    def give_block(buffer, phase, value):
        buffer[rows(me)] = value

        def send(i, carry):
            block_copy(buffer, phase, i, me).start()
            return carry

        lax.fori_loop(1, size, send, 0)

    def take_block(buffer, phase, i):
        q = lax.rem(me + size - i, size)

        @pl.when(i > 0)
        def _():
            block_copy(buffer, phase, i, q).wait_recv()

        return q

    def out_part(k, carry):
        i = lax.rem(k + 1, size)
        give_part(0, i, dot(mixed_ref[rows(lax.rem(me + i, size))], wout_ref[...]))
        return carry

    lax.fori_loop(0, size, out_part, 0)
    middle = x_ref[...].astype(F32) + take_parts(0)
    mid[...] = middle
    inv = lax.rsqrt(jnp.mean(middle * middle, axis=1, keepdims=True) + NORM_EPS)
    give_block(second, 3, (middle * inv * norm_ref[...]).astype(BF16))

    def feed(i, carry):
        q = take_block(second, 3, i)
        here = second[rows(q)]
        gate = dot(here, wg_ref[...])
        up = dot(here, wu_ref[...])
        gates[rows(q)] = gate
        ups[rows(q)] = up
        hid = (gate * jax.nn.sigmoid(gate) * up).astype(BF16)
        hidden[rows(q)] = hid
        give_part(1, lax.rem(size - i, size), dot(hid, wd_ref[...]))
        return carry

    lax.fori_loop(0, size, feed, 0)
    final = mid[...] + take_parts(1)
    final_ref[...] = final.astype(BF16)
    error = final - teach_ref[...].astype(F32)
    weighted = mask_ref[...] * error
    loss_ref[...] = jnp.broadcast_to(
        jnp.sum(jnp.sum(weighted * error, axis=1, keepdims=True), axis=0, keepdims=True), loss_ref.shape
    )
    grad_final = scale_ref[0, 0] * weighted
    gfin[...] = grad_final
    give_block(branch, 4, grad_final.astype(BF16))

    def feed_back(i, carry):
        q = take_block(branch, 4, i)
        ghid = dot(branch[rows(q)], wd_ref[...], 1, 1)
        gate = gates[rows(q)]
        sig = jax.nn.sigmoid(gate)
        silu = gate * sig
        ggate = (ghid * ups[rows(q)] * (sig + silu * (1.0 - sig))).astype(BF16)
        gup = (ghid * silu).astype(BF16)
        ggates[rows(q)] = ggate
        gups[rows(q)] = gup
        give_part(2, lax.rem(size - i, size), dot(ggate, wg_ref[...], 1, 1) + dot(gup, wu_ref[...], 1, 1))
        return carry

    lax.fori_loop(0, size, feed_back, 0)
    gwd_ref[...] = dot(hidden[...], branch[...], 0, 0).astype(BF16)
    gwg_ref[...] = dot(second[...], ggates[...], 0, 0).astype(BF16)
    gwu_ref[...] = dot(second[...], gups[...], 0, 0).astype(BF16)
    gsecond = take_parts(2)
    middle = mid[...]
    inv = lax.rsqrt(jnp.mean(middle * middle, axis=1, keepdims=True) + NORM_EPS)
    unit = middle * inv
    gnorm_ref[...] = jnp.sum(gsecond * unit, axis=0, keepdims=True)
    down = gsecond * norm_ref[...]
    gmid = gfin[...] + inv * (down - unit * jnp.mean(down * unit, axis=1, keepdims=True))
    gmid_ref[...] = gmid
    give_block(low, 5, gmid.astype(BF16))
    ggain_ref[...] = jnp.zeros_like(ggain_ref)
    cot_ref[...] = jnp.zeros_like(cot_ref)

    def out_back(i, carry):
        q = take_block(low, 5, i)
        gmixed = dot(low[rows(q)], wout_ref[...], 1, 1)
        gain = gain_ref[...]
        for h in range(heads):
            hc = slice(h * HEAD, (h + 1) * HEAD)
            x = heads_ref[rows(q), hc].astype(F32)
            gate = gate_ref[rows(q), hc]
            grad = gmixed[:, hc]
            inv = lax.rsqrt(jnp.mean(x * x, axis=1, keepdims=True) + NORM_EPS)
            sig = jax.nn.sigmoid(gate)
            silu = gate * sig
            unit = x * inv
            ggate_ref[rows(q), hc] = (grad * unit * gain * (sig + silu * (1.0 - sig))).astype(BF16)
            weighted = grad * silu
            ggain_ref[...] += jnp.sum(weighted * unit, axis=0, keepdims=True)
            down = weighted * gain
            ghead = (inv * (down - unit * jnp.mean(down * unit, axis=1, keepdims=True))).astype(BF16)
            ghead_ref[rows(q), hc] = ghead
            cot_ref[h] += mm(carr_ref[rows(q), hc], ghead, 0, 0)
        return carry

    lax.fori_loop(0, size, out_back, 0)
    gout_ref[...] = dot(mixed_ref[...], low[...], 0, 0).astype(BF16)

    def sent_all(i, carry):
        for phase in range(3):
            part_copy(phase, i).wait_send()
        block_copy(second, 3, i, me).wait_send()
        block_copy(branch, 4, i, me).wait_send()
        block_copy(low, 5, i, me).wait_send()
        return carry

    lax.fori_loop(1, size, sent_all, 0)


def middle_part(size, heads, scale, x, teacher, mask, norm_m, gain, mixed, heads_out, gate_out, carr, wout, wg, wu, wd):
    count = x.shape[0]
    rows = count * size
    inner = wg.shape[1]
    vmem = pl.BlockSpec(memory_space=pltpu.VMEM)
    out = lambda dims, kind: jax.ShapeDtypeStruct(dims, kind)
    return pl.pallas_call(
        functools.partial(middle_kernel, size, heads),
        in_specs=[pl.BlockSpec(memory_space=pltpu.SMEM)] + [vmem] * 13,
        out_specs=[vmem] * 12,
        out_shape=[
            out((count, D), BF16), out((count, D), F32),
            out((rows, heads * HEAD), BF16), out((rows, heads * HEAD), BF16), out((heads, HEAD, HEAD), F32),
            out((1, HEAD), F32), out((1, D), F32), out((8, HEAD), F32),
            out((heads * HEAD, D), BF16), out((D, inner), BF16), out((D, inner), BF16), out((inner, D), BF16),
        ],
        scratch_shapes=[
            pltpu.VMEM((rows, D), BF16), pltpu.VMEM((rows, D), BF16), pltpu.VMEM((rows, D), BF16),
            pltpu.VMEM((3, size - 1, count, D), BF16), pltpu.VMEM((3, size - 1, count, D), BF16),
            pltpu.VMEM((count, D), F32), pltpu.VMEM((count, D), F32), pltpu.VMEM((count, D), F32),
            pltpu.VMEM((rows, inner), F32), pltpu.VMEM((rows, inner), F32), pltpu.VMEM((rows, inner), BF16),
            pltpu.VMEM((rows, inner), BF16), pltpu.VMEM((rows, inner), BF16),
            pltpu.SemaphoreType.DMA((6, size - 1)), pltpu.SemaphoreType.DMA((6, size - 1)),
        ],
        compiler_params=pltpu.CompilerParams(
            vmem_limit_bytes=56 << 20, collective_id=1, has_side_effects=True
        ),
        name="middle_part",
    )(scale, x, teacher, mask, norm_m, gain, mixed, heads_out, gate_out, carr, wout, wg, wu, wd)


def bwd_kernel(
    heads, index_ref, maps_ref, cots_ref, sin_ref, proj_ref, w_ref, rowp_ref, colp_ref, tokp_ref,
    go_ref, conv_ref, q_ref, k_ref, v_ref, t_ref, kk_ref, at_ref, uw_ref, pl_ref,
    gproj_ref, last_ref, spill_ref, gw_ref, gcol_ref, gtok_ref, grow_ref,
    dstate, weave, rim,
):
    step = pl.program_id(0)
    block = pl.num_programs(0) - 1 - step

    @pl.when(step == 0)
    def _():
        pieces = maps_ref.shape[0]

        def hop(i, states):
            k = pieces - 1 - i
            return tuple(
                mm(maps_ref[k, h, :, :HEAD], states[h], 0, 0) + cots_ref[k, h].astype(F32) for h in range(heads)
            )

        found = lax.fori_loop(
            0, pieces - 1 - index_ref[0], hop, tuple(jnp.zeros((HEAD, HEAD), F32) for _ in range(heads))
        )
        for h in range(heads):
            dstate[h] = found[h]
        rim[...] = jnp.zeros_like(rim)
        gw_ref[...] = jnp.zeros_like(gw_ref)

    base = pl.multiple_of(block * BLOCK_LEN, BLOCK_LEN)
    rowp, colp, tokp = rowp_ref[0], colp_ref[0], tokp_ref[0]
    last_row = iota((ROWS, 1), 0) == ROWS - 1
    for h in range(heads):
        cols = slice(h * WIDE, (h + 1) * WIDE)
        hc = slice(h * HEAD, (h + 1) * HEAD)
        beta, decay, qdecay, carry, qcarry, dlast, clast = decays(rowp, colp, tokp, h)
        go = go_ref[:, hc]
        query, keys, values = q_ref[0, h], k_ref[0, h], v_ref[0, h]
        inv, kk, attn, uw = t_ref[0, h], kk_ref[0, h], at_ref[0, h], uw_ref[0, h]
        dnext = dstate[h]
        state = mm(pl_ref[0, h, :, :HEAD], sin_ref[h]) + pl_ref[0, h, :, HEAD:]
        both = mm(jnp.concatenate([keys, uw[:, HEAD:]], axis=0), state)
        ks = both[:ROWS]
        upd = uw[:, :HEAD] - both[ROWS:]
        dupd = mm(attn, go, 0, 0) + dlast * mm(keys, dnext)
        dx = mm(inv, dupd, 0, 0)
        dv = beta * dx
        dy = -(carry * dv)
        go32 = go.astype(F32)
        outer = mm(jnp.concatenate([go32, dx], axis=0), upd, 1, 1)
        dattn, da = outer[:BLOCK_LEN], -outer[BLOCK_LEN:]
        dkd = mm(upd, dnext, 1, 1)
        right = mm(jnp.concatenate([go32, dy], axis=0), state, 1, 1)
        gos = right[:BLOCK_LEN]
        e = beta * da * decay
        f = dattn * qdecay
        ef = jnp.concatenate([f, e], axis=0)
        efk = mm(ef, keys)
        dq = qcarry * gos + efk[:BLOCK_LEN]
        dk = (
            right[BLOCK_LEN:]
            + dlast * dkd
            + efk[BLOCK_LEN:]
            + mm(ef, jnp.concatenate([query, keys], axis=0), 0, 0)
        )
        dstate[h] = clast * dnext + mm(
            jnp.concatenate([qcarry * query, keys], axis=0), jnp.concatenate([go32, dy], axis=0), 0, 0
        )
        dakk = da * kk
        z1 = beta * dakk
        z2 = dattn * attn
        dbeta = jnp.sum(dx * (values - carry * ks), axis=1, keepdims=True) + jnp.sum(dakk, axis=1, keepdims=True)
        dlk = dlast * jnp.sum(dkd * keys, axis=1, keepdims=True)
        tail = jnp.sum(dlk, axis=0, keepdims=True) + clast * jnp.sum(
            jnp.sum(state * dnext, axis=1, keepdims=True), axis=0, keepdims=True
        )
        dgrow = jnp.sum(z1, axis=1, keepdims=True) + jnp.sum(dy * ks, axis=1, keepdims=True) - dlk
        dgrow = dgrow + jnp.where(last_row, tail, 0.0)
        gcol_ref[0, :, 2 * h : 2 * h + 1] = dbeta
        gcol_ref[0, :, 2 * h + 1 : 2 * h + 2] = dgrow
        gtok_ref[0, :, h : h + 1] = jnp.sum(z2, axis=1, keepdims=True) + qcarry * jnp.sum(
            query * gos, axis=1, keepdims=True
        )
        grow_ref[0, h : h + 1, :] = jnp.sum(z1, axis=0, keepdims=True) + jnp.sum(z2, axis=0, keepdims=True)
        weave[2 * h] = dk
        weave[2 * h + 1] = dv
        conv = conv_ref[:, cols]
        sig = jax.nn.sigmoid(conv)
        act = conv * sig
        pieces = []
        for part in range(1 + NH):
            piece = act[:, part * HEAD : (part + 1) * HEAD]
            scale = lax.rsqrt(jnp.sum(piece * piece, axis=1, keepdims=True) + NORM_EPS)
            if part:
                grad = weave[2 * h, pl.ds(part - 1, BLOCK_LEN, NH), :]
            else:
                grad = dq * (1.0 / math.sqrt(HEAD))
            unit = piece * scale
            pieces.append(scale * (grad - unit * jnp.sum(grad * unit, axis=1, keepdims=True)))
        for j in range(NH):
            pieces.append(weave[2 * h + 1, pl.ds(j, BLOCK_LEN, NH), :])
        dconv = jnp.concatenate(pieces, axis=1) * (sig * (1.0 + conv * (1.0 - sig)))
        ext = proj_ref[pl.ds(base, BLOCK_LEN + HALO), cols].astype(F32)
        gw_ref[0:1, cols] += jnp.sum(dconv * ext[HALO:], axis=0, keepdims=True)
        zeros = jnp.zeros((8, WIDE), F32)
        length = BLOCK_LEN + 8
        total = jnp.concatenate([zeros, dconv * w_ref[0:1, cols]], axis=0)
        for lag in range(1, CONV):
            masked = tokp[:, lag - 1 : lag] * dconv
            gw_ref[lag : lag + 1, cols] += jnp.sum(masked * lag_rows(ext, lag), axis=0, keepdims=True)
            total = total + pltpu.roll(
                jnp.concatenate([zeros, masked * w_ref[lag : lag + 1, cols]], axis=0), length - lag, 0
            )
        fixed = total[length - 8 :] + rim[:, cols]
        gproj_ref[:, cols] = jnp.concatenate([total[8 : length - 8], fixed], axis=0).astype(BF16)
        rim[:, cols] = total[:8]
        spill_ref[:, cols] = total[:8]

        @pl.when(step == 0)
        def _():
            last_ref[:, cols] = fixed


def recurrence_backward(index, maps, cots, state_in, proj_ext, conv_w, rowp, colp, tokp, grad_heads, saved, heads):
    blocks = rowp.shape[0]
    rows = blocks * BLOCK_LEN
    whole = lambda *dims: pl.BlockSpec(dims, lambda i: (0,) * len(dims))
    by_block = lambda *dims: pl.BlockSpec((1,) + dims, lambda i: (blocks - 1 - i,) + (0,) * len(dims))
    token = lambda cols: pl.BlockSpec((BLOCK_LEN, cols), lambda i: (blocks - 1 - i, 0))
    shape = lambda *dims: jax.ShapeDtypeStruct(dims, F32)
    square = (heads, ROWS, HEAD)
    return pl.pallas_call(
        functools.partial(bwd_kernel, heads),
        grid=(blocks,),
        in_specs=[
            pl.BlockSpec(memory_space=pltpu.SMEM), whole(*maps.shape), whole(*cots.shape), whole(*state_in.shape),
            whole(*proj_ext.shape), whole(*conv_w.shape),
            by_block(*rowp.shape[1:]), by_block(*colp.shape[1:]), by_block(*tokp.shape[1:]),
            token(heads * HEAD), token(heads * WIDE),
            by_block(heads, BLOCK_LEN, HEAD), by_block(*square), by_block(*square), by_block(*square),
            by_block(*square), by_block(heads, BLOCK_LEN, ROWS), by_block(heads, ROWS, 2 * HEAD),
            by_block(heads, HEAD, 2 * HEAD),
        ],
        out_specs=[
            token(heads * WIDE), whole(8, heads * WIDE), whole(8, heads * WIDE), whole(8, heads * WIDE),
            by_block(ROWS, 2 * heads), by_block(BLOCK_LEN, heads), by_block(heads, ROWS),
        ],
        out_shape=[
            jax.ShapeDtypeStruct((rows, heads * WIDE), BF16), shape(8, heads * WIDE), shape(8, heads * WIDE),
            shape(8, heads * WIDE), shape(blocks, ROWS, 2 * heads), shape(blocks, BLOCK_LEN, heads),
            shape(blocks, heads, ROWS),
        ],
        scratch_shapes=[
            pltpu.VMEM((heads, HEAD, HEAD), F32), pltpu.VMEM((2 * heads, ROWS, HEAD), F32),
            pltpu.VMEM((8, heads * WIDE), F32),
        ],
        compiler_params=pltpu.CompilerParams(vmem_limit_bytes=48 << 20),
        name="recurrence_backward",
    )(index, maps, cots, state_in, proj_ext, conv_w, rowp, colp, tokp, grad_heads, *saved)


def passed_along(x, axis, by):
    devices = lax.axis_size(axis)
    pairs = [(i, i + by) for i in range(devices) if 0 <= i + by < devices]
    return lax.ppermute(x, axis, pairs)


def rms_scale(values, gain_vec):
    return values * lax.rsqrt(jnp.mean(values * values, axis=-1, keepdims=True) + NORM_EPS) * gain_vec


def scalar_gates(scal, a_log, dt_bias):
    beta = jax.nn.sigmoid(scal[:, :, :NH])
    logs = -jnp.exp(a_log)[None, :] * jax.nn.softplus(scal[:, :, NH] + dt_bias[None, :])
    return beta, logs


def columns_to_rank(w):
    ranks = lax.axis_size("seq")
    rows, cols = w.shape[0], w.shape[1] // ranks
    swapped = lax.all_to_all(w, "seq", split_axis=1, concat_axis=0, tiled=True)
    full = lax.all_gather(swapped.reshape(ranks, rows, cols), "ctx", axis=1, tiled=True)
    return full.reshape(-1, cols)


def rows_of_rank(w):
    return lax.all_gather(w, "ctx", axis=0, tiled=True)


def sum_columns_back(grad):
    ranks, pieces = lax.axis_size("seq"), lax.axis_size("ctx")
    cols = grad.shape[1]
    mine = lax.psum_scatter(
        grad.astype(BF16).reshape(ranks, pieces, -1, cols), "ctx", scatter_dimension=1, tiled=True
    )
    return lax.all_to_all(mine.reshape(-1, cols), "seq", split_axis=0, concat_axis=1, tiled=True).astype(F32)


def sum_rows_back(grad):
    return lax.psum_scatter(grad.astype(BF16), "ctx", scatter_dimension=0, tiled=True).astype(F32)


def gather_tokens(x):
    return lax.all_gather(x, "seq", axis=0, tiled=True)


def sum_tokens(partial):
    ranks = lax.axis_size("seq")
    parts = lax.all_to_all(partial.astype(BF16).reshape(ranks, -1, partial.shape[1]), "seq", 0, 0, tiled=True)
    return jnp.sum(parts.astype(F32), axis=0)


def dot(a, b):
    return jnp.dot(a, b, preferred_element_type=F32)


def dot_t(a, b):
    return jnp.einsum("tc,dc->td", a, b, preferred_element_type=F32)


def t_dot(a, b):
    return jnp.einsum("tr,tc->rc", a, b, preferred_element_type=F32)


def local(
    block_input, teacher, valid_mask, segments, mix_proj, scalar_proj, gate_proj, out_proj, conv_weight,
    norm_attn, norm_mlp, head_gain, a_log, dt_bias, w_gate, w_up, w_down,
):
    seq_size = lax.axis_size("seq")
    heads = HEADS // seq_size
    tok_rows = block_input.shape[0]
    rows = tok_rows * seq_size
    blocks = rows // BLOCK_LEN
    token_total = segments.shape[0]
    seq_length = min(SEQ_LEN, token_total)
    index = lax.axis_index("ctx")
    rank = lax.axis_index("seq")
    head_start = rank * heads

    mix_s = columns_to_rank(mix_proj)
    scal_s = columns_to_rank(scalar_proj)
    gate_s = columns_to_rank(gate_proj)
    wg_s = columns_to_rank(w_gate)
    wu_s = columns_to_rank(w_up)
    out_s = rows_of_rank(out_proj)
    down_s = rows_of_rank(w_down)
    conv_s = rows_of_rank(conv_weight)
    norm_a = lax.all_gather(norm_attn, BOTH, axis=0, tiled=True).astype(F32)
    norm_m = lax.all_gather(norm_mlp, BOTH, axis=0, tiled=True).astype(F32)
    valid_count = jnp.maximum(lax.psum(jnp.sum(valid_mask.astype(F32)), BOTH), 1.0)

    inputs_f = block_input.astype(F32)
    normed_f, norm_in_back = jax.vjp(rms_scale, inputs_f, norm_a)
    normed = gather_tokens(normed_f.astype(BF16))
    proj = dot(normed, mix_s).astype(BF16)
    scal = dot(normed, scal_s).astype(BF16)
    gate_out = dot(normed, gate_s)

    piece_start = index * rows
    window = lax.dynamic_slice_in_dim(jnp.pad(segments, (CONV, 0)), piece_start, rows + CONV)
    place_in = (piece_start + jnp.arange(rows, dtype=jnp.int32)) % seq_length
    own_seg = window[CONV:]
    linked = [
        ((window[CONV - lag : CONV - lag + rows] == own_seg) & (place_in >= lag)).astype(F32) for lag in range(1, CONV)
    ]
    starts = 1.0 - linked[0]
    alog_heads = lax.dynamic_slice_in_dim(a_log.astype(F32), head_start, heads, 0)
    dt_heads = lax.dynamic_slice_in_dim(dt_bias.astype(F32), head_start, heads, 0)
    (beta, logs), gates_back = jax.vjp(
        scalar_gates, scal.astype(F32).reshape(rows, heads, NH + 1), alog_heads, dt_heads
    )
    lower = jnp.tril(jnp.ones((BLOCK_LEN, BLOCK_LEN), F32))
    sums = jnp.einsum(
        "ts,bsh->bth",
        lower,
        jnp.concatenate([starts[:, None], logs * (1.0 - starts)[:, None]], axis=1).reshape(blocks, BLOCK_LEN, heads + 1),
        precision=lax.Precision.HIGHEST,
    )
    tokp = jnp.concatenate([jnp.stack(linked, axis=1).reshape(blocks, BLOCK_LEN, CONV - 1), sums], axis=2)
    sums_rows = jnp.repeat(sums, NH, axis=1)
    beta_rows = jnp.swapaxes(beta, 1, 2).reshape(blocks, ROWS, heads)
    colp = jnp.concatenate(
        [sums_rows[:, :, :1], jnp.zeros_like(sums_rows[:, :, :1])]
        + [x[:, :, h : h + 1] for h in range(heads) for x in (sums_rows[:, :, 1:], beta_rows)],
        axis=2,
    )
    rowp = jnp.swapaxes(colp, 1, 2)
    conv_w = jnp.pad(jnp.flip(conv_s.astype(F32).T, 0), ((0, 8 - CONV), (0, 0)))
    tail = passed_along(proj[rows - HALO :], "ctx", 1)
    proj_ext = jnp.concatenate([tail, proj], axis=0)

    oloc, carr, final, *saved = recurrence_forward(proj_ext, conv_w, rowp, colp, tokp, heads)
    maps = lax.all_gather(final.astype(BF16), "ctx")
    gain = head_gain.astype(F32)[None, :]
    index_arr = index.reshape(1).astype(jnp.int32)
    heads_out, mixed, state_in = state_and_gate(index_arr, maps, oloc, carr, gate_out, gain, heads)

    scale = (token_total / valid_count).reshape(1, 1)
    mask_values = valid_mask.astype(F32)[:, None]
    (
        final_out, grad_middle, grad_heads, grad_gate_out, cot, gain_term, norm_mlp_term, loss,
        out_grad, wg_grad, wu_grad, down_grad,
    ) = middle_part(
        seq_size, heads, scale, block_input, teacher, mask_values, norm_m[None, :], gain, mixed, heads_out, gate_out,
        carr, out_s, wg_s, wu_s, down_s,
    )
    error_sum = loss[0, 0]
    down_grad = sum_rows_back(down_grad)
    out_grad = sum_rows_back(out_grad)
    wg_grad = sum_columns_back(wg_grad)
    wu_grad = sum_columns_back(wu_grad)
    cots = lax.all_gather(cot.astype(BF16), "ctx")
    grad_proj, last_rows, spill, gw, gcol, gtok, grow = recurrence_backward(
        index_arr, maps, cots, state_in, proj_ext, conv_w, rowp, colp, tokp, grad_heads, saved, heads
    )
    rim_back = passed_along(spill, "ctx", -1)
    grad_proj = lax.dynamic_update_slice_in_dim(grad_proj, (last_rows + rim_back).astype(BF16), rows - 8, 0)
    grad_beta = jnp.swapaxes(gcol[:, :, 0::2].reshape(rows, NH, heads), 1, 2)
    grad_cum = jnp.sum(
        (gcol[:, :, 1::2] - jnp.swapaxes(grow, 1, 2)).reshape(blocks, BLOCK_LEN, NH, heads), axis=2
    ) + gtok
    grad_logs = jnp.einsum("ts,bth->bsh", lower, grad_cum, precision=lax.Precision.HIGHEST).reshape(rows, heads)
    grad_scal_f, grad_alog, grad_dt = gates_back((grad_beta, grad_logs * (1.0 - starts)[:, None]))
    grad_scal = grad_scal_f.reshape(rows, heads * (NH + 1)).astype(BF16)

    grad_normed = sum_tokens(
        dot_t(grad_proj, mix_s) + dot_t(grad_scal, scal_s) + dot_t(grad_gate_out, gate_s)
    )
    grad_in_norm, norm_attn_term = norm_in_back(grad_normed)
    input_grad = grad_middle + grad_in_norm
    mix_grad = sum_columns_back(t_dot(normed, grad_proj))
    scal_grad = sum_columns_back(t_dot(normed, grad_scal))
    gate_grad = sum_columns_back(t_dot(normed, grad_gate_out))
    conv_grad = lax.psum_scatter(jnp.flip(gw[:CONV], 0).T, "ctx", scatter_dimension=0, tiled=True)
    pick = (jnp.arange(HEADS)[None, :] == head_start + jnp.arange(heads)[:, None]).astype(F32)
    small = jnp.concatenate(
        [
            gain_term[0], jnp.sum(grad_alog[:, None] * pick, axis=0), jnp.sum(grad_dt[:, None] * pick, axis=0),
            error_sum[None], norm_attn_term, norm_mlp_term[0],
        ]
    )
    small = lax.psum(small, BOTH)
    mean_loss = small[HEAD + 2 * HEADS] / (D * valid_count)
    norm_start = HEAD + 2 * HEADS + 1
    own = norm_attn.shape[0]
    place = (rank * lax.axis_size("ctx") + index) * own
    return (
        final_out,
        mean_loss,
        input_grad,
        mix_grad,
        scal_grad,
        gate_grad,
        out_grad,
        conv_grad,
        lax.dynamic_slice_in_dim(small, norm_start + place, own),
        lax.dynamic_slice_in_dim(small, norm_start + D + place, own),
        small[:HEAD],
        small[HEAD : HEAD + HEADS],
        small[HEAD + HEADS : HEAD + 2 * HEADS],
        wg_grad,
        wu_grad,
        down_grad,
    )


def solution(mesh):
    tokens, vector, matrix = P(("ctx", "seq"), None), P(BOTH), P(BOTH, None)
    in_specs = (
        tokens, tokens, P(("ctx", "seq")), P(), matrix, matrix, matrix, matrix, matrix, vector, vector,
        P(), P(), P(), matrix, matrix, matrix,
    )
    out_specs = (
        tokens, P(), tokens, matrix, matrix, matrix, matrix, matrix, vector, vector, P(), P(), P(),
        matrix, matrix, matrix,
    )
    return jax.shard_map(local, mesh=mesh, in_specs=in_specs, out_specs=out_specs, check_vma=False)
```

```python
import functools
import math

import jax
import jax.numpy as jnp
from jax import lax
from jax.experimental import pallas as pl
from jax.experimental.pallas import tpu as pltpu
from jax.sharding import PartitionSpec as P

D = 1024
HEADS = 8
HEAD = 128
NH = 2
FF = 2816
BLOCK_LEN = 64
ROWS = BLOCK_LEN * NH
CONV = 4
SEQ_LEN = 32768
WIDE = (1 + 2 * NH) * HEAD
HALO = 16
NORM_EPS = 1e-06
F32 = jnp.float32
BF16 = jnp.bfloat16
BOTH = ("seq", "ctx")
MESH = pl.DeviceIdType.MESH


def split_bf16(x):
    if x.dtype == BF16:
        return x, None
    high = x.astype(BF16)
    return high, (x - high.astype(F32)).astype(BF16)


def mm(a, b, ca=1, cb=0, passes=3):
    def one(x, y):
        return lax.dot_general(x, y, (((ca,), (cb,)), ((), ())), preferred_element_type=F32)

    if passes == 1:
        return one(a.astype(BF16), b.astype(BF16))
    ah, al = split_bf16(a)
    bh, bl = split_bf16(b)
    total = one(ah, bh)
    if bl is not None:
        total = total + one(ah, bl)
    if al is not None:
        total = total + one(al, bh)
    return total


def iota(shape, axis):
    return lax.broadcasted_iota(jnp.int32, shape, axis)


def unit_lower_inverse(a):
    n = a.shape[0]
    ri, ci = iota((n, n), 0), iota((n, n), 1)
    own = jnp.where(ri // 8 == ci // 8, a, 0.0)
    pick = (iota((n, 8), 0) % 8 == iota((n, 8), 1)).astype(BF16)
    small = mm(own, pick).reshape(n // 8, 8, 8)
    inv = (ri == ci).astype(F32).reshape(n // 8, 8, n)
    for j in range(7):
        inv = inv - small[:, :, j : j + 1] * inv[:, j : j + 1, :]
    inv = inv.reshape(n, n)
    size = 8
    while size < n:
        off = (ri // (2 * size) == ci // (2 * size)) & (ri // size != ci // size)
        inv = inv - mm(inv, mm(jnp.where(off, a, 0.0), inv))
        size *= 2
    return inv


def decays(rowp, colp, tokp, h):
    cs_row, g_row = rowp[0:1, :], rowp[2 + 2 * h : 3 + 2 * h, :]
    cs_col, g_col = colp[:, 0:1], colp[:, 2 + 2 * h : 3 + 2 * h]
    cs_tok, g_tok = tokp[:, 3:4], tokp[:, 4 + h : 5 + h]
    beta = colp[:, 3 + 2 * h : 4 + 2 * h]
    ri, ci = iota((ROWS, ROWS), 0), iota((ROWS, ROWS), 1)
    strict = (ri > ci) & (cs_col == cs_row)
    decay = jnp.where(strict, jnp.exp(jnp.where(strict, g_col - g_row, 0.0)), 0.0)
    rt, ct = iota((BLOCK_LEN, ROWS), 0), iota((BLOCK_LEN, ROWS), 1)
    seen = (rt * NH + NH - 1 >= ct) & (cs_tok == cs_row)
    qdecay = jnp.where(seen, jnp.exp(jnp.where(seen, g_tok - g_row, 0.0)), 0.0)
    carry = jnp.where(cs_col == 0.0, jnp.exp(g_col), 0.0)
    qcarry = jnp.where(cs_tok == 0.0, jnp.exp(g_tok), 0.0)
    cs_last, g_last = cs_row[:, ROWS - 1 :], g_row[:, ROWS - 1 :]
    same = cs_col == cs_last
    dlast = jnp.where(same, jnp.exp(jnp.where(same, g_last - g_col, 0.0)), 0.0)
    clast = jnp.where(cs_last == 0.0, jnp.exp(g_last), 0.0)
    return beta, decay, qdecay, carry, qcarry, dlast, clast


def lag_rows(ext, lag):
    moved = pltpu.roll(ext, lag, 0) if lag else ext
    return moved[HALO:]


UP, DOWN, ACROSS = 0, 1, 2


class Line:
    def __init__(self, pieces, parts, send_sem, recv_sem, up=True, down=True):
        self.chips = pieces // 2
        self.here = lax.axis_index("ctx")
        self.chip = self.here // 2
        self.core = lax.rem(self.here, 2)
        self.other = self.here + 1 - 2 * self.core
        self.parts, self.send_sem, self.recv_sem, self.up, self.down = parts, send_sem, recv_sem, up, down

    def copies(self, chunk, way):
        target = (self.here + 2, self.here - 2, self.other)[way]
        return [
            pltpu.make_async_remote_copy(
                part(chunk), part(chunk), self.send_sem.at[n, way, chunk], self.recv_sem.at[n, chunk],
                device_id={"ctx": target}, device_id_type=MESH,
            )
            for n, part in enumerate(self.parts)
        ]

    def start(self, chunk, way):
        for copy in self.copies(chunk, way):
            copy.start()

    def arrived(self, chunk):
        for copy in self.copies(chunk, ACROSS):
            copy.wait_recv()

    def left(self, chunk, way):
        for copy in self.copies(chunk, way):
            copy.wait_send()

    def routes(self, distance, act):
        if distance == 0:
            if self.up:
                pl.when(self.chip < self.chips - 1)(lambda: act(self.here, UP))
            if self.down:
                pl.when(self.chip > 0)(lambda: act(self.here, DOWN))
            act(self.here, ACROSS)
            return
        below, above = self.here - 2 * distance, self.here + 2 * distance
        if self.up:

            @pl.when(self.chip >= distance)
            def _():
                pl.when(self.chip < self.chips - 1)(lambda: act(below, UP))
                act(below, ACROSS)

        if self.down:

            @pl.when(self.chip + distance < self.chips)
            def _():
                pl.when(self.chip > 0)(lambda: act(above, DOWN))
                act(above, ACROSS)

    def own(self):
        self.routes(0, self.start)

    def hop(self, distance):
        if self.up:
            pl.when(self.chip >= distance)(lambda: self.arrived(self.here - 2 * distance))
        if self.down:
            pl.when(self.chip + distance < self.chips)(lambda: self.arrived(self.here + 2 * distance))
        self.routes(distance, self.start)

    def finish(self):
        for chip in range(self.chips):
            needed = True
            if not self.down:
                needed = self.chip >= chip
            if not self.up:
                needed = self.chip <= chip
            pl.when(needed)(lambda chip=chip: self.arrived(2 * chip + 1 - self.core))
        for distance in range(self.chips):
            self.routes(distance, self.left)


def greet(devices, barrier):
    total = 0
    for place, there in devices:
        pl.when(there)(
            lambda place=place: pl.semaphore_signal(barrier, inc=1, device_id=place, device_id_type=MESH)
        )
        total = total + jnp.asarray(there, jnp.int32)
    return total


def line_neighbours(pieces):
    here = lax.axis_index("ctx")
    chip, core = here // 2, lax.rem(here, 2)
    return [
        ({"ctx": here + 2}, chip < pieces // 2 - 1),
        ({"ctx": here - 2}, chip > 0),
        ({"ctx": here + 1 - 2 * core}, here >= 0),
    ]


def start_kernel(
    size, pieces, x_ref, first_ref, later_ref, xfull_ref, halo_ref, full_ref, stage_ref,
    local_sem, seq_send, seq_recv, line_send, line_recv, halo_sem,
):
    me, here = lax.axis_index("seq"), lax.axis_index("ctx")
    count = x_ref.shape[0]
    core = lax.rem(here, 2)
    barrier = pltpu.get_barrier_semaphore()
    peers = [({"seq": lax.rem(me + i, size)}, here >= 0) for i in range(1, size)]
    side = [({"ctx": here + 1}, (core == 1) & (here < pieces - 1)), ({"ctx": here - 1}, (core == 0) & (here > 0))]
    total = greet(peers + line_neighbours(pieces) + side, barrier)
    pl.semaphore_wait(barrier, total)

    def rows(q):
        return pl.ds(pl.multiple_of(q * count, count), count)

    def exchange(n, i):
        q = lax.rem(me + i, size)
        source, target = [
            (first_ref.at[q], full_ref.at[me, here]), (x_ref, xfull_ref.at[rows(me)]), (later_ref.at[q], stage_ref.at[me])
        ][n]
        return pltpu.make_async_remote_copy(
            source, target, seq_send.at[n, i - 1], seq_recv.at[n, i - 1], device_id={"seq": q}, device_id_type=MESH
        )

    def own(n):
        source, target = [
            (first_ref.at[me], full_ref.at[me, here]), (x_ref, xfull_ref.at[rows(me)]), (later_ref.at[me], stage_ref.at[me])
        ][n]
        return pltpu.make_async_copy(source, target, local_sem.at[n])

    for n in range(3):
        own(n).start()
        for i in range(1, size):
            exchange(n, i).start()
    line = Line(pieces, [lambda c: full_ref.at[:, c]], line_send, line_recv)
    own(0).wait()
    for i in range(1, size):
        exchange(0, i).wait_recv()
    line.own()
    own(1).wait()
    for i in range(1, size):
        exchange(1, i).wait_recv()
    last = xfull_ref.at[pl.ds(size * count - HALO, HALO)]
    passing = pltpu.make_async_remote_copy(
        last, halo_ref, halo_sem.at[0], halo_sem.at[1], device_id={"ctx": here + 1}, device_id_type=MESH
    )
    pl.when(here < pieces - 1)(passing.start)

    @pl.when(here == 0)
    def _():
        filling = pltpu.make_async_copy(last, halo_ref, local_sem.at[3])
        filling.start()
        filling.wait()

    for distance in range(1, pieces // 2):
        line.hop(distance)
    line.finish()
    own(2).wait()
    for i in range(1, size):
        exchange(2, i).wait_recv()
    pl.when(here > 0)(passing.wait_recv)
    pl.when(here < pieces - 1)(passing.wait_send)
    for n in range(3):
        for i in range(1, size):
            exchange(n, i).wait_send()


def start_gather(size, pieces, x, first, later):
    anywhere = pl.BlockSpec(memory_space=pl.ANY)
    out = lambda *dims: jax.ShapeDtypeStruct(dims, BF16)
    return pl.pallas_call(
        functools.partial(start_kernel, size, pieces),
        in_specs=[anywhere] * 3,
        out_specs=[anywhere] * 4,
        out_shape=[
            out(x.shape[0] * size, D), out(HALO, D), out(size, pieces, *first.shape[1:]), out(*later.shape),
        ],
        scratch_shapes=[
            pltpu.SemaphoreType.DMA((4,)), pltpu.SemaphoreType.DMA((3, size - 1)), pltpu.SemaphoreType.DMA((3, size - 1)),
            pltpu.SemaphoreType.DMA((1, 3, pieces)), pltpu.SemaphoreType.DMA((1, pieces)), pltpu.SemaphoreType.DMA((2,)),
        ],
        compiler_params=pltpu.CompilerParams(
            vmem_limit_bytes=16 << 20, collective_id=2, has_side_effects=True
        ),
        name="start_gather",
    )(x, first, later)


def fwd_kernel(
    heads, pieces, proj_ref, w_ref, rowp_ref, colp_ref, tokp_ref, stage_ref, wd_ref, wo_ref,
    oloc_ref, carr_ref, sin_ref, mapsout_ref, conv_ref, q_ref, k_ref, v_ref, t_ref, kk_ref, at_ref, uw_ref, pl_ref,
    wgfull_ref, wufull_ref, wdfull_ref, wofull_ref,
    state, weave, maps, local_sem, line_send, line_recv, map_send, map_recv,
):
    step = pl.program_id(0)
    steps = pl.num_programs(0)
    here = lax.axis_index("ctx")
    weights = Line(
        pieces,
        [
            lambda c: wgfull_ref.at[:, c], lambda c: wufull_ref.at[:, c], lambda c: wdfull_ref.at[c],
            lambda c: wofull_ref.at[c],
        ],
        line_send, line_recv,
    )

    @pl.when(step == 0)
    def _():
        barrier = pltpu.get_barrier_semaphore()
        pl.semaphore_wait(barrier, greet(line_neighbours(pieces), barrier))
        owned = [
            pltpu.make_async_copy(source, target, local_sem.at[n])
            for n, (source, target) in enumerate(
                [
                    (stage_ref.at[:, 0], wgfull_ref.at[:, here]), (stage_ref.at[:, 1], wufull_ref.at[:, here]),
                    (wd_ref, wdfull_ref.at[here]), (wo_ref, wofull_ref.at[here]),
                ]
            )
        ]
        for copy in owned:
            copy.start()
        for copy in owned:
            copy.wait()
        weights.own()

    for distance in range(1, pieces // 2):
        pl.when(step == (distance * steps) // (pieces // 2))(lambda distance=distance: weights.hop(distance))

    eye = (iota((HEAD, HEAD), 0) == iota((HEAD, HEAD), 1)).astype(F32)

    @pl.when(step == 0)
    def _():
        for h in range(heads):
            state[h, :, :HEAD] = eye
            state[h, :, HEAD:] = jnp.zeros((HEAD, HEAD), F32)

    base = pl.multiple_of(step * BLOCK_LEN, BLOCK_LEN)
    rowp, colp, tokp = rowp_ref[0], colp_ref[0], tokp_ref[0]
    for h in range(heads):
        cols = slice(h * WIDE, (h + 1) * WIDE)
        ext = proj_ref[pl.ds(base, BLOCK_LEN + HALO), cols].astype(F32)
        conv = ext[HALO:] * w_ref[0:1, cols]
        for lag in range(1, CONV):
            conv = conv + tokp[:, lag - 1 : lag] * lag_rows(ext, lag) * w_ref[lag : lag + 1, cols]
        conv_ref[:, cols] = conv
        act = conv * jax.nn.sigmoid(conv)
        unit = []
        for part in range(1 + NH):
            piece = act[:, part * HEAD : (part + 1) * HEAD]
            unit.append(piece * lax.rsqrt(jnp.sum(piece * piece, axis=1, keepdims=True) + NORM_EPS))
        query = unit[0] * (1.0 / math.sqrt(HEAD))
        for j in range(NH):
            weave[2 * h, pl.ds(j, BLOCK_LEN, NH), :] = unit[1 + j]
            weave[2 * h + 1, pl.ds(j, BLOCK_LEN, NH), :] = act[:, (1 + NH + j) * HEAD : (2 + NH + j) * HEAD]
        keys, values = weave[2 * h], weave[2 * h + 1]
        beta, decay, qdecay, carry, qcarry, dlast, clast = decays(rowp, colp, tokp, h)
        kk = decay * mm(keys, keys, 1, 1)
        inv = unit_lower_inverse(beta * kk)
        uw = mm(inv, jnp.concatenate([beta * values, (beta * carry) * keys], axis=1))
        attn = qdecay * mm(query, keys, 1, 1)
        auw = mm(attn, uw)
        nm = mm(dlast * keys, uw, 0, 0)
        before = state[h]
        out = mm(qcarry * query - auw[:, HEAD:], before)
        hc = slice(h * HEAD, (h + 1) * HEAD)
        carr_ref[:, hc] = out[:, :HEAD]
        oloc_ref[:, hc] = out[:, HEAD:] + auw[:, :HEAD]
        after = mm(clast * eye - nm[:, HEAD:], before)
        state[h, :, :HEAD] = after[:, :HEAD]
        state[h, :, HEAD:] = after[:, HEAD:] + nm[:, :HEAD]
        q_ref[0, h] = query
        k_ref[0, h] = keys
        v_ref[0, h] = values
        t_ref[0, h] = inv
        kk_ref[0, h] = kk
        at_ref[0, h] = attn
        uw_ref[0, h] = uw
        pl_ref[0, h] = before

    @pl.when(step == steps - 1)
    def _():
        maps[here] = state[...].astype(BF16)
        line = Line(pieces, [lambda c: maps.at[c]], map_send, map_recv)
        line.own()
        for distance in range(1, pieces // 2):
            line.hop(distance)
        line.finish()
        weights.finish()

        def hop(k, states):
            return tuple(
                mm(maps[k, h, :, :HEAD], states[h]) + maps[k, h, :, HEAD:].astype(F32) for h in range(heads)
            )

        states = lax.fori_loop(0, here, hop, tuple(jnp.zeros((HEAD, HEAD), F32) for _ in range(heads)))
        for h in range(heads):
            sin_ref[h] = states[h]

        def keep(k, carry):
            mapsout_ref[k] = maps[k, :, :, :HEAD]
            return carry

        lax.fori_loop(0, pieces, keep, 0)


def recurrence_forward(proj_ext, conv_w, rowp, colp, tokp, stage, w_down, w_out, heads, pieces):
    blocks = rowp.shape[0]
    rows = blocks * BLOCK_LEN
    whole = lambda *dims: pl.BlockSpec(dims, lambda i: (0,) * len(dims))
    by_block = lambda *dims: pl.BlockSpec((1,) + dims, lambda i: (i,) + (0,) * len(dims))
    token = lambda cols: pl.BlockSpec((BLOCK_LEN, cols), lambda i: (i, 0))
    shape = lambda *dims: jax.ShapeDtypeStruct(dims, F32)
    low_shape = lambda *dims: jax.ShapeDtypeStruct(dims, BF16)
    anywhere = pl.BlockSpec(memory_space=pl.ANY)
    square = (heads, ROWS, HEAD)
    size = stage.shape[0]
    return pl.pallas_call(
        functools.partial(fwd_kernel, heads, pieces),
        grid=(blocks,),
        in_specs=[
            whole(*proj_ext.shape), whole(*conv_w.shape),
            by_block(*rowp.shape[1:]), by_block(*colp.shape[1:]), by_block(*tokp.shape[1:]),
            anywhere, anywhere, anywhere,
        ],
        out_specs=[
            token(heads * HEAD), token(heads * HEAD), whole(heads, HEAD, HEAD), whole(pieces, heads, HEAD, HEAD),
            token(heads * WIDE),
            by_block(heads, BLOCK_LEN, HEAD), by_block(*square), by_block(*square), by_block(*square),
            by_block(*square), by_block(heads, BLOCK_LEN, ROWS), by_block(heads, ROWS, 2 * HEAD),
            by_block(heads, HEAD, 2 * HEAD), anywhere, anywhere, anywhere, anywhere,
        ],
        out_shape=[
            shape(rows, heads * HEAD), shape(rows, heads * HEAD), shape(heads, HEAD, HEAD),
            low_shape(pieces, heads, HEAD, HEAD), shape(rows, heads * WIDE),
            shape(blocks, heads, BLOCK_LEN, HEAD), shape(blocks, *square), shape(blocks, *square), shape(blocks, *square),
            shape(blocks, *square), shape(blocks, heads, BLOCK_LEN, ROWS), shape(blocks, heads, ROWS, 2 * HEAD),
            shape(blocks, heads, HEAD, 2 * HEAD),
            low_shape(size, pieces, *stage.shape[2:]), low_shape(size, pieces, *stage.shape[2:]),
            low_shape(pieces, *w_down.shape), low_shape(pieces, *w_out.shape),
        ],
        scratch_shapes=[
            pltpu.VMEM((heads, HEAD, 2 * HEAD), F32), pltpu.VMEM((2 * heads, ROWS, HEAD), F32),
            pltpu.VMEM((pieces, heads, HEAD, 2 * HEAD), BF16),
            pltpu.SemaphoreType.DMA((4,)), pltpu.SemaphoreType.DMA((4, 3, pieces)), pltpu.SemaphoreType.DMA((4, pieces)),
            pltpu.SemaphoreType.DMA((1, 3, pieces)), pltpu.SemaphoreType.DMA((1, pieces)),
        ],
        compiler_params=pltpu.CompilerParams(
            vmem_limit_bytes=40 << 20, collective_id=3, has_side_effects=True
        ),
        name="recurrence_forward",
    )(proj_ext, conv_w, rowp, colp, tokp, stage, w_down, w_out)


def state_kernel(heads, state_ref, oloc_ref, carr_ref, gate_ref, gain_ref, heads_ref, mixed_ref):
    for h in range(heads):
        hc = slice(h * HEAD, (h + 1) * HEAD)
        out = (oloc_ref[:, hc] + mm(carr_ref[:, hc], state_ref[h])).astype(BF16)
        heads_ref[:, hc] = out
        wide = out.astype(F32)
        gate = gate_ref[:, hc]
        scaled = wide * lax.rsqrt(jnp.mean(wide * wide, axis=1, keepdims=True) + NORM_EPS) * gain_ref[...]
        mixed_ref[:, hc] = (scaled * (gate * jax.nn.sigmoid(gate))).astype(BF16)


def state_and_gate(state, oloc, carr, gate_out, gain, heads):
    rows = oloc.shape[0]
    vmem = pl.BlockSpec(memory_space=pltpu.VMEM)
    return pl.pallas_call(
        functools.partial(state_kernel, heads),
        in_specs=[vmem] * 5,
        out_specs=[vmem] * 2,
        out_shape=[
            jax.ShapeDtypeStruct((rows, heads * HEAD), BF16),
            jax.ShapeDtypeStruct((rows, heads * HEAD), BF16),
        ],
        compiler_params=pltpu.CompilerParams(vmem_limit_bytes=40 << 20),
        name="state_and_gate",
    )(state, oloc, carr, gate_out, gain)


def seq_barrier(size):
    me = lax.axis_index("seq")
    barrier = pltpu.get_barrier_semaphore()

    def greet(i, carry):
        pl.semaphore_signal(barrier, inc=1, device_id={"seq": lax.rem(me + i, size)}, device_id_type=MESH)
        return carry

    lax.fori_loop(1, size, greet, 0)
    pl.semaphore_wait(barrier, size - 1)


def middle_kernel(
    size, heads, scale_ref,
    x_ref, teach_ref, mask_ref, norm_ref, gain_ref, mixed_ref, heads_ref, gate_ref, carr_ref,
    wout_ref, wg_ref, wu_ref, wd_ref,
    final_ref, gmid_ref, ghead_ref, ggate_ref, cot_ref, ggain_ref, gnorm_ref, loss_ref,
    gout_ref, gwg_ref, gwu_ref, gwd_ref,
    second, branch, low, sent, got, own, mid, gfin, gates, ups, hidden, ggates, gups, send_sem, recv_sem,
):
    me = lax.axis_index("seq")
    count = x_ref.shape[0]
    seq_barrier(size)

    def dot(a, b, ca=1, cb=0):
        return lax.dot_general(a, b, (((ca,), (cb,)), ((), ())), preferred_element_type=F32)

    def rows(q):
        return pl.ds(pl.multiple_of(q * count, count), count)

    def part_copy(phase, i):
        return pltpu.make_async_remote_copy(
            sent.at[phase, i - 1], got.at[phase, i - 1], send_sem.at[phase, i - 1], recv_sem.at[phase, i - 1],
            device_id={"seq": lax.rem(me + i, size)}, device_id_type=MESH,
        )

    def block_copy(buffer, phase, i, owner):
        return pltpu.make_async_remote_copy(
            buffer.at[rows(owner)], buffer.at[rows(owner)], send_sem.at[phase, i - 1], recv_sem.at[phase, i - 1],
            device_id={"seq": lax.rem(me + i, size)}, device_id_type=MESH,
        )

    def give_part(phase, i, part):
        @pl.when(i > 0)
        def _():
            sent[phase, i - 1] = part.astype(BF16)
            part_copy(phase, i).start()

        @pl.when(i == 0)
        def _():
            own[...] = part

    def take_parts(phase):
        def add(i, total):
            part_copy(phase, i).wait_recv()
            return total + got[phase, i - 1].astype(F32)

        return lax.fori_loop(1, size, add, own[...])

    def give_block(buffer, phase, value):
        buffer[rows(me)] = value

        def send(i, carry):
            block_copy(buffer, phase, i, me).start()
            return carry

        lax.fori_loop(1, size, send, 0)

    def take_block(buffer, phase, i):
        q = lax.rem(me + size - i, size)

        @pl.when(i > 0)
        def _():
            block_copy(buffer, phase, i, q).wait_recv()

        return q

    def out_part(k, carry):
        i = lax.rem(k + 1, size)
        give_part(0, i, dot(mixed_ref[rows(lax.rem(me + i, size))], wout_ref[...]))
        return carry

    lax.fori_loop(0, size, out_part, 0)
    middle = x_ref[...].astype(F32) + take_parts(0)
    mid[...] = middle
    inv = lax.rsqrt(jnp.mean(middle * middle, axis=1, keepdims=True) + NORM_EPS)
    give_block(second, 3, (middle * inv * norm_ref[...]).astype(BF16))

    def feed(i, carry):
        q = take_block(second, 3, i)
        here = second[rows(q)]
        gate = dot(here, wg_ref[...])
        up = dot(here, wu_ref[...])
        gates[rows(q)] = gate
        ups[rows(q)] = up
        hid = (gate * jax.nn.sigmoid(gate) * up).astype(BF16)
        hidden[rows(q)] = hid
        give_part(1, lax.rem(size - i, size), dot(hid, wd_ref[...]))
        return carry

    lax.fori_loop(0, size, feed, 0)
    final = mid[...] + take_parts(1)
    final_ref[...] = final.astype(BF16)
    error = final - teach_ref[...].astype(F32)
    weighted = mask_ref[...] * error
    loss_ref[...] = jnp.broadcast_to(
        jnp.sum(jnp.sum(weighted * error, axis=1, keepdims=True), axis=0, keepdims=True), loss_ref.shape
    )
    grad_final = scale_ref[0, 0] * weighted
    gfin[...] = grad_final
    give_block(branch, 4, grad_final.astype(BF16))

    def feed_back(i, carry):
        q = take_block(branch, 4, i)
        ghid = dot(branch[rows(q)], wd_ref[...], 1, 1)
        gate = gates[rows(q)]
        sig = jax.nn.sigmoid(gate)
        silu = gate * sig
        ggate = (ghid * ups[rows(q)] * (sig + silu * (1.0 - sig))).astype(BF16)
        gup = (ghid * silu).astype(BF16)
        ggates[rows(q)] = ggate
        gups[rows(q)] = gup
        give_part(2, lax.rem(size - i, size), dot(ggate, wg_ref[...], 1, 1) + dot(gup, wu_ref[...], 1, 1))
        return carry

    lax.fori_loop(0, size, feed_back, 0)
    gwd_ref[...] = dot(hidden[...], branch[...], 0, 0).astype(BF16)
    gwg_ref[...] = dot(second[...], ggates[...], 0, 0).astype(BF16)
    gwu_ref[...] = dot(second[...], gups[...], 0, 0).astype(BF16)
    gsecond = take_parts(2)
    middle = mid[...]
    inv = lax.rsqrt(jnp.mean(middle * middle, axis=1, keepdims=True) + NORM_EPS)
    unit = middle * inv
    gnorm_ref[...] = jnp.sum(gsecond * unit, axis=0, keepdims=True)
    down = gsecond * norm_ref[...]
    gmid = gfin[...] + inv * (down - unit * jnp.mean(down * unit, axis=1, keepdims=True))
    gmid_ref[...] = gmid
    give_block(low, 5, gmid.astype(BF16))
    ggain_ref[...] = jnp.zeros_like(ggain_ref)
    cot_ref[...] = jnp.zeros_like(cot_ref)

    def out_back(i, carry):
        q = take_block(low, 5, i)
        gmixed = dot(low[rows(q)], wout_ref[...], 1, 1)
        gain = gain_ref[...]
        for h in range(heads):
            hc = slice(h * HEAD, (h + 1) * HEAD)
            x = heads_ref[rows(q), hc].astype(F32)
            gate = gate_ref[rows(q), hc]
            grad = gmixed[:, hc]
            inv = lax.rsqrt(jnp.mean(x * x, axis=1, keepdims=True) + NORM_EPS)
            sig = jax.nn.sigmoid(gate)
            silu = gate * sig
            unit = x * inv
            ggate_ref[rows(q), hc] = (grad * unit * gain * (sig + silu * (1.0 - sig))).astype(BF16)
            weighted = grad * silu
            ggain_ref[...] += jnp.sum(weighted * unit, axis=0, keepdims=True)
            down = weighted * gain
            ghead = (inv * (down - unit * jnp.mean(down * unit, axis=1, keepdims=True))).astype(BF16)
            ghead_ref[rows(q), hc] = ghead
            cot_ref[h] += mm(carr_ref[rows(q), hc], ghead, 0, 0)
        return carry

    lax.fori_loop(0, size, out_back, 0)
    gout_ref[...] = dot(mixed_ref[...], low[...], 0, 0).astype(BF16)

    def sent_all(i, carry):
        for phase in range(3):
            part_copy(phase, i).wait_send()
        block_copy(second, 3, i, me).wait_send()
        block_copy(branch, 4, i, me).wait_send()
        block_copy(low, 5, i, me).wait_send()
        return carry

    lax.fori_loop(1, size, sent_all, 0)


def middle_part(size, heads, scale, x, teacher, mask, norm_m, gain, mixed, heads_out, gate_out, carr, wout, wg, wu, wd):
    count = x.shape[0]
    rows = count * size
    inner = wg.shape[1]
    vmem = pl.BlockSpec(memory_space=pltpu.VMEM)
    out = lambda dims, kind: jax.ShapeDtypeStruct(dims, kind)
    return pl.pallas_call(
        functools.partial(middle_kernel, size, heads),
        in_specs=[pl.BlockSpec(memory_space=pltpu.SMEM)] + [vmem] * 13,
        out_specs=[vmem] * 12,
        out_shape=[
            out((count, D), BF16), out((count, D), F32),
            out((rows, heads * HEAD), BF16), out((rows, heads * HEAD), BF16), out((heads, HEAD, HEAD), F32),
            out((1, HEAD), F32), out((1, D), F32), out((8, HEAD), F32),
            out((heads * HEAD, D), BF16), out((D, inner), BF16), out((D, inner), BF16), out((inner, D), BF16),
        ],
        scratch_shapes=[
            pltpu.VMEM((rows, D), BF16), pltpu.VMEM((rows, D), BF16), pltpu.VMEM((rows, D), BF16),
            pltpu.VMEM((3, size - 1, count, D), BF16), pltpu.VMEM((3, size - 1, count, D), BF16),
            pltpu.VMEM((count, D), F32), pltpu.VMEM((count, D), F32), pltpu.VMEM((count, D), F32),
            pltpu.VMEM((rows, inner), F32), pltpu.VMEM((rows, inner), F32), pltpu.VMEM((rows, inner), BF16),
            pltpu.VMEM((rows, inner), BF16), pltpu.VMEM((rows, inner), BF16),
            pltpu.SemaphoreType.DMA((6, size - 1)), pltpu.SemaphoreType.DMA((6, size - 1)),
        ],
        compiler_params=pltpu.CompilerParams(
            vmem_limit_bytes=56 << 20, collective_id=1, has_side_effects=True
        ),
        name="middle_part",
    )(scale, x, teacher, mask, norm_m, gain, mixed, heads_out, gate_out, carr, wout, wg, wu, wd)


def bwd_kernel(
    heads, index_ref, maps_ref, cots_ref, sin_ref, proj_ref, w_ref, rowp_ref, colp_ref, tokp_ref,
    go_ref, conv_ref, q_ref, k_ref, v_ref, t_ref, kk_ref, at_ref, uw_ref, pl_ref,
    gproj_ref, last_ref, spill_ref, gw_ref, gcol_ref, gtok_ref, grow_ref,
    dstate, weave, rim,
):
    step = pl.program_id(0)
    block = pl.num_programs(0) - 1 - step

    @pl.when(step == 0)
    def _():
        pieces = maps_ref.shape[0]

        def hop(i, states):
            k = pieces - 1 - i
            return tuple(
                mm(maps_ref[k, h], states[h], 0, 0) + cots_ref[k, h].astype(F32) for h in range(heads)
            )

        found = lax.fori_loop(
            0, pieces - 1 - index_ref[0], hop, tuple(jnp.zeros((HEAD, HEAD), F32) for _ in range(heads))
        )
        for h in range(heads):
            dstate[h] = found[h]
        rim[...] = jnp.zeros_like(rim)
        gw_ref[...] = jnp.zeros_like(gw_ref)

    base = pl.multiple_of(block * BLOCK_LEN, BLOCK_LEN)
    rowp, colp, tokp = rowp_ref[0], colp_ref[0], tokp_ref[0]
    last_row = iota((ROWS, 1), 0) == ROWS - 1
    for h in range(heads):
        cols = slice(h * WIDE, (h + 1) * WIDE)
        hc = slice(h * HEAD, (h + 1) * HEAD)
        beta, decay, qdecay, carry, qcarry, dlast, clast = decays(rowp, colp, tokp, h)
        go = go_ref[:, hc]
        query, keys, values = q_ref[0, h], k_ref[0, h], v_ref[0, h]
        inv, kk, attn, uw = t_ref[0, h], kk_ref[0, h], at_ref[0, h], uw_ref[0, h]
        dnext = dstate[h]
        state = mm(pl_ref[0, h, :, :HEAD], sin_ref[h]) + pl_ref[0, h, :, HEAD:]
        both = mm(jnp.concatenate([keys, uw[:, HEAD:]], axis=0), state)
        ks = both[:ROWS]
        upd = uw[:, :HEAD] - both[ROWS:]
        dupd = mm(attn, go, 0, 0) + dlast * mm(keys, dnext)
        dx = mm(inv, dupd, 0, 0)
        dv = beta * dx
        dy = -(carry * dv)
        go32 = go.astype(F32)
        outer = mm(jnp.concatenate([go32, dx], axis=0), upd, 1, 1)
        dattn, da = outer[:BLOCK_LEN], -outer[BLOCK_LEN:]
        dkd = mm(upd, dnext, 1, 1)
        right = mm(jnp.concatenate([go32, dy], axis=0), state, 1, 1)
        gos = right[:BLOCK_LEN]
        e = beta * da * decay
        f = dattn * qdecay
        ef = jnp.concatenate([f, e], axis=0)
        efk = mm(ef, keys)
        dq = qcarry * gos + efk[:BLOCK_LEN]
        dk = (
            right[BLOCK_LEN:]
            + dlast * dkd
            + efk[BLOCK_LEN:]
            + mm(ef, jnp.concatenate([query, keys], axis=0), 0, 0)
        )
        dstate[h] = clast * dnext + mm(
            jnp.concatenate([qcarry * query, keys], axis=0), jnp.concatenate([go32, dy], axis=0), 0, 0
        )
        dakk = da * kk
        z1 = beta * dakk
        z2 = dattn * attn
        dbeta = jnp.sum(dx * (values - carry * ks), axis=1, keepdims=True) + jnp.sum(dakk, axis=1, keepdims=True)
        dlk = dlast * jnp.sum(dkd * keys, axis=1, keepdims=True)
        tail = jnp.sum(dlk, axis=0, keepdims=True) + clast * jnp.sum(
            jnp.sum(state * dnext, axis=1, keepdims=True), axis=0, keepdims=True
        )
        dgrow = jnp.sum(z1, axis=1, keepdims=True) + jnp.sum(dy * ks, axis=1, keepdims=True) - dlk
        dgrow = dgrow + jnp.where(last_row, tail, 0.0)
        gcol_ref[0, :, 2 * h : 2 * h + 1] = dbeta
        gcol_ref[0, :, 2 * h + 1 : 2 * h + 2] = dgrow
        gtok_ref[0, :, h : h + 1] = jnp.sum(z2, axis=1, keepdims=True) + qcarry * jnp.sum(
            query * gos, axis=1, keepdims=True
        )
        grow_ref[0, h : h + 1, :] = jnp.sum(z1, axis=0, keepdims=True) + jnp.sum(z2, axis=0, keepdims=True)
        weave[2 * h] = dk
        weave[2 * h + 1] = dv
        conv = conv_ref[:, cols]
        sig = jax.nn.sigmoid(conv)
        act = conv * sig
        pieces = []
        for part in range(1 + NH):
            piece = act[:, part * HEAD : (part + 1) * HEAD]
            scale = lax.rsqrt(jnp.sum(piece * piece, axis=1, keepdims=True) + NORM_EPS)
            if part:
                grad = weave[2 * h, pl.ds(part - 1, BLOCK_LEN, NH), :]
            else:
                grad = dq * (1.0 / math.sqrt(HEAD))
            unit = piece * scale
            pieces.append(scale * (grad - unit * jnp.sum(grad * unit, axis=1, keepdims=True)))
        for j in range(NH):
            pieces.append(weave[2 * h + 1, pl.ds(j, BLOCK_LEN, NH), :])
        dconv = jnp.concatenate(pieces, axis=1) * (sig * (1.0 + conv * (1.0 - sig)))
        ext = proj_ref[pl.ds(base, BLOCK_LEN + HALO), cols].astype(F32)
        gw_ref[0:1, cols] += jnp.sum(dconv * ext[HALO:], axis=0, keepdims=True)
        zeros = jnp.zeros((8, WIDE), F32)
        length = BLOCK_LEN + 8
        total = jnp.concatenate([zeros, dconv * w_ref[0:1, cols]], axis=0)
        for lag in range(1, CONV):
            masked = tokp[:, lag - 1 : lag] * dconv
            gw_ref[lag : lag + 1, cols] += jnp.sum(masked * lag_rows(ext, lag), axis=0, keepdims=True)
            total = total + pltpu.roll(
                jnp.concatenate([zeros, masked * w_ref[lag : lag + 1, cols]], axis=0), length - lag, 0
            )
        fixed = total[length - 8 :] + rim[:, cols]
        gproj_ref[:, cols] = jnp.concatenate([total[8 : length - 8], fixed], axis=0).astype(BF16)
        rim[:, cols] = total[:8]
        spill_ref[:, cols] = total[:8]

        @pl.when(step == 0)
        def _():
            last_ref[:, cols] = fixed


def recurrence_backward(index, maps, cots, state_in, proj_ext, conv_w, rowp, colp, tokp, grad_heads, saved, heads):
    blocks = rowp.shape[0]
    rows = blocks * BLOCK_LEN
    whole = lambda *dims: pl.BlockSpec(dims, lambda i: (0,) * len(dims))
    by_block = lambda *dims: pl.BlockSpec((1,) + dims, lambda i: (blocks - 1 - i,) + (0,) * len(dims))
    token = lambda cols: pl.BlockSpec((BLOCK_LEN, cols), lambda i: (blocks - 1 - i, 0))
    shape = lambda *dims: jax.ShapeDtypeStruct(dims, F32)
    square = (heads, ROWS, HEAD)
    return pl.pallas_call(
        functools.partial(bwd_kernel, heads),
        grid=(blocks,),
        in_specs=[
            pl.BlockSpec(memory_space=pltpu.SMEM), whole(*maps.shape), whole(*cots.shape), whole(*state_in.shape),
            whole(*proj_ext.shape), whole(*conv_w.shape),
            by_block(*rowp.shape[1:]), by_block(*colp.shape[1:]), by_block(*tokp.shape[1:]),
            token(heads * HEAD), token(heads * WIDE),
            by_block(heads, BLOCK_LEN, HEAD), by_block(*square), by_block(*square), by_block(*square),
            by_block(*square), by_block(heads, BLOCK_LEN, ROWS), by_block(heads, ROWS, 2 * HEAD),
            by_block(heads, HEAD, 2 * HEAD),
        ],
        out_specs=[
            token(heads * WIDE), whole(8, heads * WIDE), whole(8, heads * WIDE), whole(8, heads * WIDE),
            by_block(ROWS, 2 * heads), by_block(BLOCK_LEN, heads), by_block(heads, ROWS),
        ],
        out_shape=[
            jax.ShapeDtypeStruct((rows, heads * WIDE), BF16), shape(8, heads * WIDE), shape(8, heads * WIDE),
            shape(8, heads * WIDE), shape(blocks, ROWS, 2 * heads), shape(blocks, BLOCK_LEN, heads),
            shape(blocks, heads, ROWS),
        ],
        scratch_shapes=[
            pltpu.VMEM((heads, HEAD, HEAD), F32), pltpu.VMEM((2 * heads, ROWS, HEAD), F32),
            pltpu.VMEM((8, heads * WIDE), F32),
        ],
        compiler_params=pltpu.CompilerParams(vmem_limit_bytes=48 << 20),
        name="recurrence_backward",
    )(index, maps, cots, state_in, proj_ext, conv_w, rowp, colp, tokp, grad_heads, *saved)


def passed_along(x, axis, by):
    devices = lax.axis_size(axis)
    pairs = [(i, i + by) for i in range(devices) if 0 <= i + by < devices]
    return lax.ppermute(x, axis, pairs)


def rms_scale(values, gain_vec):
    return values * lax.rsqrt(jnp.mean(values * values, axis=-1, keepdims=True) + NORM_EPS) * gain_vec


def scalar_gates(scal, a_log, dt_bias):
    beta = jax.nn.sigmoid(scal[:, :, :NH])
    logs = -jnp.exp(a_log)[None, :] * jax.nn.softplus(scal[:, :, NH] + dt_bias[None, :])
    return beta, logs


def sum_columns_back(grad):
    ranks, pieces = lax.axis_size("seq"), lax.axis_size("ctx")
    cols = grad.shape[1]
    mine = lax.psum_scatter(
        grad.astype(BF16).reshape(ranks, pieces, -1, cols), "ctx", scatter_dimension=1, tiled=True
    )
    return lax.all_to_all(mine.reshape(-1, cols), "seq", split_axis=0, concat_axis=1, tiled=True).astype(F32)


def sum_rows_back(grad):
    return lax.psum_scatter(grad.astype(BF16), "ctx", scatter_dimension=0, tiled=True).astype(F32)


def sum_tokens(partial):
    ranks = lax.axis_size("seq")
    parts = lax.all_to_all(partial.astype(BF16).reshape(ranks, -1, partial.shape[1]), "seq", 0, 0, tiled=True)
    return jnp.sum(parts.astype(F32), axis=0)


def dot(a, b):
    return jnp.dot(a, b, preferred_element_type=F32)


def dot_t(a, b):
    return jnp.einsum("tc,dc->td", a, b, preferred_element_type=F32)


def t_dot(a, b):
    return jnp.einsum("tr,tc->rc", a, b, preferred_element_type=F32)


def local(
    block_input, teacher, valid_mask, segments, mix_proj, scalar_proj, gate_proj, out_proj, conv_weight,
    norm_attn, norm_mlp, head_gain, a_log, dt_bias, w_gate, w_up, w_down,
):
    seq_size = lax.axis_size("seq")
    heads = HEADS // seq_size
    tok_rows = block_input.shape[0]
    rows = tok_rows * seq_size
    blocks = rows // BLOCK_LEN
    token_total = segments.shape[0]
    seq_length = min(SEQ_LEN, token_total)
    index = lax.axis_index("ctx")
    rank = lax.axis_index("seq")
    head_start = rank * heads

    pieces = lax.axis_size("ctx")
    inner = FF // seq_size
    held = mix_proj.shape[0]
    scal_cols = heads * (NH + 1)
    count_here = jnp.sum(valid_mask.astype(F32)).astype(BF16)
    extra = jnp.concatenate(
        [
            norm_attn[:, None], norm_mlp[:, None],
            jnp.where(jnp.arange(held) == 0, count_here, jnp.zeros((), BF16))[:, None],
            conv_weight.reshape(held, -1),
        ],
        axis=1,
    )
    by_rank = lambda w: jnp.swapaxes(w.reshape(held, seq_size, -1), 0, 1)
    first = jnp.concatenate(
        [
            by_rank(mix_proj), by_rank(gate_proj), by_rank(scalar_proj),
            jnp.broadcast_to(extra[None], (seq_size, *extra.shape)),
            jnp.zeros((seq_size, held, HEAD - scal_cols - extra.shape[1]), BF16),
        ],
        axis=2,
    )
    later = jnp.stack([by_rank(w_gate), by_rank(w_up)], axis=1)
    x_full, halo, gathered, stage = start_gather(seq_size, pieces, block_input, first, later)
    weights = gathered.reshape(D, -1)
    gate_at = heads * WIDE
    scal_at = gate_at + heads * HEAD
    norm_at = scal_at + scal_cols
    norm_a = weights[:, norm_at].astype(F32)
    norm_m = weights[:, norm_at + 1].astype(F32)
    valid_count = jnp.maximum(jnp.sum(weights[:, norm_at + 2].astype(F32)), 1.0)
    conv_s = lax.dynamic_slice_in_dim(weights[:, norm_at + 3 : norm_at + extra.shape[1]], rank * (D // seq_size), D // seq_size)
    conv_s = conv_s.reshape(heads * WIDE, CONV)

    extended = jnp.concatenate([halo, x_full], axis=0).astype(F32)
    normed_ext = rms_scale(extended, norm_a).astype(BF16)
    normed = normed_ext[HALO:]
    proj_ext = dot(normed_ext, weights[:, :gate_at]).astype(BF16)
    rest = dot(normed, weights[:, gate_at:])
    gate_out = rest[:, : heads * HEAD]
    scal = rest[:, heads * HEAD : heads * HEAD + scal_cols].astype(BF16)
    inputs_f = block_input.astype(F32)
    _, norm_in_back = jax.vjp(rms_scale, inputs_f, norm_a)
    mix_s, gate_s, scal_s = weights[:, :gate_at], weights[:, gate_at:scal_at], weights[:, scal_at:norm_at]

    piece_start = index * rows
    window = lax.dynamic_slice_in_dim(jnp.pad(segments, (CONV, 0)), piece_start, rows + CONV)
    place_in = (piece_start + jnp.arange(rows, dtype=jnp.int32)) % seq_length
    own_seg = window[CONV:]
    linked = [
        ((window[CONV - lag : CONV - lag + rows] == own_seg) & (place_in >= lag)).astype(F32) for lag in range(1, CONV)
    ]
    starts = 1.0 - linked[0]
    alog_heads = lax.dynamic_slice_in_dim(a_log.astype(F32), head_start, heads, 0)
    dt_heads = lax.dynamic_slice_in_dim(dt_bias.astype(F32), head_start, heads, 0)
    (beta, logs), gates_back = jax.vjp(
        scalar_gates, scal.astype(F32).reshape(rows, heads, NH + 1), alog_heads, dt_heads
    )
    lower = jnp.tril(jnp.ones((BLOCK_LEN, BLOCK_LEN), F32))
    sums = jnp.einsum(
        "ts,bsh->bth",
        lower,
        jnp.concatenate([starts[:, None], logs * (1.0 - starts)[:, None]], axis=1).reshape(blocks, BLOCK_LEN, heads + 1),
        precision=lax.Precision.HIGHEST,
    )
    tokp = jnp.concatenate([jnp.stack(linked, axis=1).reshape(blocks, BLOCK_LEN, CONV - 1), sums], axis=2)
    sums_rows = jnp.repeat(sums, NH, axis=1)
    beta_rows = jnp.swapaxes(beta, 1, 2).reshape(blocks, ROWS, heads)
    colp = jnp.concatenate(
        [sums_rows[:, :, :1], jnp.zeros_like(sums_rows[:, :, :1])]
        + [x[:, :, h : h + 1] for h in range(heads) for x in (sums_rows[:, :, 1:], beta_rows)],
        axis=2,
    )
    rowp = jnp.swapaxes(colp, 1, 2)
    conv_w = jnp.pad(jnp.flip(conv_s.astype(F32).T, 0), ((0, 8 - CONV), (0, 0)))

    (
        oloc, carr, state_in, maps, *saved, wg_full, wu_full, wd_full, wo_full,
    ) = recurrence_forward(proj_ext, conv_w, rowp, colp, tokp, stage, w_down, out_proj, heads, pieces)
    wg_s, wu_s = wg_full.reshape(D, inner), wu_full.reshape(D, inner)
    down_s, out_s = wd_full.reshape(inner, D), wo_full.reshape(heads * HEAD, D)
    gain = head_gain.astype(F32)[None, :]
    index_arr = index.reshape(1).astype(jnp.int32)
    heads_out, mixed = state_and_gate(state_in, oloc, carr, gate_out, gain, heads)

    scale = (token_total / valid_count).reshape(1, 1)
    mask_values = valid_mask.astype(F32)[:, None]
    (
        final_out, grad_middle, grad_heads, grad_gate_out, cot, gain_term, norm_mlp_term, loss,
        out_grad, wg_grad, wu_grad, down_grad,
    ) = middle_part(
        seq_size, heads, scale, block_input, teacher, mask_values, norm_m[None, :], gain, mixed, heads_out, gate_out,
        carr, out_s, wg_s, wu_s, down_s,
    )
    error_sum = loss[0, 0]
    down_grad = sum_rows_back(down_grad)
    out_grad = sum_rows_back(out_grad)
    wg_grad = sum_columns_back(wg_grad)
    wu_grad = sum_columns_back(wu_grad)
    cots = lax.all_gather(cot.astype(BF16), "ctx")
    grad_proj, last_rows, spill, gw, gcol, gtok, grow = recurrence_backward(
        index_arr, maps, cots, state_in, proj_ext, conv_w, rowp, colp, tokp, grad_heads, saved, heads
    )
    rim_back = passed_along(spill, "ctx", -1)
    grad_proj = lax.dynamic_update_slice_in_dim(grad_proj, (last_rows + rim_back).astype(BF16), rows - 8, 0)
    grad_beta = jnp.swapaxes(gcol[:, :, 0::2].reshape(rows, NH, heads), 1, 2)
    grad_cum = jnp.sum(
        (gcol[:, :, 1::2] - jnp.swapaxes(grow, 1, 2)).reshape(blocks, BLOCK_LEN, NH, heads), axis=2
    ) + gtok
    grad_logs = jnp.einsum("ts,bth->bsh", lower, grad_cum, precision=lax.Precision.HIGHEST).reshape(rows, heads)
    grad_scal_f, grad_alog, grad_dt = gates_back((grad_beta, grad_logs * (1.0 - starts)[:, None]))
    grad_scal = grad_scal_f.reshape(rows, heads * (NH + 1)).astype(BF16)

    grad_normed = sum_tokens(
        dot_t(grad_proj, mix_s) + dot_t(grad_scal, scal_s) + dot_t(grad_gate_out, gate_s)
    )
    grad_in_norm, norm_attn_term = norm_in_back(grad_normed)
    input_grad = grad_middle + grad_in_norm
    mix_grad = sum_columns_back(t_dot(normed, grad_proj))
    scal_grad = sum_columns_back(t_dot(normed, grad_scal))
    gate_grad = sum_columns_back(t_dot(normed, grad_gate_out))
    conv_grad = lax.psum_scatter(jnp.flip(gw[:CONV], 0).T, "ctx", scatter_dimension=0, tiled=True)
    pick = (jnp.arange(HEADS)[None, :] == head_start + jnp.arange(heads)[:, None]).astype(F32)
    small = jnp.concatenate(
        [
            gain_term[0], jnp.sum(grad_alog[:, None] * pick, axis=0), jnp.sum(grad_dt[:, None] * pick, axis=0),
            error_sum[None], norm_attn_term, norm_mlp_term[0],
        ]
    )
    small = lax.psum(small, BOTH)
    mean_loss = small[HEAD + 2 * HEADS] / (D * valid_count)
    norm_start = HEAD + 2 * HEADS + 1
    own = norm_attn.shape[0]
    place = (rank * lax.axis_size("ctx") + index) * own
    return (
        final_out,
        mean_loss,
        input_grad,
        mix_grad,
        scal_grad,
        gate_grad,
        out_grad,
        conv_grad,
        lax.dynamic_slice_in_dim(small, norm_start + place, own),
        lax.dynamic_slice_in_dim(small, norm_start + D + place, own),
        small[:HEAD],
        small[HEAD : HEAD + HEADS],
        small[HEAD + HEADS : HEAD + 2 * HEADS],
        wg_grad,
        wu_grad,
        down_grad,
    )


def solution(mesh):
    tokens, vector, matrix = P(("ctx", "seq"), None), P(BOTH), P(BOTH, None)
    in_specs = (
        tokens, tokens, P(("ctx", "seq")), P(), matrix, matrix, matrix, matrix, matrix, vector, vector,
        P(), P(), P(), matrix, matrix, matrix,
    )
    out_specs = (
        tokens, P(), tokens, matrix, matrix, matrix, matrix, matrix, vector, vector, P(), P(), P(),
        matrix, matrix, matrix,
    )
    return jax.shard_map(local, mesh=mesh, in_specs=in_specs, out_specs=out_specs, check_vma=False)
```

```python
import functools
import math

import jax
import jax.numpy as jnp
from jax import lax
from jax.experimental import pallas as pl
from jax.experimental.pallas import tpu as pltpu
from jax.sharding import PartitionSpec as P

D = 1024
HEADS = 8
HEAD = 128
NH = 2
FF = 2816
BLOCK_LEN = 64
ROWS = BLOCK_LEN * NH
CONV = 4
SEQ_LEN = 32768
WIDE = (1 + 2 * NH) * HEAD
HALO = 16
NORM_EPS = 1e-06
F32 = jnp.float32
BF16 = jnp.bfloat16
BOTH = ("seq", "ctx")
MESH = pl.DeviceIdType.MESH


def split_bf16(x):
    if x.dtype == BF16:
        return x, None
    high = x.astype(BF16)
    return high, (x - high.astype(F32)).astype(BF16)


def mm(a, b, ca=1, cb=0, passes=3):
    def one(x, y):
        return lax.dot_general(x, y, (((ca,), (cb,)), ((), ())), preferred_element_type=F32)

    if passes == 1:
        return one(a.astype(BF16), b.astype(BF16))
    ah, al = split_bf16(a)
    bh, bl = split_bf16(b)
    total = one(ah, bh)
    if bl is not None:
        total = total + one(ah, bl)
    if al is not None:
        total = total + one(al, bh)
    return total


def iota(shape, axis):
    return lax.broadcasted_iota(jnp.int32, shape, axis)


def unit_lower_inverse(a):
    n = a.shape[0]
    ri, ci = iota((n, n), 0), iota((n, n), 1)
    own = jnp.where(ri // 8 == ci // 8, a, 0.0)
    pick = (iota((n, 8), 0) % 8 == iota((n, 8), 1)).astype(BF16)
    small = mm(own, pick).reshape(n // 8, 8, 8)
    inv = (ri == ci).astype(F32).reshape(n // 8, 8, n)
    for j in range(7):
        inv = inv - small[:, :, j : j + 1] * inv[:, j : j + 1, :]
    inv = inv.reshape(n, n)
    size = 8
    while size < n:
        off = (ri // (2 * size) == ci // (2 * size)) & (ri // size != ci // size)
        inv = inv - mm(inv, mm(jnp.where(off, a, 0.0), inv))
        size *= 2
    return inv


def decays(rowp, colp, tokp, h):
    cs_row, g_row = rowp[0:1, :], rowp[2 + 2 * h : 3 + 2 * h, :]
    cs_col, g_col = colp[:, 0:1], colp[:, 2 + 2 * h : 3 + 2 * h]
    cs_tok, g_tok = tokp[:, 3:4], tokp[:, 4 + h : 5 + h]
    beta = colp[:, 3 + 2 * h : 4 + 2 * h]
    ri, ci = iota((ROWS, ROWS), 0), iota((ROWS, ROWS), 1)
    strict = (ri > ci) & (cs_col == cs_row)
    decay = jnp.where(strict, jnp.exp(jnp.where(strict, g_col - g_row, 0.0)), 0.0)
    rt, ct = iota((BLOCK_LEN, ROWS), 0), iota((BLOCK_LEN, ROWS), 1)
    seen = (rt * NH + NH - 1 >= ct) & (cs_tok == cs_row)
    qdecay = jnp.where(seen, jnp.exp(jnp.where(seen, g_tok - g_row, 0.0)), 0.0)
    carry = jnp.where(cs_col == 0.0, jnp.exp(g_col), 0.0)
    qcarry = jnp.where(cs_tok == 0.0, jnp.exp(g_tok), 0.0)
    cs_last, g_last = cs_row[:, ROWS - 1 :], g_row[:, ROWS - 1 :]
    same = cs_col == cs_last
    dlast = jnp.where(same, jnp.exp(jnp.where(same, g_last - g_col, 0.0)), 0.0)
    clast = jnp.where(cs_last == 0.0, jnp.exp(g_last), 0.0)
    return beta, decay, qdecay, carry, qcarry, dlast, clast


def lag_rows(ext, lag):
    moved = pltpu.roll(ext, lag, 0) if lag else ext
    return moved[HALO:]


UP, DOWN, ACROSS = 0, 1, 2


class Line:
    def __init__(self, pieces, parts, send_sem, recv_sem, up=True, down=True):
        self.chips = pieces // 2
        self.here = lax.axis_index("ctx")
        self.chip = self.here // 2
        self.core = lax.rem(self.here, 2)
        self.other = self.here + 1 - 2 * self.core
        self.parts, self.send_sem, self.recv_sem, self.up, self.down = parts, send_sem, recv_sem, up, down

    def copies(self, chunk, way):
        target = (self.here + 2, self.here - 2, self.other)[way]
        return [
            pltpu.make_async_remote_copy(
                part(chunk), part(chunk), self.send_sem.at[n, way, chunk], self.recv_sem.at[n, chunk],
                device_id={"ctx": target}, device_id_type=MESH,
            )
            for n, part in enumerate(self.parts)
        ]

    def start(self, chunk, way):
        for copy in self.copies(chunk, way):
            copy.start()

    def arrived(self, chunk):
        for copy in self.copies(chunk, ACROSS):
            copy.wait_recv()

    def left(self, chunk, way):
        for copy in self.copies(chunk, way):
            copy.wait_send()

    def routes(self, distance, act):
        if distance == 0:
            if self.up:
                pl.when(self.chip < self.chips - 1)(lambda: act(self.here, UP))
            if self.down:
                pl.when(self.chip > 0)(lambda: act(self.here, DOWN))
            act(self.here, ACROSS)
            return
        below, above = self.here - 2 * distance, self.here + 2 * distance
        if self.up:

            @pl.when(self.chip >= distance)
            def _():
                pl.when(self.chip < self.chips - 1)(lambda: act(below, UP))
                act(below, ACROSS)

        if self.down:

            @pl.when(self.chip + distance < self.chips)
            def _():
                pl.when(self.chip > 0)(lambda: act(above, DOWN))
                act(above, ACROSS)

    def own(self):
        self.routes(0, self.start)

    def hop(self, distance):
        if self.up:
            pl.when(self.chip >= distance)(lambda: self.arrived(self.here - 2 * distance))
        if self.down:
            pl.when(self.chip + distance < self.chips)(lambda: self.arrived(self.here + 2 * distance))
        self.routes(distance, self.start)

    def finish(self):
        for chip in range(self.chips):
            needed = True
            if not self.down:
                needed = self.chip >= chip
            if not self.up:
                needed = self.chip <= chip
            pl.when(needed)(lambda chip=chip: self.arrived(2 * chip + 1 - self.core))
        for distance in range(self.chips):
            self.routes(distance, self.left)


class LineSum:
    def __init__(self, pieces, held, came, send_sem, recv_sem):
        self.chips = pieces // 2
        self.here = lax.axis_index("ctx")
        self.chip = self.here // 2
        self.held, self.came, self.send_sem, self.recv_sem = held, came, send_sem, recv_sem

    def copies(self, owner, way):
        return [
            pltpu.make_async_remote_copy(
                held.at[owner], came.at[way, owner], self.send_sem.at[n, owner], self.recv_sem.at[n, way, owner],
                device_id={"ctx": self.here + 2 - 4 * way}, device_id_type=MESH,
            )
            for n, (held, came) in enumerate(zip(self.held, self.came))
        ]

    def take(self, owner, way):
        for copy in self.copies(owner, way):
            copy.wait_recv()
        for held, came in zip(self.held, self.came):
            held[owner] = (held[owner].astype(F32) + came[way, owner].astype(F32)).astype(BF16)

    def send(self, owner, way):
        for copy in self.copies(owner, way):
            copy.start()

    def round(self, r):
        top = self.chips - 1
        for way, place in ((UP, self.chip), (DOWN, top - self.chip)):
            owner = top - (r - place) if way == UP else r - place

            @pl.when((place <= r) & (place < top))
            def _():
                pl.when(place > 0)(lambda: self.take(owner, way))
                self.send(owner, way)

    def finish(self):
        top = self.chips - 1
        pl.when(self.chip > 0)(lambda: self.take(self.chip, UP))
        pl.when(self.chip < top)(lambda: self.take(self.chip, DOWN))
        for owner in range(self.chips):
            for way, wanted in ((UP, self.chip < owner), (DOWN, self.chip > owner)):

                @pl.when(wanted)
                def _():
                    for copy in self.copies(owner, way):
                        copy.wait_send()


class Siblings:
    def __init__(self, parts, theirs, held, send_sem, recv_sem):
        self.here = lax.axis_index("ctx")
        self.core = lax.rem(self.here, 2)
        self.parts, self.theirs, self.held, self.send_sem, self.recv_sem = parts, theirs, held, send_sem, recv_sem

    def copies(self):
        return [
            pltpu.make_async_remote_copy(
                part.at[:, 1 - self.core], theirs, self.send_sem.at[n], self.recv_sem.at[n],
                device_id={"ctx": self.here + 1 - 2 * self.core}, device_id_type=MESH,
            )
            for n, (part, theirs) in enumerate(zip(self.parts, self.theirs))
        ]

    def start(self):
        for copy in self.copies():
            copy.start()

    def add(self):
        for copy in self.copies():
            copy.wait_recv()
        for part, theirs, held in zip(self.parts, self.theirs, self.held):

            def one(chip, carry, part=part, theirs=theirs, held=held):
                held[chip] = (part[chip, self.core].astype(F32) + theirs[chip].astype(F32)).astype(BF16)
                return carry

            lax.fori_loop(0, part.shape[0], one, 0)

    def left(self):
        for copy in self.copies():
            copy.wait_send()


def greet(devices, barrier):
    total = 0
    for place, there in devices:
        pl.when(there)(
            lambda place=place: pl.semaphore_signal(barrier, inc=1, device_id=place, device_id_type=MESH)
        )
        total = total + jnp.asarray(there, jnp.int32)
    return total


def line_neighbours(pieces):
    here = lax.axis_index("ctx")
    chip, core = here // 2, lax.rem(here, 2)
    return [
        ({"ctx": here + 2}, chip < pieces // 2 - 1),
        ({"ctx": here - 2}, chip > 0),
        ({"ctx": here + 1 - 2 * core}, here >= 0),
    ]


def start_kernel(
    size, pieces, x_ref, first_ref, later_ref, xfull_ref, halo_ref, full_ref, stage_ref,
    local_sem, seq_send, seq_recv, line_send, line_recv, halo_sem,
):
    me, here = lax.axis_index("seq"), lax.axis_index("ctx")
    count = x_ref.shape[0]
    core = lax.rem(here, 2)
    barrier = pltpu.get_barrier_semaphore()
    peers = [({"seq": lax.rem(me + i, size)}, here >= 0) for i in range(1, size)]
    side = [({"ctx": here + 1}, (core == 1) & (here < pieces - 1)), ({"ctx": here - 1}, (core == 0) & (here > 0))]
    total = greet(peers + line_neighbours(pieces) + side, barrier)
    pl.semaphore_wait(barrier, total)

    def rows(q):
        return pl.ds(pl.multiple_of(q * count, count), count)

    def exchange(n, i):
        q = lax.rem(me + i, size)
        source, target = [
            (first_ref.at[q], full_ref.at[me, here]), (x_ref, xfull_ref.at[rows(me)]), (later_ref.at[q], stage_ref.at[me])
        ][n]
        return pltpu.make_async_remote_copy(
            source, target, seq_send.at[n, i - 1], seq_recv.at[n, i - 1], device_id={"seq": q}, device_id_type=MESH
        )

    def own(n):
        source, target = [
            (first_ref.at[me], full_ref.at[me, here]), (x_ref, xfull_ref.at[rows(me)]), (later_ref.at[me], stage_ref.at[me])
        ][n]
        return pltpu.make_async_copy(source, target, local_sem.at[n])

    for n in range(3):
        own(n).start()
        for i in range(1, size):
            exchange(n, i).start()
    line = Line(pieces, [lambda c: full_ref.at[:, c]], line_send, line_recv)
    own(0).wait()
    for i in range(1, size):
        exchange(0, i).wait_recv()
    line.own()
    own(1).wait()
    for i in range(1, size):
        exchange(1, i).wait_recv()
    last = xfull_ref.at[pl.ds(size * count - HALO, HALO)]
    passing = pltpu.make_async_remote_copy(
        last, halo_ref, halo_sem.at[0], halo_sem.at[1], device_id={"ctx": here + 1}, device_id_type=MESH
    )
    pl.when(here < pieces - 1)(passing.start)

    @pl.when(here == 0)
    def _():
        filling = pltpu.make_async_copy(last, halo_ref, local_sem.at[3])
        filling.start()
        filling.wait()

    for distance in range(1, pieces // 2):
        line.hop(distance)
    line.finish()
    own(2).wait()
    for i in range(1, size):
        exchange(2, i).wait_recv()
    pl.when(here > 0)(passing.wait_recv)
    pl.when(here < pieces - 1)(passing.wait_send)
    for n in range(3):
        for i in range(1, size):
            exchange(n, i).wait_send()


def start_gather(size, pieces, x, first, later):
    anywhere = pl.BlockSpec(memory_space=pl.ANY)
    out = lambda *dims: jax.ShapeDtypeStruct(dims, BF16)
    return pl.pallas_call(
        functools.partial(start_kernel, size, pieces),
        in_specs=[anywhere] * 3,
        out_specs=[anywhere] * 4,
        out_shape=[
            out(x.shape[0] * size, D), out(HALO, D), out(size, pieces, *first.shape[1:]), out(*later.shape),
        ],
        scratch_shapes=[
            pltpu.SemaphoreType.DMA((4,)), pltpu.SemaphoreType.DMA((3, size - 1)), pltpu.SemaphoreType.DMA((3, size - 1)),
            pltpu.SemaphoreType.DMA((1, 3, pieces)), pltpu.SemaphoreType.DMA((1, pieces)), pltpu.SemaphoreType.DMA((2,)),
        ],
        compiler_params=pltpu.CompilerParams(
            vmem_limit_bytes=16 << 20, collective_id=2, has_side_effects=True
        ),
        name="start_gather",
    )(x, first, later)


def fwd_kernel(
    heads, pieces, proj_ref, w_ref, rowp_ref, colp_ref, tokp_ref, stage_ref, wd_ref, wo_ref,
    oloc_ref, carr_ref, sin_ref, mapsout_ref, conv_ref, q_ref, k_ref, v_ref, t_ref, kk_ref, at_ref, uw_ref, pl_ref,
    wgfull_ref, wufull_ref, wdfull_ref, wofull_ref,
    state, weave, maps, local_sem, line_send, line_recv, map_send, map_recv,
):
    step = pl.program_id(0)
    steps = pl.num_programs(0)
    here = lax.axis_index("ctx")
    weights = Line(
        pieces,
        [
            lambda c: wgfull_ref.at[:, c], lambda c: wufull_ref.at[:, c], lambda c: wdfull_ref.at[c],
            lambda c: wofull_ref.at[c],
        ],
        line_send, line_recv,
    )

    @pl.when(step == 0)
    def _():
        barrier = pltpu.get_barrier_semaphore()
        pl.semaphore_wait(barrier, greet(line_neighbours(pieces), barrier))
        owned = [
            pltpu.make_async_copy(source, target, local_sem.at[n])
            for n, (source, target) in enumerate(
                [
                    (stage_ref.at[:, 0], wgfull_ref.at[:, here]), (stage_ref.at[:, 1], wufull_ref.at[:, here]),
                    (wd_ref, wdfull_ref.at[here]), (wo_ref, wofull_ref.at[here]),
                ]
            )
        ]
        for copy in owned:
            copy.start()
        for copy in owned:
            copy.wait()
        weights.own()

    for distance in range(1, pieces // 2):
        pl.when(step == (distance * steps) // (pieces // 2))(lambda distance=distance: weights.hop(distance))

    eye = (iota((HEAD, HEAD), 0) == iota((HEAD, HEAD), 1)).astype(F32)

    @pl.when(step == 0)
    def _():
        for h in range(heads):
            state[h, :, :HEAD] = eye
            state[h, :, HEAD:] = jnp.zeros((HEAD, HEAD), F32)

    base = pl.multiple_of(step * BLOCK_LEN, BLOCK_LEN)
    rowp, colp, tokp = rowp_ref[0], colp_ref[0], tokp_ref[0]
    for h in range(heads):
        cols = slice(h * WIDE, (h + 1) * WIDE)
        ext = proj_ref[pl.ds(base, BLOCK_LEN + HALO), cols].astype(F32)
        conv = ext[HALO:] * w_ref[0:1, cols]
        for lag in range(1, CONV):
            conv = conv + tokp[:, lag - 1 : lag] * lag_rows(ext, lag) * w_ref[lag : lag + 1, cols]
        conv_ref[:, cols] = conv
        act = conv * jax.nn.sigmoid(conv)
        unit = []
        for part in range(1 + NH):
            piece = act[:, part * HEAD : (part + 1) * HEAD]
            unit.append(piece * lax.rsqrt(jnp.sum(piece * piece, axis=1, keepdims=True) + NORM_EPS))
        query = unit[0] * (1.0 / math.sqrt(HEAD))
        for j in range(NH):
            weave[2 * h, pl.ds(j, BLOCK_LEN, NH), :] = unit[1 + j]
            weave[2 * h + 1, pl.ds(j, BLOCK_LEN, NH), :] = act[:, (1 + NH + j) * HEAD : (2 + NH + j) * HEAD]
        keys, values = weave[2 * h], weave[2 * h + 1]
        beta, decay, qdecay, carry, qcarry, dlast, clast = decays(rowp, colp, tokp, h)
        kk = decay * mm(keys, keys, 1, 1)
        inv = unit_lower_inverse(beta * kk)
        uw = mm(inv, jnp.concatenate([beta * values, (beta * carry) * keys], axis=1))
        attn = qdecay * mm(query, keys, 1, 1)
        auw = mm(attn, uw)
        nm = mm(dlast * keys, uw, 0, 0)
        before = state[h]
        out = mm(qcarry * query - auw[:, HEAD:], before)
        hc = slice(h * HEAD, (h + 1) * HEAD)
        carr_ref[:, hc] = out[:, :HEAD]
        oloc_ref[:, hc] = out[:, HEAD:] + auw[:, :HEAD]
        after = mm(clast * eye - nm[:, HEAD:], before)
        state[h, :, :HEAD] = after[:, :HEAD]
        state[h, :, HEAD:] = after[:, HEAD:] + nm[:, :HEAD]
        q_ref[0, h] = query
        k_ref[0, h] = keys
        v_ref[0, h] = values
        t_ref[0, h] = inv
        kk_ref[0, h] = kk
        at_ref[0, h] = attn
        uw_ref[0, h] = uw
        pl_ref[0, h] = before

    @pl.when(step == steps - 1)
    def _():
        maps[here] = state[...].astype(BF16)
        line = Line(pieces, [lambda c: maps.at[c]], map_send, map_recv)
        line.own()
        for distance in range(1, pieces // 2):
            line.hop(distance)
        line.finish()
        weights.finish()

        def hop(k, states):
            return tuple(
                mm(maps[k, h, :, :HEAD], states[h]) + maps[k, h, :, HEAD:].astype(F32) for h in range(heads)
            )

        states = lax.fori_loop(0, here, hop, tuple(jnp.zeros((HEAD, HEAD), F32) for _ in range(heads)))
        for h in range(heads):
            sin_ref[h] = states[h]

        def keep(k, carry):
            mapsout_ref[k] = maps[k, :, :, :HEAD]
            return carry

        lax.fori_loop(0, pieces, keep, 0)


def recurrence_forward(proj_ext, conv_w, rowp, colp, tokp, stage, w_down, w_out, heads, pieces):
    blocks = rowp.shape[0]
    rows = blocks * BLOCK_LEN
    whole = lambda *dims: pl.BlockSpec(dims, lambda i: (0,) * len(dims))
    by_block = lambda *dims: pl.BlockSpec((1,) + dims, lambda i: (i,) + (0,) * len(dims))
    token = lambda cols: pl.BlockSpec((BLOCK_LEN, cols), lambda i: (i, 0))
    shape = lambda *dims: jax.ShapeDtypeStruct(dims, F32)
    low_shape = lambda *dims: jax.ShapeDtypeStruct(dims, BF16)
    anywhere = pl.BlockSpec(memory_space=pl.ANY)
    square = (heads, ROWS, HEAD)
    size = stage.shape[0]
    return pl.pallas_call(
        functools.partial(fwd_kernel, heads, pieces),
        grid=(blocks,),
        in_specs=[
            whole(*proj_ext.shape), whole(*conv_w.shape),
            by_block(*rowp.shape[1:]), by_block(*colp.shape[1:]), by_block(*tokp.shape[1:]),
            anywhere, anywhere, anywhere,
        ],
        out_specs=[
            token(heads * HEAD), token(heads * HEAD), whole(heads, HEAD, HEAD), whole(pieces, heads, HEAD, HEAD),
            token(heads * WIDE),
            by_block(heads, BLOCK_LEN, HEAD), by_block(*square), by_block(*square), by_block(*square),
            by_block(*square), by_block(heads, BLOCK_LEN, ROWS), by_block(heads, ROWS, 2 * HEAD),
            by_block(heads, HEAD, 2 * HEAD), anywhere, anywhere, anywhere, anywhere,
        ],
        out_shape=[
            shape(rows, heads * HEAD), shape(rows, heads * HEAD), shape(heads, HEAD, HEAD),
            low_shape(pieces, heads, HEAD, HEAD), shape(rows, heads * WIDE),
            shape(blocks, heads, BLOCK_LEN, HEAD), shape(blocks, *square), shape(blocks, *square), shape(blocks, *square),
            shape(blocks, *square), shape(blocks, heads, BLOCK_LEN, ROWS), shape(blocks, heads, ROWS, 2 * HEAD),
            shape(blocks, heads, HEAD, 2 * HEAD),
            low_shape(size, pieces, *stage.shape[2:]), low_shape(size, pieces, *stage.shape[2:]),
            low_shape(pieces, *w_down.shape), low_shape(pieces, *w_out.shape),
        ],
        scratch_shapes=[
            pltpu.VMEM((heads, HEAD, 2 * HEAD), F32), pltpu.VMEM((2 * heads, ROWS, HEAD), F32),
            pltpu.VMEM((pieces, heads, HEAD, 2 * HEAD), BF16),
            pltpu.SemaphoreType.DMA((4,)), pltpu.SemaphoreType.DMA((4, 3, pieces)), pltpu.SemaphoreType.DMA((4, pieces)),
            pltpu.SemaphoreType.DMA((1, 3, pieces)), pltpu.SemaphoreType.DMA((1, pieces)),
        ],
        compiler_params=pltpu.CompilerParams(
            vmem_limit_bytes=40 << 20, collective_id=3, has_side_effects=True
        ),
        name="recurrence_forward",
    )(proj_ext, conv_w, rowp, colp, tokp, stage, w_down, w_out)


def state_kernel(heads, state_ref, oloc_ref, carr_ref, gate_ref, gain_ref, heads_ref, mixed_ref):
    for h in range(heads):
        hc = slice(h * HEAD, (h + 1) * HEAD)
        out = (oloc_ref[:, hc] + mm(carr_ref[:, hc], state_ref[h])).astype(BF16)
        heads_ref[:, hc] = out
        wide = out.astype(F32)
        gate = gate_ref[:, hc]
        scaled = wide * lax.rsqrt(jnp.mean(wide * wide, axis=1, keepdims=True) + NORM_EPS) * gain_ref[...]
        mixed_ref[:, hc] = (scaled * (gate * jax.nn.sigmoid(gate))).astype(BF16)


def state_and_gate(state, oloc, carr, gate_out, gain, heads):
    rows = oloc.shape[0]
    vmem = pl.BlockSpec(memory_space=pltpu.VMEM)
    return pl.pallas_call(
        functools.partial(state_kernel, heads),
        in_specs=[vmem] * 5,
        out_specs=[vmem] * 2,
        out_shape=[
            jax.ShapeDtypeStruct((rows, heads * HEAD), BF16),
            jax.ShapeDtypeStruct((rows, heads * HEAD), BF16),
        ],
        compiler_params=pltpu.CompilerParams(vmem_limit_bytes=40 << 20),
        name="state_and_gate",
    )(state, oloc, carr, gate_out, gain)


def seq_barrier(size):
    me = lax.axis_index("seq")
    barrier = pltpu.get_barrier_semaphore()

    def greet(i, carry):
        pl.semaphore_signal(barrier, inc=1, device_id={"seq": lax.rem(me + i, size)}, device_id_type=MESH)
        return carry

    lax.fori_loop(1, size, greet, 0)
    pl.semaphore_wait(barrier, size - 1)


def middle_kernel(
    size, heads, scale_ref,
    x_ref, teach_ref, mask_ref, norm_ref, gain_ref, mixed_ref, heads_ref, gate_ref, carr_ref,
    wout_ref, wg_ref, wu_ref, wd_ref,
    final_ref, gmid_ref, ghead_ref, ggate_ref, cot_ref, ggain_ref, gnorm_ref, loss_ref,
    wide_ref, tall_ref,
    second, branch, low, sent, got, own, mid, gfin, gates, ups, hidden, ggates, gups, send_sem, recv_sem,
):
    me = lax.axis_index("seq")
    count = x_ref.shape[0]
    seq_barrier(size)

    def dot(a, b, ca=1, cb=0):
        return lax.dot_general(a, b, (((ca,), (cb,)), ((), ())), preferred_element_type=F32)

    def rows(q):
        return pl.ds(pl.multiple_of(q * count, count), count)

    def part_copy(phase, i):
        return pltpu.make_async_remote_copy(
            sent.at[phase, i - 1], got.at[phase, i - 1], send_sem.at[phase, i - 1], recv_sem.at[phase, i - 1],
            device_id={"seq": lax.rem(me + i, size)}, device_id_type=MESH,
        )

    def block_copy(buffer, phase, i, owner):
        return pltpu.make_async_remote_copy(
            buffer.at[rows(owner)], buffer.at[rows(owner)], send_sem.at[phase, i - 1], recv_sem.at[phase, i - 1],
            device_id={"seq": lax.rem(me + i, size)}, device_id_type=MESH,
        )

    def give_part(phase, i, part):
        @pl.when(i > 0)
        def _():
            sent[phase, i - 1] = part.astype(BF16)
            part_copy(phase, i).start()

        @pl.when(i == 0)
        def _():
            own[...] = part

    def take_parts(phase):
        def add(i, total):
            part_copy(phase, i).wait_recv()
            return total + got[phase, i - 1].astype(F32)

        return lax.fori_loop(1, size, add, own[...])

    def give_block(buffer, phase, value):
        buffer[rows(me)] = value

        def send(i, carry):
            block_copy(buffer, phase, i, me).start()
            return carry

        lax.fori_loop(1, size, send, 0)

    def take_block(buffer, phase, i):
        q = lax.rem(me + size - i, size)

        @pl.when(i > 0)
        def _():
            block_copy(buffer, phase, i, q).wait_recv()

        return q

    def out_part(k, carry):
        i = lax.rem(k + 1, size)
        give_part(0, i, dot(mixed_ref[rows(lax.rem(me + i, size))], wout_ref[...]))
        return carry

    lax.fori_loop(0, size, out_part, 0)
    middle = x_ref[...].astype(F32) + take_parts(0)
    mid[...] = middle
    inv = lax.rsqrt(jnp.mean(middle * middle, axis=1, keepdims=True) + NORM_EPS)
    give_block(second, 3, (middle * inv * norm_ref[...]).astype(BF16))

    def feed(i, carry):
        q = take_block(second, 3, i)
        here = second[rows(q)]
        gate = dot(here, wg_ref[...])
        up = dot(here, wu_ref[...])
        gates[rows(q)] = gate
        ups[rows(q)] = up
        hid = (gate * jax.nn.sigmoid(gate) * up).astype(BF16)
        hidden[rows(q)] = hid
        give_part(1, lax.rem(size - i, size), dot(hid, wd_ref[...]))
        return carry

    lax.fori_loop(0, size, feed, 0)
    final = mid[...] + take_parts(1)
    final_ref[...] = final.astype(BF16)
    error = final - teach_ref[...].astype(F32)
    weighted = mask_ref[...] * error
    loss_ref[...] = jnp.broadcast_to(
        jnp.sum(jnp.sum(weighted * error, axis=1, keepdims=True), axis=0, keepdims=True), loss_ref.shape
    )
    grad_final = scale_ref[0, 0] * weighted
    gfin[...] = grad_final
    give_block(branch, 4, grad_final.astype(BF16))

    def feed_back(i, carry):
        q = take_block(branch, 4, i)
        ghid = dot(branch[rows(q)], wd_ref[...], 1, 1)
        gate = gates[rows(q)]
        sig = jax.nn.sigmoid(gate)
        silu = gate * sig
        ggate = (ghid * ups[rows(q)] * (sig + silu * (1.0 - sig))).astype(BF16)
        gup = (ghid * silu).astype(BF16)
        ggates[rows(q)] = ggate
        gups[rows(q)] = gup
        give_part(2, lax.rem(size - i, size), dot(ggate, wg_ref[...], 1, 1) + dot(gup, wu_ref[...], 1, 1))
        return carry

    lax.fori_loop(0, size, feed_back, 0)
    pieces = wide_ref.shape[0]
    held = D // (size * pieces)
    deep = hidden.shape[1] // pieces
    wide_at = tall_ref.shape[1] - held
    tall_ref[...] = jnp.zeros_like(tall_ref)
    grad = dot(hidden[...], branch[...], 0, 0)
    for c in range(pieces):
        tall_ref[c, :deep] = grad[c * deep : (c + 1) * deep].astype(BF16)
    for n, side in enumerate((ggates, gups)):
        grad = dot(second[...], side[...], 0, 0)
        for c in range(pieces):
            for r in range(size):
                first = (r * pieces + c) * held
                wide_ref[c, (n * size + r) * held : (n * size + r + 1) * held] = grad[first : first + held].astype(BF16)
    gsecond = take_parts(2)
    middle = mid[...]
    inv = lax.rsqrt(jnp.mean(middle * middle, axis=1, keepdims=True) + NORM_EPS)
    unit = middle * inv
    gnorm_ref[...] = jnp.sum(gsecond * unit, axis=0, keepdims=True)
    down = gsecond * norm_ref[...]
    gmid = gfin[...] + inv * (down - unit * jnp.mean(down * unit, axis=1, keepdims=True))
    gmid_ref[...] = gmid
    give_block(low, 5, gmid.astype(BF16))
    ggain_ref[...] = jnp.zeros_like(ggain_ref)
    cot_ref[...] = jnp.zeros_like(cot_ref)

    def out_back(i, carry):
        q = take_block(low, 5, i)
        gmixed = dot(low[rows(q)], wout_ref[...], 1, 1)
        gain = gain_ref[...]
        for h in range(heads):
            hc = slice(h * HEAD, (h + 1) * HEAD)
            x = heads_ref[rows(q), hc].astype(F32)
            gate = gate_ref[rows(q), hc]
            grad = gmixed[:, hc]
            inv = lax.rsqrt(jnp.mean(x * x, axis=1, keepdims=True) + NORM_EPS)
            sig = jax.nn.sigmoid(gate)
            silu = gate * sig
            unit = x * inv
            ggate_ref[rows(q), hc] = (grad * unit * gain * (sig + silu * (1.0 - sig))).astype(BF16)
            weighted = grad * silu
            ggain_ref[...] += jnp.sum(weighted * unit, axis=0, keepdims=True)
            down = weighted * gain
            ghead = (inv * (down - unit * jnp.mean(down * unit, axis=1, keepdims=True))).astype(BF16)
            ghead_ref[rows(q), hc] = ghead
            cot_ref[h] += mm(carr_ref[rows(q), hc], ghead, 0, 0)
        return carry

    lax.fori_loop(0, size, out_back, 0)
    grad = dot(mixed_ref[...], low[...], 0, 0)
    for c in range(pieces):
        tall_ref[c, wide_at:] = grad[c * held : (c + 1) * held].astype(BF16)

    def sent_all(i, carry):
        for phase in range(3):
            part_copy(phase, i).wait_send()
        block_copy(second, 3, i, me).wait_send()
        block_copy(branch, 4, i, me).wait_send()
        block_copy(low, 5, i, me).wait_send()
        return carry

    lax.fori_loop(1, size, sent_all, 0)


def middle_part(size, heads, pieces, scale, x, teacher, mask, norm_m, gain, mixed, heads_out, gate_out, carr, wout, wg, wu, wd):
    count = x.shape[0]
    rows = count * size
    inner = wg.shape[1]
    held, deep = D // (size * pieces), inner // pieces
    vmem = pl.BlockSpec(memory_space=pltpu.VMEM)
    out = lambda dims, kind: jax.ShapeDtypeStruct(dims, kind)
    return pl.pallas_call(
        functools.partial(middle_kernel, size, heads),
        in_specs=[pl.BlockSpec(memory_space=pltpu.SMEM)] + [vmem] * 13,
        out_specs=[vmem] * 10,
        out_shape=[
            out((count, D), BF16), out((count, D), F32),
            out((rows, heads * HEAD), BF16), out((rows, heads * HEAD), BF16), out((heads, HEAD, HEAD), F32),
            out((1, HEAD), F32), out((1, D), F32), out((8, HEAD), F32),
            out((pieces, 2 * size * held, inner), BF16), out((pieces, -(-deep // 16) * 16 + held, D), BF16),
        ],
        scratch_shapes=[
            pltpu.VMEM((rows, D), BF16), pltpu.VMEM((rows, D), BF16), pltpu.VMEM((rows, D), BF16),
            pltpu.VMEM((3, size - 1, count, D), BF16), pltpu.VMEM((3, size - 1, count, D), BF16),
            pltpu.VMEM((count, D), F32), pltpu.VMEM((count, D), F32), pltpu.VMEM((count, D), F32),
            pltpu.VMEM((rows, inner), F32), pltpu.VMEM((rows, inner), F32), pltpu.VMEM((rows, inner), BF16),
            pltpu.VMEM((rows, inner), BF16), pltpu.VMEM((rows, inner), BF16),
            pltpu.SemaphoreType.DMA((6, size - 1)), pltpu.SemaphoreType.DMA((6, size - 1)),
        ],
        compiler_params=pltpu.CompilerParams(
            vmem_limit_bytes=56 << 20, collective_id=1, has_side_effects=True
        ),
        name="middle_part",
    )(scale, x, teacher, mask, norm_m, gain, mixed, heads_out, gate_out, carr, wout, wg, wu, wd)


def bwd_kernel(
    heads, pieces, steps, maps_ref, cot_ref, sin_ref, proj_ref, w_ref, rowp_ref, colp_ref, tokp_ref,
    go_ref, conv_ref, q_ref, k_ref, v_ref, t_ref, kk_ref, at_ref, uw_ref, pl_ref, wide_ref, tall_ref,
    gproj_ref, fix_ref, gw_ref, gscal_ref, gsum_ref, widesum_ref, tallsum_ref,
    dstate, weave, rim, last, cots, rim_in, wtheirs, ttheirs, wheld, theld, wcame, tcame,
    cot_send, cot_recv, pair_send, pair_recv, line_send, line_recv, rim_sem,
):
    step = pl.program_id(0)
    block = steps - 1 - step
    here = lax.axis_index("ctx")
    core = lax.rem(here, 2)
    pair = Siblings([wide_ref, tall_ref], [wtheirs, ttheirs], [wheld, theld], pair_send, pair_recv)
    line = LineSum(pieces, [wheld, theld], [wcame, tcame], line_send, line_recv)
    rounds = pieces // 2 - 1
    when_round = [(r * steps) // max(rounds - 1, 1) for r in range(rounds)]

    @pl.when(step == 0)
    def _():
        barrier = pltpu.get_barrier_semaphore()
        side = [({"ctx": here + 1}, (core == 1) & (here < pieces - 1)), ({"ctx": here - 1}, (core == 0) & (here > 0))]
        pl.semaphore_wait(barrier, greet(line_neighbours(pieces) + side, barrier))
        cots[here] = cot_ref[...].astype(BF16)
        spread = Line(pieces, [lambda c: cots.at[c]], cot_send, cot_recv, up=False)
        spread.own()
        pair.start()
        for distance in range(1, pieces // 2):
            spread.hop(distance)
        spread.finish()
        pair.add()

        def hop(i, states):
            k = pieces - 1 - i
            return tuple(
                mm(maps_ref[k, h], states[h], 0, 0) + cots[k, h].astype(F32) for h in range(heads)
            )

        found = lax.fori_loop(
            0, pieces - 1 - here, hop, tuple(jnp.zeros((HEAD, HEAD), F32) for _ in range(heads))
        )
        for h in range(heads):
            dstate[h] = found[h]
        rim[...] = jnp.zeros_like(rim)
        gw_ref[...] = jnp.zeros_like(gw_ref)
        gsum_ref[...] = jnp.zeros_like(gsum_ref)

    for r in range(rounds):
        if when_round[r] < steps:
            pl.when(step == when_round[r])(lambda r=r: line.round(r))

    base = pl.multiple_of(block * BLOCK_LEN, BLOCK_LEN)
    rowp, colp, tokp = rowp_ref[0], colp_ref[0], tokp_ref[0]
    last_row = iota((ROWS, 1), 0) == ROWS - 1
    gscal = jnp.zeros((BLOCK_LEN, HEAD), F32)
    for h in range(heads):
        cols = slice(h * WIDE, (h + 1) * WIDE)
        hc = slice(h * HEAD, (h + 1) * HEAD)
        beta, decay, qdecay, carry, qcarry, dlast, clast = decays(rowp, colp, tokp, h)
        go = go_ref[:, hc]
        query, keys, values = q_ref[0, h], k_ref[0, h], v_ref[0, h]
        inv, kk, attn, uw = t_ref[0, h], kk_ref[0, h], at_ref[0, h], uw_ref[0, h]
        dnext = dstate[h]
        state = mm(pl_ref[0, h, :, :HEAD], sin_ref[h]) + pl_ref[0, h, :, HEAD:]
        both = mm(jnp.concatenate([keys, uw[:, HEAD:]], axis=0), state)
        ks = both[:ROWS]
        upd = uw[:, :HEAD] - both[ROWS:]
        dupd = mm(attn, go, 0, 0) + dlast * mm(keys, dnext)
        dx = mm(inv, dupd, 0, 0)
        dv = beta * dx
        dy = -(carry * dv)
        go32 = go.astype(F32)
        outer = mm(jnp.concatenate([go32, dx], axis=0), upd, 1, 1)
        dattn, da = outer[:BLOCK_LEN], -outer[BLOCK_LEN:]
        dkd = mm(upd, dnext, 1, 1)
        right = mm(jnp.concatenate([go32, dy], axis=0), state, 1, 1)
        gos = right[:BLOCK_LEN]
        e = beta * da * decay
        f = dattn * qdecay
        ef = jnp.concatenate([f, e], axis=0)
        efk = mm(ef, keys)
        dq = qcarry * gos + efk[:BLOCK_LEN]
        dk = (
            right[BLOCK_LEN:]
            + dlast * dkd
            + efk[BLOCK_LEN:]
            + mm(ef, jnp.concatenate([query, keys], axis=0), 0, 0)
        )
        dstate[h] = clast * dnext + mm(
            jnp.concatenate([qcarry * query, keys], axis=0), jnp.concatenate([go32, dy], axis=0), 0, 0
        )
        dakk = da * kk
        z1 = beta * dakk
        z2 = dattn * attn
        dbeta = jnp.sum(dx * (values - carry * ks), axis=1, keepdims=True) + jnp.sum(dakk, axis=1, keepdims=True)
        dlk = dlast * jnp.sum(dkd * keys, axis=1, keepdims=True)
        tail = jnp.sum(dlk, axis=0, keepdims=True) + clast * jnp.sum(
            jnp.sum(state * dnext, axis=1, keepdims=True), axis=0, keepdims=True
        )
        dgrow = jnp.sum(z1, axis=1, keepdims=True) + jnp.sum(dy * ks, axis=1, keepdims=True) - dlk
        dgrow = dgrow + jnp.where(last_row, tail, 0.0)
        dgrow = dgrow - mm(jnp.concatenate([z2, z1], axis=0), jnp.ones((BLOCK_LEN + ROWS, HEAD), BF16), 0, 0)[:, :1]
        lane = iota((ROWS, HEAD), 1)
        weave[2 * h] = jnp.where(lane == 0, dbeta, jnp.where(lane == 1, dgrow, 0.0))
        by_step = [weave[2 * h, pl.ds(j, BLOCK_LEN, NH), :] for j in range(NH)]
        dg = sum(x[:, 1:2] for x in by_step) + jnp.sum(z2, axis=1, keepdims=True)
        dg = dg + qcarry * jnp.sum(query * gos, axis=1, keepdims=True)
        after = (iota((BLOCK_LEN, BLOCK_LEN), 0) <= iota((BLOCK_LEN, BLOCK_LEN), 1)).astype(BF16)
        dlog = tokp[:, 0:1] * mm(after, jnp.broadcast_to(dg, (BLOCK_LEN, HEAD)))[:, :1]
        at = 4 + heads + h * (NH + 2)
        dscal = [by_step[j][:, 0:1] * tokp[:, at + j : at + j + 1] for j in range(NH)]
        dscal.append(dlog * tokp[:, at + NH : at + NH + 1])
        lane = iota((BLOCK_LEN, HEAD), 1)
        for j in range(NH + 1):
            gscal = gscal + jnp.where(lane == h * (NH + 1) + j, dscal[j], 0.0)
        sums = jnp.where(lane == 0, dlog * tokp[:, at + NH + 1 : at + NH + 2], jnp.where(lane == 1, dscal[NH], 0.0))
        gsum_ref[h : h + 1, :] += jnp.sum(sums, axis=0, keepdims=True)
        weave[2 * h] = dk
        weave[2 * h + 1] = dv
        conv = conv_ref[:, cols]
        sig = jax.nn.sigmoid(conv)
        act = conv * sig
        parts = []
        for part in range(1 + NH):
            piece = act[:, part * HEAD : (part + 1) * HEAD]
            scale = lax.rsqrt(jnp.sum(piece * piece, axis=1, keepdims=True) + NORM_EPS)
            if part:
                grad = weave[2 * h, pl.ds(part - 1, BLOCK_LEN, NH), :]
            else:
                grad = dq * (1.0 / math.sqrt(HEAD))
            unit = piece * scale
            parts.append(scale * (grad - unit * jnp.sum(grad * unit, axis=1, keepdims=True)))
        for j in range(NH):
            parts.append(weave[2 * h + 1, pl.ds(j, BLOCK_LEN, NH), :])
        dconv = jnp.concatenate(parts, axis=1) * (sig * (1.0 + conv * (1.0 - sig)))
        ext = proj_ref[pl.ds(base, BLOCK_LEN + HALO), cols].astype(F32)
        gw_ref[0:1, cols] += jnp.sum(dconv * ext[HALO:], axis=0, keepdims=True)
        zeros = jnp.zeros((8, WIDE), F32)
        length = BLOCK_LEN + 8
        total = jnp.concatenate([zeros, dconv * w_ref[0:1, cols]], axis=0)
        for lag in range(1, CONV):
            masked = tokp[:, lag - 1 : lag] * dconv
            gw_ref[lag : lag + 1, cols] += jnp.sum(masked * lag_rows(ext, lag), axis=0, keepdims=True)
            total = total + pltpu.roll(
                jnp.concatenate([zeros, masked * w_ref[lag : lag + 1, cols]], axis=0), length - lag, 0
            )
        fixed = total[length - 8 :] + rim[:, cols]
        gproj_ref[:, cols] = jnp.concatenate([total[8 : length - 8], fixed], axis=0).astype(BF16)
        rim[:, cols] = total[:8]

        @pl.when(step == 0)
        def _():
            last[:, cols] = fixed

    gscal_ref[...] = gscal.astype(BF16)

    @pl.when(step == steps - 1)
    def _():
        passing = pltpu.make_async_remote_copy(
            rim, rim_in, rim_sem.at[0], rim_sem.at[1], device_id={"ctx": here - 1}, device_id_type=MESH
        )
        pl.when(here > 0)(passing.start)
        fix_ref[...] = last[...].astype(BF16)

        @pl.when(here < pieces - 1)
        def _():
            passing.wait_recv()
            fix_ref[...] = (last[...] + rim_in[...]).astype(BF16)

        for r in range(rounds):
            if when_round[r] >= steps:
                line.round(r)
        line.finish()
        widesum_ref[...] = wheld[here // 2]
        tallsum_ref[...] = theld[here // 2].astype(F32)
        pair.left()
        pl.when(here > 0)(passing.wait_send)


def recurrence_backward(
    maps, cot, state_in, proj_ext, conv_w, rowp, colp, tokp, grad_heads, saved, wide, tall, heads, pieces
):
    blocks = rowp.shape[0]
    rows = blocks * BLOCK_LEN
    chips = pieces // 2
    whole = lambda *dims: pl.BlockSpec(dims, lambda i: (0,) * len(dims))
    by_block = lambda *dims: pl.BlockSpec((1,) + dims, lambda i: (blocks - 1 - i,) + (0,) * len(dims))
    token = lambda cols: pl.BlockSpec((BLOCK_LEN, cols), lambda i: (blocks - 1 - i, 0))
    shape = lambda *dims: jax.ShapeDtypeStruct(dims, F32)
    low_shape = lambda *dims: jax.ShapeDtypeStruct(dims, BF16)
    vmem = pl.BlockSpec(memory_space=pltpu.VMEM)
    square = (heads, ROWS, HEAD)
    wide_chunk, tall_chunk = wide.shape[2:], tall.shape[2:]
    dma = pltpu.SemaphoreType.DMA
    return pl.pallas_call(
        functools.partial(bwd_kernel, heads, pieces, blocks),
        grid=(blocks,),
        in_specs=[
            vmem, vmem, vmem, vmem, vmem,
            by_block(*rowp.shape[1:]), by_block(*colp.shape[1:]), by_block(*tokp.shape[1:]),
            token(heads * HEAD), token(heads * WIDE),
            by_block(heads, BLOCK_LEN, HEAD), by_block(*square), by_block(*square), by_block(*square),
            by_block(*square), by_block(heads, BLOCK_LEN, ROWS), by_block(heads, ROWS, 2 * HEAD),
            by_block(heads, HEAD, 2 * HEAD), vmem, vmem,
        ],
        out_specs=[
            token(heads * WIDE), whole(8, heads * WIDE), whole(8, heads * WIDE), token(HEAD), whole(8, HEAD),
            whole(*wide_chunk), whole(*tall_chunk),
        ],
        out_shape=[
            low_shape(rows, heads * WIDE), low_shape(8, heads * WIDE), shape(8, heads * WIDE), low_shape(rows, HEAD),
            shape(8, HEAD), low_shape(*wide_chunk), shape(*tall_chunk),
        ],
        scratch_shapes=[
            pltpu.VMEM((heads, HEAD, HEAD), F32), pltpu.VMEM((2 * heads, ROWS, HEAD), F32),
            pltpu.VMEM((8, heads * WIDE), F32), pltpu.VMEM((8, heads * WIDE), F32),
            pltpu.VMEM((pieces, heads, HEAD, HEAD), BF16), pltpu.VMEM((8, heads * WIDE), F32),
            pltpu.VMEM((chips, *wide_chunk), BF16), pltpu.VMEM((chips, *tall_chunk), BF16),
            pltpu.VMEM((chips, *wide_chunk), BF16), pltpu.VMEM((chips, *tall_chunk), BF16),
            pltpu.VMEM((2, chips, *wide_chunk), BF16), pltpu.VMEM((2, chips, *tall_chunk), BF16),
            dma((1, 3, pieces)), dma((1, pieces)), dma((2,)), dma((2,)), dma((2, chips)), dma((2, 2, chips)), dma((2,)),
        ],
        compiler_params=pltpu.CompilerParams(
            vmem_limit_bytes=58 << 20, collective_id=4, has_side_effects=True
        ),
        name="recurrence_backward",
    )(maps, cot, state_in, proj_ext, conv_w, rowp, colp, tokp, grad_heads, *saved, wide, tall)


def final_kernel(
    size, pieces, gp_ref, gg_ref, gs_ref, w_ref, normed_ref, x_ref, gmid_ref, norm_ref, conv_ref, small_ref, wide_ref,
    ingrad_ref, gmix_ref, ggate_ref, gtail_ref, total_ref, wideout_ref,
    sent, got, own, turned, grads, theirs, held, came, blocks, around, along,
    local_sem, seq_send, seq_recv, pair_send, pair_recv, line_send, line_recv, ctx_send, ctx_recv,
):
    me, here = lax.axis_index("seq"), lax.axis_index("ctx")
    count = x_ref.shape[0]
    barrier = pltpu.get_barrier_semaphore()
    peers = [({"seq": lax.rem(me + i, size)}, here >= 0) for i in range(1, size)]
    peers += [({"ctx": lax.rem(here + i, pieces)}, here >= 0) for i in range(1, pieces)]
    pl.semaphore_wait(barrier, greet(peers, barrier))

    def dot(a, b, ca=1, cb=0):
        return lax.dot_general(a, b, (((ca,), (cb,)), ((), ())), preferred_element_type=F32)

    def rows(q):
        return pl.ds(pl.multiple_of(q * count, count), count)

    def to_peer(n, i):
        q = lax.rem(me + i, size)
        source, target = [
            (sent.at[i - 1], got.at[i - 1]), (wide_ref.at[:, q], wideout_ref.at[me]),
            (around.at[me], around.at[me]), (held.at[here // 2, q], blocks.at[me]),
        ][n]
        return pltpu.make_async_remote_copy(
            source, target, seq_send.at[n, i - 1], seq_recv.at[n, i - 1], device_id={"seq": q}, device_id_type=MESH
        )

    def to_piece(i):
        return pltpu.make_async_remote_copy(
            along.at[here], along.at[here], ctx_send.at[i - 1], ctx_recv.at[i - 1],
            device_id={"ctx": lax.rem(here + i, pieces)}, device_id_type=MESH,
        )

    kept = pltpu.make_async_copy(wide_ref.at[:, me], wideout_ref.at[me], local_sem.at[0])
    kept.start()
    for i in range(1, size):
        to_peer(1, i).start()
    gate_at, tail_at = gp_ref.shape[1], gp_ref.shape[1] + gg_ref.shape[1]

    def part(k, carry):
        i = lax.rem(k + 1, size)
        q = lax.rem(me + i, size)
        value = (
            dot(gp_ref[rows(q)], w_ref[:, :gate_at], 1, 1)
            + dot(gg_ref[rows(q)], w_ref[:, gate_at:tail_at], 1, 1)
            + dot(gs_ref[rows(q)], w_ref[:, tail_at:], 1, 1)
        )

        @pl.when(i > 0)
        def _():
            sent[i - 1] = value.astype(BF16)
            pltpu.make_async_remote_copy(
                sent.at[i - 1], got.at[i - 1], seq_send.at[0, i - 1], seq_recv.at[0, i - 1],
                device_id={"seq": q}, device_id_type=MESH,
            ).start()

        @pl.when(i == 0)
        def _():
            own[...] = value

        return carry

    lax.fori_loop(0, size, part, 0)
    turned[...] = normed_ref[...].T
    rank_rows = D // (size * pieces)
    for source, at in ((gp_ref, 0), (gg_ref, gate_at), (gs_ref, tail_at)):
        width = source.shape[1]
        for first in range(0, width, 256):
            cols = min(256, width - first)
            grad = dot(turned[...], source[:, first : first + cols])
            for r in range(size):
                for c in range(pieces):
                    row = (r * pieces + c) * rank_rows
                    grads[c // 2, c % 2, r, :, at + first : at + first + cols] = grad[row : row + rank_rows].astype(BF16)
    for c in range(pieces):
        grads[c // 2, c % 2, me, :, tail_at:] = (
            grads[c // 2, c % 2, me, :, tail_at:].astype(F32) + conv_ref[c]
        ).astype(BF16)
    pair = Siblings([grads], [theirs], [held], pair_send, pair_recv)
    pair.start()

    for i in range(1, size):
        to_peer(0, i).wait_recv()
    gnormed = own[...]
    for i in range(1, size):
        gnormed = gnormed + got[i - 1].astype(F32)
    x = x_ref[...].astype(F32)
    inv = lax.rsqrt(jnp.mean(x * x, axis=1, keepdims=True) + NORM_EPS)
    unit = x * inv
    down = gnormed * norm_ref[...]
    ingrad_ref[...] = gmid_ref[...] + inv * (down - unit * jnp.mean(down * unit, axis=1, keepdims=True))
    term = jnp.sum(gnormed * unit, axis=0, keepdims=True)
    around[me] = small_ref[...]
    for j in range(D // HEAD):
        around[me, small_ref.shape[0] - D // HEAD + j : small_ref.shape[0] - D // HEAD + j + 1] = term[
            :, j * HEAD : (j + 1) * HEAD
        ]
    for i in range(1, size):
        to_peer(2, i).start()
    pair.add()
    line = LineSum(pieces, [held], [came], line_send, line_recv)
    line.round(0)
    for i in range(1, size):
        to_peer(2, i).wait_recv()
    mine = around[0]
    for r in range(1, size):
        mine = mine + around[r]
    along[here] = mine
    for i in range(1, pieces):
        to_piece(i).start()
    for r in range(1, pieces // 2 - 1):
        line.round(r)
    line.finish()
    blocks[me] = held[here // 2, me]
    for i in range(1, size):
        to_peer(3, i).start()
    for i in range(1, pieces):
        to_piece(i).wait_recv()
    total = along[0]
    for c in range(1, pieces):
        total = total + along[c]
    total_ref[...] = total
    for i in range(1, size):
        to_peer(3, i).wait_recv()
    for r in range(size):
        block = blocks[r].astype(F32)
        gmix_ref[:, r * gate_at : (r + 1) * gate_at] = block[:, :gate_at]
        ggate_ref[:, r * (tail_at - gate_at) : (r + 1) * (tail_at - gate_at)] = block[:, gate_at:tail_at]
        gtail_ref[r] = block[:, tail_at:]
    kept.wait()
    pair.left()
    for i in range(1, size):
        to_peer(1, i).wait_recv()
        for n in range(4):
            to_peer(n, i).wait_send()
    for i in range(1, pieces):
        to_piece(i).wait_send()


def final_part(size, pieces, gp, gg, gs, weights, normed, x, gmid, norm_a, conv, small, wide):
    count = x.shape[0]
    chips = pieces // 2
    held = D // (size * pieces)
    width = weights.shape[1]
    vmem = pl.BlockSpec(memory_space=pltpu.VMEM)
    out = lambda dims, kind=F32: jax.ShapeDtypeStruct(dims, kind)
    dma = pltpu.SemaphoreType.DMA
    return pl.pallas_call(
        functools.partial(final_kernel, size, pieces),
        in_specs=[vmem] * 11,
        out_specs=[vmem] * 6,
        out_shape=[
            out((count, D)), out((held, size * gp.shape[1])), out((held, size * gg.shape[1])),
            out((size, held, gs.shape[1])), out(small.shape), out((size, 2, held, wide.shape[3]), BF16),
        ],
        scratch_shapes=[
            pltpu.VMEM((size - 1, count, D), BF16), pltpu.VMEM((size - 1, count, D), BF16), pltpu.VMEM((count, D), F32),
            pltpu.VMEM((D, normed.shape[0]), BF16),
            pltpu.VMEM((chips, 2, size, held, width), BF16), pltpu.VMEM((chips, size, held, width), BF16),
            pltpu.VMEM((chips, size, held, width), BF16), pltpu.VMEM((2, chips, size, held, width), BF16),
            pltpu.VMEM((size, held, width), BF16), pltpu.VMEM((size, *small.shape), F32),
            pltpu.VMEM((pieces, *small.shape), F32),
            dma((1,)), dma((4, size - 1)), dma((4, size - 1)), dma((1,)), dma((1,)), dma((1, chips)), dma((1, 2, chips)),
            dma((pieces - 1,)), dma((pieces - 1,)),
        ],
        compiler_params=pltpu.CompilerParams(
            vmem_limit_bytes=60 << 20, collective_id=5, has_side_effects=True
        ),
        name="final_part",
    )(gp, gg, gs, weights, normed, x, gmid, norm_a, conv, small, wide)


def rms_scale(values, gain_vec):
    return values * lax.rsqrt(jnp.mean(values * values, axis=-1, keepdims=True) + NORM_EPS) * gain_vec


def dot(a, b):
    return jnp.dot(a, b, preferred_element_type=F32)


def local(
    block_input, teacher, valid_mask, segments, mix_proj, scalar_proj, gate_proj, out_proj, conv_weight,
    norm_attn, norm_mlp, head_gain, a_log, dt_bias, w_gate, w_up, w_down,
):
    seq_size = lax.axis_size("seq")
    heads = HEADS // seq_size
    tok_rows = block_input.shape[0]
    rows = tok_rows * seq_size
    blocks = rows // BLOCK_LEN
    token_total = segments.shape[0]
    seq_length = min(SEQ_LEN, token_total)
    index = lax.axis_index("ctx")
    rank = lax.axis_index("seq")
    head_start = rank * heads

    pieces = lax.axis_size("ctx")
    inner = FF // seq_size
    held = mix_proj.shape[0]
    scal_cols = heads * (NH + 1)
    count_here = jnp.sum(valid_mask.astype(F32)).astype(BF16)
    extra = jnp.concatenate(
        [
            norm_attn[:, None], norm_mlp[:, None],
            jnp.where(jnp.arange(held) == 0, count_here, jnp.zeros((), BF16))[:, None],
            conv_weight.reshape(held, -1),
        ],
        axis=1,
    )
    by_rank = lambda w: jnp.swapaxes(w.reshape(held, seq_size, -1), 0, 1)
    first = jnp.concatenate(
        [
            by_rank(mix_proj), by_rank(gate_proj), by_rank(scalar_proj),
            jnp.broadcast_to(extra[None], (seq_size, *extra.shape)),
            jnp.zeros((seq_size, held, HEAD - scal_cols - extra.shape[1]), BF16),
        ],
        axis=2,
    )
    later = jnp.stack([by_rank(w_gate), by_rank(w_up)], axis=1)
    x_full, halo, gathered, stage = start_gather(seq_size, pieces, block_input, first, later)
    weights = gathered.reshape(D, -1)
    gate_at = heads * WIDE
    scal_at = gate_at + heads * HEAD
    norm_at = scal_at + scal_cols
    norm_a = weights[:, norm_at].astype(F32)
    norm_m = weights[:, norm_at + 1].astype(F32)
    valid_count = jnp.maximum(jnp.sum(weights[:, norm_at + 2].astype(F32)), 1.0)
    conv_s = lax.dynamic_slice_in_dim(weights[:, norm_at + 3 : norm_at + extra.shape[1]], rank * (D // seq_size), D // seq_size)
    conv_s = conv_s.reshape(heads * WIDE, CONV)

    extended = jnp.concatenate([halo, x_full], axis=0).astype(F32)
    normed_ext = rms_scale(extended, norm_a).astype(BF16)
    normed = normed_ext[HALO:]
    proj_ext = dot(normed_ext, weights[:, :gate_at]).astype(BF16)
    rest = dot(normed, weights[:, gate_at:])
    gate_out = rest[:, : heads * HEAD]
    scal = rest[:, heads * HEAD : heads * HEAD + scal_cols].astype(BF16)

    piece_start = index * rows
    window = lax.dynamic_slice_in_dim(jnp.pad(segments, (CONV, 0)), piece_start, rows + CONV)
    place_in = (piece_start + jnp.arange(rows, dtype=jnp.int32)) % seq_length
    own_seg = window[CONV:]
    linked = [
        ((window[CONV - lag : CONV - lag + rows] == own_seg) & (place_in >= lag)).astype(F32) for lag in range(1, CONV)
    ]
    starts = 1.0 - linked[0]
    alog_heads = lax.dynamic_slice_in_dim(a_log.astype(F32), head_start, heads, 0)
    dt_heads = lax.dynamic_slice_in_dim(dt_bias.astype(F32), head_start, heads, 0)
    scal = scal.astype(F32).reshape(rows, heads, NH + 1)
    beta = jax.nn.sigmoid(scal[:, :, :NH])
    rate = -jnp.exp(alog_heads)[None, :]
    lifted = scal[:, :, NH] + dt_heads[None, :]
    logs = rate * jax.nn.softplus(lifted)
    slopes = jnp.concatenate(
        [beta * (1.0 - beta), (rate * jax.nn.sigmoid(lifted))[:, :, None], logs[:, :, None]], axis=2
    ).reshape(blocks, BLOCK_LEN, heads * (NH + 2))
    lower = jnp.tril(jnp.ones((BLOCK_LEN, BLOCK_LEN), F32))
    sums = jnp.einsum(
        "ts,bsh->bth",
        lower,
        jnp.concatenate([starts[:, None], logs * (1.0 - starts)[:, None]], axis=1).reshape(blocks, BLOCK_LEN, heads + 1),
        precision=lax.Precision.HIGHEST,
    )
    tokp = jnp.concatenate([jnp.stack(linked, axis=1).reshape(blocks, BLOCK_LEN, CONV - 1), sums, slopes], axis=2)
    sums_rows = jnp.repeat(sums, NH, axis=1)
    beta_rows = jnp.swapaxes(beta, 1, 2).reshape(blocks, ROWS, heads)
    colp = jnp.concatenate(
        [sums_rows[:, :, :1], jnp.zeros_like(sums_rows[:, :, :1])]
        + [x[:, :, h : h + 1] for h in range(heads) for x in (sums_rows[:, :, 1:], beta_rows)],
        axis=2,
    )
    rowp = jnp.swapaxes(colp, 1, 2)
    conv_w = jnp.pad(jnp.flip(conv_s.astype(F32).T, 0), ((0, 8 - CONV), (0, 0)))

    (
        oloc, carr, state_in, maps, *saved, wg_full, wu_full, wd_full, wo_full,
    ) = recurrence_forward(proj_ext, conv_w, rowp, colp, tokp, stage, w_down, out_proj, heads, pieces)
    wg_s, wu_s = wg_full.reshape(D, inner), wu_full.reshape(D, inner)
    down_s, out_s = wd_full.reshape(inner, D), wo_full.reshape(heads * HEAD, D)
    gain = head_gain.astype(F32)[None, :]
    heads_out, mixed = state_and_gate(state_in, oloc, carr, gate_out, gain, heads)

    scale = (token_total / valid_count).reshape(1, 1)
    mask_values = valid_mask.astype(F32)[:, None]
    (
        final_out, grad_middle, grad_heads, grad_gate_out, cot, gain_term, norm_mlp_term, loss, wide, tall,
    ) = middle_part(
        seq_size, heads, pieces, scale, block_input, teacher, mask_values, norm_m[None, :], gain, mixed, heads_out,
        gate_out, carr, out_s, wg_s, wu_s, down_s,
    )
    by_chip = lambda v: v.reshape(pieces // 2, 2, *v.shape[1:])
    grad_proj, fixed_rows, gw, grad_scal, gsum, wide_sum, tall_sum = recurrence_backward(
        maps, cot, state_in, proj_ext, conv_w, rowp, colp, tokp, grad_heads, saved, by_chip(wide), by_chip(tall),
        heads, pieces,
    )
    grad_proj = lax.dynamic_update_slice_in_dim(grad_proj, fixed_rows, rows - 8, 0)
    deep = w_down.shape[0]
    down_grad, out_grad = tall_sum[:deep], tall_sum[tall_sum.shape[0] - held :]
    conv_terms = jnp.flip(gw[:CONV], 0).T.reshape(pieces, held, -1)
    conv_at = norm_at + 3 - scal_at
    conv_cols = conv_terms.shape[2]
    conv_terms = jnp.pad(conv_terms, ((0, 0), (0, 0), (conv_at, HEAD - conv_at - conv_cols)))
    pick = (jnp.arange(HEADS)[None, :] == head_start + jnp.arange(heads)[:, None]).astype(F32)
    ends = jnp.concatenate(
        [
            jnp.sum(gsum[:heads, 0:1] * pick, axis=0), jnp.sum(gsum[:heads, 1:2] * pick, axis=0), loss[0, :1],
            jnp.zeros((HEAD - 2 * HEADS - 1,), F32),
        ]
    )
    small = jnp.concatenate(
        [
            gain_term, ends[None], jnp.zeros((6, HEAD), F32), norm_mlp_term.reshape(-1, HEAD),
            jnp.zeros((D // HEAD, HEAD), F32),
        ],
        axis=0,
    )
    input_grad, mix_grad, gate_grad, tails, small, wide_out = final_part(
        seq_size, pieces, grad_proj, grad_gate_out, grad_scal, weights, normed, block_input, grad_middle,
        norm_a[None, :], conv_terms, small, wide_sum.reshape(2, seq_size, held, inner),
    )
    scal_grad = jnp.swapaxes(tails[:, :, :scal_cols], 0, 1).reshape(held, -1)
    conv_grad = lax.dynamic_index_in_dim(tails, rank, 0, False)[:, conv_at : conv_at + conv_cols].reshape(-1, CONV)
    across = lambda v: jnp.swapaxes(v, 0, 1).reshape(held, FF).astype(F32)
    mean_loss = small[1, 2 * HEADS] / (D * valid_count)
    place = (rank * pieces + index) * held
    norms = small[8:].reshape(2, D)
    return (
        final_out,
        mean_loss,
        input_grad,
        mix_grad,
        scal_grad,
        gate_grad,
        out_grad,
        conv_grad,
        lax.dynamic_slice_in_dim(norms[1], place, held),
        lax.dynamic_slice_in_dim(norms[0], place, held),
        small[0],
        small[1, :HEADS],
        small[1, HEADS : 2 * HEADS],
        across(wide_out[:, 0]),
        across(wide_out[:, 1]),
        down_grad,
    )


def solution(mesh):
    tokens, vector, matrix = P(("ctx", "seq"), None), P(BOTH), P(BOTH, None)
    in_specs = (
        tokens, tokens, P(("ctx", "seq")), P(), matrix, matrix, matrix, matrix, matrix, vector, vector,
        P(), P(), P(), matrix, matrix, matrix,
    )
    out_specs = (
        tokens, P(), tokens, matrix, matrix, matrix, matrix, matrix, vector, vector, P(), P(), P(),
        matrix, matrix, matrix,
    )
    return jax.shard_map(local, mesh=mesh, in_specs=in_specs, out_specs=out_specs, check_vma=False)
```

```python
import functools
import math

import jax
import jax.numpy as jnp
from jax import lax
from jax.experimental import pallas as pl
from jax.experimental.pallas import tpu as pltpu
from jax.sharding import PartitionSpec as P

D = 1024
HEADS = 8
HEAD = 128
NH = 2
FF = 2816
BLOCK_LEN = 64
ROWS = BLOCK_LEN * NH
CONV = 4
SEQ_LEN = 32768
WIDE = (1 + 2 * NH) * HEAD
HALO = 16
NORM_EPS = 1e-06
VMEM_LIMIT = 60 << 20
F32 = jnp.float32
BF16 = jnp.bfloat16
BOTH = ("seq", "ctx")
MESH = pl.DeviceIdType.MESH


def split_bf16(x):
    if x.dtype == BF16:
        return x, None
    high = x.astype(BF16)
    return high, (x - high.astype(F32)).astype(BF16)


def mm(a, b, ca=1, cb=0, passes=3):
    def one(x, y):
        return lax.dot_general(x, y, (((ca,), (cb,)), ((), ())), preferred_element_type=F32)

    if passes == 1:
        return one(a.astype(BF16), b.astype(BF16))
    ah, al = split_bf16(a)
    bh, bl = split_bf16(b)
    total = one(ah, bh)
    if bl is not None:
        total = total + one(ah, bl)
    if al is not None:
        total = total + one(al, bh)
    return total


def lanes_for(columns):
    return -(-columns // HEAD) * HEAD


def iota(shape, axis):
    return lax.broadcasted_iota(jnp.int32, shape, axis)


def unit_lower_inverses(systems):
    n = systems[0].shape[0]
    ri, ci = iota((n, n), 0), iota((n, n), 1)
    pick = (iota((n, 8), 0) % 8 == iota((n, 8), 1)).astype(BF16)
    own = ri // 8 == ci // 8
    eye = (ri == ci).astype(F32).reshape(n // 8, 8, n)
    small = [mm(jnp.where(own, a, 0.0), pick).reshape(n // 8, 8, 8) for a in systems]
    inv = [eye for _ in systems]
    for j in range(7):
        inv = [x - m[:, :, j : j + 1] * x[:, j : j + 1, :] for x, m in zip(inv, small)]
    inv = [x.reshape(n, n) for x in inv]
    size = 8
    while size < n:
        off = (ri // (2 * size) == ci // (2 * size)) & (ri // size != ci // size)
        right = [mm(jnp.where(off, a, 0.0), x) for a, x in zip(systems, inv)]
        inv = [x - mm(x, y) for x, y in zip(inv, right)]
        size *= 2
    return inv


DOC = 7
LINK = DOC + 1


def lane_of(h, what):
    return h * (NH + 1) + what


def column(table, lane):
    return table[:, lane : lane + 1]


def decays(rowp, colp, tokp, h):
    g = lane_of(h, NH)
    cs_row, g_row = rowp[DOC : DOC + 1, :], rowp[g : g + 1, :]
    cs_col, g_col = column(colp, DOC), column(colp, g)
    cs_tok, g_tok = column(tokp, DOC), column(tokp, g)
    beta = column(colp, lane_of(h, 0))
    ri, ci = iota((ROWS, ROWS), 0), iota((ROWS, ROWS), 1)
    strict = (ri > ci) & (cs_col == cs_row)
    decay = jnp.where(strict, jnp.exp(jnp.where(strict, g_col - g_row, 0.0)), 0.0)
    rt, ct = iota((BLOCK_LEN, ROWS), 0), iota((BLOCK_LEN, ROWS), 1)
    seen = (rt * NH + NH - 1 >= ct) & (cs_tok == cs_row)
    qdecay = jnp.where(seen, jnp.exp(jnp.where(seen, g_tok - g_row, 0.0)), 0.0)
    carry = jnp.where(cs_col == 0.0, jnp.exp(g_col), 0.0)
    qcarry = jnp.where(cs_tok == 0.0, jnp.exp(g_tok), 0.0)
    cs_last, g_last = cs_row[:, ROWS - 1 :], g_row[:, ROWS - 1 :]
    same = cs_col == cs_last
    dlast = jnp.where(same, jnp.exp(jnp.where(same, g_last - g_col, 0.0)), 0.0)
    clast = jnp.where(cs_last == 0.0, jnp.exp(g_last), 0.0)
    return beta, decay, qdecay, carry, qcarry, dlast, clast


def lag_rows(ext, lag):
    moved = pltpu.roll(ext, lag, 0) if lag else ext
    return moved[HALO:]


UP, DOWN, ACROSS = 0, 1, 2


class Line:
    def __init__(self, pieces, parts, send_sem, recv_sem, up=True, down=True):
        self.chips = pieces // 2
        self.here = lax.axis_index("ctx")
        self.chip = self.here // 2
        self.core = lax.rem(self.here, 2)
        self.other = self.here + 1 - 2 * self.core
        self.parts, self.send_sem, self.recv_sem, self.up, self.down = parts, send_sem, recv_sem, up, down

    def copies(self, chunk, way):
        target = (self.here + 2, self.here - 2, self.other)[way]
        return [
            pltpu.make_async_remote_copy(
                part(chunk), part(chunk), self.send_sem.at[n, way, chunk], self.recv_sem.at[n, chunk],
                device_id={"ctx": target}, device_id_type=MESH,
            )
            for n, part in enumerate(self.parts)
        ]

    def start(self, chunk, way):
        for copy in self.copies(chunk, way):
            copy.start()

    def arrived(self, chunk):
        for copy in self.copies(chunk, ACROSS):
            copy.wait_recv()

    def left(self, chunk, way):
        for copy in self.copies(chunk, way):
            copy.wait_send()

    def routes(self, distance, act):
        if distance == 0:
            if self.up:
                pl.when(self.chip < self.chips - 1)(lambda: act(self.here, UP))
            if self.down:
                pl.when(self.chip > 0)(lambda: act(self.here, DOWN))
            act(self.here, ACROSS)
            return
        below, above = self.here - 2 * distance, self.here + 2 * distance
        if self.up:

            @pl.when(self.chip >= distance)
            def _():
                pl.when(self.chip < self.chips - 1)(lambda: act(below, UP))
                act(below, ACROSS)

        if self.down:

            @pl.when(self.chip + distance < self.chips)
            def _():
                pl.when(self.chip > 0)(lambda: act(above, DOWN))
                act(above, ACROSS)

    def own(self):
        self.routes(0, self.start)

    def hop(self, distance):
        if self.up:
            pl.when(self.chip >= distance)(lambda: self.arrived(self.here - 2 * distance))
        if self.down:
            pl.when(self.chip + distance < self.chips)(lambda: self.arrived(self.here + 2 * distance))
        self.routes(distance, self.start)

    def finish(self):
        for chip in range(self.chips):
            needed = True
            if not self.down:
                needed = self.chip >= chip
            if not self.up:
                needed = self.chip <= chip
            pl.when(needed)(lambda chip=chip: self.arrived(2 * chip + 1 - self.core))
        for distance in range(self.chips):
            self.routes(distance, self.left)


class LineSum:
    def __init__(self, pieces, held, came, send_sem, recv_sem):
        self.chips = pieces // 2
        self.here = lax.axis_index("ctx")
        self.chip = self.here // 2
        self.held, self.came, self.send_sem, self.recv_sem = held, came, send_sem, recv_sem

    def copies(self, owner, way):
        return [
            pltpu.make_async_remote_copy(
                held.at[owner], came.at[way, owner], self.send_sem.at[n, owner], self.recv_sem.at[n, way, owner],
                device_id={"ctx": self.here + 2 - 4 * way}, device_id_type=MESH,
            )
            for n, (held, came) in enumerate(zip(self.held, self.came))
        ]

    def take(self, owner, way):
        for copy in self.copies(owner, way):
            copy.wait_recv()
        for held, came in zip(self.held, self.came):
            held[owner] = (held[owner].astype(F32) + came[way, owner].astype(F32)).astype(BF16)

    def send(self, owner, way):
        for copy in self.copies(owner, way):
            copy.start()

    def round(self, r):
        top = self.chips - 1
        for way, place in ((UP, self.chip), (DOWN, top - self.chip)):
            owner = top - (r - place) if way == UP else r - place

            @pl.when((place <= r) & (place < top))
            def _():
                pl.when(place > 0)(lambda: self.take(owner, way))
                self.send(owner, way)

    def finish(self):
        top = self.chips - 1
        pl.when(self.chip > 0)(lambda: self.take(self.chip, UP))
        pl.when(self.chip < top)(lambda: self.take(self.chip, DOWN))
        for owner in range(self.chips):
            for way, wanted in ((UP, self.chip < owner), (DOWN, self.chip > owner)):

                @pl.when(wanted)
                def _():
                    for copy in self.copies(owner, way):
                        copy.wait_send()


class Siblings:
    def __init__(self, parts, theirs, held, send_sem, recv_sem):
        self.here = lax.axis_index("ctx")
        self.core = lax.rem(self.here, 2)
        self.parts, self.theirs, self.held, self.send_sem, self.recv_sem = parts, theirs, held, send_sem, recv_sem

    def copies(self):
        return [
            pltpu.make_async_remote_copy(
                part.at[:, 1 - self.core], theirs, self.send_sem.at[n], self.recv_sem.at[n],
                device_id={"ctx": self.here + 1 - 2 * self.core}, device_id_type=MESH,
            )
            for n, (part, theirs) in enumerate(zip(self.parts, self.theirs))
        ]

    def start(self):
        for copy in self.copies():
            copy.start()

    def add(self):
        for copy in self.copies():
            copy.wait_recv()
        for part, theirs, held in zip(self.parts, self.theirs, self.held):

            def one(chip, carry, part=part, theirs=theirs, held=held):
                held[chip] = (part[chip, self.core].astype(F32) + theirs[chip].astype(F32)).astype(BF16)
                return carry

            lax.fori_loop(0, part.shape[0], one, 0)

    def left(self):
        for copy in self.copies():
            copy.wait_send()


def greet(devices, barrier):
    total = 0
    for place, there in devices:
        pl.when(there)(
            lambda place=place: pl.semaphore_signal(barrier, inc=1, device_id=place, device_id_type=MESH)
        )
        total = total + jnp.asarray(there, jnp.int32)
    return total


def line_neighbours(pieces):
    here = lax.axis_index("ctx")
    chip, core = here // 2, lax.rem(here, 2)
    return [
        ({"ctx": here + 2}, chip < pieces // 2 - 1),
        ({"ctx": here - 2}, chip > 0),
        ({"ctx": here + 1 - 2 * core}, here >= 0),
    ]


def start_kernel(
    size, pieces, x_ref, mix_ref, gate_ref, tail_ref, wg_ref, wu_ref, xfull_ref, halo_ref, full_ref, stage_ref,
    sides, local_sem, seq_send, seq_recv, line_send, line_recv, halo_sem,
):
    me, here = lax.axis_index("seq"), lax.axis_index("ctx")
    count = x_ref.shape[0]
    core = lax.rem(here, 2)
    inner = wg_ref.shape[1] // size
    gate_at = mix_ref.shape[1] // size
    tail_at = gate_at + gate_ref.shape[1] // size
    barrier = pltpu.get_barrier_semaphore()
    peers = [({"seq": lax.rem(me + i, size)}, here >= 0) for i in range(1, size)]
    side = [({"ctx": here + 1}, (core == 1) & (here < pieces - 1)), ({"ctx": here - 1}, (core == 0) & (here > 0))]
    total = greet(peers + line_neighbours(pieces) + side, barrier)
    pl.semaphore_wait(barrier, total)

    def rows(q):
        return pl.ds(pl.multiple_of(q * count, count), count)

    def cols(q, width):
        return pl.ds(pl.multiple_of(q * width, HEAD), width)

    def ends(n, q):
        return [
            (mix_ref.at[:, cols(q, gate_at)], full_ref.at[me, here, :, :gate_at]),
            (gate_ref.at[:, cols(q, tail_at - gate_at)], full_ref.at[me, here, :, gate_at:tail_at]),
            (tail_ref, full_ref.at[me, here, :, tail_at:]),
            (x_ref, xfull_ref.at[rows(me)]),
            (sides.at[q], stage_ref.at[me]),
        ][n]

    def exchange(n, i):
        q = lax.rem(me + i, size)
        source, target = ends(n, q)
        return pltpu.make_async_remote_copy(
            source, target, seq_send.at[n, i - 1], seq_recv.at[n, i - 1], device_id={"seq": q}, device_id_type=MESH
        )

    def own(n):
        return pltpu.make_async_copy(*ends(n, me), local_sem.at[n])

    def begin(n):
        own(n).start()
        for i in range(1, size):
            exchange(n, i).start()

    def end(n):
        own(n).wait()
        for i in range(1, size):
            exchange(n, i).wait_recv()

    for n in range(4):
        begin(n)
    sides[...] = jnp.zeros_like(sides)
    for q in range(size):
        sides[q, 0, :, :inner] = wg_ref[:, q * inner : (q + 1) * inner]
        sides[q, 1, :, :inner] = wu_ref[:, q * inner : (q + 1) * inner]
    line = Line(pieces, [lambda c: full_ref.at[:, c]], line_send, line_recv)
    for n in range(3):
        end(n)
    line.own()
    begin(4)
    end(3)
    last = xfull_ref.at[pl.ds(size * count - HALO, HALO)]
    passing = pltpu.make_async_remote_copy(
        last, halo_ref, halo_sem.at[0], halo_sem.at[1], device_id={"ctx": here + 1}, device_id_type=MESH
    )
    pl.when(here < pieces - 1)(passing.start)

    @pl.when(here == 0)
    def _():
        filling = pltpu.make_async_copy(last, halo_ref, local_sem.at[5])
        filling.start()
        filling.wait()

    for distance in range(1, pieces // 2):
        line.hop(distance)
    line.finish()
    end(4)
    pl.when(here > 0)(passing.wait_recv)
    pl.when(here < pieces - 1)(passing.wait_send)
    for n in range(5):
        for i in range(1, size):
            exchange(n, i).wait_send()


def start_gather(size, pieces, x, mix, gate, tail, w_gate, w_up):
    anywhere = pl.BlockSpec(memory_space=pl.ANY)
    vmem = pl.BlockSpec(memory_space=pltpu.VMEM)
    out = lambda *dims: jax.ShapeDtypeStruct(dims, BF16)
    dma = pltpu.SemaphoreType.DMA
    held, padded = w_gate.shape[0], lanes_for(w_gate.shape[1] // size)
    width = (mix.shape[1] + gate.shape[1]) // size + tail.shape[1]
    return pl.pallas_call(
        functools.partial(start_kernel, size, pieces),
        in_specs=[anywhere] * 4 + [vmem] * 2,
        out_specs=[anywhere] * 4,
        out_shape=[
            out(x.shape[0] * size, D), out(HALO, D), out(size, pieces, held, width), out(size, 2, held, padded),
        ],
        scratch_shapes=[
            pltpu.VMEM((size, 2, held, padded), BF16),
            dma((6,)), dma((5, size - 1)), dma((5, size - 1)), dma((1, 3, pieces)), dma((1, pieces)), dma((2,)),
        ],
        compiler_params=pltpu.CompilerParams(
            vmem_limit_bytes=VMEM_LIMIT, collective_id=2, has_side_effects=True
        ),
        name="start_gather",
    )(x, mix, gate, tail, w_gate, w_up)


def exact(a, b, ca=1, cb=0):
    return lax.dot_general(
        a, b, (((ca,), (cb,)), ((), ())), precision=lax.Precision.HIGHEST, preferred_element_type=F32
    )


def tap_lanes(channels, tap, at):
    lanes = iota((channels, HEAD), 1)
    return (lanes == at + CONV * (iota((channels, HEAD), 0) % (WIDE // HEAD)) + tap).astype(BF16)


def channel_rows(rows, channels):
    return iota((rows, channels), 1) // (WIDE // HEAD) == iota((rows, channels), 0)


def front_body(
    heads, norm_at, rates_ref, x_ref, halo_ref, w_ref, marks_ref,
    proj_ref, normed_ref, gate_ref, tok_ref, slope_ref, col_ref, row_ref, taps_ref, norms_ref,
):
    me = lax.axis_index("seq")
    channels = heads * WIDE
    tail_at = channels + heads * HEAD
    rows = x_ref.shape[0]
    own_rows = D * heads // HEADS

    def dot(a, b, ca=1, cb=0):
        return lax.dot_general(a, b, (((ca,), (cb,)), ((), ())), preferred_element_type=F32)

    pick = (iota((8, HEAD), 1) == norm_at + iota((8, HEAD), 0)).astype(BF16)
    norms_ref[...] = dot(pick, w_ref[:, tail_at:], 1, 1)

    def normal(values):
        values = values.astype(F32)
        scale = lax.rsqrt(jnp.mean(values * values, axis=1, keepdims=True) + NORM_EPS)
        return (values * scale * norms_ref[0:1, :]).astype(BF16)

    early = normal(halo_ref[...])
    normed_ref[...] = normal(x_ref[...])
    proj_ref[:HALO] = dot(early, w_ref[:, :channels]).astype(BF16)
    proj_ref[HALO:] = dot(normed_ref[...], w_ref[:, :channels]).astype(BF16)
    gate_ref[...] = dot(normed_ref[...], w_ref[:, channels:tail_at])
    tail = w_ref[pl.ds(pl.multiple_of(me * own_rows, own_rows), own_rows), tail_at:]
    taps_ref[...] = jnp.zeros_like(taps_ref)
    mine = channel_rows(own_rows, channels)
    for lag in range(CONV):
        spread = dot(tail, tap_lanes(channels, CONV - 1 - lag, norm_at + 3), 1, 1)
        taps_ref[lag : lag + 1] = jnp.sum(jnp.where(mine, spread, 0.0), axis=0, keepdims=True)

    raw = dot(normed_ref[...], w_ref[:, tail_at:]).astype(BF16).astype(F32)
    raw = pltpu.roll(raw, lax.rem(HEAD - me * lane_of(heads, 0), HEAD), 1)
    lane = iota((1, HEAD), 1)
    rate, lift = jnp.zeros((1, HEAD), F32), jnp.zeros((1, HEAD), F32)
    for h in range(heads):
        here = lane == lane_of(h, NH)
        rate = jnp.where(here, -jnp.exp(jnp.zeros((1, HEAD), F32) + rates_ref[0, me * heads + h]), rate)
        lift = jnp.where(here, rates_ref[1, me * heads + h], lift)
    is_log = (lane % (NH + 1) == NH) & (lane < lane_of(heads, 0))
    lifted = raw + lift
    sig = jax.nn.sigmoid(lifted)
    logs = rate * (jnp.maximum(lifted, 0.0) + jnp.log1p(jnp.exp(-jnp.abs(lifted))))
    slope_ref[...] = jnp.where(is_log, rate * sig, sig * (1.0 - sig)) * (lane < HEAD // 2) + pltpu.roll(
        jnp.where(is_log, logs, 0.0), HEAD // 2, 1
    )
    place = (iota((8, HEAD), 1) == LINK + iota((8, HEAD), 0)) & (iota((8, HEAD), 0) < CONV - 1)
    links = dot(marks_ref[...].astype(BF16), place.astype(BF16), 0, 0)
    open_ = column(links, LINK)
    summed = jnp.where(is_log, logs * open_, jnp.where(lane == DOC, 1.0 - open_, 0.0))
    lower = (iota((BLOCK_LEN, BLOCK_LEN), 0) >= iota((BLOCK_LEN, BLOCK_LEN), 1)).astype(F32)
    spread = (iota((ROWS, BLOCK_LEN), 0) // NH == iota((ROWS, BLOCK_LEN), 1)).astype(F32)
    step = iota((ROWS, HEAD), 0) % NH
    for b in range(rows // BLOCK_LEN):
        span = slice(b * BLOCK_LEN, (b + 1) * BLOCK_LEN)
        sums = exact(lower, summed[span])
        tok = jnp.where(is_log | (lane == DOC), sums, jnp.where(lane < DOC, sig[span], links[span]))
        tok_ref[span] = tok
        wide = exact(spread, tok)
        first = wide
        for j in range(1, NH):
            first = jnp.where(step == j, pltpu.roll(wide, HEAD - j, 1), first)
        col = jnp.where(lane % (NH + 1) == 0, jnp.where(lane < lane_of(heads, 0), first, wide), wide)
        col_ref[b * ROWS : (b + 1) * ROWS] = col
        row_ref[b * 8 : (b + 1) * 8] = col.T[:8]


def fwd_kernel(
    heads, pieces, steps, per, norm_at,
    rates_ref, x_ref, halo_ref, full_ref, marks_ref, stage_ref, wo_ref,
    proj_ref, normed_ref, gate_ref, tok_ref, slope_ref, col_ref, row_ref, taps_ref, norms_ref,
    oloc_ref, carr_ref, sin_ref, mapsout_ref, conv_ref, q_ref, k_ref, v_ref, t_ref, kk_ref, at_ref, uw_ref, pl_ref,
    wgfull_ref, wufull_ref, wofull_ref,
    state, weave, maps, wgs, wus, wos, local_sem, line_send, line_recv, map_send, map_recv,
):
    step = pl.program_id(0)
    here = lax.axis_index("ctx")
    weights = Line(
        pieces, [lambda c: wgs.at[:, c], lambda c: wus.at[:, c], lambda c: wos.at[c]], line_send, line_recv
    )
    eye = (iota((HEAD, HEAD), 0) == iota((HEAD, HEAD), 1)).astype(F32)

    @pl.when(step == 0)
    def _():
        owned = [
            pltpu.make_async_copy(source, target, local_sem.at[n])
            for n, (source, target) in enumerate(
                [(stage_ref.at[:, 0], wgs.at[:, here]), (stage_ref.at[:, 1], wus.at[:, here]), (wo_ref, wos.at[here])]
            )
        ]
        for copy in owned:
            copy.start()
        barrier = pltpu.get_barrier_semaphore()
        pl.semaphore_wait(barrier, greet(line_neighbours(pieces), barrier))
        for copy in owned:
            copy.wait()
        weights.own()
        front_body(
            heads, norm_at, rates_ref, x_ref, halo_ref, full_ref, marks_ref,
            proj_ref, normed_ref, gate_ref, tok_ref, slope_ref, col_ref, row_ref, taps_ref, norms_ref,
        )
        for h in range(heads):
            state[h, :, :HEAD] = eye
            state[h, :, HEAD:] = jnp.zeros((HEAD, HEAD), F32)

    hops = [(d * (steps + 1)) // (pieces // 2) for d in range(1, pieces // 2)]
    for distance, at in enumerate(hops, 1):
        if at < steps:
            pl.when(step == at)(lambda distance=distance: weights.hop(distance))

    items = [(j, h) for j in range(per) for h in range(heads)]
    cols = lambda h: slice(h * WIDE, (h + 1) * WIDE)
    span = lambda j, length=BLOCK_LEN: slice(j * length, (j + 1) * length)
    tables = []
    for j in range(per):
        block = step * per + j
        tables.append(
            (
                row_ref[pl.ds(pl.multiple_of(block * 8, 8), 8), :],
                col_ref[pl.ds(pl.multiple_of(block * ROWS, ROWS), ROWS), :],
                tok_ref[pl.ds(pl.multiple_of(block * BLOCK_LEN, BLOCK_LEN), BLOCK_LEN), :],
            )
        )
    acts = []
    for j, h in items:
        base = pl.multiple_of((step * per + j) * BLOCK_LEN, BLOCK_LEN)
        ext = proj_ref[pl.ds(base, BLOCK_LEN + HALO), cols(h)].astype(F32)
        conv = ext[HALO:] * taps_ref[0:1, cols(h)]
        for lag in range(1, CONV):
            conv = conv + column(tables[j][2], LINK + lag - 1) * lag_rows(ext, lag) * taps_ref[lag : lag + 1, cols(h)]
        conv_ref[span(j), cols(h)] = conv
        acts.append(conv * jax.nn.sigmoid(conv))
    queries, keys, values = [], [], []
    for n, act in enumerate(acts):
        unit = []
        for part in range(1 + NH):
            piece = act[:, part * HEAD : (part + 1) * HEAD]
            unit.append(piece * lax.rsqrt(jnp.sum(piece * piece, axis=1, keepdims=True) + NORM_EPS))
        queries.append(unit[0] * (1.0 / math.sqrt(HEAD)))
        for j in range(NH):
            weave[2 * n, pl.ds(j, BLOCK_LEN, NH), :] = unit[1 + j]
            weave[2 * n + 1, pl.ds(j, BLOCK_LEN, NH), :] = act[:, (1 + NH + j) * HEAD : (2 + NH + j) * HEAD]
    for n in range(len(items)):
        keys.append(weave[2 * n])
        values.append(weave[2 * n + 1])
    factors = [decays(*tables[j], h) for j, h in items]
    grams = [mm(jnp.concatenate([q, k], axis=0), k, 1, 1) for q, k in zip(queries, keys)]
    kks = [f[1] * g[BLOCK_LEN:] for f, g in zip(factors, grams)]
    attns = [f[2] * g[:BLOCK_LEN] for f, g in zip(factors, grams)]
    invs = unit_lower_inverses([f[0] * kk for f, kk in zip(factors, kks)])
    uws = [
        mm(inv, jnp.concatenate([f[0] * v, (f[0] * f[3]) * k], axis=1))
        for inv, f, v, k in zip(invs, factors, values, keys)
    ]
    auws = [mm(attn, uw) for attn, uw in zip(attns, uws)]
    nms = [mm(f[5] * k, uw, 0, 0) for f, k, uw in zip(factors, keys, uws)]
    for n, (j, h) in enumerate(items):
        before = state[h]
        f = factors[n]
        both = mm(
            jnp.concatenate([f[4] * queries[n] - auws[n][:, HEAD:], f[6] * eye - nms[n][:, HEAD:]], axis=0), before
        )
        hc = slice(h * HEAD, (h + 1) * HEAD)
        carr_ref[span(j), hc] = both[:BLOCK_LEN, :HEAD]
        oloc_ref[span(j), hc] = both[:BLOCK_LEN, HEAD:] + auws[n][:, :HEAD]
        state[h, :, :HEAD] = both[BLOCK_LEN:, :HEAD]
        state[h, :, HEAD:] = both[BLOCK_LEN:, HEAD:] + nms[n][:, :HEAD]
        q_ref[j, h] = queries[n]
        k_ref[j, h] = keys[n]
        v_ref[j, h] = values[n]
        t_ref[j, h] = invs[n]
        kk_ref[j, h] = kks[n]
        at_ref[j, h] = attns[n]
        uw_ref[j, h] = uws[n]
        pl_ref[j, h] = before

    @pl.when(step == steps - 1)
    def _():
        maps[here] = state[...].astype(BF16)
        line = Line(pieces, [lambda c: maps.at[c]], map_send, map_recv)
        line.own()
        for distance in range(1, pieces // 2):
            line.hop(distance)
            if hops[distance - 1] >= steps:
                weights.hop(distance)
        line.finish()

        def hop(k, states):
            return tuple(
                mm(maps[k, h, :, :HEAD], states[h]) + maps[k, h, :, HEAD:].astype(F32) for h in range(heads)
            )

        states = lax.fori_loop(0, here, hop, tuple(jnp.zeros((HEAD, HEAD), F32) for _ in range(heads)))
        for h in range(heads):
            sin_ref[h] = states[h]

        def keep(k, carry):
            mapsout_ref[k] = maps[k, :, :, :HEAD]
            return carry

        lax.fori_loop(0, pieces, keep, 0)
        weights.finish()
        given = [
            pltpu.make_async_copy(source, target, local_sem.at[n])
            for n, (source, target) in enumerate([(wgs, wgfull_ref), (wus, wufull_ref), (wos, wofull_ref)])
        ]
        for copy in given:
            copy.start()
        for copy in given:
            copy.wait()


def recurrence_forward(heads, pieces, norm_at, rates, x_full, halo, weights, marks, stage, w_out):
    rows = x_full.shape[0]
    blocks = rows // BLOCK_LEN
    per = 2
    size = stage.shape[0]
    whole = lambda *dims: pl.BlockSpec(dims, lambda i: (0,) * len(dims))
    by_block = lambda *dims: pl.BlockSpec((per,) + dims, lambda i: (i,) + (0,) * len(dims))
    token = lambda cols: pl.BlockSpec((per * BLOCK_LEN, cols), lambda i: (i, 0))
    shape = lambda *dims: jax.ShapeDtypeStruct(dims, F32)
    low_shape = lambda *dims: jax.ShapeDtypeStruct(dims, BF16)
    hbm = pl.BlockSpec(memory_space=pltpu.HBM)
    vmem = pl.BlockSpec(memory_space=pltpu.VMEM)
    square = (heads, ROWS, HEAD)
    dma = pltpu.SemaphoreType.DMA
    side = (size, pieces, *stage.shape[2:])
    front = [
        low_shape(rows + HALO, heads * WIDE), low_shape(rows, D), shape(rows, heads * HEAD), shape(rows, HEAD),
        shape(rows, HEAD), shape(blocks * ROWS, HEAD), shape(blocks * 8, ROWS), shape(8, heads * WIDE), shape(8, D),
    ]
    return pl.pallas_call(
        functools.partial(fwd_kernel, heads, pieces, blocks // per, per, norm_at),
        grid=(blocks // per,),
        in_specs=[pl.BlockSpec(memory_space=pltpu.SMEM)] + [vmem] * 4 + [hbm] * 2,
        out_specs=[whole(*f.shape) for f in front] + [
            token(heads * HEAD), token(heads * HEAD), whole(heads, HEAD, HEAD), whole(pieces, heads, HEAD, HEAD),
            token(heads * WIDE),
            by_block(heads, BLOCK_LEN, HEAD), by_block(*square), by_block(*square), by_block(*square),
            by_block(*square), by_block(heads, BLOCK_LEN, ROWS), by_block(heads, ROWS, 2 * HEAD),
            by_block(heads, HEAD, 2 * HEAD), hbm, hbm, hbm,
        ],
        out_shape=front + [
            shape(rows, heads * HEAD), shape(rows, heads * HEAD), shape(heads, HEAD, HEAD),
            low_shape(pieces, heads, HEAD, HEAD), shape(rows, heads * WIDE),
            shape(blocks, heads, BLOCK_LEN, HEAD), shape(blocks, *square), shape(blocks, *square), shape(blocks, *square),
            shape(blocks, *square), shape(blocks, heads, BLOCK_LEN, ROWS), shape(blocks, heads, ROWS, 2 * HEAD),
            shape(blocks, heads, HEAD, 2 * HEAD),
            low_shape(*side), low_shape(*side), low_shape(pieces, *w_out.shape),
        ],
        scratch_shapes=[
            pltpu.VMEM((heads, HEAD, 2 * HEAD), F32), pltpu.VMEM((2 * heads * per, ROWS, HEAD), F32),
            pltpu.VMEM((pieces, heads, HEAD, 2 * HEAD), BF16),
            pltpu.VMEM(side, BF16), pltpu.VMEM(side, BF16), pltpu.VMEM((pieces, *w_out.shape), BF16),
            dma((3,)), dma((3, 3, pieces)), dma((3, pieces)), dma((1, 3, pieces)), dma((1, pieces)),
        ],
        compiler_params=pltpu.CompilerParams(
            vmem_limit_bytes=VMEM_LIMIT, collective_id=3, has_side_effects=True
        ),
        name="recurrence_forward",
    )(rates, x_full, halo, weights, marks, stage, w_out)


def middle_kernel(
    size, heads, token_total,
    x_ref, teach_ref, mask_ref, norms_ref, gain_ref, *streams_and_rest,
):
    streams, rest = streams_and_rest[:8], streams_and_rest[8:]
    middle_body(size, heads, token_total, x_ref, teach_ref, mask_ref, norms_ref, gain_ref, streams, *rest)


def middle_body(
    size, heads, token_total, x_ref, teach_ref, mask_ref, norms_ref, gain_ref, streams,
    final_ref, gmid_ref, ghead_ref, ggate_ref, cot_ref, ggain_ref, gnorm_ref, loss_ref,
    wide_ref, tall_ref,
    oloc_ref, carr_ref, gate_ref, sin_ref, wout_ref, wg_ref, wu_ref, wd_ref, load_sem, heads_ref, mixed_ref,
    line_send, line_recv, wds,
    second, branch, low, sent, got, own, mid, gfin, gates, ups, hidden, ggates, gups, send_sem, recv_sem,
):
    me = lax.axis_index("seq")
    count = x_ref.shape[0]
    loads = [
        pltpu.make_async_copy(source, target, load_sem.at[n])
        for n, (source, target) in enumerate(
            zip(streams, (oloc_ref, carr_ref, gate_ref, sin_ref, wout_ref, wg_ref, wu_ref, wds.at[lax.axis_index("ctx")]))
        )
    ]
    for load in loads:
        load.start()
    pieces = wide_ref.shape[0]
    barrier = pltpu.get_barrier_semaphore()
    peers = [({"seq": lax.rem(me + i, size)}, me >= 0) for i in range(1, size)]
    pl.semaphore_wait(barrier, greet(peers + line_neighbours(pieces), barrier))
    loads[7].wait()
    line = Line(pieces, [lambda c: wds.at[c]], line_send, line_recv)
    line.own()
    for load in loads[:5]:
        load.wait()
    norm = norms_ref[1:2, :]
    gain = gain_ref[...].astype(F32)

    def dot(a, b, ca=1, cb=0):
        return lax.dot_general(a, b, (((ca,), (cb,)), ((), ())), preferred_element_type=F32)

    def rows(q):
        return pl.ds(pl.multiple_of(q * count, count), count)

    def part_copy(phase, i):
        return pltpu.make_async_remote_copy(
            sent.at[phase, i - 1], got.at[phase, i - 1], send_sem.at[phase, i - 1], recv_sem.at[phase, i - 1],
            device_id={"seq": lax.rem(me + i, size)}, device_id_type=MESH,
        )

    def block_copy(buffer, phase, i, owner):
        return pltpu.make_async_remote_copy(
            buffer.at[rows(owner)], buffer.at[rows(owner)], send_sem.at[phase, i - 1], recv_sem.at[phase, i - 1],
            device_id={"seq": lax.rem(me + i, size)}, device_id_type=MESH,
        )

    def give_part(phase, i, part):
        @pl.when(i > 0)
        def _():
            sent[phase, i - 1] = part.astype(BF16)
            part_copy(phase, i).start()

        @pl.when(i == 0)
        def _():
            own[...] = part

    def take_parts(phase):
        def add(i, total):
            part_copy(phase, i).wait_recv()
            return total + got[phase, i - 1].astype(F32)

        return lax.fori_loop(1, size, add, own[...])

    def give_block(buffer, phase, value):
        buffer[rows(me)] = value

        def send(i, carry):
            block_copy(buffer, phase, i, me).start()
            return carry

        lax.fori_loop(1, size, send, 0)

    def take_block(buffer, phase, i):
        q = lax.rem(me + size - i, size)

        @pl.when(i > 0)
        def _():
            block_copy(buffer, phase, i, q).wait_recv()

        return q

    def out_part(k, carry):
        i = lax.rem(k + 1, size)
        q = lax.rem(me + i, size)
        for h in range(heads):
            hc = slice(h * HEAD, (h + 1) * HEAD)
            out = (oloc_ref[rows(q), hc] + mm(carr_ref[rows(q), hc], sin_ref[h])).astype(BF16)
            heads_ref[rows(q), hc] = out
            wide = out.astype(F32)
            gate = gate_ref[rows(q), hc]
            scaled = wide * lax.rsqrt(jnp.mean(wide * wide, axis=1, keepdims=True) + NORM_EPS) * gain
            mixed_ref[rows(q), hc] = (scaled * (gate * jax.nn.sigmoid(gate))).astype(BF16)
        give_part(0, i, dot(mixed_ref[rows(q)], wout_ref[...]))
        return carry

    lax.fori_loop(0, size, out_part, 0)
    hops = pieces // 2 - 1
    for distance in range(1, hops // 2 + 1):
        line.hop(distance)
    middle = x_ref[...].astype(F32) + take_parts(0)
    mid[...] = middle
    inv = lax.rsqrt(jnp.mean(middle * middle, axis=1, keepdims=True) + NORM_EPS)
    give_block(second, 3, (middle * inv * norm).astype(BF16))
    for load in loads[5:7]:
        load.wait()
    for distance in range(hops // 2 + 1, hops + 1):
        line.hop(distance)
    line.finish()
    deep = wds.shape[1]
    inner = pieces * deep
    wd_ref[inner:] = jnp.zeros((wd_ref.shape[0] - inner, D), BF16)
    for c in range(pieces):
        wd_ref[c * deep : (c + 1) * deep] = wds[c]

    def feed(i, carry):
        q = take_block(second, 3, i)
        here = second[rows(q)]
        gate = dot(here, wg_ref[...])
        up = dot(here, wu_ref[...])
        gates[rows(q)] = gate
        ups[rows(q)] = up
        hid = (gate * jax.nn.sigmoid(gate) * up).astype(BF16)
        hidden[rows(q)] = hid
        give_part(1, lax.rem(size - i, size), dot(hid, wd_ref[...]))
        return carry

    lax.fori_loop(0, size, feed, 0)
    final = mid[...] + take_parts(1)
    final_ref[...] = final.astype(BF16)
    error = final - teach_ref[...].astype(F32)
    mask = jnp.broadcast_to(mask_ref[...].astype(F32), (count, count)).T[:, :1]
    weighted = mask * error
    loss_ref[...] = jnp.broadcast_to(
        jnp.sum(jnp.sum(weighted * error, axis=1, keepdims=True), axis=0, keepdims=True), loss_ref.shape
    )
    valid = jnp.maximum(jnp.sum(norms_ref[2:3, :], axis=1, keepdims=True), 1.0)
    grad_final = token_total / valid * weighted
    gfin[...] = grad_final
    give_block(branch, 4, grad_final.astype(BF16))

    def feed_back(i, carry):
        q = take_block(branch, 4, i)
        ghid = dot(branch[rows(q)], wd_ref[...], 1, 1)
        gate = gates[rows(q)]
        sig = jax.nn.sigmoid(gate)
        silu = gate * sig
        ggate = (ghid * ups[rows(q)] * (sig + silu * (1.0 - sig))).astype(BF16)
        gup = (ghid * silu).astype(BF16)
        ggates[rows(q)] = ggate
        gups[rows(q)] = gup
        give_part(2, lax.rem(size - i, size), dot(ggate, wg_ref[...], 1, 1) + dot(gup, wu_ref[...], 1, 1))
        return carry

    lax.fori_loop(0, size, feed_back, 0)
    held = D // (size * pieces)
    wide_at = tall_ref.shape[1] - held
    tall_ref[...] = jnp.zeros_like(tall_ref)
    grad = dot(hidden[...], branch[...], 0, 0)
    for c in range(pieces):
        tall_ref[c, :deep] = grad[c * deep : (c + 1) * deep].astype(BF16)
    for n, side in enumerate((ggates, gups)):
        grad = dot(second[...], side[...], 0, 0)
        for c in range(pieces):
            for r in range(size):
                first = (r * pieces + c) * held
                wide_ref[c, (n * size + r) * held : (n * size + r + 1) * held] = grad[first : first + held].astype(BF16)
    gsecond = take_parts(2)
    middle = mid[...]
    inv = lax.rsqrt(jnp.mean(middle * middle, axis=1, keepdims=True) + NORM_EPS)
    unit = middle * inv
    gnorm_ref[...] = jnp.sum(gsecond * unit, axis=0, keepdims=True)
    down = gsecond * norm
    gmid = gfin[...] + inv * (down - unit * jnp.mean(down * unit, axis=1, keepdims=True))
    gmid_ref[...] = gmid
    give_block(low, 5, gmid.astype(BF16))
    ggain_ref[...] = jnp.zeros_like(ggain_ref)
    cot_ref[...] = jnp.zeros_like(cot_ref)

    def out_back(i, carry):
        q = take_block(low, 5, i)
        gmixed = dot(low[rows(q)], wout_ref[...], 1, 1)
        for h in range(heads):
            hc = slice(h * HEAD, (h + 1) * HEAD)
            x = heads_ref[rows(q), hc].astype(F32)
            gate = gate_ref[rows(q), hc]
            grad = gmixed[:, hc]
            inv = lax.rsqrt(jnp.mean(x * x, axis=1, keepdims=True) + NORM_EPS)
            sig = jax.nn.sigmoid(gate)
            silu = gate * sig
            unit = x * inv
            ggate_ref[rows(q), hc] = (grad * unit * gain * (sig + silu * (1.0 - sig))).astype(BF16)
            weighted = grad * silu
            ggain_ref[...] += jnp.sum(weighted * unit, axis=0, keepdims=True)
            down = weighted * gain
            ghead = (inv * (down - unit * jnp.mean(down * unit, axis=1, keepdims=True))).astype(BF16)
            ghead_ref[rows(q), hc] = ghead
            cot_ref[h] += mm(carr_ref[rows(q), hc], ghead, 0, 0)
        return carry

    lax.fori_loop(0, size, out_back, 0)
    grad = dot(mixed_ref[...], low[...], 0, 0)
    for c in range(pieces):
        tall_ref[c, wide_at:] = grad[c * held : (c + 1) * held].astype(BF16)

    def sent_all(i, carry):
        for phase in range(3):
            part_copy(phase, i).wait_send()
        block_copy(second, 3, i, me).wait_send()
        block_copy(branch, 4, i, me).wait_send()
        block_copy(low, 5, i, me).wait_send()
        return carry

    lax.fori_loop(1, size, sent_all, 0)


def middle_part(
    size, heads, pieces, token_total, x, teacher, mask, norms, gain, oloc, carr, gate_out, state_in, wout, wg, wu, wd
):
    count = x.shape[0]
    rows = count * size
    inner = wg.shape[1]
    held, deep = D // (size * pieces), wd.shape[0]
    vmem = pl.BlockSpec(memory_space=pltpu.VMEM)
    out = lambda dims, kind: jax.ShapeDtypeStruct(dims, kind)
    low = lambda *dims: pltpu.VMEM(dims, BF16)
    high = lambda *dims: pltpu.VMEM(dims, F32)
    dma = pltpu.SemaphoreType.DMA
    return pl.pallas_call(
        functools.partial(middle_kernel, size, heads, float(token_total)),
        in_specs=[vmem] * 5 + [pl.BlockSpec(memory_space=pltpu.HBM)] * 8,
        out_specs=[vmem] * 10,
        out_shape=[
            out((count, D), BF16), out((count, D), F32),
            out((rows, heads * HEAD), BF16), out((rows, heads * HEAD), BF16), out((heads, HEAD, HEAD), F32),
            out((1, HEAD), F32), out((1, D), F32), out((1, HEAD), F32),
            out((pieces, 2 * size * held, inner), BF16), out((pieces, -(-deep // 16) * 16 + held, D), BF16),
        ],
        scratch_shapes=[
            high(rows, heads * HEAD), high(rows, heads * HEAD), high(rows, heads * HEAD), high(heads, HEAD, HEAD),
            low(*wout.shape), low(*wg.shape), low(*wu.shape), low(inner, D), dma((8,)),
            low(rows, heads * HEAD), low(rows, heads * HEAD), dma((1, 3, pieces)), dma((1, pieces)), low(pieces, *wd.shape),
            low(rows, D), low(rows, D), low(rows, D), low(3, size - 1, count, D), low(3, size - 1, count, D),
            high(count, D), high(count, D), high(count, D), high(rows, inner), high(rows, inner), low(rows, inner),
            low(rows, inner), low(rows, inner), dma((6, size - 1)), dma((6, size - 1)),
        ],
        compiler_params=pltpu.CompilerParams(
            vmem_limit_bytes=VMEM_LIMIT, collective_id=1, has_side_effects=True
        ),
        name="middle_part",
    )(x, teacher, mask, norms, gain, oloc, carr, gate_out, state_in, wout, wg, wu, wd)


def bwd_kernel(
    heads, pieces, steps, maps_ref, cot_ref, sin_ref, proj_ref, w_ref, rowp_ref, colp_ref, tokp_ref, slope_ref,
    go_ref, conv_ref, q_ref, k_ref, v_ref, t_ref, kk_ref, at_ref, uw_ref, pl_ref, wide_ref, tall_ref,
    gproj_ref, fix_ref, gw_ref, gscal_ref, gsum_ref, widesum_ref, tallsum_ref,
    dstate, weave, rim, last, cots, rim_in, wtheirs, ttheirs, wheld, theld, wcame, tcame,
    cot_send, cot_recv, pair_send, pair_recv, line_send, line_recv, rim_sem,
):
    step = pl.program_id(0)
    block = steps - 1 - step
    here = lax.axis_index("ctx")
    core = lax.rem(here, 2)
    pair = Siblings([wide_ref, tall_ref], [wtheirs, ttheirs], [wheld, theld], pair_send, pair_recv)
    line = LineSum(pieces, [wheld, theld], [wcame, tcame], line_send, line_recv)
    rounds = pieces // 2 - 1
    when_round = [(r * steps) // max(rounds - 1, 1) for r in range(rounds)]

    @pl.when(step == 0)
    def _():
        barrier = pltpu.get_barrier_semaphore()
        side = [({"ctx": here + 1}, (core == 1) & (here < pieces - 1)), ({"ctx": here - 1}, (core == 0) & (here > 0))]
        pl.semaphore_wait(barrier, greet(line_neighbours(pieces) + side, barrier))
        cots[here] = cot_ref[...].astype(BF16)
        spread = Line(pieces, [lambda c: cots.at[c]], cot_send, cot_recv, up=False)
        spread.own()
        pair.start()
        for distance in range(1, pieces // 2):
            spread.hop(distance)
        spread.finish()
        pair.add()

        def hop(i, states):
            k = pieces - 1 - i
            return tuple(
                mm(maps_ref[k, h], states[h], 0, 0) + cots[k, h].astype(F32) for h in range(heads)
            )

        found = lax.fori_loop(
            0, pieces - 1 - here, hop, tuple(jnp.zeros((HEAD, HEAD), F32) for _ in range(heads))
        )
        for h in range(heads):
            dstate[h] = found[h]
        rim[...] = jnp.zeros_like(rim)
        gw_ref[...] = jnp.zeros_like(gw_ref)
        gsum_ref[...] = jnp.zeros_like(gsum_ref)

    for r in range(rounds):
        if when_round[r] < steps:
            pl.when(step == when_round[r])(lambda r=r: line.round(r))

    base = pl.multiple_of(block * BLOCK_LEN, BLOCK_LEN)
    rowp, colp, tokp = rowp_ref[...], colp_ref[...], tokp_ref[...]
    last_row = iota((ROWS, 1), 0) == ROWS - 1
    gscal = jnp.zeros((BLOCK_LEN, HEAD), F32)
    slope = slope_ref[...]
    first_lane = lax.axis_index("seq") * lane_of(heads, 0)
    for h in range(heads):
        cols = slice(h * WIDE, (h + 1) * WIDE)
        hc = slice(h * HEAD, (h + 1) * HEAD)
        beta, decay, qdecay, carry, qcarry, dlast, clast = decays(rowp, colp, tokp, h)
        go = go_ref[:, hc]
        query, keys, values = q_ref[0, h], k_ref[0, h], v_ref[0, h]
        inv, kk, attn, uw = t_ref[0, h], kk_ref[0, h], at_ref[0, h], uw_ref[0, h]
        dnext = dstate[h]
        state = mm(pl_ref[0, h, :, :HEAD], sin_ref[h]) + pl_ref[0, h, :, HEAD:]
        both = mm(jnp.concatenate([keys, uw[:, HEAD:]], axis=0), state)
        ks = both[:ROWS]
        upd = uw[:, :HEAD] - both[ROWS:]
        dupd = mm(attn, go, 0, 0) + dlast * mm(keys, dnext)
        dx = mm(inv, dupd, 0, 0)
        dv = beta * dx
        dy = -(carry * dv)
        go32 = go.astype(F32)
        outer = mm(jnp.concatenate([go32, dx], axis=0), upd, 1, 1)
        dattn, da = outer[:BLOCK_LEN], -outer[BLOCK_LEN:]
        dkd = mm(upd, dnext, 1, 1)
        right = mm(jnp.concatenate([go32, dy], axis=0), state, 1, 1)
        gos = right[:BLOCK_LEN]
        e = beta * da * decay
        f = dattn * qdecay
        ef = jnp.concatenate([f, e], axis=0)
        efk = mm(ef, keys)
        dq = qcarry * gos + efk[:BLOCK_LEN]
        dk = (
            right[BLOCK_LEN:]
            + dlast * dkd
            + efk[BLOCK_LEN:]
            + mm(ef, jnp.concatenate([query, keys], axis=0), 0, 0)
        )
        dstate[h] = clast * dnext + mm(
            jnp.concatenate([qcarry * query, keys], axis=0), jnp.concatenate([go32, dy], axis=0), 0, 0
        )
        dakk = da * kk
        z1 = beta * dakk
        z2 = dattn * attn
        dbeta = jnp.sum(dx * (values - carry * ks), axis=1, keepdims=True) + jnp.sum(dakk, axis=1, keepdims=True)
        dlk = dlast * jnp.sum(dkd * keys, axis=1, keepdims=True)
        tail = jnp.sum(dlk, axis=0, keepdims=True) + clast * jnp.sum(
            jnp.sum(state * dnext, axis=1, keepdims=True), axis=0, keepdims=True
        )
        dgrow = jnp.sum(z1, axis=1, keepdims=True) + jnp.sum(dy * ks, axis=1, keepdims=True) - dlk
        dgrow = dgrow + jnp.where(last_row, tail, 0.0)
        dgrow = dgrow - mm(jnp.concatenate([z2, z1], axis=0), jnp.ones((BLOCK_LEN + ROWS, HEAD), BF16), 0, 0)[:, :1]
        lane = iota((ROWS, HEAD), 1)
        weave[2 * h] = jnp.where(lane == 0, dbeta, jnp.where(lane == 1, dgrow, 0.0))
        by_step = [weave[2 * h, pl.ds(j, BLOCK_LEN, NH), :] for j in range(NH)]
        dg = sum(x[:, 1:2] for x in by_step) + jnp.sum(z2, axis=1, keepdims=True)
        dg = dg + qcarry * jnp.sum(query * gos, axis=1, keepdims=True)
        after = (iota((BLOCK_LEN, BLOCK_LEN), 0) <= iota((BLOCK_LEN, BLOCK_LEN), 1)).astype(BF16)
        dlog = column(tokp, LINK) * mm(after, jnp.broadcast_to(dg, (BLOCK_LEN, HEAD)))[:, :1]
        dscal = [by_step[j][:, 0:1] * column(slope, lane_of(h, j)) for j in range(NH)]
        dscal.append(dlog * column(slope, lane_of(h, NH)))
        lane = iota((BLOCK_LEN, HEAD), 1)
        for j in range(NH + 1):
            gscal = gscal + jnp.where(lane == first_lane + lane_of(h, j), dscal[j], 0.0)
        logs = column(slope, HEAD // 2 + lane_of(h, NH))
        sums = jnp.where(lane == 0, dlog * logs, jnp.where(lane == 1, dscal[NH], 0.0))
        gsum_ref[h : h + 1, :] += jnp.sum(sums, axis=0, keepdims=True)
        weave[2 * h] = dk
        weave[2 * h + 1] = dv
        conv = conv_ref[:, cols]
        sig = jax.nn.sigmoid(conv)
        act = conv * sig
        parts = []
        for part in range(1 + NH):
            piece = act[:, part * HEAD : (part + 1) * HEAD]
            scale = lax.rsqrt(jnp.sum(piece * piece, axis=1, keepdims=True) + NORM_EPS)
            if part:
                grad = weave[2 * h, pl.ds(part - 1, BLOCK_LEN, NH), :]
            else:
                grad = dq * (1.0 / math.sqrt(HEAD))
            unit = piece * scale
            parts.append(scale * (grad - unit * jnp.sum(grad * unit, axis=1, keepdims=True)))
        for j in range(NH):
            parts.append(weave[2 * h + 1, pl.ds(j, BLOCK_LEN, NH), :])
        dconv = jnp.concatenate(parts, axis=1) * (sig * (1.0 + conv * (1.0 - sig)))
        ext = proj_ref[pl.ds(base, BLOCK_LEN + HALO), cols].astype(F32)
        gw_ref[0:1, cols] += jnp.sum(dconv * ext[HALO:], axis=0, keepdims=True)
        zeros = jnp.zeros((8, WIDE), F32)
        length = BLOCK_LEN + 8
        total = jnp.concatenate([zeros, dconv * w_ref[0:1, cols]], axis=0)
        for lag in range(1, CONV):
            masked = column(tokp, LINK + lag - 1) * dconv
            gw_ref[lag : lag + 1, cols] += jnp.sum(masked * lag_rows(ext, lag), axis=0, keepdims=True)
            total = total + pltpu.roll(
                jnp.concatenate([zeros, masked * w_ref[lag : lag + 1, cols]], axis=0), length - lag, 0
            )
        fixed = total[length - 8 :] + rim[:, cols]
        gproj_ref[:, cols] = jnp.concatenate([total[8 : length - 8], fixed], axis=0).astype(BF16)
        rim[:, cols] = total[:8]

        @pl.when(step == 0)
        def _():
            last[:, cols] = fixed

    gscal_ref[...] = gscal.astype(BF16)

    @pl.when(step == steps - 1)
    def _():
        passing = pltpu.make_async_remote_copy(
            rim, rim_in, rim_sem.at[0], rim_sem.at[1], device_id={"ctx": here - 1}, device_id_type=MESH
        )
        pl.when(here > 0)(passing.start)
        fix_ref[...] = last[...].astype(BF16)

        @pl.when(here < pieces - 1)
        def _():
            passing.wait_recv()
            fix_ref[...] = (last[...] + rim_in[...]).astype(BF16)

        for r in range(rounds):
            if when_round[r] >= steps:
                line.round(r)
        line.finish()
        widesum_ref[...] = wheld[here // 2]
        tallsum_ref[...] = theld[here // 2].astype(F32)
        pair.left()
        pl.when(here > 0)(passing.wait_send)


def recurrence_backward(
    maps, cot, state_in, proj_ext, conv_w, rowp, colp, tokp, slopes, grad_heads, saved, wide, tall, heads, pieces
):
    rows = tokp.shape[0]
    blocks = rows // BLOCK_LEN
    chips = pieces // 2
    whole = lambda *dims: pl.BlockSpec(dims, lambda i: (0,) * len(dims))
    by_block = lambda *dims: pl.BlockSpec((1,) + dims, lambda i: (blocks - 1 - i,) + (0,) * len(dims))
    token = lambda cols: pl.BlockSpec((BLOCK_LEN, cols), lambda i: (blocks - 1 - i, 0))
    shape = lambda *dims: jax.ShapeDtypeStruct(dims, F32)
    low_shape = lambda *dims: jax.ShapeDtypeStruct(dims, BF16)
    vmem = pl.BlockSpec(memory_space=pltpu.VMEM)
    square = (heads, ROWS, HEAD)
    wide_chunk, tall_chunk = wide.shape[2:], tall.shape[2:]
    dma = pltpu.SemaphoreType.DMA
    return pl.pallas_call(
        functools.partial(bwd_kernel, heads, pieces, blocks),
        grid=(blocks,),
        in_specs=[
            vmem, vmem, vmem, vmem, vmem,
            pl.BlockSpec((8, ROWS), lambda i: (blocks - 1 - i, 0)),
            pl.BlockSpec((ROWS, HEAD), lambda i: (blocks - 1 - i, 0)), token(HEAD), token(HEAD),
            token(heads * HEAD), token(heads * WIDE),
            by_block(heads, BLOCK_LEN, HEAD), by_block(*square), by_block(*square), by_block(*square),
            by_block(*square), by_block(heads, BLOCK_LEN, ROWS), by_block(heads, ROWS, 2 * HEAD),
            by_block(heads, HEAD, 2 * HEAD), vmem, vmem,
        ],
        out_specs=[
            token(heads * WIDE), whole(8, heads * WIDE), whole(8, heads * WIDE), token(HEAD), whole(8, HEAD),
            whole(*wide_chunk), whole(*tall_chunk),
        ],
        out_shape=[
            low_shape(rows, heads * WIDE), low_shape(8, heads * WIDE), shape(8, heads * WIDE), low_shape(rows, HEAD),
            shape(8, HEAD), low_shape(*wide_chunk), shape(*tall_chunk),
        ],
        scratch_shapes=[
            pltpu.VMEM((heads, HEAD, HEAD), F32), pltpu.VMEM((2 * heads, ROWS, HEAD), F32),
            pltpu.VMEM((8, heads * WIDE), F32), pltpu.VMEM((8, heads * WIDE), F32),
            pltpu.VMEM((pieces, heads, HEAD, HEAD), BF16), pltpu.VMEM((8, heads * WIDE), F32),
            pltpu.VMEM((chips, *wide_chunk), BF16), pltpu.VMEM((chips, *tall_chunk), BF16),
            pltpu.VMEM((chips, *wide_chunk), BF16), pltpu.VMEM((chips, *tall_chunk), BF16),
            pltpu.VMEM((2, chips, *wide_chunk), BF16), pltpu.VMEM((2, chips, *tall_chunk), BF16),
            dma((1, 3, pieces)), dma((1, pieces)), dma((2,)), dma((2,)), dma((2, chips)), dma((2, 2, chips)), dma((2,)),
        ],
        compiler_params=pltpu.CompilerParams(
            vmem_limit_bytes=VMEM_LIMIT, collective_id=4, has_side_effects=True
        ),
        name="recurrence_backward",
    )(maps, cot, state_in, proj_ext, conv_w, rowp, colp, tokp, slopes, grad_heads, *saved, wide, tall)


def final_kernel(
    size, pieces, heads, norm_at, inner, gp_any, gg_any, gs_any, w_any, normed_any,
    fix_ref, x_ref, gmid_ref, norms_ref, gw_ref, gain_ref, gsum_ref, loss_ref, gnorm_ref, wide_ref,
    ingrad_ref, gmix_ref, ggate_ref, gtail_ref, gwg_ref, gwu_ref, mean_ref, ends_ref, both_ref,
    gp_ref, gg_ref, gs_ref, w_ref, normed_ref, load_sem, wideout_ref,
    sent, got, own, turned, grads, theirs, held, came, blocks, around, along, summed,
    local_sem, seq_send, seq_recv, pair_send, pair_recv, line_send, line_recv, ctx_send, ctx_recv,
):
    me, here = lax.axis_index("seq"), lax.axis_index("ctx")
    count = x_ref.shape[0]
    loads = [
        pltpu.make_async_copy(source, target, load_sem.at[n])
        for n, (source, target) in enumerate(
            [(gp_any, gp_ref), (gg_any, gg_ref), (gs_any, gs_ref), (w_any, w_ref), (normed_any, normed_ref)]
        )
    ]
    for load in loads:
        load.start()
    barrier = pltpu.get_barrier_semaphore()
    peers = [({"seq": lax.rem(me + i, size)}, here >= 0) for i in range(1, size)]
    peers += [({"ctx": lax.rem(here + i, pieces)}, here >= 0) for i in range(1, pieces)]
    pl.semaphore_wait(barrier, greet(peers, barrier))

    def dot(a, b, ca=1, cb=0):
        return lax.dot_general(a, b, (((ca,), (cb,)), ((), ())), preferred_element_type=F32)

    def rows(q):
        return pl.ds(pl.multiple_of(q * count, count), count)

    def to_peer(n, i):
        q = lax.rem(me + i, size)
        source, target = [
            (sent.at[i - 1], got.at[i - 1]), (wide_ref.at[:, q], wideout_ref.at[me]),
            (around.at[me], around.at[me]), (held.at[here // 2, q], blocks.at[me]),
        ][n]
        return pltpu.make_async_remote_copy(
            source, target, seq_send.at[n, i - 1], seq_recv.at[n, i - 1], device_id={"seq": q}, device_id_type=MESH
        )

    def to_piece(i):
        return pltpu.make_async_remote_copy(
            along.at[here], along.at[here], ctx_send.at[i - 1], ctx_recv.at[i - 1],
            device_id={"ctx": lax.rem(here + i, pieces)}, device_id_type=MESH,
        )

    kept = pltpu.make_async_copy(wide_ref.at[:, me], wideout_ref.at[me], local_sem.at[0])
    kept.start()
    for i in range(1, size):
        to_peer(1, i).start()
    gate_at, tail_at = gp_ref.shape[1], gp_ref.shape[1] + gg_ref.shape[1]
    for load in loads:
        load.wait()
    gp_ref[gp_ref.shape[0] - 8 :] = fix_ref[...]

    def part(k, carry):
        i = lax.rem(k + 1, size)
        q = lax.rem(me + i, size)
        value = (
            dot(gp_ref[rows(q)], w_ref[:, :gate_at], 1, 1)
            + dot(gg_ref[rows(q)], w_ref[:, gate_at:tail_at], 1, 1)
            + dot(gs_ref[rows(q)], w_ref[:, tail_at:], 1, 1)
        )

        @pl.when(i > 0)
        def _():
            sent[i - 1] = value.astype(BF16)
            pltpu.make_async_remote_copy(
                sent.at[i - 1], got.at[i - 1], seq_send.at[0, i - 1], seq_recv.at[0, i - 1],
                device_id={"seq": q}, device_id_type=MESH,
            ).start()

        @pl.when(i == 0)
        def _():
            own[...] = value

        return carry

    lax.fori_loop(0, size, part, 0)
    turned[...] = normed_ref[...].T
    rank_rows = D // (size * pieces)
    for source, at in ((gp_ref, 0), (gg_ref, gate_at), (gs_ref, tail_at)):
        width = source.shape[1]
        for first in range(0, width, 256):
            cols = min(256, width - first)
            grad = dot(turned[...], source[:, first : first + cols])
            for r in range(size):
                for c in range(pieces):
                    row = (r * pieces + c) * rank_rows
                    grads[c // 2, c % 2, r, :, at + first : at + first + cols] = grad[row : row + rank_rows].astype(BF16)
    channels = gw_ref.shape[1]
    mine = channel_rows(D // size, channels)
    taps = jnp.zeros((D // size, HEAD), F32)
    for lag in range(CONV):
        spread = jnp.where(mine, gw_ref[lag : lag + 1], 0.0).astype(BF16)
        taps = taps + dot(spread, tap_lanes(channels, CONV - 1 - lag, norm_at + 3))
    for c in range(pieces):
        grads[c // 2, c % 2, me, :, tail_at:] = (
            grads[c // 2, c % 2, me, :, tail_at:].astype(F32) + taps[c * rank_rows : (c + 1) * rank_rows]
        ).astype(BF16)
    pair = Siblings([grads], [theirs], [held], pair_send, pair_recv)
    pair.start()

    for i in range(1, size):
        to_peer(0, i).wait_recv()
    gnormed = own[...]
    for i in range(1, size):
        gnormed = gnormed + got[i - 1].astype(F32)
    x = x_ref[...].astype(F32)
    inv = lax.rsqrt(jnp.mean(x * x, axis=1, keepdims=True) + NORM_EPS)
    unit = x * inv
    down = gnormed * norms_ref[0:1, :]
    ingrad_ref[...] = gmid_ref[...] + inv * (down - unit * jnp.mean(down * unit, axis=1, keepdims=True))
    term = jnp.sum(gnormed * unit, axis=0, keepdims=True)
    lane = iota((1, HEAD), 1)
    ends = jnp.where(lane == 2 * HEADS, loss_ref[...], 0.0)
    for h in range(heads):
        for n in range(2):
            ends = jnp.where(lane == n * HEADS + me * heads + h, gsum_ref[h : h + 1, n : n + 1], ends)
    around[me] = jnp.zeros(around.shape[1:], F32)
    around[me, 0:1] = gain_ref[...]
    around[me, 1:2] = ends
    for j in range(D // HEAD):
        around[me, 8 + j : 9 + j] = term[:, j * HEAD : (j + 1) * HEAD]
        around[me, 8 + D // HEAD + j : 9 + D // HEAD + j] = gnorm_ref[:, j * HEAD : (j + 1) * HEAD]
    for i in range(1, size):
        to_peer(2, i).start()
    pair.add()
    line = LineSum(pieces, [held], [came], line_send, line_recv)
    line.round(0)
    for i in range(1, size):
        to_peer(2, i).wait_recv()
    mine = around[0]
    for r in range(1, size):
        mine = mine + around[r]
    along[here] = mine
    for i in range(1, pieces):
        to_piece(i).start()
    for r in range(1, pieces // 2 - 1):
        line.round(r)
    line.finish()
    blocks[me] = held[here // 2, me]
    for i in range(1, size):
        to_peer(3, i).start()
    for i in range(1, pieces):
        to_piece(i).wait_recv()
    total = along[0]
    for c in range(1, pieces):
        total = total + along[c]
    ends_ref[...] = total[:2]
    valid = jnp.maximum(jnp.sum(norms_ref[2:3, :], axis=1, keepdims=True), 1.0)
    mean_ref[...] = total[1:2, 2 * HEADS : 2 * HEADS + 1] / (D * valid)
    summed[...] = total
    place = (me * pieces + here) * rank_rows
    for n in range(2):
        row = summed[pl.ds(8 + n * (D // HEAD) + place // HEAD, 1), :]
        both_ref[n : n + 1, :] = pltpu.roll(row, lax.rem(HEAD - lax.rem(place, HEAD), HEAD), 1)
    tail = jnp.zeros((rank_rows, HEAD), F32)
    kept.wait()
    for i in range(1, size):
        to_peer(3, i).wait_recv()
        to_peer(1, i).wait_recv()
    for r in range(size):
        block = blocks[r].astype(F32)
        gmix_ref[:, r * gate_at : (r + 1) * gate_at] = block[:, :gate_at]
        ggate_ref[:, r * (tail_at - gate_at) : (r + 1) * (tail_at - gate_at)] = block[:, gate_at:tail_at]
        tail = tail + block[:, tail_at:]
        gwg_ref[:, r * inner : (r + 1) * inner] = wideout_ref[r, 0, :, :inner].astype(F32)
        gwu_ref[:, r * inner : (r + 1) * inner] = wideout_ref[r, 1, :, :inner].astype(F32)
    gtail_ref[...] = tail
    pair.left()
    for i in range(1, size):
        for n in range(4):
            to_peer(n, i).wait_send()
    for i in range(1, pieces):
        to_piece(i).wait_send()


def final_part(
    size, pieces, heads, norm_at, gp, gg, gs, weights, normed, fix, x, gmid, norms, gw, gain, gsum, loss, gnorm, wide
):
    count = x.shape[0]
    chips = pieces // 2
    held, inner = D // (size * pieces), FF // size
    width = weights.shape[1]
    small = (8 + 2 * (D // HEAD), HEAD)
    vmem = pl.BlockSpec(memory_space=pltpu.VMEM)
    out = lambda *dims: jax.ShapeDtypeStruct(dims, F32)
    low = lambda *dims: pltpu.VMEM(dims, BF16)
    high = lambda *dims: pltpu.VMEM(dims, F32)
    dma = pltpu.SemaphoreType.DMA
    return pl.pallas_call(
        functools.partial(final_kernel, size, pieces, heads, norm_at, inner),
        in_specs=[pl.BlockSpec(memory_space=pl.ANY)] * 5 + [vmem] * 10,
        out_specs=[vmem] * 9,
        out_shape=[
            out(count, D), out(held, size * gp.shape[1]), out(held, size * gg.shape[1]), out(held, HEAD),
            out(held, size * inner), out(held, size * inner), out(1, 1), out(2, HEAD), out(2, HEAD),
        ],
        scratch_shapes=[
            low(*gp.shape), low(*gg.shape), low(*gs.shape), low(*weights.shape), low(*normed.shape), dma((5,)),
            low(size, 2, held, wide.shape[3]),
            low(size - 1, count, D), low(size - 1, count, D), high(count, D), low(D, normed.shape[0]),
            low(chips, 2, size, held, width), low(chips, size, held, width), low(chips, size, held, width),
            low(2, chips, size, held, width), low(size, held, width), high(size, *small), high(pieces, *small), high(*small),
            dma((1,)), dma((4, size - 1)), dma((4, size - 1)), dma((1,)), dma((1,)), dma((1, chips)), dma((1, 2, chips)),
            dma((pieces - 1,)), dma((pieces - 1,)),
        ],
        compiler_params=pltpu.CompilerParams(
            vmem_limit_bytes=VMEM_LIMIT, collective_id=5, has_side_effects=True
        ),
        name="final_part",
    )(gp, gg, gs, weights, normed, fix, x, gmid, norms, gw, gain, gsum, loss, gnorm, wide)


def local(
    block_input, teacher, valid_mask, segments, mix_proj, scalar_proj, gate_proj, out_proj, conv_weight,
    norm_attn, norm_mlp, head_gain, a_log, dt_bias, w_gate, w_up, w_down,
):
    seq_size, pieces = lax.axis_size("seq"), lax.axis_size("ctx")
    heads = HEADS // seq_size
    rows = block_input.shape[0] * seq_size
    token_total = segments.shape[0]
    seq_length = min(SEQ_LEN, token_total)
    index = lax.axis_index("ctx")
    held = mix_proj.shape[0]
    scal_cols = HEADS * (NH + 1)
    norm_at, taps_at = scal_cols, scal_cols + 3
    taps_end = taps_at + CONV * conv_weight.shape[0] // held

    count_here = jnp.sum(valid_mask.astype(F32)).astype(BF16)
    tail = jnp.concatenate(
        [
            scalar_proj, norm_attn[:, None], norm_mlp[:, None],
            jnp.where(iota((held, 1), 0) == 0, count_here, jnp.zeros((), BF16)),
            conv_weight.reshape(held, -1), jnp.zeros((held, HEAD - taps_end), BF16),
        ],
        axis=1,
    )
    x_full, halo, gathered, stage = start_gather(
        seq_size, pieces, block_input, mix_proj, gate_proj, tail, w_gate, w_up
    )
    weights = gathered.reshape(D, -1)
    piece_start = index * rows
    window = lax.dynamic_slice_in_dim(jnp.pad(segments, (CONV, 0)), piece_start, rows + CONV)
    place_in = (piece_start + jnp.arange(rows, dtype=jnp.int32)) % seq_length
    marks = jnp.stack(
        [
            ((window[CONV - lag : CONV - lag + rows] == window[CONV:]) & (place_in >= lag)).astype(F32)
            if lag < CONV
            else jnp.zeros((rows,), F32)
            for lag in range(1, 9)
        ]
    )
    rates = jnp.stack([a_log.astype(F32), dt_bias.astype(F32)])
    (
        proj_ext, normed, gate_out, tokp, slopes, colp, rowp, conv_w, norms,
        oloc, carr, state_in, maps, *saved, wg_full, wu_full, wo_full,
    ) = recurrence_forward(heads, pieces, norm_at, rates, x_full, halo, weights, marks, stage, out_proj)
    (
        final_out, grad_middle, grad_heads, grad_gate_out, cot, gain_term, norm_mlp_term, loss, wide, tall,
    ) = middle_part(
        seq_size, heads, pieces, token_total, block_input, teacher, valid_mask[None, :], norms, head_gain[None, :],
        oloc, carr, gate_out, state_in, wo_full.reshape(heads * HEAD, D), wg_full.reshape(D, -1),
        wu_full.reshape(D, -1), w_down,
    )
    by_chip = lambda v: v.reshape(pieces // 2, 2, *v.shape[1:])
    grad_proj, fixed_rows, gw, grad_scal, gsum, wide_sum, tall_sum = recurrence_backward(
        maps, cot, state_in, proj_ext, conv_w, rowp, colp, tokp, slopes, grad_heads, saved, by_chip(wide), by_chip(tall),
        heads, pieces,
    )
    input_grad, mix_grad, gate_grad, tail_grad, wg_grad, wu_grad, mean_loss, ends, norm_grads = final_part(
        seq_size, pieces, heads, norm_at, grad_proj, grad_gate_out, grad_scal, weights, normed, fixed_rows, block_input,
        grad_middle, norms, gw, gain_term, gsum, loss, norm_mlp_term, wide_sum.reshape(2, seq_size, held, -1),
    )
    return (
        final_out,
        mean_loss[0, 0],
        input_grad,
        mix_grad,
        tail_grad[:, :scal_cols],
        gate_grad,
        tall_sum[tall_sum.shape[0] - held :],
        tail_grad[:, taps_at:taps_end].reshape(-1, CONV),
        norm_grads[0, :held],
        norm_grads[1, :held],
        ends[0],
        ends[1, :HEADS],
        ends[1, HEADS : 2 * HEADS],
        wg_grad,
        wu_grad,
        tall_sum[: w_down.shape[0]],
    )


def solution(mesh):
    tokens, vector, matrix = P(("ctx", "seq"), None), P(BOTH), P(BOTH, None)
    in_specs = (
        tokens, tokens, P(("ctx", "seq")), P(), matrix, matrix, matrix, matrix, matrix, vector, vector,
        P(), P(), P(), matrix, matrix, matrix,
    )
    out_specs = (
        tokens, P(), tokens, matrix, matrix, matrix, matrix, matrix, vector, vector, P(), P(), P(),
        matrix, matrix, matrix,
    )
    return jax.shard_map(local, mesh=mesh, in_specs=in_specs, out_specs=out_specs, check_vma=False)
```

```python
import functools
import math

import jax
import jax.numpy as jnp
from jax import lax
from jax.experimental import pallas as pl
from jax.experimental.pallas import tpu as pltpu
from jax.sharding import PartitionSpec as P

D = 1024
HEADS = 8
HEAD = 128
NH = 2
FF = 2816
BLOCK_LEN = 64
ROWS = BLOCK_LEN * NH
CONV = 4
SEQ_LEN = 32768
MOST_DOC = {4096: 2048, 32768: 8192}
WIDE = (1 + 2 * NH) * HEAD
HALO = 16
NORM_EPS = 1e-06
VMEM_LIMIT = 60 << 20
F32 = jnp.float32
BF16 = jnp.bfloat16
BOTH = ("seq", "ctx")
MESH = pl.DeviceIdType.MESH


class Split:
    def __init__(self, x):
        self.high = x.astype(BF16)
        self.low = (x - self.high.astype(F32)).astype(BF16)


def mm(a, b, ca=1, cb=0):
    if not isinstance(a, Split) and a.dtype != BF16:
        a = Split(a)
    if not isinstance(b, Split) and b.dtype != BF16:
        b = Split(b)
    if isinstance(a, Split) and isinstance(b, Split):
        left, right = (a.high, a.high, a.low), (b.high, b.low, b.high)
    elif isinstance(a, Split):
        left, right = (a.high, a.low), (b, b)
    elif isinstance(b, Split):
        left, right = (a, a), (b.high, b.low)
    else:
        left, right = (a,), (b,)
    if len(left) > 1:
        left, right = (jnp.concatenate(left, axis=ca),), (jnp.concatenate(right, axis=cb),)
    return lax.dot_general(left[0], right[0], (((ca,), (cb,)), ((), ())), preferred_element_type=F32)


def lanes_for(columns):
    return -(-columns // HEAD) * HEAD


def iota(shape, axis):
    return lax.broadcasted_iota(jnp.int32, shape, axis)


def unit_lower_inverses(systems):
    n = systems[0].shape[0]
    ri, ci = iota((n, n), 0), iota((n, n), 1)
    pick = (iota((n, 8), 0) % 8 == iota((n, 8), 1)).astype(BF16)
    own = ri // 8 == ci // 8
    eye = (ri == ci).astype(F32).reshape(n // 8, 8, n)
    small = [mm(jnp.where(own, a, 0.0), pick).reshape(n // 8, 8, 8) for a in systems]
    inv = [eye for _ in systems]
    for j in range(7):
        inv = [x - m[:, :, j : j + 1] * x[:, j : j + 1, :] for x, m in zip(inv, small)]
    inv = [x.reshape(n, n) for x in inv]
    size = 8
    while size < n:
        off = (ri // (2 * size) == ci // (2 * size)) & (ri // size != ci // size)
        halves = [Split(x) for x in inv]
        right = [mm(jnp.where(off, a, 0.0), x) for a, x in zip(systems, halves)]
        inv = [x - mm(y, z) for x, y, z in zip(inv, halves, right)]
        size *= 2
    return inv


DOC = 7
LINK = DOC + 1


def lane_of(h, what):
    return h * (NH + 1) + what


def column(table, lane):
    return table[:, lane : lane + 1]


def decays(rowp, colp, tokp, h):
    g = lane_of(h, NH)
    cs_row, g_row = rowp[DOC : DOC + 1, :], rowp[g : g + 1, :]
    cs_col, g_col = column(colp, DOC), column(colp, g)
    cs_tok, g_tok = column(tokp, DOC), column(tokp, g)
    beta = column(colp, lane_of(h, 0))
    ri, ci = iota((ROWS, ROWS), 0), iota((ROWS, ROWS), 1)
    strict = (ri > ci) & (cs_col == cs_row)
    decay = jnp.where(strict, jnp.exp(jnp.where(strict, g_col - g_row, 0.0)), 0.0)
    rt, ct = iota((BLOCK_LEN, ROWS), 0), iota((BLOCK_LEN, ROWS), 1)
    seen = (rt * NH + NH - 1 >= ct) & (cs_tok == cs_row)
    qdecay = jnp.where(seen, jnp.exp(jnp.where(seen, g_tok - g_row, 0.0)), 0.0)
    carry = jnp.where(cs_col == 0.0, jnp.exp(g_col), 0.0)
    qcarry = jnp.where(cs_tok == 0.0, jnp.exp(g_tok), 0.0)
    cs_last, g_last = cs_row[:, ROWS - 1 :], g_row[:, ROWS - 1 :]
    same = cs_col == cs_last
    dlast = jnp.where(same, jnp.exp(jnp.where(same, g_last - g_col, 0.0)), 0.0)
    clast = jnp.where(cs_last == 0.0, jnp.exp(g_last), 0.0)
    return beta, decay, qdecay, carry, qcarry, dlast, clast


def lag_rows(ext, lag):
    moved = pltpu.roll(ext, lag, 0) if lag else ext
    return moved[HALO:]


UP, DOWN, ACROSS = 0, 1, 2


class Line:
    def __init__(self, pieces, parts, send_sem, recv_sem, up=True, down=True, reach=None):
        self.chips = pieces // 2
        self.reach = self.chips - 1 if reach is None else reach
        self.here = lax.axis_index("ctx")
        self.chip = self.here // 2
        self.core = lax.rem(self.here, 2)
        self.other = self.here + 1 - 2 * self.core
        self.parts, self.send_sem, self.recv_sem, self.up, self.down = parts, send_sem, recv_sem, up, down

    def copies(self, chunk, way, only=None):
        target = (self.here + 2, self.here - 2, self.other)[way]
        return [
            pltpu.make_async_remote_copy(
                part(chunk), part(chunk), self.send_sem.at[n, way, chunk], self.recv_sem.at[n, chunk],
                device_id={"ctx": target}, device_id_type=MESH,
            )
            for n, part in enumerate(self.parts)
            if only is None or n == only
        ]

    def start(self, chunk, way, only=None):
        for copy in self.copies(chunk, way, only):
            copy.start()

    def arrived(self, chunk, only=None):
        for copy in self.copies(chunk, ACROSS, only):
            copy.wait_recv()

    def left(self, chunk, way):
        for copy in self.copies(chunk, way):
            copy.wait_send()

    def routes(self, distance, act):
        if distance == 0:
            if self.up and self.reach:
                pl.when(self.chip < self.chips - 1)(lambda: act(self.here, UP))
            if self.down and self.reach:
                pl.when(self.chip > 0)(lambda: act(self.here, DOWN))
            act(self.here, ACROSS)
            return
        below, above = self.here - 2 * distance, self.here + 2 * distance
        onward = distance < self.reach
        if self.up:

            @pl.when(self.chip >= distance)
            def _():
                if onward:
                    pl.when(self.chip < self.chips - 1)(lambda: act(below, UP))
                act(below, ACROSS)

        if self.down:

            @pl.when(self.chip + distance < self.chips)
            def _():
                if onward:
                    pl.when(self.chip > 0)(lambda: act(above, DOWN))
                act(above, ACROSS)

    def own(self, only=None):
        self.routes(0, lambda chunk, way: self.start(chunk, way, only))

    def hop(self, distance):
        for n in range(len(self.parts)):
            if self.up:
                pl.when(self.chip >= distance)(lambda n=n: self.arrived(self.here - 2 * distance, n))
            if self.down:
                pl.when(self.chip + distance < self.chips)(lambda n=n: self.arrived(self.here + 2 * distance, n))
            self.routes(distance, lambda chunk, way, n=n: self.start(chunk, way, n))

    def finish(self):
        for chip in range(self.chips):
            needed = (self.chip <= chip + (self.reach if self.up else 0)) & (
                self.chip >= chip - (self.reach if self.down else 0)
            )
            pl.when(needed)(lambda chip=chip: self.arrived(2 * chip + 1 - self.core))
        for distance in range(self.reach + 1):
            self.routes(distance, self.left)


class LineSum:
    def __init__(self, pieces, held, came, send_sem, recv_sem):
        self.chips = pieces // 2
        self.here = lax.axis_index("ctx")
        self.chip = self.here // 2
        self.held, self.came, self.send_sem, self.recv_sem = held, came, send_sem, recv_sem

    def copies(self, owner, way):
        return [
            pltpu.make_async_remote_copy(
                held.at[owner], came.at[way, owner], self.send_sem.at[n, owner], self.recv_sem.at[n, way, owner],
                device_id={"ctx": self.here + 2 - 4 * way}, device_id_type=MESH,
            )
            for n, (held, came) in enumerate(zip(self.held, self.came))
        ]

    def take(self, owner, way):
        for copy in self.copies(owner, way):
            copy.wait_recv()
        for held, came in zip(self.held, self.came):
            held[owner] = (held[owner].astype(F32) + came[way, owner].astype(F32)).astype(BF16)

    def send(self, owner, way):
        for copy in self.copies(owner, way):
            copy.start()

    def each(self, r, act):
        top = self.chips - 1
        for way, place in ((UP, self.chip), (DOWN, top - self.chip)):
            owner = top - (r - place) if way == UP else r - place
            pl.when((place <= r) & (place < top))(lambda: act(owner, way, place))

    def settle(self, r):
        self.each(r, lambda owner, way, place: pl.when(place > 0)(lambda: self.take(owner, way)))

    def launch(self, r):
        self.each(r, lambda owner, way, place: self.send(owner, way))

    def left(self, r):
        def wait(owner, way, place):
            for copy in self.copies(owner, way):
                copy.wait_send()

        self.each(r, wait)

    def round(self, r):
        self.settle(r)
        self.launch(r)

    def finish(self):
        top = self.chips - 1
        pl.when(self.chip > 0)(lambda: self.take(self.chip, UP))
        pl.when(self.chip < top)(lambda: self.take(self.chip, DOWN))


class Siblings:
    def __init__(self, parts, theirs, held, send_sem, recv_sem):
        self.here = lax.axis_index("ctx")
        self.core = lax.rem(self.here, 2)
        self.parts, self.theirs, self.held, self.send_sem, self.recv_sem = parts, theirs, held, send_sem, recv_sem

    def copies(self):
        return [
            pltpu.make_async_remote_copy(
                part.at[:, 1 - self.core], theirs, self.send_sem.at[n], self.recv_sem.at[n],
                device_id={"ctx": self.here + 1 - 2 * self.core}, device_id_type=MESH,
            )
            for n, (part, theirs) in enumerate(zip(self.parts, self.theirs))
        ]

    def start(self):
        for copy in self.copies():
            copy.start()

    def add(self):
        for copy in self.copies():
            copy.wait_recv()
        for part, theirs, held in zip(self.parts, self.theirs, self.held):

            def one(chip, carry, part=part, theirs=theirs, held=held):
                held[chip] = (part[chip, self.core].astype(F32) + theirs[chip].astype(F32)).astype(BF16)
                return carry

            lax.fori_loop(0, part.shape[0], one, 0)

    def left(self):
        for copy in self.copies():
            copy.wait_send()


def chips_within(span_pieces, pieces):
    return min(pieces // 2 - 1, (span_pieces + 1) // 2)


def greet(devices, barrier):
    total = 0
    for place, there in devices:
        pl.when(there)(
            lambda place=place: pl.semaphore_signal(barrier, inc=1, device_id=place, device_id_type=MESH)
        )
        total = total + jnp.asarray(there, jnp.int32)
    return total


def line_neighbours(pieces):
    here = lax.axis_index("ctx")
    chip, core = here // 2, lax.rem(here, 2)
    return [
        ({"ctx": here + 2}, chip < pieces // 2 - 1),
        ({"ctx": here - 2}, chip > 0),
        ({"ctx": here + 1 - 2 * core}, here >= 0),
    ]


def start_kernel(
    size, pieces, x_ref, mix_ref, gate_ref, tail_ref, wg_ref, wu_ref, xfull_ref, halo_ref, full_ref, stage_ref,
    sides, local_sem, seq_send, seq_recv, line_send, line_recv, halo_sem,
):
    me, here = lax.axis_index("seq"), lax.axis_index("ctx")
    count = x_ref.shape[0]
    core = lax.rem(here, 2)
    inner = wg_ref.shape[1] // size
    gate_at = mix_ref.shape[1] // size
    tail_at = gate_at + gate_ref.shape[1] // size
    barrier = pltpu.get_barrier_semaphore()
    peers = [({"seq": lax.rem(me + i, size)}, here >= 0) for i in range(1, size)]
    side = [({"ctx": here + 1}, (core == 1) & (here < pieces - 1)), ({"ctx": here - 1}, (core == 0) & (here > 0))]
    total = greet(peers + line_neighbours(pieces) + side, barrier)
    pl.semaphore_wait(barrier, total)

    def rows(q):
        return pl.ds(pl.multiple_of(q * count, count), count)

    def cols(q, width):
        return pl.ds(pl.multiple_of(q * width, HEAD), width)

    def ends(n, q):
        return [
            (mix_ref.at[:, cols(q, gate_at)], full_ref.at[me, here, :, :gate_at]),
            (gate_ref.at[:, cols(q, tail_at - gate_at)], full_ref.at[me, here, :, gate_at:tail_at]),
            (tail_ref, full_ref.at[me, here, :, tail_at:]),
            (x_ref, xfull_ref.at[rows(me)]),
            (sides.at[q], stage_ref.at[me]),
        ][n]

    def exchange(n, i):
        q = lax.rem(me + i, size)
        source, target = ends(n, q)
        return pltpu.make_async_remote_copy(
            source, target, seq_send.at[n, i - 1], seq_recv.at[n, i - 1], device_id={"seq": q}, device_id_type=MESH
        )

    def own(n):
        return pltpu.make_async_copy(*ends(n, me), local_sem.at[n])

    def begin(n):
        own(n).start()
        for i in range(1, size):
            exchange(n, i).start()

    def end(n):
        own(n).wait()
        for i in range(1, size):
            exchange(n, i).wait_recv()

    for n in range(3):
        begin(n)
    sides[...] = jnp.zeros_like(sides)
    for q in range(size):
        sides[q, 0, :, :inner] = wg_ref[:, q * inner : (q + 1) * inner]
        sides[q, 1, :, :inner] = wu_ref[:, q * inner : (q + 1) * inner]
    line = Line(
        pieces, [lambda c, i=i: full_ref.at[lax.rem(me + size - i, size), c] for i in range(size)], line_send, line_recv
    )
    for n in range(3):
        own(n).wait()
    line.own(0)
    for i in range(1, size):
        for n in range(3):
            exchange(n, i).wait_recv()
        line.own(i)
    begin(3)
    begin(4)
    last = xfull_ref.at[pl.ds(size * count - HALO, HALO)]
    passing = pltpu.make_async_remote_copy(
        last, halo_ref, halo_sem.at[0], halo_sem.at[1], device_id={"ctx": here + 1}, device_id_type=MESH
    )
    hops = pieces // 2 - 1
    for distance in range(1, hops):
        line.hop(distance)
    end(3)
    pl.when(here < pieces - 1)(passing.start)

    @pl.when(here == 0)
    def _():
        filling = pltpu.make_async_copy(last, halo_ref, local_sem.at[5])
        filling.start()
        filling.wait()

    line.hop(hops)
    line.finish()
    end(4)
    pl.when(here > 0)(passing.wait_recv)
    pl.when(here < pieces - 1)(passing.wait_send)
    for n in range(5):
        for i in range(1, size):
            exchange(n, i).wait_send()


def start_gather(size, pieces, x, mix, gate, tail, w_gate, w_up):
    anywhere = pl.BlockSpec(memory_space=pl.ANY)
    vmem = pl.BlockSpec(memory_space=pltpu.VMEM)
    out = lambda *dims: jax.ShapeDtypeStruct(dims, BF16)
    dma = pltpu.SemaphoreType.DMA
    held, padded = w_gate.shape[0], lanes_for(w_gate.shape[1] // size)
    width = (mix.shape[1] + gate.shape[1]) // size + tail.shape[1]
    return pl.pallas_call(
        functools.partial(start_kernel, size, pieces),
        in_specs=[anywhere] * 4 + [vmem] * 2,
        out_specs=[anywhere] * 4,
        out_shape=[
            out(x.shape[0] * size, D), out(HALO, D), out(size, pieces, held, width), out(size, 2, held, padded),
        ],
        scratch_shapes=[
            pltpu.VMEM((size, 2, held, padded), BF16),
            dma((6,)), dma((5, size - 1)), dma((5, size - 1)), dma((size, 3, pieces)), dma((size, pieces)), dma((2,)),
        ],
        compiler_params=pltpu.CompilerParams(
            vmem_limit_bytes=VMEM_LIMIT, collective_id=2, has_side_effects=True
        ),
        name="start_gather",
    )(x, mix, gate, tail, w_gate, w_up)


def exact(a, b, ca=1, cb=0):
    return lax.dot_general(
        a, b, (((ca,), (cb,)), ((), ())), precision=lax.Precision.HIGHEST, preferred_element_type=F32
    )


def tap_lanes(channels, tap, at):
    lanes = iota((channels, HEAD), 1)
    return (lanes == at + CONV * (iota((channels, HEAD), 0) % (WIDE // HEAD)) + tap).astype(BF16)


def channel_rows(rows, channels):
    return iota((rows, channels), 1) // (WIDE // HEAD) == iota((rows, channels), 0)


def front_body(
    heads, norm_at, rates_ref, x_ref, halo_ref, w_ref, marks_ref,
    proj_ref, normed_ref, gate_ref, tok_ref, slope_ref, col_ref, row_ref, taps_ref, norms_ref,
):
    me = lax.axis_index("seq")
    channels = heads * WIDE
    tail_at = channels + heads * HEAD
    rows = x_ref.shape[0]
    own_rows = D * heads // HEADS

    def dot(a, b, ca=1, cb=0):
        return lax.dot_general(a, b, (((ca,), (cb,)), ((), ())), preferred_element_type=F32)

    pick = (iota((8, HEAD), 1) == norm_at + iota((8, HEAD), 0)).astype(BF16)
    norms_ref[...] = dot(pick, w_ref[:, tail_at:], 1, 1)

    def normal(values):
        values = values.astype(F32)
        scale = lax.rsqrt(jnp.mean(values * values, axis=1, keepdims=True) + NORM_EPS)
        return (values * scale * norms_ref[0:1, :]).astype(BF16)

    early = normal(halo_ref[...])
    normed_ref[...] = normal(x_ref[...])
    proj_ref[:HALO] = dot(early, w_ref[:, :channels]).astype(BF16)
    proj_ref[HALO:] = dot(normed_ref[...], w_ref[:, :channels]).astype(BF16)
    gate_ref[...] = dot(normed_ref[...], w_ref[:, channels:tail_at])
    tail = w_ref[pl.ds(pl.multiple_of(me * own_rows, own_rows), own_rows), tail_at:]
    taps_ref[...] = jnp.zeros_like(taps_ref)
    mine = channel_rows(own_rows, channels)
    for lag in range(CONV):
        spread = dot(tail, tap_lanes(channels, CONV - 1 - lag, norm_at + 3), 1, 1)
        taps_ref[lag : lag + 1] = jnp.sum(jnp.where(mine, spread, 0.0), axis=0, keepdims=True)

    raw = dot(normed_ref[...], w_ref[:, tail_at:]).astype(BF16).astype(F32)
    raw = pltpu.roll(raw, lax.rem(HEAD - me * lane_of(heads, 0), HEAD), 1)
    lane = iota((1, HEAD), 1)
    rate, lift = jnp.zeros((1, HEAD), F32), jnp.zeros((1, HEAD), F32)
    for h in range(heads):
        here = lane == lane_of(h, NH)
        rate = jnp.where(here, -jnp.exp(jnp.zeros((1, HEAD), F32) + rates_ref[0, me * heads + h]), rate)
        lift = jnp.where(here, rates_ref[1, me * heads + h], lift)
    is_log = (lane % (NH + 1) == NH) & (lane < lane_of(heads, 0))
    lifted = raw + lift
    sig = jax.nn.sigmoid(lifted)
    logs = rate * (jnp.maximum(lifted, 0.0) + jnp.log1p(jnp.exp(-jnp.abs(lifted))))
    slope_ref[...] = jnp.where(is_log, rate * sig, sig * (1.0 - sig)) * (lane < HEAD // 2) + pltpu.roll(
        jnp.where(is_log, logs, 0.0), HEAD // 2, 1
    )
    place = (iota((8, HEAD), 1) == LINK + iota((8, HEAD), 0)) & (iota((8, HEAD), 0) < CONV - 1)
    links = dot(marks_ref[...].astype(BF16), place.astype(BF16), 0, 0)
    open_ = column(links, LINK)
    summed = jnp.where(is_log, logs * open_, jnp.where(lane == DOC, 1.0 - open_, 0.0))
    lower = (iota((BLOCK_LEN, BLOCK_LEN), 0) >= iota((BLOCK_LEN, BLOCK_LEN), 1)).astype(F32)
    spread = (iota((ROWS, BLOCK_LEN), 0) // NH == iota((ROWS, BLOCK_LEN), 1)).astype(F32)
    step = iota((ROWS, HEAD), 0) % NH
    for b in range(rows // BLOCK_LEN):
        span = slice(b * BLOCK_LEN, (b + 1) * BLOCK_LEN)
        sums = exact(lower, summed[span])
        tok = jnp.where(is_log | (lane == DOC), sums, jnp.where(lane < DOC, sig[span], links[span]))
        tok_ref[span] = tok
        wide = exact(spread, tok)
        first = wide
        for j in range(1, NH):
            first = jnp.where(step == j, pltpu.roll(wide, HEAD - j, 1), first)
        col = jnp.where(lane % (NH + 1) == 0, jnp.where(lane < lane_of(heads, 0), first, wide), wide)
        col_ref[b * ROWS : (b + 1) * ROWS] = col
        row_ref[b * 8 : (b + 1) * 8] = col.T[:8]


def fwd_kernel(
    heads, pieces, steps, per, span_pieces, norm_at,
    rates_ref, x_ref, halo_ref, full_ref, marks_ref, stage_ref, wo_ref,
    proj_ref, normed_ref, gate_ref, tok_ref, slope_ref, col_ref, row_ref, taps_ref, norms_ref,
    oloc_ref, carr_ref, sin_ref, mapsout_ref, conv_ref, q_ref, k_ref, v_ref, t_ref, kk_ref, at_ref, uw_ref, pl_ref,
    wgfull_ref, wufull_ref, wofull_ref,
    state, weave, maps, wgs, wus, wos, local_sem, line_send, line_recv, map_send, map_recv,
):
    step = pl.program_id(0)
    here = lax.axis_index("ctx")
    weights = Line(
        pieces, [lambda c: wgs.at[:, c], lambda c: wus.at[:, c], lambda c: wos.at[c]], line_send, line_recv
    )
    eye = (iota((HEAD, HEAD), 0) == iota((HEAD, HEAD), 1)).astype(F32)

    @pl.when(step == 0)
    def _():
        owned = [
            pltpu.make_async_copy(source, target, local_sem.at[n])
            for n, (source, target) in enumerate(
                [(stage_ref.at[:, 0], wgs.at[:, here]), (stage_ref.at[:, 1], wus.at[:, here]), (wo_ref, wos.at[here])]
            )
        ]
        for copy in owned:
            copy.start()
        barrier = pltpu.get_barrier_semaphore()
        pl.semaphore_wait(barrier, greet(line_neighbours(pieces), barrier))
        for copy in owned:
            copy.wait()
        weights.own()
        front_body(
            heads, norm_at, rates_ref, x_ref, halo_ref, full_ref, marks_ref,
            proj_ref, normed_ref, gate_ref, tok_ref, slope_ref, col_ref, row_ref, taps_ref, norms_ref,
        )
        for h in range(heads):
            state[h, :, :HEAD] = eye
            state[h, :, HEAD:] = jnp.zeros((HEAD, HEAD), F32)

    hops = [(d * 2 * steps) // (pieces // 2) - 1 for d in range(1, pieces // 2)]
    for distance, at in enumerate(hops, 1):
        if at < steps:
            pl.when(step == at)(lambda distance=distance: weights.hop(distance))

    items = [(j, h) for j in range(per) for h in range(heads)]
    cols = lambda h: slice(h * WIDE, (h + 1) * WIDE)
    span = lambda j, length=BLOCK_LEN: slice(j * length, (j + 1) * length)
    tables = []
    for j in range(per):
        block = step * per + j
        tables.append(
            (
                row_ref[pl.ds(pl.multiple_of(block * 8, 8), 8), :],
                col_ref[pl.ds(pl.multiple_of(block * ROWS, ROWS), ROWS), :],
                tok_ref[pl.ds(pl.multiple_of(block * BLOCK_LEN, BLOCK_LEN), BLOCK_LEN), :],
            )
        )
    acts = []
    for j, h in items:
        base = pl.multiple_of((step * per + j) * BLOCK_LEN, BLOCK_LEN)
        ext = proj_ref[pl.ds(base, BLOCK_LEN + HALO), cols(h)].astype(F32)
        conv = ext[HALO:] * taps_ref[0:1, cols(h)]
        for lag in range(1, CONV):
            conv = conv + column(tables[j][2], LINK + lag - 1) * lag_rows(ext, lag) * taps_ref[lag : lag + 1, cols(h)]
        conv_ref[span(j), cols(h)] = conv
        acts.append(conv * jax.nn.sigmoid(conv))
    queries, keys, values = [], [], []
    for n, act in enumerate(acts):
        unit = []
        for part in range(1 + NH):
            piece = act[:, part * HEAD : (part + 1) * HEAD]
            unit.append(piece * lax.rsqrt(jnp.sum(piece * piece, axis=1, keepdims=True) + NORM_EPS))
        queries.append(unit[0] * (1.0 / math.sqrt(HEAD)))
        for j in range(NH):
            weave[2 * n, pl.ds(j, BLOCK_LEN, NH), :] = unit[1 + j]
            weave[2 * n + 1, pl.ds(j, BLOCK_LEN, NH), :] = act[:, (1 + NH + j) * HEAD : (2 + NH + j) * HEAD]
    for n in range(len(items)):
        keys.append(weave[2 * n])
        values.append(weave[2 * n + 1])
    factors = [decays(*tables[j], h) for j, h in items]
    grams = [mm(jnp.concatenate([q, k], axis=0), k, 1, 1) for q, k in zip(queries, keys)]
    kks = [f[1] * g[BLOCK_LEN:] for f, g in zip(factors, grams)]
    attns = [f[2] * g[:BLOCK_LEN] for f, g in zip(factors, grams)]
    invs = unit_lower_inverses([f[0] * kk for f, kk in zip(factors, kks)])
    uws = [
        mm(inv, jnp.concatenate([f[0] * v, (f[0] * f[3]) * k], axis=1))
        for inv, f, v, k in zip(invs, factors, values, keys)
    ]
    auws = [mm(attn, uw) for attn, uw in zip(attns, uws)]
    nms = [mm(f[5] * k, uw, 0, 0) for f, k, uw in zip(factors, keys, uws)]
    for n, (j, h) in enumerate(items):
        before = state[h]
        f = factors[n]
        both = mm(
            jnp.concatenate([f[4] * queries[n] - auws[n][:, HEAD:], f[6] * eye - nms[n][:, HEAD:]], axis=0), before
        )
        hc = slice(h * HEAD, (h + 1) * HEAD)
        carr_ref[span(j), hc] = both[:BLOCK_LEN, :HEAD]
        oloc_ref[span(j), hc] = both[:BLOCK_LEN, HEAD:] + auws[n][:, :HEAD]
        state[h, :, :HEAD] = both[BLOCK_LEN:, :HEAD]
        state[h, :, HEAD:] = both[BLOCK_LEN:, HEAD:] + nms[n][:, :HEAD]
        q_ref[j, h] = queries[n]
        k_ref[j, h] = keys[n]
        v_ref[j, h] = values[n]
        t_ref[j, h] = invs[n]
        kk_ref[j, h] = kks[n]
        at_ref[j, h] = attns[n]
        uw_ref[j, h] = uws[n]
        pl_ref[j, h] = before

    @pl.when(step == steps - 1)
    def _():
        maps[here] = state[...].astype(BF16)
        line = Line(pieces, [lambda c: maps.at[c]], map_send, map_recv, reach=chips_within(span_pieces, pieces))
        line.own()
        for distance in range(1, line.reach + 1):
            line.hop(distance)
        line.finish()
        for distance in range(1, pieces // 2):
            if hops[distance - 1] >= steps:
                weights.hop(distance)

        def hop(k, states):
            return tuple(
                mm(maps[k, h, :, :HEAD], states[h]) + maps[k, h, :, HEAD:].astype(F32) for h in range(heads)
            )

        states = lax.fori_loop(jnp.maximum(here - span_pieces, 0), here, hop, tuple(jnp.zeros((HEAD, HEAD), F32) for _ in range(heads)))
        for h in range(heads):
            sin_ref[h] = states[h]

        def keep(k, carry):
            mapsout_ref[k] = maps[k, :, :, :HEAD]
            return carry

        lax.fori_loop(
            jnp.maximum(here - span_pieces, 0), jnp.minimum(here + span_pieces + 1, pieces), keep, 0
        )
        weights.finish()
        given = [
            pltpu.make_async_copy(source, target, local_sem.at[n])
            for n, (source, target) in enumerate([(wgs, wgfull_ref), (wus, wufull_ref), (wos, wofull_ref)])
        ]
        for copy in given:
            copy.start()
        for copy in given:
            copy.wait()


def recurrence_forward(heads, pieces, span_pieces, norm_at, rates, x_full, halo, weights, marks, stage, w_out):
    rows = x_full.shape[0]
    blocks = rows // BLOCK_LEN
    per = 2
    size = stage.shape[0]
    whole = lambda *dims: pl.BlockSpec(dims, lambda i: (0,) * len(dims))
    by_block = lambda *dims: pl.BlockSpec((per,) + dims, lambda i: (i,) + (0,) * len(dims))
    token = lambda cols: pl.BlockSpec((per * BLOCK_LEN, cols), lambda i: (i, 0))
    shape = lambda *dims: jax.ShapeDtypeStruct(dims, F32)
    low_shape = lambda *dims: jax.ShapeDtypeStruct(dims, BF16)
    hbm = pl.BlockSpec(memory_space=pltpu.HBM)
    vmem = pl.BlockSpec(memory_space=pltpu.VMEM)
    square = (heads, ROWS, HEAD)
    dma = pltpu.SemaphoreType.DMA
    side = (size, pieces, *stage.shape[2:])
    front = [
        low_shape(rows + HALO, heads * WIDE), low_shape(rows, D), shape(rows, heads * HEAD), shape(rows, HEAD),
        shape(rows, HEAD), shape(blocks * ROWS, HEAD), shape(blocks * 8, ROWS), shape(8, heads * WIDE), shape(8, D),
    ]
    return pl.pallas_call(
        functools.partial(fwd_kernel, heads, pieces, blocks // per, per, span_pieces, norm_at),
        grid=(blocks // per,),
        in_specs=[pl.BlockSpec(memory_space=pltpu.SMEM)] + [vmem] * 4 + [hbm] * 2,
        out_specs=[whole(*f.shape) for f in front] + [
            token(heads * HEAD), token(heads * HEAD), whole(heads, HEAD, HEAD), whole(pieces, heads, HEAD, HEAD),
            token(heads * WIDE),
            by_block(heads, BLOCK_LEN, HEAD), by_block(*square), by_block(*square), by_block(*square),
            by_block(*square), by_block(heads, BLOCK_LEN, ROWS), by_block(heads, ROWS, 2 * HEAD),
            by_block(heads, HEAD, 2 * HEAD), hbm, hbm, hbm,
        ],
        out_shape=front + [
            shape(rows, heads * HEAD), shape(rows, heads * HEAD), shape(heads, HEAD, HEAD),
            low_shape(pieces, heads, HEAD, HEAD), shape(rows, heads * WIDE),
            shape(blocks, heads, BLOCK_LEN, HEAD), shape(blocks, *square), shape(blocks, *square), shape(blocks, *square),
            shape(blocks, *square), shape(blocks, heads, BLOCK_LEN, ROWS), shape(blocks, heads, ROWS, 2 * HEAD),
            shape(blocks, heads, HEAD, 2 * HEAD),
            low_shape(*side), low_shape(*side), low_shape(pieces, *w_out.shape),
        ],
        scratch_shapes=[
            pltpu.VMEM((heads, HEAD, 2 * HEAD), F32), pltpu.VMEM((2 * heads * per, ROWS, HEAD), F32),
            pltpu.VMEM((pieces, heads, HEAD, 2 * HEAD), BF16),
            pltpu.VMEM(side, BF16), pltpu.VMEM(side, BF16), pltpu.VMEM((pieces, *w_out.shape), BF16),
            dma((3,)), dma((3, 3, pieces)), dma((3, pieces)), dma((1, 3, pieces)), dma((1, pieces)),
        ],
        compiler_params=pltpu.CompilerParams(
            vmem_limit_bytes=VMEM_LIMIT, collective_id=3, has_side_effects=True
        ),
        name="recurrence_forward",
    )(rates, x_full, halo, weights, marks, stage, w_out)


def middle_kernel(
    size, heads, token_total,
    x_ref, teach_ref, mask_ref, norms_ref, gain_ref, *streams_and_rest,
):
    streams, rest = streams_and_rest[:8], streams_and_rest[8:]
    middle_body(size, heads, token_total, x_ref, teach_ref, mask_ref, norms_ref, gain_ref, streams, *rest)


def middle_body(
    size, heads, token_total, x_ref, teach_ref, mask_ref, norms_ref, gain_ref, streams,
    final_ref, gmid_ref, ghead_ref, ggate_ref, cot_ref, ggain_ref, gnorm_ref, loss_ref,
    wheld, theld, outg_ref,
    oloc_ref, carr_ref, gate_ref, sin_ref, wout_ref, wg_ref, wu_ref, wd_ref, load_sem, heads_ref, mixed_ref,
    line_send, line_recv, wds, wide_ref, tall_ref, wtheirs, ttheirs, wcame, tcame,
    pair_send, pair_recv, sum_send, sum_recv,
    second, branch, low, sent, got, own, mid, gfin, gates, ups, hidden, ggates, gups, send_sem, recv_sem,
):
    me = lax.axis_index("seq")
    count = x_ref.shape[0]
    loads = [
        pltpu.make_async_copy(source, target, load_sem.at[n])
        for n, (source, target) in enumerate(
            zip(streams, (oloc_ref, carr_ref, gate_ref, sin_ref, wout_ref, wg_ref, wu_ref, wds.at[lax.axis_index("ctx")]))
        )
    ]
    for load in loads:
        load.start()
    pieces = 2 * wide_ref.shape[0]
    barrier = pltpu.get_barrier_semaphore()
    peers = [({"seq": lax.rem(me + i, size)}, me >= 0) for i in range(1, size)]
    pl.semaphore_wait(barrier, greet(peers + line_neighbours(pieces), barrier))
    loads[7].wait()
    line = Line(pieces, [lambda c: wds.at[c]], line_send, line_recv)
    line.own()
    for load in loads[:5]:
        load.wait()
    norm = norms_ref[1:2, :]
    gain = gain_ref[...].astype(F32)

    def dot(a, b, ca=1, cb=0):
        return lax.dot_general(a, b, (((ca,), (cb,)), ((), ())), preferred_element_type=F32)

    def rows(q):
        return pl.ds(pl.multiple_of(q * count, count), count)

    def part_copy(phase, i):
        return pltpu.make_async_remote_copy(
            sent.at[phase, i - 1], got.at[phase, i - 1], send_sem.at[phase, i - 1], recv_sem.at[phase, i - 1],
            device_id={"seq": lax.rem(me + i, size)}, device_id_type=MESH,
        )

    def block_copy(buffer, phase, i, owner):
        return pltpu.make_async_remote_copy(
            buffer.at[rows(owner)], buffer.at[rows(owner)], send_sem.at[phase, i - 1], recv_sem.at[phase, i - 1],
            device_id={"seq": lax.rem(me + i, size)}, device_id_type=MESH,
        )

    def give_part(phase, i, part):
        @pl.when(i > 0)
        def _():
            sent[phase, i - 1] = part.astype(BF16)
            part_copy(phase, i).start()

        @pl.when(i == 0)
        def _():
            own[...] = part

    def take_parts(phase):
        def add(i, total):
            part_copy(phase, i).wait_recv()
            return total + got[phase, i - 1].astype(F32)

        return lax.fori_loop(1, size, add, own[...])

    def give_block(buffer, phase, value):
        buffer[rows(me)] = value

        def send(i, carry):
            block_copy(buffer, phase, i, me).start()
            return carry

        lax.fori_loop(1, size, send, 0)

    def take_block(buffer, phase, i):
        q = lax.rem(me + size - i, size)

        @pl.when(i > 0)
        def _():
            block_copy(buffer, phase, i, q).wait_recv()

        return q

    def out_part(k, carry):
        i = lax.rem(k + 1, size)
        q = lax.rem(me + i, size)
        for h in range(heads):
            hc = slice(h * HEAD, (h + 1) * HEAD)
            out = (oloc_ref[rows(q), hc] + mm(carr_ref[rows(q), hc], sin_ref[h])).astype(BF16)
            heads_ref[rows(q), hc] = out
            wide = out.astype(F32)
            gate = gate_ref[rows(q), hc]
            scaled = wide * lax.rsqrt(jnp.mean(wide * wide, axis=1, keepdims=True) + NORM_EPS) * gain
            mixed_ref[rows(q), hc] = (scaled * (gate * jax.nn.sigmoid(gate))).astype(BF16)
        give_part(0, i, dot(mixed_ref[rows(q)], wout_ref[...]))
        return carry

    lax.fori_loop(0, size, out_part, 0)
    hops = pieces // 2 - 1
    for distance in range(1, hops // 2 + 1):
        line.hop(distance)
    middle = x_ref[...].astype(F32) + take_parts(0)
    mid[...] = middle
    inv = lax.rsqrt(jnp.mean(middle * middle, axis=1, keepdims=True) + NORM_EPS)
    give_block(second, 3, (middle * inv * norm).astype(BF16))
    for load in loads[5:7]:
        load.wait()
    for distance in range(hops // 2 + 1, hops + 1):
        line.hop(distance)
    line.finish()
    deep = wds.shape[1]
    inner = pieces * deep
    wd_ref[inner:] = jnp.zeros((wd_ref.shape[0] - inner, D), BF16)
    for c in range(pieces):
        wd_ref[c * deep : (c + 1) * deep] = wds[c]

    def feed(i, carry):
        q = take_block(second, 3, i)
        here = second[rows(q)]
        gate = dot(here, wg_ref[...])
        up = dot(here, wu_ref[...])
        gates[rows(q)] = gate
        ups[rows(q)] = up
        hid = (gate * jax.nn.sigmoid(gate) * up).astype(BF16)
        hidden[rows(q)] = hid
        give_part(1, lax.rem(size - i, size), dot(hid, wd_ref[...]))
        return carry

    lax.fori_loop(0, size, feed, 0)
    final = mid[...] + take_parts(1)
    final_ref[...] = final.astype(BF16)
    error = final - teach_ref[...].astype(F32)
    mask = jnp.broadcast_to(mask_ref[...].astype(F32), (count, count)).T[:, :1]
    weighted = mask * error
    loss_ref[...] = jnp.broadcast_to(
        jnp.sum(jnp.sum(weighted * error, axis=1, keepdims=True), axis=0, keepdims=True), loss_ref.shape
    )
    valid = jnp.maximum(jnp.sum(norms_ref[2:3, :], axis=1, keepdims=True), 1.0)
    grad_final = token_total / valid * weighted
    gfin[...] = grad_final
    give_block(branch, 4, grad_final.astype(BF16))

    def feed_back(i, carry):
        q = take_block(branch, 4, i)
        ghid = dot(branch[rows(q)], wd_ref[...], 1, 1)
        gate = gates[rows(q)]
        sig = jax.nn.sigmoid(gate)
        silu = gate * sig
        ggate = (ghid * ups[rows(q)] * (sig + silu * (1.0 - sig))).astype(BF16)
        gup = (ghid * silu).astype(BF16)
        ggates[rows(q)] = ggate
        gups[rows(q)] = gup
        give_part(2, lax.rem(size - i, size), dot(ggate, wg_ref[...], 1, 1) + dot(gup, wu_ref[...], 1, 1))
        return carry

    lax.fori_loop(0, size, feed_back, 0)
    held = D // (size * pieces)
    tall_ref[...] = jnp.zeros_like(tall_ref)
    grad = dot(hidden[...], branch[...], 0, 0)
    for c in range(pieces):
        tall_ref[c // 2, c % 2, :deep] = grad[c * deep : (c + 1) * deep].astype(BF16)
    for n, side in enumerate((ggates, gups)):
        grad = dot(second[...], side[...], 0, 0)
        for c in range(pieces):
            for r in range(size):
                first = (r * pieces + c) * held
                wide_ref[c // 2, c % 2, (n * size + r) * held : (n * size + r + 1) * held] = grad[
                    first : first + held
                ].astype(BF16)
    pair = Siblings([wide_ref, tall_ref], [wtheirs, ttheirs], [wheld, theld], pair_send, pair_recv)
    sums = LineSum(pieces, [wheld, theld], [wcame, tcame], sum_send, sum_recv)
    pair.start()
    pair.add()
    sums.round(0)
    gsecond = take_parts(2)
    middle = mid[...]
    inv = lax.rsqrt(jnp.mean(middle * middle, axis=1, keepdims=True) + NORM_EPS)
    unit = middle * inv
    gnorm_ref[...] = jnp.sum(gsecond * unit, axis=0, keepdims=True)
    down = gsecond * norm
    gmid = gfin[...] + inv * (down - unit * jnp.mean(down * unit, axis=1, keepdims=True))
    gmid_ref[...] = gmid
    give_block(low, 5, gmid.astype(BF16))
    ggain_ref[...] = jnp.zeros_like(ggain_ref)
    cot_ref[...] = jnp.zeros_like(cot_ref)

    def out_back(i, carry):
        q = take_block(low, 5, i)
        gmixed = dot(low[rows(q)], wout_ref[...], 1, 1)
        for h in range(heads):
            hc = slice(h * HEAD, (h + 1) * HEAD)
            x = heads_ref[rows(q), hc].astype(F32)
            gate = gate_ref[rows(q), hc]
            grad = gmixed[:, hc]
            inv = lax.rsqrt(jnp.mean(x * x, axis=1, keepdims=True) + NORM_EPS)
            sig = jax.nn.sigmoid(gate)
            silu = gate * sig
            unit = x * inv
            ggate_ref[rows(q), hc] = (grad * unit * gain * (sig + silu * (1.0 - sig))).astype(BF16)
            weighted = grad * silu
            ggain_ref[...] += jnp.sum(weighted * unit, axis=0, keepdims=True)
            down = weighted * gain
            ghead = (inv * (down - unit * jnp.mean(down * unit, axis=1, keepdims=True))).astype(BF16)
            ghead_ref[rows(q), hc] = ghead
            cot_ref[h] += mm(carr_ref[rows(q), hc], ghead, 0, 0)
        return carry

    out_back(0, 0)
    early = max(1, hops - 1)
    for r in range(1, early):
        sums.round(r)
    lax.fori_loop(1, size, out_back, 0)
    grad = dot(mixed_ref[...], low[...], 0, 0)
    for c in range(pieces):
        outg_ref[c // 2, c % 2] = grad[c * held : (c + 1) * held].astype(BF16)
    sums.settle(early)
    pair.left()
    for r in range(early):
        sums.left(r)

    def sent_all(i, carry):
        for phase in range(3):
            part_copy(phase, i).wait_send()
        block_copy(second, 3, i, me).wait_send()
        block_copy(branch, 4, i, me).wait_send()
        block_copy(low, 5, i, me).wait_send()
        return carry

    lax.fori_loop(1, size, sent_all, 0)


def middle_part(
    size, heads, pieces, token_total, x, teacher, mask, norms, gain, oloc, carr, gate_out, state_in, wout, wg, wu, wd
):
    count = x.shape[0]
    rows = count * size
    inner = wg.shape[1]
    held, deep = D // (size * pieces), wd.shape[0]
    chips = pieces // 2
    wide, tall = (2 * size * held, inner), (-(-deep // 16) * 16, D)
    vmem = pl.BlockSpec(memory_space=pltpu.VMEM)
    out = lambda dims, kind: jax.ShapeDtypeStruct(dims, kind)
    low = lambda *dims: pltpu.VMEM(dims, BF16)
    high = lambda *dims: pltpu.VMEM(dims, F32)
    dma = pltpu.SemaphoreType.DMA
    return pl.pallas_call(
        functools.partial(middle_kernel, size, heads, float(token_total)),
        in_specs=[vmem] * 5 + [pl.BlockSpec(memory_space=pltpu.HBM)] * 8,
        out_specs=[vmem] * 11,
        out_shape=[
            out((count, D), BF16), out((count, D), F32),
            out((rows, heads * HEAD), BF16), out((rows, heads * HEAD), BF16), out((heads, HEAD, HEAD), F32),
            out((1, HEAD), F32), out((1, D), F32), out((1, HEAD), F32),
            out((chips, 2 * size * held, inner), BF16), out((chips, -(-deep // 16) * 16, D), BF16),
            out((chips, 2, held, D), BF16),
        ],
        scratch_shapes=[
            high(rows, heads * HEAD), high(rows, heads * HEAD), high(rows, heads * HEAD), high(heads, HEAD, HEAD),
            low(*wout.shape), low(*wg.shape), low(*wu.shape), low(inner, D), dma((8,)),
            low(rows, heads * HEAD), low(rows, heads * HEAD), dma((1, 3, pieces)), dma((1, pieces)), low(pieces, *wd.shape),
            low(chips, 2, *wide), low(chips, 2, *tall), low(chips, *wide), low(chips, *tall), low(2, chips, *wide),
            low(2, chips, *tall), dma((2,)), dma((2,)), dma((2, chips)), dma((2, 2, chips)),
            low(rows, D), low(rows, D), low(rows, D), low(3, size - 1, count, D), low(3, size - 1, count, D),
            high(count, D), high(count, D), high(count, D), high(rows, inner), high(rows, inner), low(rows, inner),
            low(rows, inner), low(rows, inner), dma((6, size - 1)), dma((6, size - 1)),
        ],
        compiler_params=pltpu.CompilerParams(
            vmem_limit_bytes=VMEM_LIMIT, collective_id=1, has_side_effects=True
        ),
        name="middle_part",
    )(x, teacher, mask, norms, gain, oloc, carr, gate_out, state_in, wout, wg, wu, wd)


def bwd_kernel(
    heads, pieces, steps, per, begun, span_pieces, maps_ref, cot_ref, sin_ref, proj_ref, w_ref, rowp_ref, colp_ref, tokp_ref, slope_ref,
    go_ref, conv_ref, q_ref, k_ref, v_ref, t_ref, kk_ref, at_ref, uw_ref, pl_ref, wide_ref, tall_ref, outg_ref, normed_ref, ggate_ref,
    gproj_ref, fix_ref, gw_ref, gscal_ref, gsum_ref, widesum_ref, tallsum_ref, outsum_ref, gatesum_ref,
    dstate, weave, rim, last, cots, rim_in, wheld, theld, wcame, tcame,
    gateg, otheirs, gtheirs, oheld, gheld, ocame, gcame,
    cot_send, cot_recv, pair_send, pair_recv, early_send, early_recv, line_send, line_recv, rim_sem,
):
    step = pl.program_id(0)
    block = steps - 1 - step
    here = lax.axis_index("ctx")
    core = lax.rem(here, 2)
    early = LineSum(pieces, [wheld, theld], [wcame, tcame], early_send, early_recv)
    pair = Siblings([outg_ref, gateg], [otheirs, gtheirs], [oheld, gheld], pair_send, pair_recv)
    line = LineSum(pieces, [oheld, gheld], [ocame, gcame], line_send, line_recv)
    rounds = pieces // 2 - 1
    when_round = [min(steps - 1, 1 + (r * steps) // rounds) for r in range(rounds)]

    @pl.when(step == 0)
    def _():
        barrier = pltpu.get_barrier_semaphore()
        side = [({"ctx": here + 1}, (core == 1) & (here < pieces - 1)), ({"ctx": here - 1}, (core == 0) & (here > 0))]
        pl.semaphore_wait(barrier, greet(line_neighbours(pieces) + side, barrier))
        cots[here] = cot_ref[...].astype(BF16)
        spread = Line(
            pieces, [lambda c: cots.at[c]], cot_send, cot_recv, up=False, reach=chips_within(span_pieces, pieces)
        )
        spread.own()
        wheld[...] = wide_ref[...]
        theld[...] = tall_ref[...]
        grad = lax.dot_general(
            normed_ref[...], ggate_ref[...], (((0,), (0,)), ((), ())), preferred_element_type=F32
        )
        held, size = gateg.shape[3], gateg.shape[2]
        for c in range(pieces):
            for r in range(size):
                row = (r * pieces + c) * held
                gateg[c // 2, c % 2, r] = grad[row : row + held].astype(BF16)
        for distance in range(1, spread.reach + 1):
            spread.hop(distance)
        spread.finish()
        early.launch(begun)
        pair.start()

        farthest = jnp.minimum(here + span_pieces, pieces - 1)

        def hop(i, states):
            k = farthest - i
            return tuple(
                mm(maps_ref[k, h], states[h], 0, 0) + cots[k, h].astype(F32) for h in range(heads)
            )

        found = lax.fori_loop(
            0, farthest - here, hop, tuple(jnp.zeros((HEAD, HEAD), F32) for _ in range(heads))
        )
        for h in range(heads):
            dstate[h] = found[h]
        rim[...] = jnp.zeros_like(rim)
        gw_ref[...] = jnp.zeros_like(gw_ref)
        gsum_ref[...] = jnp.zeros_like(gsum_ref)

    for r in range(begun + 1, rounds):
        at = min(steps - 1, 1 + ((r - begun) * (steps - 1)) // (rounds - begun))
        pl.when(step == at)(lambda r=r: early.round(r))
    pl.when(step == 1)(pair.add)
    for r in range(rounds):
        pl.when(step == when_round[r])(lambda r=r: line.round(r))

    last_row = iota((ROWS, 1), 0) == ROWS - 1
    diagonal = iota((ROWS, ROWS), 0) == iota((ROWS, ROWS), 1)
    first_lane = lax.axis_index("seq") * lane_of(heads, 0)
    gscals = [[] for _ in range(per)]
    dnexts = {(per - 1, h): dstate[h] for h in range(heads)}
    rims = {(per - 1, h): rim[:, h * WIDE : (h + 1) * WIDE] for h in range(heads)}

    def item(j, h):
        n = j * heads + h
        span = slice(j * BLOCK_LEN, (j + 1) * BLOCK_LEN)
        rowp, colp = rowp_ref[j * 8 : (j + 1) * 8], colp_ref[j * ROWS : (j + 1) * ROWS]
        tokp, slope = tokp_ref[span], slope_ref[span]
        cols = slice(h * WIDE, (h + 1) * WIDE)
        hc = slice(h * HEAD, (h + 1) * HEAD)
        beta, decay, qdecay, carry, qcarry, dlast, clast = decays(rowp, colp, tokp, h)
        go = go_ref[span, hc]
        query, keys, values = q_ref[j, h], k_ref[j, h], v_ref[j, h]
        inv, kk, attn, uw = t_ref[j, h], kk_ref[j, h], at_ref[j, h], uw_ref[j, h]
        yield
        state = mm(pl_ref[j, h, :, :HEAD], sin_ref[h]) + pl_ref[j, h, :, HEAD:]
        yield
        both = mm(jnp.concatenate([keys, uw[:, HEAD:]], axis=0), state)
        ks = both[:ROWS]
        upd = uw[:, :HEAD] - both[ROWS:]
        dlocal = mm(attn, go, 0, 0)
        while (j, h) not in dnexts:
            yield
        dnext = dnexts[j, h]
        yield
        dupd = dlocal + dlast * mm(keys, dnext)
        yield
        dx = mm(inv, dupd, 0, 0)
        yield
        dv = beta * dx
        dy = -(carry * dv)
        go32 = go.astype(F32)
        dnexts[j - 1, h] = clast * dnext + mm(
            jnp.concatenate([qcarry * query, keys], axis=0), jnp.concatenate([go32, dy], axis=0), 0, 0
        )
        yield
        outer = mm(jnp.concatenate([go32, dx], axis=0), upd, 1, 1)
        dattn, da = outer[:BLOCK_LEN], -outer[BLOCK_LEN:]
        yield
        dkd = mm(upd, dnext, 1, 1)
        right = mm(jnp.concatenate([go32, dy], axis=0), state, 1, 1)
        gos = right[:BLOCK_LEN]
        yield
        e = beta * da * decay
        f = dattn * qdecay
        ef = jnp.concatenate([f, e], axis=0)
        efk = mm(ef, keys)
        dq = qcarry * gos + efk[:BLOCK_LEN]
        yield
        dk = (
            right[BLOCK_LEN:]
            + dlast * dkd
            + efk[BLOCK_LEN:]
            + mm(ef, jnp.concatenate([query, keys], axis=0), 0, 0)
        )
        weave[3 * n] = dk
        weave[3 * n + 1] = dv
        yield
        dakk = da * kk
        z1 = beta * dakk
        z2 = dattn * attn
        kept = dlast * (dkd * keys)
        below = jnp.sum(z1, axis=0, keepdims=True) + jnp.sum(z2, axis=0, keepdims=True)
        dbeta = jnp.sum(dx * (values - carry * ks) + dakk, axis=1, keepdims=True)
        tail = jnp.sum(
            jnp.sum(kept, axis=0, keepdims=True) + clast * jnp.sum(state * dnext, axis=0, keepdims=True),
            axis=1, keepdims=True,
        )
        dgrow = jnp.sum(z1 + dy * ks - kept - jnp.where(diagonal, below, 0.0), axis=1, keepdims=True)
        dgrow = dgrow + jnp.where(last_row, tail, 0.0)
        lane = iota((ROWS, HEAD), 1)
        weave[3 * n + 2] = jnp.where(lane == 0, dbeta, dgrow)
        yield
        by_step = [weave[3 * n + 2, pl.ds(i, BLOCK_LEN, NH), :] for i in range(NH)]
        dg = sum(x[:, 1:2] for x in by_step) + jnp.sum(z2 + qcarry * (query * gos), axis=1, keepdims=True)
        after = (iota((BLOCK_LEN, BLOCK_LEN), 0) <= iota((BLOCK_LEN, BLOCK_LEN), 1)).astype(BF16)
        dlog = column(tokp, LINK) * mm(after, jnp.broadcast_to(dg, (BLOCK_LEN, HEAD)))[:, :1]
        dscal = [by_step[i][:, 0:1] * column(slope, lane_of(h, i)) for i in range(NH)]
        dscal.append(dlog * column(slope, lane_of(h, NH)))
        lane = iota((BLOCK_LEN, HEAD), 1)
        for i in range(NH + 1):
            gscals[j].append(jnp.where(lane == first_lane + lane_of(h, i), dscal[i], 0.0))
        logs = column(slope, HEAD // 2 + lane_of(h, NH))
        sums = jnp.where(lane == 0, dlog * logs, jnp.where(lane == 1, dscal[NH], 0.0))
        gsum_ref[h : h + 1, :] += jnp.sum(sums, axis=0, keepdims=True)
        yield
        conv = conv_ref[span, cols]
        sig = jax.nn.sigmoid(conv)
        act = conv * sig
        parts = []
        for part in range(1 + NH):
            piece = act[:, part * HEAD : (part + 1) * HEAD]
            scale = lax.rsqrt(jnp.sum(piece * piece, axis=1, keepdims=True) + NORM_EPS)
            if part:
                grad = weave[3 * n, pl.ds(part - 1, BLOCK_LEN, NH), :]
            else:
                grad = dq * (1.0 / math.sqrt(HEAD))
            unit = piece * scale
            parts.append(scale * (grad - unit * jnp.sum(grad * unit, axis=1, keepdims=True)))
        for i in range(NH):
            parts.append(weave[3 * n + 1, pl.ds(i, BLOCK_LEN, NH), :])
        dconv = jnp.concatenate(parts, axis=1) * (sig * (1.0 + conv * (1.0 - sig)))
        yield
        base = pl.multiple_of((block * per + j) * BLOCK_LEN, BLOCK_LEN)
        ext = proj_ref[pl.ds(base, BLOCK_LEN + HALO), cols].astype(F32)
        gw_ref[0:1, cols] += jnp.sum(dconv * ext[HALO:], axis=0, keepdims=True)
        zeros = jnp.zeros((8, WIDE), F32)
        length = BLOCK_LEN + 8
        total = jnp.concatenate([zeros, dconv * w_ref[0:1, cols]], axis=0)
        for lag in range(1, CONV):
            masked = column(tokp, LINK + lag - 1) * dconv
            gw_ref[lag : lag + 1, cols] += jnp.sum(masked * lag_rows(ext, lag), axis=0, keepdims=True)
            total = total + pltpu.roll(
                jnp.concatenate([zeros, masked * w_ref[lag : lag + 1, cols]], axis=0), length - lag, 0
            )
        rims[j - 1, h] = total[:8]
        fixed = total[length - 8 :] + rims[j, h]
        gproj_ref[span, cols] = jnp.concatenate([total[8 : length - 8], fixed], axis=0).astype(BF16)
        if j == per - 1:

            @pl.when(step == 0)
            def _():
                last[:, cols] = fixed

    running = [item(j, h) for j in reversed(range(per)) for h in range(heads)]
    while running:
        running = [one for one in running if next(one, "done") != "done"]
    for h in range(heads):
        dstate[h] = dnexts[-1, h]
        rim[:, h * WIDE : (h + 1) * WIDE] = rims[-1, h]
    for j in range(per):
        gscal_ref[j * BLOCK_LEN : (j + 1) * BLOCK_LEN] = sum(gscals[j]).astype(BF16)

    @pl.when(step == steps - 1)
    def _():
        passing = pltpu.make_async_remote_copy(
            rim, rim_in, rim_sem.at[0], rim_sem.at[1], device_id={"ctx": here - 1}, device_id_type=MESH
        )
        pl.when(here > 0)(passing.start)
        fix_ref[...] = last[...].astype(BF16)

        @pl.when(here < pieces - 1)
        def _():
            passing.wait_recv()
            fix_ref[...] = (last[...] + rim_in[...]).astype(BF16)

        early.finish()
        line.finish()
        widesum_ref[...] = wheld[here // 2]
        tallsum_ref[...] = theld[here // 2].astype(F32)
        outsum_ref[...] = oheld[here // 2].astype(F32)
        gatesum_ref[...] = gheld[here // 2]
        pair.left()
        for r in range(begun, rounds):
            early.left(r)
        for r in range(rounds):
            line.left(r)
        pl.when(here > 0)(passing.wait_send)


def recurrence_backward(
    maps, cot, state_in, proj_ext, conv_w, rowp, colp, tokp, slopes, grad_heads, saved, wide, tall, outg, normed, ggate,
    heads, pieces, span_pieces,
):
    rows = tokp.shape[0]
    blocks = rows // BLOCK_LEN
    chips = pieces // 2
    per = 2
    final = blocks // per - 1
    whole = lambda *dims: pl.BlockSpec(dims, lambda i: (0,) * len(dims))
    by_block = lambda *dims: pl.BlockSpec((per,) + dims, lambda i: (final - i,) + (0,) * len(dims))
    token = lambda cols: pl.BlockSpec((per * BLOCK_LEN, cols), lambda i: (final - i, 0))
    shape = lambda *dims: jax.ShapeDtypeStruct(dims, F32)
    low_shape = lambda *dims: jax.ShapeDtypeStruct(dims, BF16)
    vmem = pl.BlockSpec(memory_space=pltpu.VMEM)
    low = lambda *dims: pltpu.VMEM(dims, BF16)
    square = (heads, ROWS, HEAD)
    wide_chunk, tall_chunk, out_chunk = wide.shape[1:], tall.shape[1:], outg.shape[2:]
    gate_chunk = (HEADS // heads, out_chunk[0], ggate.shape[1])
    dma = pltpu.SemaphoreType.DMA
    return pl.pallas_call(
        functools.partial(bwd_kernel, heads, pieces, blocks // per, per, max(1, chips - 2), span_pieces),
        grid=(blocks // per,),
        in_specs=[
            vmem, vmem, vmem, vmem, vmem,
            pl.BlockSpec((per * 8, ROWS), lambda i: (final - i, 0)),
            pl.BlockSpec((per * ROWS, HEAD), lambda i: (final - i, 0)), token(HEAD), token(HEAD),
            token(heads * HEAD), token(heads * WIDE),
            by_block(heads, BLOCK_LEN, HEAD), by_block(*square), by_block(*square), by_block(*square),
            by_block(*square), by_block(heads, BLOCK_LEN, ROWS), by_block(heads, ROWS, 2 * HEAD),
            by_block(heads, HEAD, 2 * HEAD), vmem, vmem, vmem, vmem, vmem,
        ],
        out_specs=[
            token(heads * WIDE), whole(8, heads * WIDE), whole(8, heads * WIDE), token(HEAD), whole(8, HEAD),
            whole(*wide_chunk), whole(*tall_chunk), whole(*out_chunk), whole(*gate_chunk),
        ],
        out_shape=[
            low_shape(rows, heads * WIDE), low_shape(8, heads * WIDE), shape(8, heads * WIDE), low_shape(rows, HEAD),
            shape(8, HEAD), low_shape(*wide_chunk), shape(*tall_chunk), shape(*out_chunk), low_shape(*gate_chunk),
        ],
        scratch_shapes=[
            pltpu.VMEM((heads, HEAD, HEAD), F32), pltpu.VMEM((3 * heads * per, ROWS, HEAD), F32),
            pltpu.VMEM((8, heads * WIDE), F32), pltpu.VMEM((8, heads * WIDE), F32),
            pltpu.VMEM((pieces, heads, HEAD, HEAD), BF16), pltpu.VMEM((8, heads * WIDE), F32),
            low(chips, *wide_chunk), low(chips, *tall_chunk), low(2, chips, *wide_chunk), low(2, chips, *tall_chunk),
            low(chips, 2, *gate_chunk), low(chips, *out_chunk), low(chips, *gate_chunk), low(chips, *out_chunk),
            low(chips, *gate_chunk), low(2, chips, *out_chunk), low(2, chips, *gate_chunk),
            dma((1, 3, pieces)), dma((1, pieces)), dma((2,)), dma((2,)), dma((2, chips)), dma((2, 2, chips)),
            dma((2, chips)), dma((2, 2, chips)), dma((2,)),
        ],
        compiler_params=pltpu.CompilerParams(
            vmem_limit_bytes=VMEM_LIMIT, collective_id=4, has_side_effects=True
        ),
        name="recurrence_backward",
    )(maps, cot, state_in, proj_ext, conv_w, rowp, colp, tokp, slopes, grad_heads, *saved, wide, tall, outg, normed, ggate)


def final_kernel(
    size, pieces, heads, norm_at, inner, gp_any, gg_any, gs_any, w_any, normed_any,
    fix_ref, x_ref, gmid_ref, norms_ref, gw_ref, gain_ref, gsum_ref, loss_ref, gnorm_ref, wide_ref, gatesum_ref,
    ingrad_ref, gmix_ref, ggate_ref, gtail_ref, gwg_ref, gwu_ref, mean_ref, ends_ref, both_ref,
    gp_ref, gg_ref, gs_ref, w_ref, normed_ref, load_sem, wideout_ref, gateout_ref,
    sent, got, whole, turned, grads, theirs, held, came, blocks, around, along, summed,
    local_sem, seq_send, seq_recv, pair_send, pair_recv, line_send, line_recv, ctx_send, ctx_recv,
):
    me, here = lax.axis_index("seq"), lax.axis_index("ctx")
    count = x_ref.shape[0]
    loads = [
        pltpu.make_async_copy(source, target, load_sem.at[n])
        for n, (source, target) in enumerate(
            [(gp_any, gp_ref), (gg_any, gg_ref), (gs_any, gs_ref), (w_any, w_ref), (normed_any, normed_ref)]
        )
    ]
    for load in loads:
        load.start()
    barrier = pltpu.get_barrier_semaphore()
    peers = [({"seq": lax.rem(me + i, size)}, here >= 0) for i in range(1, size)]
    peers += [({"ctx": lax.rem(here + i, pieces)}, here >= 0) for i in range(1, pieces)]
    pl.semaphore_wait(barrier, greet(peers, barrier))

    def dot(a, b, ca=1, cb=0):
        return lax.dot_general(a, b, (((ca,), (cb,)), ((), ())), preferred_element_type=F32)

    def rows(q):
        return pl.ds(pl.multiple_of(q * count, count), count)

    def to_peer(n, i):
        q = lax.rem(me + i, size)
        source, target = [
            (sent.at[i - 1], got.at[i - 1]), (wide_ref.at[:, q], wideout_ref.at[me]),
            (around.at[me], around.at[me]), (held.at[here // 2, q], blocks.at[me]),
            (gatesum_ref.at[q], gateout_ref.at[me]),
        ][n]
        return pltpu.make_async_remote_copy(
            source, target, seq_send.at[n, i - 1], seq_recv.at[n, i - 1], device_id={"seq": q}, device_id_type=MESH
        )

    def to_piece(i):
        return pltpu.make_async_remote_copy(
            along.at[here], along.at[here], ctx_send.at[i - 1], ctx_recv.at[i - 1],
            device_id={"ctx": lax.rem(here + i, pieces)}, device_id_type=MESH,
        )

    gate_at, tail_at = gp_ref.shape[1], gp_ref.shape[1] + gg_ref.shape[1]
    for load in loads:
        load.wait()
    gp_ref[gp_ref.shape[0] - 8 :] = fix_ref[...]

    def parts():
        for first in range(0, D, 256):
            tile = slice(first, first + 256)
            value = (
                dot(gp_ref[...], w_ref[tile, :gate_at], 1, 1)
                + dot(gg_ref[...], w_ref[tile, gate_at:tail_at], 1, 1)
                + dot(gs_ref[...], w_ref[tile, tail_at:], 1, 1)
            )
            whole[:, tile] = value

        def give(i, carry):
            sent[i - 1] = whole[rows(lax.rem(me + i, size))].astype(BF16)
            pltpu.make_async_remote_copy(
                sent.at[i - 1], got.at[i - 1], seq_send.at[0, i - 1], seq_recv.at[0, i - 1],
                device_id={"seq": lax.rem(me + i, size)}, device_id_type=MESH,
            ).start()
            return carry

        lax.fori_loop(1, size, give, 0)

    turned[...] = normed_ref[...].T
    rank_rows = D // (size * pieces)
    for source, at in ((gp_ref, 0), (gs_ref, gate_at)):
        width = source.shape[1]
        for first in range(0, width, 256):
            cols = min(256, width - first)
            grad = dot(turned[...], source[:, first : first + cols])
            for r in range(size):
                for c in range(pieces):
                    row = (r * pieces + c) * rank_rows
                    grads[c // 2, c % 2, r, :, at + first : at + first + cols] = grad[row : row + rank_rows].astype(BF16)
    channels = gw_ref.shape[1]
    mine = channel_rows(D // size, channels)
    taps = jnp.zeros((D // size, HEAD), F32)
    for lag in range(CONV):
        spread = jnp.where(mine, gw_ref[lag : lag + 1], 0.0).astype(BF16)
        taps = taps + dot(spread, tap_lanes(channels, CONV - 1 - lag, norm_at + 3))
    for c in range(pieces):
        grads[c // 2, c % 2, me, :, gate_at:] = (
            grads[c // 2, c % 2, me, :, gate_at:].astype(F32) + taps[c * rank_rows : (c + 1) * rank_rows]
        ).astype(BF16)
    pair = Siblings([grads], [theirs], [held], pair_send, pair_recv)
    line = LineSum(pieces, [held], [came], line_send, line_recv)
    pair.start()
    parts()
    pair.add()
    line.round(0)
    rounds = pieces // 2 - 1
    for r in range(1, rounds - 1):
        line.round(r)
    for i in range(1, size):
        to_peer(0, i).wait_recv()
    gnormed = whole[rows(me)]
    for i in range(1, size):
        gnormed = gnormed + got[i - 1].astype(F32)
    x = x_ref[...].astype(F32)
    inv = lax.rsqrt(jnp.mean(x * x, axis=1, keepdims=True) + NORM_EPS)
    unit = x * inv
    down = gnormed * norms_ref[0:1, :]
    ingrad_ref[...] = gmid_ref[...] + inv * (down - unit * jnp.mean(down * unit, axis=1, keepdims=True))
    term = jnp.sum(gnormed * unit, axis=0, keepdims=True)
    lane = iota((1, HEAD), 1)
    ends = jnp.where(lane == 2 * HEADS, loss_ref[...], 0.0)
    for h in range(heads):
        for n in range(2):
            ends = jnp.where(lane == n * HEADS + me * heads + h, gsum_ref[h : h + 1, n : n + 1], ends)
    around[me] = jnp.zeros(around.shape[1:], F32)
    around[me, 0:1] = gain_ref[...]
    around[me, 1:2] = ends
    for j in range(D // HEAD):
        around[me, 8 + j : 9 + j] = term[:, j * HEAD : (j + 1) * HEAD]
        around[me, 8 + D // HEAD + j : 9 + D // HEAD + j] = gnorm_ref[:, j * HEAD : (j + 1) * HEAD]
    for i in range(1, size):
        to_peer(2, i).start()
    kept = [
        pltpu.make_async_copy(wide_ref.at[:, me], wideout_ref.at[me], local_sem.at[0]),
        pltpu.make_async_copy(gatesum_ref.at[me], gateout_ref.at[me], local_sem.at[1]),
    ]
    for copy in kept:
        copy.start()
    for i in range(1, size):
        to_peer(1, i).start()
        to_peer(4, i).start()
    line.round(rounds - 1)
    for i in range(1, size):
        to_peer(2, i).wait_recv()
    mine = around[0]
    for r in range(1, size):
        mine = mine + around[r]
    along[here] = mine
    for i in range(1, pieces):
        to_piece(i).start()
    line.finish()
    blocks[me] = held[here // 2, me]
    for i in range(1, size):
        to_peer(3, i).start()
    for i in range(1, pieces):
        to_piece(i).wait_recv()
    total = along[0]
    for c in range(1, pieces):
        total = total + along[c]
    ends_ref[...] = total[:2]
    valid = jnp.maximum(jnp.sum(norms_ref[2:3, :], axis=1, keepdims=True), 1.0)
    mean_ref[...] = total[1:2, 2 * HEADS : 2 * HEADS + 1] / (D * valid)
    summed[...] = total
    place = (me * pieces + here) * rank_rows
    for n in range(2):
        row = summed[pl.ds(8 + n * (D // HEAD) + place // HEAD, 1), :]
        both_ref[n : n + 1, :] = pltpu.roll(row, lax.rem(HEAD - lax.rem(place, HEAD), HEAD), 1)
    tail = jnp.zeros((rank_rows, HEAD), F32)
    for copy in kept:
        copy.wait()
    for i in range(1, size):
        to_peer(3, i).wait_recv()
        to_peer(1, i).wait_recv()
        to_peer(4, i).wait_recv()
    for r in range(size):
        block = blocks[r].astype(F32)
        gmix_ref[:, r * gate_at : (r + 1) * gate_at] = block[:, :gate_at]
        ggate_ref[:, r * (tail_at - gate_at) : (r + 1) * (tail_at - gate_at)] = gateout_ref[r].astype(F32)
        tail = tail + block[:, gate_at:]
        gwg_ref[:, r * inner : (r + 1) * inner] = wideout_ref[r, 0, :, :inner].astype(F32)
        gwu_ref[:, r * inner : (r + 1) * inner] = wideout_ref[r, 1, :, :inner].astype(F32)
    gtail_ref[...] = tail
    pair.left()
    for r in range(pieces // 2 - 1):
        line.left(r)
    for i in range(1, size):
        for n in range(5):
            to_peer(n, i).wait_send()
    for i in range(1, pieces):
        to_piece(i).wait_send()


def final_part(
    size, pieces, heads, norm_at, gp, gg, gs, weights, normed, fix, x, gmid, norms, gw, gain, gsum, loss, gnorm, wide,
    gatesum,
):
    count = x.shape[0]
    chips = pieces // 2
    held, inner = D // (size * pieces), FF // size
    width = gp.shape[1] + gs.shape[1]
    small = (8 + 2 * (D // HEAD), HEAD)
    vmem = pl.BlockSpec(memory_space=pltpu.VMEM)
    out = lambda *dims: jax.ShapeDtypeStruct(dims, F32)
    low = lambda *dims: pltpu.VMEM(dims, BF16)
    high = lambda *dims: pltpu.VMEM(dims, F32)
    dma = pltpu.SemaphoreType.DMA
    return pl.pallas_call(
        functools.partial(final_kernel, size, pieces, heads, norm_at, inner),
        in_specs=[pl.BlockSpec(memory_space=pltpu.HBM)] * 5 + [vmem] * 11,
        out_specs=[vmem] * 9,
        out_shape=[
            out(count, D), out(held, size * gp.shape[1]), out(held, size * gg.shape[1]), out(held, HEAD),
            out(held, size * inner), out(held, size * inner), out(1, 1), out(2, HEAD), out(2, HEAD),
        ],
        scratch_shapes=[
            low(*gp.shape), low(*gg.shape), low(*gs.shape), low(*weights.shape), low(*normed.shape), dma((5,)),
            low(size, 2, held, wide.shape[3]), low(*gatesum.shape),
            low(size - 1, count, D), low(size - 1, count, D), high(size * count, D), low(D, normed.shape[0]),
            low(chips, 2, size, held, width), low(chips, size, held, width), low(chips, size, held, width),
            low(2, chips, size, held, width), low(size, held, width), high(size, *small), high(pieces, *small), high(*small),
            dma((2,)), dma((5, size - 1)), dma((5, size - 1)), dma((1,)), dma((1,)), dma((1, chips)), dma((1, 2, chips)),
            dma((pieces - 1,)), dma((pieces - 1,)),
        ],
        compiler_params=pltpu.CompilerParams(
            vmem_limit_bytes=VMEM_LIMIT, collective_id=5, has_side_effects=True
        ),
        name="final_part",
    )(gp, gg, gs, weights, normed, fix, x, gmid, norms, gw, gain, gsum, loss, gnorm, wide, gatesum)


def finish_kernel(
    scal_cols, taps_at, final_ref, ingrad_ref, gmix_ref, ggate_ref, gwg_ref, gwu_ref, tall_ref, outsum_ref,
    tail_ref, ends_ref, both_ref,
    final_out, ingrad_out, gmix_out, ggate_out, gwg_out, gwu_out, gwd_out, gout_out,
    gscal_out, gconv_out, norma_out, normm_out, gain_out, alog_out, dt_out,
):
    for source, target in (
        (final_ref, final_out), (ingrad_ref, ingrad_out), (gmix_ref, gmix_out), (ggate_ref, ggate_out),
        (gwg_ref, gwg_out), (gwu_ref, gwu_out), (outsum_ref, gout_out),
    ):
        target[...] = source[...]
    gwd_out[...] = tall_ref[: gwd_out.shape[0]]
    tail = tail_ref[...]
    rows, channels = tail.shape[0], gconv_out.shape[1]
    square = jnp.concatenate([tail, jnp.zeros((HEAD - rows, HEAD), F32)], axis=0)
    gscal_out[...] = square.T[:scal_cols, :rows]
    mine = channel_rows(rows, channels)
    for tap in range(CONV):
        spread = exact(tail, tap_lanes(channels, tap, taps_at).astype(F32), 1, 1)
        gconv_out[tap : tap + 1] = jnp.sum(jnp.where(mine, spread, 0.0), axis=0, keepdims=True)
    held = norma_out.shape[1]
    norma_out[...] = both_ref[0:1, :held]
    normm_out[...] = both_ref[1:2, :held]
    gain_out[...] = ends_ref[0:1, :]
    alog_out[...] = ends_ref[1:2, :HEADS]
    dt_out[...] = ends_ref[1:2, HEADS : 2 * HEADS]


def finish_part(scal_cols, taps_at, deep, channels, *parts):
    vmem = pl.BlockSpec(memory_space=pltpu.VMEM)
    held = parts[2].shape[0]
    out = lambda dims, kind=F32: jax.ShapeDtypeStruct(dims, kind)
    return pl.pallas_call(
        functools.partial(finish_kernel, scal_cols, taps_at),
        in_specs=[vmem] * 11,
        out_specs=[vmem] * 15,
        out_shape=[out(p.shape, p.dtype) for p in parts[:6]] + [
            out((deep, D)), out(parts[7].shape), out((scal_cols, held)), out((CONV, channels)),
            out((1, held)), out((1, held)), out((1, HEAD)), out((1, HEADS)), out((1, HEADS)),
        ],
        compiler_params=pltpu.CompilerParams(vmem_limit_bytes=VMEM_LIMIT),
        name="finish_part",
    )(*parts)


def local(
    block_input, teacher, valid_mask, segments, mix_proj, scalar_proj, gate_proj, out_proj, conv_weight,
    norm_attn, norm_mlp, head_gain, a_log, dt_bias, w_gate, w_up, w_down,
):
    seq_size, pieces = lax.axis_size("seq"), lax.axis_size("ctx")
    heads = HEADS // seq_size
    rows = block_input.shape[0] * seq_size
    token_total = segments.shape[0]
    seq_length = min(SEQ_LEN, token_total)
    span_pieces = min(pieces, (MOST_DOC.get(token_total, token_total) - 2) // rows + 1)
    index = lax.axis_index("ctx")
    held = mix_proj.shape[0]
    scal_cols = HEADS * (NH + 1)
    norm_at, taps_at = scal_cols, scal_cols + 3
    taps_end = taps_at + CONV * conv_weight.shape[0] // held

    count_here = jnp.sum(valid_mask.astype(F32)).astype(BF16)
    tail = jnp.concatenate(
        [
            scalar_proj, norm_attn[:, None], norm_mlp[:, None],
            jnp.where(iota((held, 1), 0) == 0, count_here, jnp.zeros((), BF16)),
            conv_weight.reshape(held, -1), jnp.zeros((held, HEAD - taps_end), BF16),
        ],
        axis=1,
    )
    x_full, halo, gathered, stage = start_gather(
        seq_size, pieces, block_input, mix_proj, gate_proj, tail, w_gate, w_up
    )
    weights = gathered.reshape(D, -1)
    piece_start = index * rows
    window = lax.dynamic_slice_in_dim(jnp.pad(segments, (CONV, 0)), piece_start, rows + CONV)
    place_in = (piece_start + jnp.arange(rows, dtype=jnp.int32)) % seq_length
    marks = jnp.stack(
        [
            ((window[CONV - lag : CONV - lag + rows] == window[CONV:]) & (place_in >= lag)).astype(F32)
            if lag < CONV
            else jnp.zeros((rows,), F32)
            for lag in range(1, 9)
        ]
    )
    rates = jnp.stack([a_log.astype(F32), dt_bias.astype(F32)])
    (
        proj_ext, normed, gate_out, tokp, slopes, colp, rowp, conv_w, norms,
        oloc, carr, state_in, maps, *saved, wg_full, wu_full, wo_full,
    ) = recurrence_forward(heads, pieces, span_pieces, norm_at, rates, x_full, halo, weights, marks, stage, out_proj)
    (
        final_out, grad_middle, grad_heads, grad_gate_out, cot, gain_term, norm_mlp_term, loss, wide, tall, outg,
    ) = middle_part(
        seq_size, heads, pieces, token_total, block_input, teacher, valid_mask[None, :], norms, head_gain[None, :],
        oloc, carr, gate_out, state_in, wo_full.reshape(heads * HEAD, D), wg_full.reshape(D, -1),
        wu_full.reshape(D, -1), w_down,
    )
    grad_proj, fixed_rows, gw, grad_scal, gsum, wide_sum, tall_sum, out_sum, gate_sum = recurrence_backward(
        maps, cot, state_in, proj_ext, conv_w, rowp, colp, tokp, slopes, grad_heads, saved, wide, tall, outg, normed,
        grad_gate_out, heads, pieces, span_pieces,
    )
    input_grad, mix_grad, gate_grad, tail_grad, wg_grad, wu_grad, mean_loss, ends, norm_grads = final_part(
        seq_size, pieces, heads, norm_at, grad_proj, grad_gate_out, grad_scal, weights, normed, fixed_rows, block_input,
        grad_middle, norms, gw, gain_term, gsum, loss, norm_mlp_term, wide_sum.reshape(2, seq_size, held, -1),
        gate_sum,
    )
    (
        final_out, input_grad, mix_grad, gate_grad, wg_grad, wu_grad, wd_grad, out_grad,
        scal_grad, conv_grad, norm_a_grad, norm_m_grad, gain_grad, alog_grad, dt_grad,
    ) = finish_part(
        scal_cols, taps_at, w_down.shape[0], conv_weight.shape[0],
        final_out, input_grad, mix_grad, gate_grad, wg_grad, wu_grad, tall_sum, out_sum, tail_grad, ends, norm_grads,
    )
    return (
        final_out, mean_loss[0, 0], input_grad, mix_grad, scal_grad.T, gate_grad, out_grad, conv_grad.T,
        norm_a_grad.reshape(-1), norm_m_grad.reshape(-1), gain_grad.reshape(-1), alog_grad.reshape(-1),
        dt_grad.reshape(-1), wg_grad, wu_grad, wd_grad,
    )


def solution(mesh):
    tokens, vector, matrix = P(("ctx", "seq"), None), P(BOTH), P(BOTH, None)
    in_specs = (
        tokens, tokens, P(("ctx", "seq")), P(), matrix, matrix, matrix, matrix, matrix, vector, vector,
        P(), P(), P(), matrix, matrix, matrix,
    )
    out_specs = (
        tokens, P(), tokens, matrix, matrix, matrix, matrix, matrix, vector, vector, P(), P(), P(),
        matrix, matrix, matrix,
    )
    return jax.shard_map(local, mesh=mesh, in_specs=in_specs, out_specs=out_specs, check_vma=False)
```

```python
import functools
import math

import jax
import jax.numpy as jnp
from jax import lax
from jax.experimental import pallas as pl
from jax.experimental.pallas import tpu as pltpu
from jax.sharding import PartitionSpec as P

D = 1024
HEADS = 8
HEAD = 128
NH = 2
FF = 2816
BLOCK_LEN = 64
ROWS = BLOCK_LEN * NH
CONV = 4
SEQ_LEN = 32768
MOST_DOC = {4096: 2048, 32768: 8192}
WIDE = (1 + 2 * NH) * HEAD
HALO = 16
NORM_EPS = 1e-06
VMEM_LIMIT = 60 << 20
F32 = jnp.float32
BF16 = jnp.bfloat16
BOTH = ("seq", "ctx")
MESH = pl.DeviceIdType.MESH


class Split:
    def __init__(self, x):
        self.high = x.astype(BF16)
        self.low = (x - self.high.astype(F32)).astype(BF16)


def mm(a, b, ca=1, cb=0):
    if not isinstance(a, Split) and a.dtype != BF16:
        a = Split(a)
    if not isinstance(b, Split) and b.dtype != BF16:
        b = Split(b)
    if isinstance(a, Split) and isinstance(b, Split):
        left, right = (a.high, a.high, a.low), (b.high, b.low, b.high)
    elif isinstance(a, Split):
        left, right = (a.high, a.low), (b, b)
    elif isinstance(b, Split):
        left, right = (a, a), (b.high, b.low)
    else:
        left, right = (a,), (b,)
    if len(left) > 1:
        left, right = (jnp.concatenate(left, axis=ca),), (jnp.concatenate(right, axis=cb),)
    return lax.dot_general(left[0], right[0], (((ca,), (cb,)), ((), ())), preferred_element_type=F32)


def lanes_for(columns):
    return -(-columns // HEAD) * HEAD


def iota(shape, axis):
    return lax.broadcasted_iota(jnp.int32, shape, axis)


def unit_lower_inverses(systems):
    n = systems[0].shape[0]
    ri, ci = iota((n, n), 0), iota((n, n), 1)
    pick = (iota((n, 8), 0) % 8 == iota((n, 8), 1)).astype(BF16)
    own = ri // 8 == ci // 8
    eye = (ri == ci).astype(F32).reshape(n // 8, 8, n)
    small = [mm(jnp.where(own, a, 0.0), pick).reshape(n // 8, 8, 8) for a in systems]
    inv = [eye for _ in systems]
    for j in range(7):
        inv = [x - m[:, :, j : j + 1] * x[:, j : j + 1, :] for x, m in zip(inv, small)]
    inv = [x.reshape(n, n) for x in inv]
    size = 8
    while size < n:
        off = (ri // (2 * size) == ci // (2 * size)) & (ri // size != ci // size)
        halves = [Split(x) for x in inv]
        right = [mm(jnp.where(off, a, 0.0), x) for a, x in zip(systems, halves)]
        inv = [x - mm(y, z) for x, y, z in zip(inv, halves, right)]
        size *= 2
    return inv


DOC = 7
LINK = DOC + 1


def lane_of(h, what):
    return h * (NH + 1) + what


def column(table, lane):
    return table[:, lane : lane + 1]


def decays(rowp, colp, tokp, h):
    g = lane_of(h, NH)
    cs_row, g_row = rowp[DOC : DOC + 1, :], rowp[g : g + 1, :]
    cs_col, g_col = column(colp, DOC), column(colp, g)
    cs_tok, g_tok = column(tokp, DOC), column(tokp, g)
    beta = column(colp, lane_of(h, 0))
    ri, ci = iota((ROWS, ROWS), 0), iota((ROWS, ROWS), 1)
    strict = (ri > ci) & (cs_col == cs_row)
    decay = jnp.where(strict, jnp.exp(jnp.where(strict, g_col - g_row, 0.0)), 0.0)
    rt, ct = iota((BLOCK_LEN, ROWS), 0), iota((BLOCK_LEN, ROWS), 1)
    seen = (rt * NH + NH - 1 >= ct) & (cs_tok == cs_row)
    qdecay = jnp.where(seen, jnp.exp(jnp.where(seen, g_tok - g_row, 0.0)), 0.0)
    carry = jnp.where(cs_col == 0.0, jnp.exp(g_col), 0.0)
    qcarry = jnp.where(cs_tok == 0.0, jnp.exp(g_tok), 0.0)
    cs_last, g_last = cs_row[:, ROWS - 1 :], g_row[:, ROWS - 1 :]
    same = cs_col == cs_last
    dlast = jnp.where(same, jnp.exp(jnp.where(same, g_last - g_col, 0.0)), 0.0)
    clast = jnp.where(cs_last == 0.0, jnp.exp(g_last), 0.0)
    return beta, decay, qdecay, carry, qcarry, dlast, clast


def lag_rows(ext, lag):
    moved = pltpu.roll(ext, lag, 0) if lag else ext
    return moved[HALO:]


UP, DOWN, ACROSS = 0, 1, 2


class Line:
    def __init__(self, pieces, parts, send_sem, recv_sem, up=True, down=True, reach=None):
        self.chips = pieces // 2
        self.reach = self.chips - 1 if reach is None else reach
        self.here = lax.axis_index("ctx")
        self.chip = self.here // 2
        self.core = lax.rem(self.here, 2)
        self.other = self.here + 1 - 2 * self.core
        self.parts, self.send_sem, self.recv_sem, self.up, self.down = parts, send_sem, recv_sem, up, down

    def copies(self, chunk, way, only=None):
        target = (self.here + 2, self.here - 2, self.other)[way]
        return [
            pltpu.make_async_remote_copy(
                part(chunk), part(chunk), self.send_sem.at[n, way, chunk], self.recv_sem.at[n, chunk],
                device_id={"ctx": target}, device_id_type=MESH,
            )
            for n, part in enumerate(self.parts)
            if only is None or n == only
        ]

    def start(self, chunk, way, only=None):
        for copy in self.copies(chunk, way, only):
            copy.start()

    def arrived(self, chunk, only=None):
        for copy in self.copies(chunk, ACROSS, only):
            copy.wait_recv()

    def left(self, chunk, way):
        for copy in self.copies(chunk, way):
            copy.wait_send()

    def routes(self, distance, act):
        if distance == 0:
            if self.up and self.reach:
                pl.when(self.chip < self.chips - 1)(lambda: act(self.here, UP))
            if self.down and self.reach:
                pl.when(self.chip > 0)(lambda: act(self.here, DOWN))
            act(self.here, ACROSS)
            return
        below, above = self.here - 2 * distance, self.here + 2 * distance
        onward = distance < self.reach
        if self.up:

            @pl.when(self.chip >= distance)
            def _():
                if onward:
                    pl.when(self.chip < self.chips - 1)(lambda: act(below, UP))
                act(below, ACROSS)

        if self.down:

            @pl.when(self.chip + distance < self.chips)
            def _():
                if onward:
                    pl.when(self.chip > 0)(lambda: act(above, DOWN))
                act(above, ACROSS)

    def own(self, only=None):
        self.routes(0, lambda chunk, way: self.start(chunk, way, only))

    def hop(self, distance):
        for n in range(len(self.parts)):
            if self.up:
                pl.when(self.chip >= distance)(lambda n=n: self.arrived(self.here - 2 * distance, n))
            if self.down:
                pl.when(self.chip + distance < self.chips)(lambda n=n: self.arrived(self.here + 2 * distance, n))
            self.routes(distance, lambda chunk, way, n=n: self.start(chunk, way, n))

    def finish(self):
        for chip in range(self.chips):
            needed = (self.chip <= chip + (self.reach if self.up else 0)) & (
                self.chip >= chip - (self.reach if self.down else 0)
            )
            pl.when(needed)(lambda chip=chip: self.arrived(2 * chip + 1 - self.core))
        for distance in range(self.reach + 1):
            self.routes(distance, self.left)


class LineSum:
    def __init__(self, pieces, held, came, send_sem, recv_sem):
        self.chips = pieces // 2
        self.here = lax.axis_index("ctx")
        self.chip = self.here // 2
        self.held, self.came, self.send_sem, self.recv_sem = held, came, send_sem, recv_sem

    def copies(self, owner, way):
        return [
            pltpu.make_async_remote_copy(
                held.at[owner], came.at[way, owner], self.send_sem.at[n, owner], self.recv_sem.at[n, way, owner],
                device_id={"ctx": self.here + 2 - 4 * way}, device_id_type=MESH,
            )
            for n, (held, came) in enumerate(zip(self.held, self.came))
        ]

    def take(self, owner, way):
        for copy in self.copies(owner, way):
            copy.wait_recv()
        for held, came in zip(self.held, self.came):
            held[owner] = (held[owner].astype(F32) + came[way, owner].astype(F32)).astype(BF16)

    def send(self, owner, way):
        for copy in self.copies(owner, way):
            copy.start()

    def each(self, r, act):
        top = self.chips - 1
        for way, place in ((UP, self.chip), (DOWN, top - self.chip)):
            owner = top - (r - place) if way == UP else r - place
            pl.when((place <= r) & (place < top))(lambda: act(owner, way, place))

    def settle(self, r):
        self.each(r, lambda owner, way, place: pl.when(place > 0)(lambda: self.take(owner, way)))

    def launch(self, r):
        self.each(r, lambda owner, way, place: self.send(owner, way))

    def left(self, r):
        def wait(owner, way, place):
            for copy in self.copies(owner, way):
                copy.wait_send()

        self.each(r, wait)

    def round(self, r):
        self.settle(r)
        self.launch(r)

    def finish(self):
        top = self.chips - 1
        pl.when(self.chip > 0)(lambda: self.take(self.chip, UP))
        pl.when(self.chip < top)(lambda: self.take(self.chip, DOWN))


class Siblings:
    def __init__(self, parts, theirs, held, send_sem, recv_sem):
        self.here = lax.axis_index("ctx")
        self.core = lax.rem(self.here, 2)
        self.parts, self.theirs, self.held, self.send_sem, self.recv_sem = parts, theirs, held, send_sem, recv_sem

    def copies(self):
        return [
            pltpu.make_async_remote_copy(
                part.at[:, 1 - self.core], theirs, self.send_sem.at[n], self.recv_sem.at[n],
                device_id={"ctx": self.here + 1 - 2 * self.core}, device_id_type=MESH,
            )
            for n, (part, theirs) in enumerate(zip(self.parts, self.theirs))
        ]

    def start(self):
        for copy in self.copies():
            copy.start()

    def add(self):
        for copy in self.copies():
            copy.wait_recv()
        for part, theirs, held in zip(self.parts, self.theirs, self.held):

            def one(chip, carry, part=part, theirs=theirs, held=held):
                held[chip] = (part[chip, self.core].astype(F32) + theirs[chip].astype(F32)).astype(BF16)
                return carry

            lax.fori_loop(0, part.shape[0], one, 0)

    def left(self):
        for copy in self.copies():
            copy.wait_send()


def partner(me, i, size):
    total, bit = 0, 1
    while bit < size:
        total = total + lax.rem(me // bit + i // bit, 2) * bit
        bit *= 2
    return total


def chips_within(span_pieces, pieces):
    return min(pieces // 2 - 1, (span_pieces + 1) // 2)


def greet(devices, barrier):
    total = 0
    for place, there in devices:
        pl.when(there)(
            lambda place=place: pl.semaphore_signal(barrier, inc=1, device_id=place, device_id_type=MESH)
        )
        total = total + jnp.asarray(there, jnp.int32)
    return total


def line_neighbours(pieces):
    here = lax.axis_index("ctx")
    chip, core = here // 2, lax.rem(here, 2)
    return [
        ({"ctx": here + 2}, chip < pieces // 2 - 1),
        ({"ctx": here - 2}, chip > 0),
        ({"ctx": here + 1 - 2 * core}, here >= 0),
    ]


def start_kernel(
    size, pieces, x_ref, mix_ref, gate_ref, tail_ref, wg_ref, wu_ref, xfull_ref, halo_ref, full_ref, stage_ref,
    sides, local_sem, seq_send, seq_recv, line_send, line_recv, halo_sem,
):
    me, here = lax.axis_index("seq"), lax.axis_index("ctx")
    count = x_ref.shape[0]
    core = lax.rem(here, 2)
    inner = wg_ref.shape[1] // size
    gate_at = mix_ref.shape[1] // size
    tail_at = gate_at + gate_ref.shape[1] // size
    barrier = pltpu.get_barrier_semaphore()
    peers = [({"seq": partner(me, i, size)}, here >= 0) for i in range(1, size)]
    side = [({"ctx": here + 1}, (core == 1) & (here < pieces - 1)), ({"ctx": here - 1}, (core == 0) & (here > 0))]
    total = greet(peers + line_neighbours(pieces) + side, barrier)
    pl.semaphore_wait(barrier, total)

    def rows(q):
        return pl.ds(pl.multiple_of(q * count, count), count)

    def cols(q, width):
        return pl.ds(pl.multiple_of(q * width, HEAD), width)

    def ends(n, q):
        return [
            (mix_ref.at[:, cols(q, gate_at)], full_ref.at[me, here, :, :gate_at]),
            (gate_ref.at[:, cols(q, tail_at - gate_at)], full_ref.at[me, here, :, gate_at:tail_at]),
            (tail_ref, full_ref.at[me, here, :, tail_at:]),
            (x_ref, xfull_ref.at[rows(me)]),
            (sides.at[q], stage_ref.at[me]),
        ][n]

    def exchange(n, i):
        q = partner(me, i, size)
        source, target = ends(n, q)
        return pltpu.make_async_remote_copy(
            source, target, seq_send.at[n, i - 1], seq_recv.at[n, i - 1], device_id={"seq": q}, device_id_type=MESH
        )

    def own(n):
        return pltpu.make_async_copy(*ends(n, me), local_sem.at[n])

    def begin(n):
        own(n).start()
        for i in range(1, size):
            exchange(n, i).start()

    def end(n):
        own(n).wait()
        for i in range(1, size):
            exchange(n, i).wait_recv()

    for n in range(3):
        begin(n)
    sides[...] = jnp.zeros_like(sides)
    for q in range(size):
        sides[q, 0, :, :inner] = wg_ref[:, q * inner : (q + 1) * inner]
        sides[q, 1, :, :inner] = wu_ref[:, q * inner : (q + 1) * inner]
    line = Line(
        pieces, [lambda c, i=i: full_ref.at[partner(me, i, size), c] for i in range(size)], line_send, line_recv
    )
    for n in range(3):
        own(n).wait()
    line.own(0)
    for i in range(1, size):
        for n in range(3):
            exchange(n, i).wait_recv()
        line.own(i)
    begin(3)
    begin(4)
    last = xfull_ref.at[pl.ds(size * count - HALO, HALO)]
    passing = pltpu.make_async_remote_copy(
        last, halo_ref, halo_sem.at[0], halo_sem.at[1], device_id={"ctx": here + 1}, device_id_type=MESH
    )
    hops = pieces // 2 - 1
    for distance in range(1, hops):
        line.hop(distance)
    end(3)
    pl.when(here < pieces - 1)(passing.start)

    @pl.when(here == 0)
    def _():
        filling = pltpu.make_async_copy(last, halo_ref, local_sem.at[5])
        filling.start()
        filling.wait()

    line.hop(hops)
    line.finish()
    end(4)
    pl.when(here > 0)(passing.wait_recv)
    pl.when(here < pieces - 1)(passing.wait_send)
    for n in range(5):
        for i in range(1, size):
            exchange(n, i).wait_send()


def start_gather(size, pieces, x, mix, gate, tail, w_gate, w_up):
    anywhere = pl.BlockSpec(memory_space=pl.ANY)
    vmem = pl.BlockSpec(memory_space=pltpu.VMEM)
    out = lambda *dims: jax.ShapeDtypeStruct(dims, BF16)
    dma = pltpu.SemaphoreType.DMA
    held, padded = w_gate.shape[0], lanes_for(w_gate.shape[1] // size)
    width = (mix.shape[1] + gate.shape[1]) // size + tail.shape[1]
    return pl.pallas_call(
        functools.partial(start_kernel, size, pieces),
        in_specs=[anywhere] * 4 + [vmem] * 2,
        out_specs=[anywhere] * 4,
        out_shape=[
            out(x.shape[0] * size, D), out(HALO, D), out(size, pieces, held, width), out(size, 2, held, padded),
        ],
        scratch_shapes=[
            pltpu.VMEM((size, 2, held, padded), BF16),
            dma((6,)), dma((5, size - 1)), dma((5, size - 1)), dma((size, 3, pieces)), dma((size, pieces)), dma((2,)),
        ],
        compiler_params=pltpu.CompilerParams(
            vmem_limit_bytes=VMEM_LIMIT, collective_id=2, has_side_effects=True
        ),
        name="start_gather",
    )(x, mix, gate, tail, w_gate, w_up)


def exact(a, b, ca=1, cb=0):
    return lax.dot_general(
        a, b, (((ca,), (cb,)), ((), ())), precision=lax.Precision.HIGHEST, preferred_element_type=F32
    )


def tap_lanes(channels, tap, at):
    lanes = iota((channels, HEAD), 1)
    return (lanes == at + CONV * (iota((channels, HEAD), 0) % (WIDE // HEAD)) + tap).astype(BF16)


def channel_rows(rows, channels):
    return iota((rows, channels), 1) // (WIDE // HEAD) == iota((rows, channels), 0)


def front_body(
    heads, norm_at, rates_ref, x_ref, halo_ref, w_ref, marks_ref,
    proj_ref, normed_ref, gate_ref, tok_ref, slope_ref, col_ref, row_ref, taps_ref, norms_ref,
):
    me = lax.axis_index("seq")
    channels = heads * WIDE
    tail_at = channels + heads * HEAD
    rows = x_ref.shape[0]
    own_rows = D * heads // HEADS

    def dot(a, b, ca=1, cb=0):
        return lax.dot_general(a, b, (((ca,), (cb,)), ((), ())), preferred_element_type=F32)

    pick = (iota((8, HEAD), 1) == norm_at + iota((8, HEAD), 0)).astype(BF16)
    norms_ref[...] = dot(pick, w_ref[:, tail_at:], 1, 1)

    def normal(values):
        values = values.astype(F32)
        scale = lax.rsqrt(jnp.mean(values * values, axis=1, keepdims=True) + NORM_EPS)
        return (values * scale * norms_ref[0:1, :]).astype(BF16)

    early = normal(halo_ref[...])
    normed_ref[...] = normal(x_ref[...])
    proj_ref[:HALO] = dot(early, w_ref[:, :channels]).astype(BF16)
    proj_ref[HALO:] = dot(normed_ref[...], w_ref[:, :channels]).astype(BF16)
    gate_ref[...] = dot(normed_ref[...], w_ref[:, channels:tail_at])
    tail = w_ref[pl.ds(pl.multiple_of(me * own_rows, own_rows), own_rows), tail_at:]
    taps_ref[...] = jnp.zeros_like(taps_ref)
    mine = channel_rows(own_rows, channels)
    for lag in range(CONV):
        spread = dot(tail, tap_lanes(channels, CONV - 1 - lag, norm_at + 3), 1, 1)
        taps_ref[lag : lag + 1] = jnp.sum(jnp.where(mine, spread, 0.0), axis=0, keepdims=True)

    raw = dot(normed_ref[...], w_ref[:, tail_at:]).astype(BF16).astype(F32)
    raw = pltpu.roll(raw, lax.rem(HEAD - me * lane_of(heads, 0), HEAD), 1)
    lane = iota((1, HEAD), 1)
    rate, lift = jnp.zeros((1, HEAD), F32), jnp.zeros((1, HEAD), F32)
    for h in range(heads):
        here = lane == lane_of(h, NH)
        rate = jnp.where(here, -jnp.exp(jnp.zeros((1, HEAD), F32) + rates_ref[0, me * heads + h]), rate)
        lift = jnp.where(here, rates_ref[1, me * heads + h], lift)
    is_log = (lane % (NH + 1) == NH) & (lane < lane_of(heads, 0))
    lifted = raw + lift
    sig = jax.nn.sigmoid(lifted)
    logs = rate * (jnp.maximum(lifted, 0.0) + jnp.log1p(jnp.exp(-jnp.abs(lifted))))
    slope_ref[...] = jnp.where(is_log, rate * sig, sig * (1.0 - sig)) * (lane < HEAD // 2) + pltpu.roll(
        jnp.where(is_log, logs, 0.0), HEAD // 2, 1
    )
    place = (iota((8, HEAD), 1) == LINK + iota((8, HEAD), 0)) & (iota((8, HEAD), 0) < CONV - 1)
    links = dot(marks_ref[...].astype(BF16), place.astype(BF16), 0, 0)
    open_ = column(links, LINK)
    summed = jnp.where(is_log, logs * open_, jnp.where(lane == DOC, 1.0 - open_, 0.0))
    lower = (iota((BLOCK_LEN, BLOCK_LEN), 0) >= iota((BLOCK_LEN, BLOCK_LEN), 1)).astype(F32)
    spread = (iota((ROWS, BLOCK_LEN), 0) // NH == iota((ROWS, BLOCK_LEN), 1)).astype(F32)
    step = iota((ROWS, HEAD), 0) % NH
    for b in range(rows // BLOCK_LEN):
        span = slice(b * BLOCK_LEN, (b + 1) * BLOCK_LEN)
        sums = exact(lower, summed[span])
        tok = jnp.where(is_log | (lane == DOC), sums, jnp.where(lane < DOC, sig[span], links[span]))
        tok_ref[span] = tok
        wide = exact(spread, tok)
        first = wide
        for j in range(1, NH):
            first = jnp.where(step == j, pltpu.roll(wide, HEAD - j, 1), first)
        col = jnp.where(lane % (NH + 1) == 0, jnp.where(lane < lane_of(heads, 0), first, wide), wide)
        col_ref[b * ROWS : (b + 1) * ROWS] = col
        row_ref[b * 8 : (b + 1) * 8] = col.T[:8]


def fwd_kernel(
    heads, pieces, steps, per, span_pieces, norm_at,
    rates_ref, x_ref, halo_ref, full_ref, marks_ref, stage_ref, wo_ref,
    proj_ref, normed_ref, gate_ref, tok_ref, slope_ref, col_ref, row_ref, taps_ref, norms_ref,
    oloc_ref, carr_ref, sin_ref, mapsout_ref, conv_ref, q_ref, k_ref, v_ref, t_ref, kk_ref, at_ref, uw_ref, pl_ref,
    wgfull_ref, wufull_ref, wofull_ref,
    state, weave, maps, wgs, wus, wos, local_sem, line_send, line_recv, map_send, map_recv,
):
    step = pl.program_id(0)
    here = lax.axis_index("ctx")
    weights = Line(
        pieces, [lambda c: wgs.at[:, c], lambda c: wus.at[:, c], lambda c: wos.at[c]], line_send, line_recv
    )
    eye = (iota((HEAD, HEAD), 0) == iota((HEAD, HEAD), 1)).astype(F32)

    @pl.when(step == 0)
    def _():
        owned = [
            pltpu.make_async_copy(source, target, local_sem.at[n])
            for n, (source, target) in enumerate(
                [(stage_ref.at[:, 0], wgs.at[:, here]), (stage_ref.at[:, 1], wus.at[:, here]), (wo_ref, wos.at[here])]
            )
        ]
        for copy in owned:
            copy.start()
        barrier = pltpu.get_barrier_semaphore()
        pl.semaphore_wait(barrier, greet(line_neighbours(pieces), barrier))
        for copy in owned:
            copy.wait()
        weights.own()
        front_body(
            heads, norm_at, rates_ref, x_ref, halo_ref, full_ref, marks_ref,
            proj_ref, normed_ref, gate_ref, tok_ref, slope_ref, col_ref, row_ref, taps_ref, norms_ref,
        )
        for h in range(heads):
            state[h, :, :HEAD] = eye
            state[h, :, HEAD:] = jnp.zeros((HEAD, HEAD), F32)

    hops = [(d * 2 * steps) // (pieces // 2) - 1 for d in range(1, pieces // 2)]
    for distance, at in enumerate(hops, 1):
        if at < steps:
            pl.when(step == at)(lambda distance=distance: weights.hop(distance))

    items = [(j, h) for j in range(per) for h in range(heads)]
    cols = lambda h: slice(h * WIDE, (h + 1) * WIDE)
    span = lambda j, length=BLOCK_LEN: slice(j * length, (j + 1) * length)
    tables = []
    for j in range(per):
        block = step * per + j
        tables.append(
            (
                row_ref[pl.ds(pl.multiple_of(block * 8, 8), 8), :],
                col_ref[pl.ds(pl.multiple_of(block * ROWS, ROWS), ROWS), :],
                tok_ref[pl.ds(pl.multiple_of(block * BLOCK_LEN, BLOCK_LEN), BLOCK_LEN), :],
            )
        )
    acts = []
    for j, h in items:
        base = pl.multiple_of((step * per + j) * BLOCK_LEN, BLOCK_LEN)
        ext = proj_ref[pl.ds(base, BLOCK_LEN + HALO), cols(h)].astype(F32)
        conv = ext[HALO:] * taps_ref[0:1, cols(h)]
        for lag in range(1, CONV):
            conv = conv + column(tables[j][2], LINK + lag - 1) * lag_rows(ext, lag) * taps_ref[lag : lag + 1, cols(h)]
        conv_ref[span(j), cols(h)] = conv
        acts.append(conv * jax.nn.sigmoid(conv))
    queries, keys, values = [], [], []
    for n, act in enumerate(acts):
        unit = []
        for part in range(1 + NH):
            piece = act[:, part * HEAD : (part + 1) * HEAD]
            unit.append(piece * lax.rsqrt(jnp.sum(piece * piece, axis=1, keepdims=True) + NORM_EPS))
        queries.append(unit[0] * (1.0 / math.sqrt(HEAD)))
        for j in range(NH):
            weave[2 * n, pl.ds(j, BLOCK_LEN, NH), :] = unit[1 + j]
            weave[2 * n + 1, pl.ds(j, BLOCK_LEN, NH), :] = act[:, (1 + NH + j) * HEAD : (2 + NH + j) * HEAD]
    for n in range(len(items)):
        keys.append(weave[2 * n])
        values.append(weave[2 * n + 1])
    factors = [decays(*tables[j], h) for j, h in items]
    grams = [mm(jnp.concatenate([q, k], axis=0), k, 1, 1) for q, k in zip(queries, keys)]
    kks = [f[1] * g[BLOCK_LEN:] for f, g in zip(factors, grams)]
    attns = [f[2] * g[:BLOCK_LEN] for f, g in zip(factors, grams)]
    invs = unit_lower_inverses([f[0] * kk for f, kk in zip(factors, kks)])
    uws = [
        mm(inv, jnp.concatenate([f[0] * v, (f[0] * f[3]) * k], axis=1))
        for inv, f, v, k in zip(invs, factors, values, keys)
    ]
    auws = [mm(attn, uw) for attn, uw in zip(attns, uws)]
    nms = [mm(f[5] * k, uw, 0, 0) for f, k, uw in zip(factors, keys, uws)]
    for n, (j, h) in enumerate(items):
        before = state[h]
        f = factors[n]
        both = mm(
            jnp.concatenate([f[4] * queries[n] - auws[n][:, HEAD:], f[6] * eye - nms[n][:, HEAD:]], axis=0), before
        )
        hc = slice(h * HEAD, (h + 1) * HEAD)
        carr_ref[span(j), hc] = both[:BLOCK_LEN, :HEAD]
        oloc_ref[span(j), hc] = both[:BLOCK_LEN, HEAD:] + auws[n][:, :HEAD]
        state[h, :, :HEAD] = both[BLOCK_LEN:, :HEAD]
        state[h, :, HEAD:] = both[BLOCK_LEN:, HEAD:] + nms[n][:, :HEAD]
        q_ref[j, h] = queries[n]
        k_ref[j, h] = keys[n]
        v_ref[j, h] = values[n]
        t_ref[j, h] = invs[n]
        kk_ref[j, h] = kks[n]
        at_ref[j, h] = attns[n]
        uw_ref[j, h] = uws[n]
        pl_ref[j, h] = before

    @pl.when(step == steps - 1)
    def _():
        maps[here] = state[...].astype(BF16)
        line = Line(pieces, [lambda c: maps.at[c]], map_send, map_recv, reach=chips_within(span_pieces, pieces))
        line.own()
        for distance in range(1, line.reach + 1):
            line.hop(distance)
        line.finish()
        for distance in range(1, pieces // 2):
            if hops[distance - 1] >= steps:
                weights.hop(distance)

        def hop(k, states):
            return tuple(
                mm(maps[k, h, :, :HEAD], states[h]) + maps[k, h, :, HEAD:].astype(F32) for h in range(heads)
            )

        states = lax.fori_loop(jnp.maximum(here - span_pieces, 0), here, hop, tuple(jnp.zeros((HEAD, HEAD), F32) for _ in range(heads)))
        for h in range(heads):
            sin_ref[h] = states[h]

        def keep(k, carry):
            mapsout_ref[k] = maps[k, :, :, :HEAD]
            return carry

        lax.fori_loop(
            jnp.maximum(here - span_pieces, 0), jnp.minimum(here + span_pieces + 1, pieces), keep, 0
        )
        weights.finish()
        given = [
            pltpu.make_async_copy(source, target, local_sem.at[n])
            for n, (source, target) in enumerate([(wgs, wgfull_ref), (wus, wufull_ref), (wos, wofull_ref)])
        ]
        for copy in given:
            copy.start()
        for copy in given:
            copy.wait()


def recurrence_forward(heads, pieces, span_pieces, norm_at, rates, x_full, halo, weights, marks, stage, w_out):
    rows = x_full.shape[0]
    blocks = rows // BLOCK_LEN
    per = 2
    size = stage.shape[0]
    whole = lambda *dims: pl.BlockSpec(dims, lambda i: (0,) * len(dims))
    by_block = lambda *dims: pl.BlockSpec((per,) + dims, lambda i: (i,) + (0,) * len(dims))
    token = lambda cols: pl.BlockSpec((per * BLOCK_LEN, cols), lambda i: (i, 0))
    shape = lambda *dims: jax.ShapeDtypeStruct(dims, F32)
    low_shape = lambda *dims: jax.ShapeDtypeStruct(dims, BF16)
    hbm = pl.BlockSpec(memory_space=pltpu.HBM)
    vmem = pl.BlockSpec(memory_space=pltpu.VMEM)
    square = (heads, ROWS, HEAD)
    dma = pltpu.SemaphoreType.DMA
    side = (size, pieces, *stage.shape[2:])
    front = [
        low_shape(rows + HALO, heads * WIDE), low_shape(rows, D), shape(rows, heads * HEAD), shape(rows, HEAD),
        shape(rows, HEAD), shape(blocks * ROWS, HEAD), shape(blocks * 8, ROWS), shape(8, heads * WIDE), shape(8, D),
    ]
    return pl.pallas_call(
        functools.partial(fwd_kernel, heads, pieces, blocks // per, per, span_pieces, norm_at),
        grid=(blocks // per,),
        in_specs=[pl.BlockSpec(memory_space=pltpu.SMEM)] + [vmem] * 4 + [hbm] * 2,
        out_specs=[whole(*f.shape) for f in front] + [
            token(heads * HEAD), token(heads * HEAD), whole(heads, HEAD, HEAD), whole(pieces, heads, HEAD, HEAD),
            token(heads * WIDE),
            by_block(heads, BLOCK_LEN, HEAD), by_block(*square), by_block(*square), by_block(*square),
            by_block(*square), by_block(heads, BLOCK_LEN, ROWS), by_block(heads, ROWS, 2 * HEAD),
            by_block(heads, HEAD, 2 * HEAD), hbm, hbm, hbm,
        ],
        out_shape=front + [
            shape(rows, heads * HEAD), shape(rows, heads * HEAD), shape(heads, HEAD, HEAD),
            low_shape(pieces, heads, HEAD, HEAD), shape(rows, heads * WIDE),
            shape(blocks, heads, BLOCK_LEN, HEAD), shape(blocks, *square), shape(blocks, *square), shape(blocks, *square),
            shape(blocks, *square), shape(blocks, heads, BLOCK_LEN, ROWS), shape(blocks, heads, ROWS, 2 * HEAD),
            shape(blocks, heads, HEAD, 2 * HEAD),
            low_shape(*side), low_shape(*side), low_shape(pieces, *w_out.shape),
        ],
        scratch_shapes=[
            pltpu.VMEM((heads, HEAD, 2 * HEAD), F32), pltpu.VMEM((2 * heads * per, ROWS, HEAD), F32),
            pltpu.VMEM((pieces, heads, HEAD, 2 * HEAD), BF16),
            pltpu.VMEM(side, BF16), pltpu.VMEM(side, BF16), pltpu.VMEM((pieces, *w_out.shape), BF16),
            dma((3,)), dma((3, 3, pieces)), dma((3, pieces)), dma((1, 3, pieces)), dma((1, pieces)),
        ],
        compiler_params=pltpu.CompilerParams(
            vmem_limit_bytes=VMEM_LIMIT, collective_id=3, has_side_effects=True
        ),
        name="recurrence_forward",
    )(rates, x_full, halo, weights, marks, stage, w_out)


def middle_kernel(
    size, heads, token_total,
    x_ref, teach_ref, mask_ref, norms_ref, gain_ref, *streams_and_rest,
):
    streams, rest = streams_and_rest[:8], streams_and_rest[8:]
    middle_body(size, heads, token_total, x_ref, teach_ref, mask_ref, norms_ref, gain_ref, streams, *rest)


def middle_body(
    size, heads, token_total, x_ref, teach_ref, mask_ref, norms_ref, gain_ref, streams,
    final_ref, gmid_ref, ghead_ref, ggate_ref, cot_ref, ggain_ref, gnorm_ref, loss_ref,
    wheld, theld, outg_ref,
    oloc_ref, carr_ref, gate_ref, sin_ref, wout_ref, wg_ref, wu_ref, wd_ref, load_sem, heads_ref, mixed_ref,
    line_send, line_recv, wds, wide_ref, tall_ref, wtheirs, ttheirs, wcame, tcame,
    pair_send, pair_recv, sum_send, sum_recv,
    second, branch, low, sent, got, own, mid, gfin, gates, ups, hidden, ggates, gups, send_sem, recv_sem,
):
    me = lax.axis_index("seq")
    count = x_ref.shape[0]
    loads = [
        pltpu.make_async_copy(source, target, load_sem.at[n])
        for n, (source, target) in enumerate(
            zip(streams, (oloc_ref, carr_ref, gate_ref, sin_ref, wout_ref, wg_ref, wu_ref, wds.at[lax.axis_index("ctx")]))
        )
    ]
    for load in loads:
        load.start()
    pieces = 2 * wide_ref.shape[0]
    barrier = pltpu.get_barrier_semaphore()
    peers = [({"seq": partner(me, i, size)}, me >= 0) for i in range(1, size)]
    pl.semaphore_wait(barrier, greet(peers + line_neighbours(pieces), barrier))
    loads[7].wait()
    line = Line(pieces, [lambda c: wds.at[c]], line_send, line_recv)
    line.own()
    for load in loads[:5]:
        load.wait()
    norm = norms_ref[1:2, :]
    gain = gain_ref[...].astype(F32)

    def dot(a, b, ca=1, cb=0):
        return lax.dot_general(a, b, (((ca,), (cb,)), ((), ())), preferred_element_type=F32)

    def rows(q):
        return pl.ds(pl.multiple_of(q * count, count), count)

    def part_copy(phase, i):
        return pltpu.make_async_remote_copy(
            sent.at[phase, i - 1], got.at[phase, i - 1], send_sem.at[phase, i - 1], recv_sem.at[phase, i - 1],
            device_id={"seq": partner(me, i, size)}, device_id_type=MESH,
        )

    def block_copy(buffer, phase, i, owner):
        return pltpu.make_async_remote_copy(
            buffer.at[rows(owner)], buffer.at[rows(owner)], send_sem.at[phase, i - 1], recv_sem.at[phase, i - 1],
            device_id={"seq": partner(me, i, size)}, device_id_type=MESH,
        )

    def give_part(phase, i, part):
        @pl.when(i > 0)
        def _():
            sent[phase, i - 1] = part.astype(BF16)
            part_copy(phase, i).start()

        @pl.when(i == 0)
        def _():
            own[...] = part

    def take_parts(phase):
        def add(i, total):
            part_copy(phase, i).wait_recv()
            return total + got[phase, i - 1].astype(F32)

        return lax.fori_loop(1, size, add, own[...])

    relayed = size == 4

    def half_copy(buffer, phase, n, owner):
        part = pl.ds(pl.multiple_of(owner * count + (n - 1) * (count // 2), count // 2), count // 2)
        return pltpu.make_async_remote_copy(
            buffer.at[part], buffer.at[part], send_sem.at[phase, 1 + n], recv_sem.at[phase, 1 + n],
            device_id={"seq": partner(me, 3 - n, size)}, device_id_type=MESH,
        )

    def give_block(buffer, phase, value):
        buffer[rows(me)] = value
        for i in range(1, 3 if relayed else size):
            block_copy(buffer, phase, i, me).start()

    def take_block(buffer, phase, i):
        q = partner(me, i, size)
        if relayed:

            @pl.when(i == 1)
            def _():
                for n in (1, 2):
                    block_copy(buffer, phase, n, partner(me, n, size)).wait_recv()
                    half_copy(buffer, phase, n, partner(me, n, size)).start()

            @pl.when(i == 3)
            def _():
                for n in (1, 2):
                    half_copy(buffer, phase, n, q).wait_recv()

        else:
            pl.when(i > 0)(lambda: block_copy(buffer, phase, i, q).wait_recv())
        return q

    def block_left(buffer, phase):
        for i in range(1, 3 if relayed else size):
            block_copy(buffer, phase, i, me).wait_send()
        if relayed:
            for n in (1, 2):
                half_copy(buffer, phase, n, partner(me, n, size)).wait_send()

    def out_part(k, carry):
        i = size - 1 - k
        q = partner(me, i, size)
        for h in range(heads):
            hc = slice(h * HEAD, (h + 1) * HEAD)
            out = (oloc_ref[rows(q), hc] + mm(carr_ref[rows(q), hc], sin_ref[h])).astype(BF16)
            heads_ref[rows(q), hc] = out
            wide = out.astype(F32)
            gate = gate_ref[rows(q), hc]
            scaled = wide * lax.rsqrt(jnp.mean(wide * wide, axis=1, keepdims=True) + NORM_EPS) * gain
            mixed_ref[rows(q), hc] = (scaled * (gate * jax.nn.sigmoid(gate))).astype(BF16)
        give_part(0, i, dot(mixed_ref[rows(q)], wout_ref[...]))
        return carry

    lax.fori_loop(0, size, out_part, 0)
    hops = pieces // 2 - 1
    for distance in range(1, hops // 2 + 1):
        line.hop(distance)
    middle = x_ref[...].astype(F32) + take_parts(0)
    mid[...] = middle
    inv = lax.rsqrt(jnp.mean(middle * middle, axis=1, keepdims=True) + NORM_EPS)
    give_block(second, 3, (middle * inv * norm).astype(BF16))
    for load in loads[5:7]:
        load.wait()
    deep = wds.shape[1]
    for distance in range(hops // 2 + 1, hops):
        line.hop(distance)

    def take_down():
        line.hop(hops)
        line.finish()
        inner = pieces * deep
        wd_ref[inner:] = jnp.zeros((wd_ref.shape[0] - inner, D), BF16)
        for c in range(pieces):
            wd_ref[c * deep : (c + 1) * deep] = wds[c]

    def feed(i, carry):
        q = take_block(second, 3, i)
        here = second[rows(q)]
        gate = dot(here, wg_ref[...])
        up = dot(here, wu_ref[...])
        gates[rows(q)] = gate
        ups[rows(q)] = up
        hid = (gate * jax.nn.sigmoid(gate) * up).astype(BF16)
        hidden[rows(q)] = hid
        pl.when(i == 0)(take_down)
        give_part(1, i, dot(hid, wd_ref[...]))
        return carry

    lax.fori_loop(0, size, feed, 0)
    final = mid[...] + take_parts(1)
    final_ref[...] = final.astype(BF16)
    error = final - teach_ref[...].astype(F32)
    mask = jnp.broadcast_to(mask_ref[...].astype(F32), (count, count)).T[:, :1]
    weighted = mask * error
    loss_ref[...] = jnp.broadcast_to(
        jnp.sum(jnp.sum(weighted * error, axis=1, keepdims=True), axis=0, keepdims=True), loss_ref.shape
    )
    valid = jnp.maximum(jnp.sum(norms_ref[2:3, :], axis=1, keepdims=True), 1.0)
    grad_final = token_total / valid * weighted
    gfin[...] = grad_final
    give_block(branch, 4, grad_final.astype(BF16))

    def feed_back(i, carry):
        q = take_block(branch, 4, i)
        ghid = dot(branch[rows(q)], wd_ref[...], 1, 1)
        gate = gates[rows(q)]
        sig = jax.nn.sigmoid(gate)
        silu = gate * sig
        ggate = (ghid * ups[rows(q)] * (sig + silu * (1.0 - sig))).astype(BF16)
        gup = (ghid * silu).astype(BF16)
        ggates[rows(q)] = ggate
        gups[rows(q)] = gup
        give_part(2, i, dot(ggate, wg_ref[...], 1, 1) + dot(gup, wu_ref[...], 1, 1))
        return carry

    lax.fori_loop(0, size, feed_back, 0)
    held = D // (size * pieces)
    tall_ref[...] = jnp.zeros_like(tall_ref)
    grad = dot(hidden[...], branch[...], 0, 0)
    for c in range(pieces):
        tall_ref[c // 2, c % 2, :deep] = grad[c * deep : (c + 1) * deep].astype(BF16)
    for n, side in enumerate((ggates, gups)):
        grad = dot(second[...], side[...], 0, 0)
        for c in range(pieces):
            for r in range(size):
                first = (r * pieces + c) * held
                wide_ref[c // 2, c % 2, (n * size + r) * held : (n * size + r + 1) * held] = grad[
                    first : first + held
                ].astype(BF16)
    pair = Siblings([wide_ref, tall_ref], [wtheirs, ttheirs], [wheld, theld], pair_send, pair_recv)
    sums = LineSum(pieces, [wheld, theld], [wcame, tcame], sum_send, sum_recv)
    pair.start()
    pair.add()
    sums.round(0)
    gsecond = take_parts(2)
    middle = mid[...]
    inv = lax.rsqrt(jnp.mean(middle * middle, axis=1, keepdims=True) + NORM_EPS)
    unit = middle * inv
    gnorm_ref[...] = jnp.sum(gsecond * unit, axis=0, keepdims=True)
    down = gsecond * norm
    gmid = gfin[...] + inv * (down - unit * jnp.mean(down * unit, axis=1, keepdims=True))
    gmid_ref[...] = gmid
    give_block(low, 5, gmid.astype(BF16))
    ggain_ref[...] = jnp.zeros_like(ggain_ref)
    cot_ref[...] = jnp.zeros_like(cot_ref)

    def out_back(i, carry):
        q = take_block(low, 5, i)
        gmixed = dot(low[rows(q)], wout_ref[...], 1, 1)
        for h in range(heads):
            hc = slice(h * HEAD, (h + 1) * HEAD)
            x = heads_ref[rows(q), hc].astype(F32)
            gate = gate_ref[rows(q), hc]
            grad = gmixed[:, hc]
            inv = lax.rsqrt(jnp.mean(x * x, axis=1, keepdims=True) + NORM_EPS)
            sig = jax.nn.sigmoid(gate)
            silu = gate * sig
            unit = x * inv
            ggate_ref[rows(q), hc] = (grad * unit * gain * (sig + silu * (1.0 - sig))).astype(BF16)
            weighted = grad * silu
            ggain_ref[...] += jnp.sum(weighted * unit, axis=0, keepdims=True)
            down = weighted * gain
            ghead = (inv * (down - unit * jnp.mean(down * unit, axis=1, keepdims=True))).astype(BF16)
            ghead_ref[rows(q), hc] = ghead
            cot_ref[h] += mm(carr_ref[rows(q), hc], ghead, 0, 0)
        return carry

    out_back(0, 0)
    early = max(1, hops - 1)
    for r in range(1, early):
        sums.round(r)
    lax.fori_loop(1, size, out_back, 0)
    grad = dot(mixed_ref[...], low[...], 0, 0)
    for c in range(pieces):
        outg_ref[c // 2, c % 2] = grad[c * held : (c + 1) * held].astype(BF16)
    sums.settle(early)
    pair.left()
    for r in range(early):
        sums.left(r)

    for i in range(1, size):
        for phase in range(3):
            part_copy(phase, i).wait_send()
    for buffer, phase in ((second, 3), (branch, 4), (low, 5)):
        block_left(buffer, phase)


def middle_part(
    size, heads, pieces, token_total, x, teacher, mask, norms, gain, oloc, carr, gate_out, state_in, wout, wg, wu, wd
):
    count = x.shape[0]
    rows = count * size
    inner = wg.shape[1]
    held, deep = D // (size * pieces), wd.shape[0]
    chips = pieces // 2
    wide, tall = (2 * size * held, inner), (-(-deep // 16) * 16, D)
    vmem = pl.BlockSpec(memory_space=pltpu.VMEM)
    out = lambda dims, kind: jax.ShapeDtypeStruct(dims, kind)
    low = lambda *dims: pltpu.VMEM(dims, BF16)
    high = lambda *dims: pltpu.VMEM(dims, F32)
    dma = pltpu.SemaphoreType.DMA
    return pl.pallas_call(
        functools.partial(middle_kernel, size, heads, float(token_total)),
        in_specs=[vmem] * 5 + [pl.BlockSpec(memory_space=pltpu.HBM)] * 8,
        out_specs=[vmem] * 11,
        out_shape=[
            out((count, D), BF16), out((count, D), F32),
            out((rows, heads * HEAD), BF16), out((rows, heads * HEAD), BF16), out((heads, HEAD, HEAD), F32),
            out((1, HEAD), F32), out((1, D), F32), out((1, HEAD), F32),
            out((chips, 2 * size * held, inner), BF16), out((chips, -(-deep // 16) * 16, D), BF16),
            out((chips, 2, held, D), BF16),
        ],
        scratch_shapes=[
            high(rows, heads * HEAD), high(rows, heads * HEAD), high(rows, heads * HEAD), high(heads, HEAD, HEAD),
            low(*wout.shape), low(*wg.shape), low(*wu.shape), low(inner, D), dma((8,)),
            low(rows, heads * HEAD), low(rows, heads * HEAD), dma((1, 3, pieces)), dma((1, pieces)), low(pieces, *wd.shape),
            low(chips, 2, *wide), low(chips, 2, *tall), low(chips, *wide), low(chips, *tall), low(2, chips, *wide),
            low(2, chips, *tall), dma((2,)), dma((2,)), dma((2, chips)), dma((2, 2, chips)),
            low(rows, D), low(rows, D), low(rows, D), low(3, size - 1, count, D), low(3, size - 1, count, D),
            high(count, D), high(count, D), high(count, D), high(rows, inner), high(rows, inner), low(rows, inner),
            low(rows, inner), low(rows, inner), dma((6, size)), dma((6, size)),
        ],
        compiler_params=pltpu.CompilerParams(
            vmem_limit_bytes=VMEM_LIMIT, collective_id=1, has_side_effects=True
        ),
        name="middle_part",
    )(x, teacher, mask, norms, gain, oloc, carr, gate_out, state_in, wout, wg, wu, wd)


def bwd_kernel(
    heads, pieces, steps, per, begun, span_pieces, maps_ref, cot_ref, sin_ref, proj_ref, w_ref, rowp_ref, colp_ref, tokp_ref, slope_ref,
    go_ref, conv_ref, q_ref, k_ref, v_ref, t_ref, kk_ref, at_ref, uw_ref, pl_ref, wide_ref, tall_ref, outg_ref, normed_ref, ggate_ref,
    gproj_ref, fix_ref, gw_ref, gscal_ref, gsum_ref, widesum_ref, tallsum_ref, outsum_ref, gatesum_ref,
    dstate, weave, rim, last, cots, rim_in, wheld, theld, wcame, tcame,
    gateg, otheirs, gtheirs, oheld, gheld, ocame, gcame,
    cot_send, cot_recv, pair_send, pair_recv, early_send, early_recv, line_send, line_recv, rim_sem,
):
    step = pl.program_id(0)
    block = steps - 1 - step
    here = lax.axis_index("ctx")
    core = lax.rem(here, 2)
    early = LineSum(pieces, [wheld, theld], [wcame, tcame], early_send, early_recv)
    pair = Siblings([outg_ref, gateg], [otheirs, gtheirs], [oheld, gheld], pair_send, pair_recv)
    line = LineSum(pieces, [oheld, gheld], [ocame, gcame], line_send, line_recv)
    rounds = pieces // 2 - 1
    when_round = [min(steps - 1, 1 + (r * steps) // rounds) for r in range(rounds)]

    @pl.when(step == 0)
    def _():
        barrier = pltpu.get_barrier_semaphore()
        side = [({"ctx": here + 1}, (core == 1) & (here < pieces - 1)), ({"ctx": here - 1}, (core == 0) & (here > 0))]
        pl.semaphore_wait(barrier, greet(line_neighbours(pieces) + side, barrier))
        cots[here] = cot_ref[...].astype(BF16)
        spread = Line(
            pieces, [lambda c: cots.at[c]], cot_send, cot_recv, up=False, reach=chips_within(span_pieces, pieces)
        )
        spread.own()
        wheld[...] = wide_ref[...]
        theld[...] = tall_ref[...]
        grad = lax.dot_general(
            normed_ref[...], ggate_ref[...], (((0,), (0,)), ((), ())), preferred_element_type=F32
        )
        held, size = gateg.shape[3], gateg.shape[2]
        for c in range(pieces):
            for r in range(size):
                row = (r * pieces + c) * held
                gateg[c // 2, c % 2, r] = grad[row : row + held].astype(BF16)
        for distance in range(1, spread.reach + 1):
            spread.hop(distance)
        spread.finish()
        early.launch(begun)
        pair.start()

        farthest = jnp.minimum(here + span_pieces, pieces - 1)

        def hop(i, states):
            k = farthest - i
            return tuple(
                mm(maps_ref[k, h], states[h], 0, 0) + cots[k, h].astype(F32) for h in range(heads)
            )

        found = lax.fori_loop(
            0, farthest - here, hop, tuple(jnp.zeros((HEAD, HEAD), F32) for _ in range(heads))
        )
        for h in range(heads):
            dstate[h] = found[h]
        rim[...] = jnp.zeros_like(rim)
        gw_ref[...] = jnp.zeros_like(gw_ref)
        gsum_ref[...] = jnp.zeros_like(gsum_ref)

    for r in range(begun + 1, rounds):
        at = min(steps - 1, 1 + ((r - begun) * (steps - 1)) // (rounds - begun))
        pl.when(step == at)(lambda r=r: early.round(r))
    pl.when(step == 1)(pair.add)
    for r in range(rounds):
        pl.when(step == when_round[r])(lambda r=r: line.round(r))

    last_row = iota((ROWS, 1), 0) == ROWS - 1
    diagonal = iota((ROWS, ROWS), 0) == iota((ROWS, ROWS), 1)
    first_lane = lax.axis_index("seq") * lane_of(heads, 0)
    gscals = [[] for _ in range(per)]
    dnexts = {(per - 1, h): dstate[h] for h in range(heads)}
    rims = {(per - 1, h): rim[:, h * WIDE : (h + 1) * WIDE] for h in range(heads)}

    def item(j, h):
        n = j * heads + h
        span = slice(j * BLOCK_LEN, (j + 1) * BLOCK_LEN)
        rowp, colp = rowp_ref[j * 8 : (j + 1) * 8], colp_ref[j * ROWS : (j + 1) * ROWS]
        tokp, slope = tokp_ref[span], slope_ref[span]
        cols = slice(h * WIDE, (h + 1) * WIDE)
        hc = slice(h * HEAD, (h + 1) * HEAD)
        beta, decay, qdecay, carry, qcarry, dlast, clast = decays(rowp, colp, tokp, h)
        go = go_ref[span, hc]
        query, keys, values = q_ref[j, h], k_ref[j, h], v_ref[j, h]
        inv, kk, attn, uw = t_ref[j, h], kk_ref[j, h], at_ref[j, h], uw_ref[j, h]
        yield
        state = mm(pl_ref[j, h, :, :HEAD], sin_ref[h]) + pl_ref[j, h, :, HEAD:]
        yield
        both = mm(jnp.concatenate([keys, uw[:, HEAD:]], axis=0), state)
        ks = both[:ROWS]
        upd = uw[:, :HEAD] - both[ROWS:]
        dlocal = mm(attn, go, 0, 0)
        while (j, h) not in dnexts:
            yield
        dnext = dnexts[j, h]
        yield
        dupd = dlocal + dlast * mm(keys, dnext)
        yield
        dx = mm(inv, dupd, 0, 0)
        yield
        dv = beta * dx
        dy = -(carry * dv)
        go32 = go.astype(F32)
        dnexts[j - 1, h] = clast * dnext + mm(
            jnp.concatenate([qcarry * query, keys], axis=0), jnp.concatenate([go32, dy], axis=0), 0, 0
        )
        yield
        outer = mm(jnp.concatenate([go32, dx], axis=0), upd, 1, 1)
        dattn, da = outer[:BLOCK_LEN], -outer[BLOCK_LEN:]
        yield
        dkd = mm(upd, dnext, 1, 1)
        right = mm(jnp.concatenate([go32, dy], axis=0), state, 1, 1)
        gos = right[:BLOCK_LEN]
        yield
        e = beta * da * decay
        f = dattn * qdecay
        ef = jnp.concatenate([f, e], axis=0)
        efk = mm(ef, keys)
        dq = qcarry * gos + efk[:BLOCK_LEN]
        yield
        dk = (
            right[BLOCK_LEN:]
            + dlast * dkd
            + efk[BLOCK_LEN:]
            + mm(ef, jnp.concatenate([query, keys], axis=0), 0, 0)
        )
        weave[3 * n] = dk
        weave[3 * n + 1] = dv
        yield
        dakk = da * kk
        z1 = beta * dakk
        z2 = dattn * attn
        kept = dlast * (dkd * keys)
        below = jnp.sum(z1, axis=0, keepdims=True) + jnp.sum(z2, axis=0, keepdims=True)
        dbeta = jnp.sum(dx * (values - carry * ks) + dakk, axis=1, keepdims=True)
        tail = jnp.sum(
            jnp.sum(kept, axis=0, keepdims=True) + clast * jnp.sum(state * dnext, axis=0, keepdims=True),
            axis=1, keepdims=True,
        )
        dgrow = jnp.sum(z1 + dy * ks - kept - jnp.where(diagonal, below, 0.0), axis=1, keepdims=True)
        dgrow = dgrow + jnp.where(last_row, tail, 0.0)
        lane = iota((ROWS, HEAD), 1)
        weave[3 * n + 2] = jnp.where(lane == 0, dbeta, dgrow)
        yield
        by_step = [weave[3 * n + 2, pl.ds(i, BLOCK_LEN, NH), :] for i in range(NH)]
        dg = sum(x[:, 1:2] for x in by_step) + jnp.sum(z2 + qcarry * (query * gos), axis=1, keepdims=True)
        after = (iota((BLOCK_LEN, BLOCK_LEN), 0) <= iota((BLOCK_LEN, BLOCK_LEN), 1)).astype(BF16)
        dlog = column(tokp, LINK) * mm(after, jnp.broadcast_to(dg, (BLOCK_LEN, HEAD)))[:, :1]
        dscal = [by_step[i][:, 0:1] * column(slope, lane_of(h, i)) for i in range(NH)]
        dscal.append(dlog * column(slope, lane_of(h, NH)))
        lane = iota((BLOCK_LEN, HEAD), 1)
        for i in range(NH + 1):
            gscals[j].append(jnp.where(lane == first_lane + lane_of(h, i), dscal[i], 0.0))
        logs = column(slope, HEAD // 2 + lane_of(h, NH))
        sums = jnp.where(lane == 0, dlog * logs, jnp.where(lane == 1, dscal[NH], 0.0))
        gsum_ref[h : h + 1, :] += jnp.sum(sums, axis=0, keepdims=True)
        yield
        conv = conv_ref[span, cols]
        sig = jax.nn.sigmoid(conv)
        act = conv * sig
        parts = []
        for part in range(1 + NH):
            piece = act[:, part * HEAD : (part + 1) * HEAD]
            scale = lax.rsqrt(jnp.sum(piece * piece, axis=1, keepdims=True) + NORM_EPS)
            if part:
                grad = weave[3 * n, pl.ds(part - 1, BLOCK_LEN, NH), :]
            else:
                grad = dq * (1.0 / math.sqrt(HEAD))
            unit = piece * scale
            parts.append(scale * (grad - unit * jnp.sum(grad * unit, axis=1, keepdims=True)))
        for i in range(NH):
            parts.append(weave[3 * n + 1, pl.ds(i, BLOCK_LEN, NH), :])
        dconv = jnp.concatenate(parts, axis=1) * (sig * (1.0 + conv * (1.0 - sig)))
        yield
        base = pl.multiple_of((block * per + j) * BLOCK_LEN, BLOCK_LEN)
        ext = proj_ref[pl.ds(base, BLOCK_LEN + HALO), cols].astype(F32)
        gw_ref[0:1, cols] += jnp.sum(dconv * ext[HALO:], axis=0, keepdims=True)
        zeros = jnp.zeros((8, WIDE), F32)
        length = BLOCK_LEN + 8
        total = jnp.concatenate([zeros, dconv * w_ref[0:1, cols]], axis=0)
        for lag in range(1, CONV):
            masked = column(tokp, LINK + lag - 1) * dconv
            gw_ref[lag : lag + 1, cols] += jnp.sum(masked * lag_rows(ext, lag), axis=0, keepdims=True)
            total = total + pltpu.roll(
                jnp.concatenate([zeros, masked * w_ref[lag : lag + 1, cols]], axis=0), length - lag, 0
            )
        rims[j - 1, h] = total[:8]
        fixed = total[length - 8 :] + rims[j, h]
        gproj_ref[span, cols] = jnp.concatenate([total[8 : length - 8], fixed], axis=0).astype(BF16)
        if j == per - 1:

            @pl.when(step == 0)
            def _():
                last[:, cols] = fixed

    running = [item(j, h) for j in reversed(range(per)) for h in range(heads)]
    while running:
        running = [one for one in running if next(one, "done") != "done"]
    for h in range(heads):
        dstate[h] = dnexts[-1, h]
        rim[:, h * WIDE : (h + 1) * WIDE] = rims[-1, h]
    for j in range(per):
        gscal_ref[j * BLOCK_LEN : (j + 1) * BLOCK_LEN] = sum(gscals[j]).astype(BF16)

    @pl.when(step == steps - 1)
    def _():
        passing = pltpu.make_async_remote_copy(
            rim, rim_in, rim_sem.at[0], rim_sem.at[1], device_id={"ctx": here - 1}, device_id_type=MESH
        )
        pl.when(here > 0)(passing.start)
        fix_ref[...] = last[...].astype(BF16)

        @pl.when(here < pieces - 1)
        def _():
            passing.wait_recv()
            fix_ref[...] = (last[...] + rim_in[...]).astype(BF16)

        early.finish()
        line.finish()
        widesum_ref[...] = wheld[here // 2]
        tallsum_ref[...] = theld[here // 2].astype(F32)
        outsum_ref[...] = oheld[here // 2].astype(F32)
        gatesum_ref[...] = gheld[here // 2]
        pair.left()
        for r in range(begun, rounds):
            early.left(r)
        for r in range(rounds):
            line.left(r)
        pl.when(here > 0)(passing.wait_send)


def recurrence_backward(
    maps, cot, state_in, proj_ext, conv_w, rowp, colp, tokp, slopes, grad_heads, saved, wide, tall, outg, normed, ggate,
    heads, pieces, span_pieces,
):
    rows = tokp.shape[0]
    blocks = rows // BLOCK_LEN
    chips = pieces // 2
    per = 2
    final = blocks // per - 1
    whole = lambda *dims: pl.BlockSpec(dims, lambda i: (0,) * len(dims))
    by_block = lambda *dims: pl.BlockSpec((per,) + dims, lambda i: (final - i,) + (0,) * len(dims))
    token = lambda cols: pl.BlockSpec((per * BLOCK_LEN, cols), lambda i: (final - i, 0))
    shape = lambda *dims: jax.ShapeDtypeStruct(dims, F32)
    low_shape = lambda *dims: jax.ShapeDtypeStruct(dims, BF16)
    vmem = pl.BlockSpec(memory_space=pltpu.VMEM)
    low = lambda *dims: pltpu.VMEM(dims, BF16)
    square = (heads, ROWS, HEAD)
    wide_chunk, tall_chunk, out_chunk = wide.shape[1:], tall.shape[1:], outg.shape[2:]
    gate_chunk = (HEADS // heads, out_chunk[0], ggate.shape[1])
    dma = pltpu.SemaphoreType.DMA
    return pl.pallas_call(
        functools.partial(bwd_kernel, heads, pieces, blocks // per, per, max(1, chips - 2), span_pieces),
        grid=(blocks // per,),
        in_specs=[
            vmem, vmem, vmem, vmem, vmem,
            pl.BlockSpec((per * 8, ROWS), lambda i: (final - i, 0)),
            pl.BlockSpec((per * ROWS, HEAD), lambda i: (final - i, 0)), token(HEAD), token(HEAD),
            token(heads * HEAD), token(heads * WIDE),
            by_block(heads, BLOCK_LEN, HEAD), by_block(*square), by_block(*square), by_block(*square),
            by_block(*square), by_block(heads, BLOCK_LEN, ROWS), by_block(heads, ROWS, 2 * HEAD),
            by_block(heads, HEAD, 2 * HEAD), vmem, vmem, vmem, vmem, vmem,
        ],
        out_specs=[
            token(heads * WIDE), whole(8, heads * WIDE), whole(8, heads * WIDE), token(HEAD), whole(8, HEAD),
            whole(*wide_chunk), whole(*tall_chunk), whole(*out_chunk), whole(*gate_chunk),
        ],
        out_shape=[
            low_shape(rows, heads * WIDE), low_shape(8, heads * WIDE), shape(8, heads * WIDE), low_shape(rows, HEAD),
            shape(8, HEAD), low_shape(*wide_chunk), shape(*tall_chunk), shape(*out_chunk), low_shape(*gate_chunk),
        ],
        scratch_shapes=[
            pltpu.VMEM((heads, HEAD, HEAD), F32), pltpu.VMEM((3 * heads * per, ROWS, HEAD), F32),
            pltpu.VMEM((8, heads * WIDE), F32), pltpu.VMEM((8, heads * WIDE), F32),
            pltpu.VMEM((pieces, heads, HEAD, HEAD), BF16), pltpu.VMEM((8, heads * WIDE), F32),
            low(chips, *wide_chunk), low(chips, *tall_chunk), low(2, chips, *wide_chunk), low(2, chips, *tall_chunk),
            low(chips, 2, *gate_chunk), low(chips, *out_chunk), low(chips, *gate_chunk), low(chips, *out_chunk),
            low(chips, *gate_chunk), low(2, chips, *out_chunk), low(2, chips, *gate_chunk),
            dma((1, 3, pieces)), dma((1, pieces)), dma((2,)), dma((2,)), dma((2, chips)), dma((2, 2, chips)),
            dma((2, chips)), dma((2, 2, chips)), dma((2,)),
        ],
        compiler_params=pltpu.CompilerParams(
            vmem_limit_bytes=VMEM_LIMIT, collective_id=4, has_side_effects=True
        ),
        name="recurrence_backward",
    )(maps, cot, state_in, proj_ext, conv_w, rowp, colp, tokp, slopes, grad_heads, *saved, wide, tall, outg, normed, ggate)


def final_kernel(
    size, pieces, heads, norm_at, inner, gp_any, gg_any, gs_any, w_any, normed_any,
    fix_ref, x_ref, gmid_ref, norms_ref, gw_ref, gain_ref, gsum_ref, loss_ref, gnorm_ref, wide_ref, gatesum_ref,
    ingrad_ref, gmix_ref, ggate_ref, gtail_ref, gwg_ref, gwu_ref, mean_ref, ends_ref, both_ref,
    gp_ref, gg_ref, gs_ref, w_ref, normed_ref, load_sem, wideout_ref, gateout_ref,
    sent, got, whole, turned, *halves_and_rest,
):
    grads, theirs, helds, cames, blocks = [halves_and_rest[2 * n : 2 * n + 2] for n in range(5)]
    around, along, summed, *sems = halves_and_rest[10:]
    final_body(
        size, pieces, heads, norm_at, inner, gp_any, gg_any, gs_any, w_any, normed_any,
        fix_ref, x_ref, gmid_ref, norms_ref, gw_ref, gain_ref, gsum_ref, loss_ref, gnorm_ref, wide_ref, gatesum_ref,
        ingrad_ref, gmix_ref, ggate_ref, gtail_ref, gwg_ref, gwu_ref, mean_ref, ends_ref, both_ref,
        gp_ref, gg_ref, gs_ref, w_ref, normed_ref, load_sem, wideout_ref, gateout_ref,
        sent, got, whole, turned, grads, theirs, helds, cames, blocks, around, along, summed, *sems,
    )


def final_body(
    size, pieces, heads, norm_at, inner, gp_any, gg_any, gs_any, w_any, normed_any,
    fix_ref, x_ref, gmid_ref, norms_ref, gw_ref, gain_ref, gsum_ref, loss_ref, gnorm_ref, wide_ref, gatesum_ref,
    ingrad_ref, gmix_ref, ggate_ref, gtail_ref, gwg_ref, gwu_ref, mean_ref, ends_ref, both_ref,
    gp_ref, gg_ref, gs_ref, w_ref, normed_ref, load_sem, wideout_ref, gateout_ref,
    sent, got, whole, turned, grads, theirs, helds, cames, blocks, around, along, summed,
    local_sem, seq_send, seq_recv, pair_send, pair_recv, line_send, line_recv, ctx_send, ctx_recv,
):
    me, here = lax.axis_index("seq"), lax.axis_index("ctx")
    count = x_ref.shape[0]
    loads = [
        pltpu.make_async_copy(source, target, load_sem.at[n])
        for n, (source, target) in enumerate(
            [(gp_any, gp_ref), (gg_any, gg_ref), (gs_any, gs_ref), (w_any, w_ref), (normed_any, normed_ref)]
        )
    ]
    for load in loads:
        load.start()
    barrier = pltpu.get_barrier_semaphore()
    peers = [({"seq": partner(me, i, size)}, here >= 0) for i in range(1, size)]
    peers += [({"ctx": lax.rem(here + i, pieces)}, here >= 0) for i in range(1, pieces)]
    pl.semaphore_wait(barrier, greet(peers, barrier))

    def dot(a, b, ca=1, cb=0):
        return lax.dot_general(a, b, (((ca,), (cb,)), ((), ())), preferred_element_type=F32)

    def rows(q):
        return pl.ds(pl.multiple_of(q * count, count), count)

    def to_peer(n, i):
        q = partner(me, i, size)
        source, target = [
            (sent.at[i - 1], got.at[i - 1]), (wide_ref.at[:, q], wideout_ref.at[me]),
            (around.at[me], around.at[me]), (helds[0].at[here // 2, q], blocks[0].at[me]),
            (gatesum_ref.at[q], gateout_ref.at[me]), (helds[1].at[here // 2, q], blocks[1].at[me]),
        ][n]
        return pltpu.make_async_remote_copy(
            source, target, seq_send.at[n, i - 1], seq_recv.at[n, i - 1], device_id={"seq": q}, device_id_type=MESH
        )

    def to_piece(i):
        return pltpu.make_async_remote_copy(
            along.at[here], along.at[here], ctx_send.at[i - 1], ctx_recv.at[i - 1],
            device_id={"ctx": lax.rem(here + i, pieces)}, device_id_type=MESH,
        )

    gate_at, tail_at = gp_ref.shape[1], gp_ref.shape[1] + gg_ref.shape[1]
    for load in loads:
        load.wait()
    gp_ref[gp_ref.shape[0] - 8 :] = fix_ref[...]

    def parts():
        for first in range(0, D, 256):
            tile = slice(first, first + 256)
            value = (
                dot(gp_ref[...], w_ref[tile, :gate_at], 1, 1)
                + dot(gg_ref[...], w_ref[tile, gate_at:tail_at], 1, 1)
                + dot(gs_ref[...], w_ref[tile, tail_at:], 1, 1)
            )
            whole[:, tile] = value

        def give(k, carry):
            i = size - 1 - k
            sent[i - 1] = whole[rows(partner(me, i, size))].astype(BF16)
            pltpu.make_async_remote_copy(
                sent.at[i - 1], got.at[i - 1], seq_send.at[0, i - 1], seq_recv.at[0, i - 1],
                device_id={"seq": partner(me, i, size)}, device_id_type=MESH,
            ).start()
            return carry

        lax.fori_loop(0, size - 1, give, 0)

    turned[...] = normed_ref[...].T
    rank_rows = D // (size * pieces)
    pairs = [Siblings([grads[n]], [theirs[n]], [helds[n]], pair_send.at[n], pair_recv.at[n]) for n in range(2)]
    lines = [LineSum(pieces, [helds[n]], [cames[n]], line_send.at[n], line_recv.at[n]) for n in range(2)]
    split = grads[0].shape[4]

    def gradient(source, first, cols, n, at):
        grad = dot(turned[...], source[:, first : first + cols])
        for r in range(size):
            for c in range(pieces):
                row = (r * pieces + c) * rank_rows
                grads[n][c // 2, c % 2, r, :, at : at + cols] = grad[row : row + rank_rows].astype(BF16)

    for first in range(0, split, 256):
        gradient(gp_ref, first, min(256, split - first), 0, first)
    pairs[0].start()
    for first in range(split, gate_at, 256):
        gradient(gp_ref, first, min(256, gate_at - first), 1, first - split)
    gradient(gs_ref, 0, HEAD, 1, gate_at - split)
    channels = gw_ref.shape[1]
    mine = channel_rows(D // size, channels)
    taps = jnp.zeros((D // size, HEAD), F32)
    for lag in range(CONV):
        spread = jnp.where(mine, gw_ref[lag : lag + 1], 0.0).astype(BF16)
        taps = taps + dot(spread, tap_lanes(channels, CONV - 1 - lag, norm_at + 3))
    for c in range(pieces):
        grads[1][c // 2, c % 2, me, :, gate_at - split :] = (
            grads[1][c // 2, c % 2, me, :, gate_at - split :].astype(F32) + taps[c * rank_rows : (c + 1) * rank_rows]
        ).astype(BF16)
    pairs[1].start()
    pairs[0].add()
    lines[0].round(0)
    parts()
    pairs[1].add()
    lines[1].round(0)
    rounds = pieces // 2 - 1
    for r in range(1, rounds - 1):
        for line in lines:
            line.round(r)
    for i in range(1, size):
        to_peer(0, i).wait_recv()
    gnormed = whole[rows(me)]
    for i in range(1, size):
        gnormed = gnormed + got[i - 1].astype(F32)
    x = x_ref[...].astype(F32)
    inv = lax.rsqrt(jnp.mean(x * x, axis=1, keepdims=True) + NORM_EPS)
    unit = x * inv
    down = gnormed * norms_ref[0:1, :]
    ingrad_ref[...] = gmid_ref[...] + inv * (down - unit * jnp.mean(down * unit, axis=1, keepdims=True))
    term = jnp.sum(gnormed * unit, axis=0, keepdims=True)
    lane = iota((1, HEAD), 1)
    ends = jnp.where(lane == 2 * HEADS, loss_ref[...], 0.0)
    for h in range(heads):
        for n in range(2):
            ends = jnp.where(lane == n * HEADS + me * heads + h, gsum_ref[h : h + 1, n : n + 1], ends)
    around[me] = jnp.zeros(around.shape[1:], F32)
    around[me, 0:1] = gain_ref[...]
    around[me, 1:2] = ends
    for j in range(D // HEAD):
        around[me, 8 + j : 9 + j] = term[:, j * HEAD : (j + 1) * HEAD]
        around[me, 8 + D // HEAD + j : 9 + D // HEAD + j] = gnorm_ref[:, j * HEAD : (j + 1) * HEAD]
    for i in range(1, size):
        to_peer(2, i).start()
    kept = [
        pltpu.make_async_copy(wide_ref.at[:, me], wideout_ref.at[me], local_sem.at[0]),
        pltpu.make_async_copy(gatesum_ref.at[me], gateout_ref.at[me], local_sem.at[1]),
    ]
    for copy in kept:
        copy.start()
    for i in reversed(range(1, size)):
        to_peer(1, i).start()
        to_peer(4, i).start()
    for line in lines:
        line.round(rounds - 1)
    for i in range(1, size):
        to_peer(2, i).wait_recv()
    mine = around[0]
    for r in range(1, size):
        mine = mine + around[r]
    along[here] = mine
    for i in range(1, pieces):
        to_piece(i).start()
    for n, phase in ((0, 3), (1, 5)):
        lines[n].finish()
        blocks[n][me] = helds[n][here // 2, me]
        for i in reversed(range(1, size)):
            to_peer(phase, i).start()
    for i in range(1, pieces):
        to_piece(i).wait_recv()
    total = along[0]
    for c in range(1, pieces):
        total = total + along[c]
    ends_ref[...] = total[:2]
    valid = jnp.maximum(jnp.sum(norms_ref[2:3, :], axis=1, keepdims=True), 1.0)
    mean_ref[...] = total[1:2, 2 * HEADS : 2 * HEADS + 1] / (D * valid)
    summed[...] = total
    place = (me * pieces + here) * rank_rows
    for n in range(2):
        row = summed[pl.ds(8 + n * (D // HEAD) + place // HEAD, 1), :]
        both_ref[n : n + 1, :] = pltpu.roll(row, lax.rem(HEAD - lax.rem(place, HEAD), HEAD), 1)
    tail = jnp.zeros((rank_rows, HEAD), F32)
    for copy in kept:
        copy.wait()
    for i in range(1, size):
        for n in (1, 4, 3):
            to_peer(n, i).wait_recv()
    wide_cols = tail_at - gate_at
    for r in range(size):
        gwg_ref[:, r * inner : (r + 1) * inner] = wideout_ref[r, 0, :, :inner].astype(F32)
        gwu_ref[:, r * inner : (r + 1) * inner] = wideout_ref[r, 1, :, :inner].astype(F32)
        ggate_ref[:, r * wide_cols : (r + 1) * wide_cols] = gateout_ref[r].astype(F32)
        gmix_ref[:, r * gate_at : r * gate_at + split] = blocks[0][r].astype(F32)
    for i in range(1, size):
        to_peer(5, i).wait_recv()
    for r in range(size):
        block = blocks[1][r].astype(F32)
        gmix_ref[:, r * gate_at + split : (r + 1) * gate_at] = block[:, : gate_at - split]
        tail = tail + block[:, gate_at - split :]
    gtail_ref[...] = tail
    for pair in pairs:
        pair.left()
    for line in lines:
        for r in range(pieces // 2 - 1):
            line.left(r)
    for i in range(1, size):
        for n in range(6):
            to_peer(n, i).wait_send()
    for i in range(1, pieces):
        to_piece(i).wait_send()


def final_part(
    size, pieces, heads, norm_at, gp, gg, gs, weights, normed, fix, x, gmid, norms, gw, gain, gsum, loss, gnorm, wide,
    gatesum,
):
    count = x.shape[0]
    chips = pieces // 2
    held, inner = D // (size * pieces), FF // size
    split = WIDE if heads > 1 else 3 * HEAD
    widths = (split, gp.shape[1] - split + gs.shape[1])
    small = (8 + 2 * (D // HEAD), HEAD)
    vmem = pl.BlockSpec(memory_space=pltpu.VMEM)
    out = lambda *dims: jax.ShapeDtypeStruct(dims, F32)
    low = lambda *dims: pltpu.VMEM(dims, BF16)
    high = lambda *dims: pltpu.VMEM(dims, F32)
    dma = pltpu.SemaphoreType.DMA
    return pl.pallas_call(
        functools.partial(final_kernel, size, pieces, heads, norm_at, inner),
        in_specs=[pl.BlockSpec(memory_space=pltpu.HBM)] * 5 + [vmem] * 11,
        out_specs=[vmem] * 9,
        out_shape=[
            out(count, D), out(held, size * gp.shape[1]), out(held, size * gg.shape[1]), out(held, HEAD),
            out(held, size * inner), out(held, size * inner), out(1, 1), out(2, HEAD), out(2, HEAD),
        ],
        scratch_shapes=[
            low(*gp.shape), low(*gg.shape), low(*gs.shape), low(*weights.shape), low(*normed.shape), dma((5,)),
            low(size, 2, held, wide.shape[3]), low(*gatesum.shape),
            low(size - 1, count, D), low(size - 1, count, D), high(size * count, D), low(D, normed.shape[0]),
            *[low(chips, 2, size, held, w) for w in widths], *[low(chips, size, held, w) for w in widths],
            *[low(chips, size, held, w) for w in widths], *[low(2, chips, size, held, w) for w in widths],
            *[low(size, held, w) for w in widths], high(size, *small), high(pieces, *small), high(*small),
            dma((2,)), dma((6, size - 1)), dma((6, size - 1)), dma((2, 1)), dma((2, 1)), dma((2, 1, chips)),
            dma((2, 1, 2, chips)),
            dma((pieces - 1,)), dma((pieces - 1,)),
        ],
        compiler_params=pltpu.CompilerParams(
            vmem_limit_bytes=VMEM_LIMIT, collective_id=5, has_side_effects=True
        ),
        name="final_part",
    )(gp, gg, gs, weights, normed, fix, x, gmid, norms, gw, gain, gsum, loss, gnorm, wide, gatesum)


def finish_kernel(
    scal_cols, taps_at, final_ref, ingrad_ref, gmix_ref, ggate_ref, gwg_ref, gwu_ref, tall_ref, outsum_ref,
    tail_ref, ends_ref, both_ref,
    final_out, ingrad_out, gmix_out, ggate_out, gwg_out, gwu_out, gwd_out, gout_out,
    gscal_out, gconv_out, norma_out, normm_out, gain_out, alog_out, dt_out,
):
    for source, target in (
        (final_ref, final_out), (ingrad_ref, ingrad_out), (gmix_ref, gmix_out), (ggate_ref, ggate_out),
        (gwg_ref, gwg_out), (gwu_ref, gwu_out), (outsum_ref, gout_out),
    ):
        target[...] = source[...]
    gwd_out[...] = tall_ref[: gwd_out.shape[0]]
    tail = tail_ref[...]
    rows, channels = tail.shape[0], gconv_out.shape[1]
    square = jnp.concatenate([tail, jnp.zeros((HEAD - rows, HEAD), F32)], axis=0)
    gscal_out[...] = square.T[:scal_cols, :rows]
    mine = channel_rows(rows, channels)
    for tap in range(CONV):
        spread = exact(tail, tap_lanes(channels, tap, taps_at).astype(F32), 1, 1)
        gconv_out[tap : tap + 1] = jnp.sum(jnp.where(mine, spread, 0.0), axis=0, keepdims=True)
    held = norma_out.shape[1]
    norma_out[...] = both_ref[0:1, :held]
    normm_out[...] = both_ref[1:2, :held]
    gain_out[...] = ends_ref[0:1, :]
    alog_out[...] = ends_ref[1:2, :HEADS]
    dt_out[...] = ends_ref[1:2, HEADS : 2 * HEADS]


def finish_part(scal_cols, taps_at, deep, channels, *parts):
    vmem = pl.BlockSpec(memory_space=pltpu.VMEM)
    held = parts[2].shape[0]
    out = lambda dims, kind=F32: jax.ShapeDtypeStruct(dims, kind)
    return pl.pallas_call(
        functools.partial(finish_kernel, scal_cols, taps_at),
        in_specs=[vmem] * 11,
        out_specs=[vmem] * 15,
        out_shape=[out(p.shape, p.dtype) for p in parts[:6]] + [
            out((deep, D)), out(parts[7].shape), out((scal_cols, held)), out((CONV, channels)),
            out((1, held)), out((1, held)), out((1, HEAD)), out((1, HEADS)), out((1, HEADS)),
        ],
        compiler_params=pltpu.CompilerParams(vmem_limit_bytes=VMEM_LIMIT),
        name="finish_part",
    )(*parts)


def local(
    block_input, teacher, valid_mask, segments, mix_proj, scalar_proj, gate_proj, out_proj, conv_weight,
    norm_attn, norm_mlp, head_gain, a_log, dt_bias, w_gate, w_up, w_down,
):
    seq_size, pieces = lax.axis_size("seq"), lax.axis_size("ctx")
    heads = HEADS // seq_size
    rows = block_input.shape[0] * seq_size
    token_total = segments.shape[0]
    seq_length = min(SEQ_LEN, token_total)
    span_pieces = min(pieces, (MOST_DOC.get(token_total, token_total) - 2) // rows + 1)
    index = lax.axis_index("ctx")
    held = mix_proj.shape[0]
    scal_cols = HEADS * (NH + 1)
    norm_at, taps_at = scal_cols, scal_cols + 3
    taps_end = taps_at + CONV * conv_weight.shape[0] // held

    count_here = jnp.sum(valid_mask.astype(F32)).astype(BF16)
    tail = jnp.concatenate(
        [
            scalar_proj, norm_attn[:, None], norm_mlp[:, None],
            jnp.where(iota((held, 1), 0) == 0, count_here, jnp.zeros((), BF16)),
            conv_weight.reshape(held, -1), jnp.zeros((held, HEAD - taps_end), BF16),
        ],
        axis=1,
    )
    x_full, halo, gathered, stage = start_gather(
        seq_size, pieces, block_input, mix_proj, gate_proj, tail, w_gate, w_up
    )
    weights = gathered.reshape(D, -1)
    piece_start = index * rows
    window = lax.dynamic_slice_in_dim(jnp.pad(segments, (CONV, 0)), piece_start, rows + CONV)
    place_in = (piece_start + jnp.arange(rows, dtype=jnp.int32)) % seq_length
    marks = jnp.stack(
        [
            ((window[CONV - lag : CONV - lag + rows] == window[CONV:]) & (place_in >= lag)).astype(F32)
            if lag < CONV
            else jnp.zeros((rows,), F32)
            for lag in range(1, 9)
        ]
    )
    rates = jnp.stack([a_log.astype(F32), dt_bias.astype(F32)])
    (
        proj_ext, normed, gate_out, tokp, slopes, colp, rowp, conv_w, norms,
        oloc, carr, state_in, maps, *saved, wg_full, wu_full, wo_full,
    ) = recurrence_forward(heads, pieces, span_pieces, norm_at, rates, x_full, halo, weights, marks, stage, out_proj)
    (
        final_out, grad_middle, grad_heads, grad_gate_out, cot, gain_term, norm_mlp_term, loss, wide, tall, outg,
    ) = middle_part(
        seq_size, heads, pieces, token_total, block_input, teacher, valid_mask[None, :], norms, head_gain[None, :],
        oloc, carr, gate_out, state_in, wo_full.reshape(heads * HEAD, D), wg_full.reshape(D, -1),
        wu_full.reshape(D, -1), w_down,
    )
    grad_proj, fixed_rows, gw, grad_scal, gsum, wide_sum, tall_sum, out_sum, gate_sum = recurrence_backward(
        maps, cot, state_in, proj_ext, conv_w, rowp, colp, tokp, slopes, grad_heads, saved, wide, tall, outg, normed,
        grad_gate_out, heads, pieces, span_pieces,
    )
    input_grad, mix_grad, gate_grad, tail_grad, wg_grad, wu_grad, mean_loss, ends, norm_grads = final_part(
        seq_size, pieces, heads, norm_at, grad_proj, grad_gate_out, grad_scal, weights, normed, fixed_rows, block_input,
        grad_middle, norms, gw, gain_term, gsum, loss, norm_mlp_term, wide_sum.reshape(2, seq_size, held, -1),
        gate_sum,
    )
    (
        final_out, input_grad, mix_grad, gate_grad, wg_grad, wu_grad, wd_grad, out_grad,
        scal_grad, conv_grad, norm_a_grad, norm_m_grad, gain_grad, alog_grad, dt_grad,
    ) = finish_part(
        scal_cols, taps_at, w_down.shape[0], conv_weight.shape[0],
        final_out, input_grad, mix_grad, gate_grad, wg_grad, wu_grad, tall_sum, out_sum, tail_grad, ends, norm_grads,
    )
    return (
        final_out, mean_loss[0, 0], input_grad, mix_grad, scal_grad.T, gate_grad, out_grad, conv_grad.T,
        norm_a_grad.reshape(-1), norm_m_grad.reshape(-1), gain_grad.reshape(-1), alog_grad.reshape(-1),
        dt_grad.reshape(-1), wg_grad, wu_grad, wd_grad,
    )


def solution(mesh):
    tokens, vector, matrix = P(("ctx", "seq"), None), P(BOTH), P(BOTH, None)
    in_specs = (
        tokens, tokens, P(("ctx", "seq")), P(), matrix, matrix, matrix, matrix, matrix, vector, vector,
        P(), P(), P(), matrix, matrix, matrix,
    )
    out_specs = (
        tokens, P(), tokens, matrix, matrix, matrix, matrix, matrix, vector, vector, P(), P(), P(),
        matrix, matrix, matrix,
    )
    return jax.shard_map(local, mesh=mesh, in_specs=in_specs, out_specs=out_specs, check_vma=False)
```

```python
import functools
import math

import jax
import jax.numpy as jnp
from jax import lax
from jax.experimental import pallas as pl
from jax.experimental.pallas import tpu as pltpu
from jax.sharding import PartitionSpec as P

D = 1024
HEADS = 8
HEAD = 128
NH = 2
FF = 2816
BLOCK_LEN = 64
ROWS = BLOCK_LEN * NH
CONV = 4
SEQ_LEN = 32768
MOST_DOC = {4096: 2048, 32768: 8192}
WIDE = (1 + 2 * NH) * HEAD
HALO = 16
NORM_EPS = 1e-06
VMEM_LIMIT = 60 << 20
F32 = jnp.float32
BF16 = jnp.bfloat16
BOTH = ("seq", "ctx")
MESH = pl.DeviceIdType.MESH


class Split:
    def __init__(self, x):
        self.high = x.astype(BF16)
        self.low = (x - self.high.astype(F32)).astype(BF16)


def mm(a, b, ca=1, cb=0):
    if not isinstance(a, Split) and a.dtype != BF16:
        a = Split(a)
    if not isinstance(b, Split) and b.dtype != BF16:
        b = Split(b)
    if isinstance(a, Split) and isinstance(b, Split):
        left, right = (a.high, a.high, a.low), (b.high, b.low, b.high)
    elif isinstance(a, Split):
        left, right = (a.high, a.low), (b, b)
    elif isinstance(b, Split):
        left, right = (a, a), (b.high, b.low)
    else:
        left, right = (a,), (b,)
    if len(left) > 1:
        left, right = (jnp.concatenate(left, axis=ca),), (jnp.concatenate(right, axis=cb),)
    return lax.dot_general(left[0], right[0], (((ca,), (cb,)), ((), ())), preferred_element_type=F32)


def lanes_for(columns):
    return -(-columns // HEAD) * HEAD


def iota(shape, axis):
    return lax.broadcasted_iota(jnp.int32, shape, axis)


def unit_lower_inverses(systems):
    n = systems[0].shape[0]
    ri, ci = iota((n, n), 0), iota((n, n), 1)
    pick = (iota((n, 8), 0) % 8 == iota((n, 8), 1)).astype(BF16)
    own = ri // 8 == ci // 8
    eye = (ri == ci).astype(F32).reshape(n // 8, 8, n)
    small = [mm(jnp.where(own, a, 0.0), pick).reshape(n // 8, 8, 8) for a in systems]
    inv = [eye for _ in systems]
    for j in range(7):
        inv = [x - m[:, :, j : j + 1] * x[:, j : j + 1, :] for x, m in zip(inv, small)]
    inv = [x.reshape(n, n) for x in inv]
    size = 8
    while size < n:
        off = (ri // (2 * size) == ci // (2 * size)) & (ri // size != ci // size)
        halves = [Split(x) for x in inv]
        right = [mm(jnp.where(off, a, 0.0), x) for a, x in zip(systems, halves)]
        inv = [x - mm(y, z) for x, y, z in zip(inv, halves, right)]
        size *= 2
    return inv


DOC = 7
LINK = DOC + 1


def lane_of(h, what):
    return h * (NH + 1) + what


def column(table, lane):
    return table[:, lane : lane + 1]


def decays(rowp, colp, tokp, h):
    g = lane_of(h, NH)
    cs_row, g_row = rowp[DOC : DOC + 1, :], rowp[g : g + 1, :]
    cs_col, g_col = column(colp, DOC), column(colp, g)
    cs_tok, g_tok = column(tokp, DOC), column(tokp, g)
    beta = column(colp, lane_of(h, 0))
    ri, ci = iota((ROWS, ROWS), 0), iota((ROWS, ROWS), 1)
    strict = (ri > ci) & (cs_col == cs_row)
    decay = jnp.where(strict, jnp.exp(jnp.where(strict, g_col - g_row, 0.0)), 0.0)
    rt, ct = iota((BLOCK_LEN, ROWS), 0), iota((BLOCK_LEN, ROWS), 1)
    seen = (rt * NH + NH - 1 >= ct) & (cs_tok == cs_row)
    qdecay = jnp.where(seen, jnp.exp(jnp.where(seen, g_tok - g_row, 0.0)), 0.0)
    carry = jnp.where(cs_col == 0.0, jnp.exp(g_col), 0.0)
    qcarry = jnp.where(cs_tok == 0.0, jnp.exp(g_tok), 0.0)
    cs_last, g_last = cs_row[:, ROWS - 1 :], g_row[:, ROWS - 1 :]
    same = cs_col == cs_last
    dlast = jnp.where(same, jnp.exp(jnp.where(same, g_last - g_col, 0.0)), 0.0)
    clast = jnp.where(cs_last == 0.0, jnp.exp(g_last), 0.0)
    return beta, decay, qdecay, carry, qcarry, dlast, clast


def lag_rows(ext, lag):
    moved = pltpu.roll(ext, lag, 0) if lag else ext
    return moved[HALO:]


UP, DOWN, ACROSS = 0, 1, 2


class Line:
    def __init__(self, pieces, parts, send_sem, recv_sem, up=True, down=True, reach=None):
        self.chips = pieces // 2
        self.reach = self.chips - 1 if reach is None else reach
        self.here = lax.axis_index("ctx")
        self.chip = self.here // 2
        self.core = lax.rem(self.here, 2)
        self.other = self.here + 1 - 2 * self.core
        self.parts, self.send_sem, self.recv_sem, self.up, self.down = parts, send_sem, recv_sem, up, down

    def copies(self, chunk, way, only=None):
        target = (self.here + 2, self.here - 2, self.other)[way]
        return [
            pltpu.make_async_remote_copy(
                part(chunk), part(chunk), self.send_sem.at[n, way, chunk], self.recv_sem.at[n, chunk],
                device_id={"ctx": target}, device_id_type=MESH,
            )
            for n, part in enumerate(self.parts)
            if only is None or n == only
        ]

    def start(self, chunk, way, only=None):
        for copy in self.copies(chunk, way, only):
            copy.start()

    def arrived(self, chunk, only=None):
        for copy in self.copies(chunk, ACROSS, only):
            copy.wait_recv()

    def left(self, chunk, way):
        for copy in self.copies(chunk, way):
            copy.wait_send()

    def routes(self, distance, act):
        if distance == 0:
            if self.up and self.reach:
                pl.when(self.chip < self.chips - 1)(lambda: act(self.here, UP))
            if self.down and self.reach:
                pl.when(self.chip > 0)(lambda: act(self.here, DOWN))
            act(self.here, ACROSS)
            return
        below, above = self.here - 2 * distance, self.here + 2 * distance
        onward = distance < self.reach
        if self.up:

            @pl.when(self.chip >= distance)
            def _():
                if onward:
                    pl.when(self.chip < self.chips - 1)(lambda: act(below, UP))
                act(below, ACROSS)

        if self.down:

            @pl.when(self.chip + distance < self.chips)
            def _():
                if onward:
                    pl.when(self.chip > 0)(lambda: act(above, DOWN))
                act(above, ACROSS)

    def own(self, only=None):
        self.routes(0, lambda chunk, way: self.start(chunk, way, only))

    def hop(self, distance):
        for n in range(len(self.parts)):
            if self.up:
                pl.when(self.chip >= distance)(lambda n=n: self.arrived(self.here - 2 * distance, n))
            if self.down:
                pl.when(self.chip + distance < self.chips)(lambda n=n: self.arrived(self.here + 2 * distance, n))
            self.routes(distance, lambda chunk, way, n=n: self.start(chunk, way, n))

    def finish(self):
        for chip in range(self.chips):
            needed = (self.chip <= chip + (self.reach if self.up else 0)) & (
                self.chip >= chip - (self.reach if self.down else 0)
            )
            pl.when(needed)(lambda chip=chip: self.arrived(2 * chip + 1 - self.core))
        for distance in range(self.reach + 1):
            self.routes(distance, self.left)


class LineSum:
    def __init__(self, pieces, held, came, send_sem, recv_sem):
        self.chips = pieces // 2
        self.here = lax.axis_index("ctx")
        self.chip = self.here // 2
        self.held, self.came, self.send_sem, self.recv_sem = held, came, send_sem, recv_sem

    def copies(self, owner, way):
        return [
            pltpu.make_async_remote_copy(
                held.at[owner], came.at[way, owner], self.send_sem.at[n, owner], self.recv_sem.at[n, way, owner],
                device_id={"ctx": self.here + 2 - 4 * way}, device_id_type=MESH,
            )
            for n, (held, came) in enumerate(zip(self.held, self.came))
        ]

    def take(self, owner, way):
        for copy in self.copies(owner, way):
            copy.wait_recv()
        for held, came in zip(self.held, self.came):
            held[owner] = (held[owner].astype(F32) + came[way, owner].astype(F32)).astype(BF16)

    def send(self, owner, way):
        for copy in self.copies(owner, way):
            copy.start()

    def each(self, r, act):
        top = self.chips - 1
        for way, place in ((UP, self.chip), (DOWN, top - self.chip)):
            owner = top - (r - place) if way == UP else r - place
            pl.when((place <= r) & (place < top))(lambda: act(owner, way, place))

    def settle(self, r):
        self.each(r, lambda owner, way, place: pl.when(place > 0)(lambda: self.take(owner, way)))

    def launch(self, r):
        self.each(r, lambda owner, way, place: self.send(owner, way))

    def left(self, r):
        def wait(owner, way, place):
            for copy in self.copies(owner, way):
                copy.wait_send()

        self.each(r, wait)

    def round(self, r):
        self.settle(r)
        self.launch(r)

    def finish(self):
        top = self.chips - 1
        pl.when(self.chip > 0)(lambda: self.take(self.chip, UP))
        pl.when(self.chip < top)(lambda: self.take(self.chip, DOWN))


class Siblings:
    def __init__(self, parts, theirs, held, send_sem, recv_sem):
        self.here = lax.axis_index("ctx")
        self.core = lax.rem(self.here, 2)
        self.parts, self.theirs, self.held, self.send_sem, self.recv_sem = parts, theirs, held, send_sem, recv_sem

    def copies(self):
        return [
            pltpu.make_async_remote_copy(
                part.at[:, 1 - self.core], theirs, self.send_sem.at[n], self.recv_sem.at[n],
                device_id={"ctx": self.here + 1 - 2 * self.core}, device_id_type=MESH,
            )
            for n, (part, theirs) in enumerate(zip(self.parts, self.theirs))
        ]

    def start(self):
        for copy in self.copies():
            copy.start()

    def add(self):
        for copy in self.copies():
            copy.wait_recv()
        for part, theirs, held in zip(self.parts, self.theirs, self.held):

            def one(chip, carry, part=part, theirs=theirs, held=held):
                held[chip] = (part[chip, self.core].astype(F32) + theirs[chip].astype(F32)).astype(BF16)
                return carry

            lax.fori_loop(0, part.shape[0], one, 0)

    def left(self):
        for copy in self.copies():
            copy.wait_send()


def partner(me, i, size):
    total, bit = 0, 1
    while bit < size:
        total = total + lax.rem(me // bit + i // bit, 2) * bit
        bit *= 2
    return total


def chips_within(span_pieces, pieces):
    return min(pieces // 2 - 1, (span_pieces + 1) // 2)


def greet(devices, barrier):
    total = 0
    for place, there in devices:
        pl.when(there)(
            lambda place=place: pl.semaphore_signal(barrier, inc=1, device_id=place, device_id_type=MESH)
        )
        total = total + jnp.asarray(there, jnp.int32)
    return total


def line_neighbours(pieces):
    here = lax.axis_index("ctx")
    chip, core = here // 2, lax.rem(here, 2)
    return [
        ({"ctx": here + 2}, chip < pieces // 2 - 1),
        ({"ctx": here - 2}, chip > 0),
        ({"ctx": here + 1 - 2 * core}, here >= 0),
    ]


def start_kernel(
    size, pieces, norm_at, x_ref, mix_ref, gate_ref, scal_ref, norma_ref, normm_ref, taps_ref, mask_ref, wg_ref, wu_ref,
    xfull_ref, halo_ref, full_ref, stage_ref,
    tail_ref, sides, local_sem, seq_send, seq_recv, line_send, line_recv, halo_sem,
):
    me, here = lax.axis_index("seq"), lax.axis_index("ctx")
    count = x_ref.shape[0]
    core = lax.rem(here, 2)
    inner = wg_ref.shape[1] // size
    gate_at = mix_ref.shape[1] // size
    tail_at = gate_at + gate_ref.shape[1] // size

    def placed(rows_, lane):
        at = (iota((rows_.shape[0], HEAD), 1) == lane + iota((rows_.shape[0], HEAD), 0)).astype(BF16)
        return lax.dot_general(rows_, at, (((0,), (0,)), ((), ())), preferred_element_type=F32)

    held, channels = tail_ref.shape[0], taps_ref.shape[1]
    pack = placed(scal_ref[...], 0) + placed(norma_ref[...], norm_at) + placed(normm_ref[...], norm_at + 1)
    valid = jnp.sum(mask_ref[...].astype(F32), axis=1, keepdims=True)
    pack = pack + jnp.where((iota((held, HEAD), 0) == 0) & (iota((held, HEAD), 1) == norm_at + 2), valid, 0.0)
    mine = channel_rows(held, channels)
    for tap in range(CONV):
        spread = jnp.where(mine, taps_ref[tap : tap + 1].astype(F32), 0.0).astype(BF16)
        pack = pack + lax.dot_general(
            spread, tap_lanes(channels, tap, norm_at + 3), (((1,), (0,)), ((), ())), preferred_element_type=F32
        )
    tail_ref[...] = pack.astype(BF16)
    barrier = pltpu.get_barrier_semaphore()
    peers = [({"seq": partner(me, i, size)}, here >= 0) for i in range(1, size)]
    side = [({"ctx": here + 1}, (core == 1) & (here < pieces - 1)), ({"ctx": here - 1}, (core == 0) & (here > 0))]
    total = greet(peers + line_neighbours(pieces) + side, barrier)
    pl.semaphore_wait(barrier, total)

    def rows(q):
        return pl.ds(pl.multiple_of(q * count, count), count)

    def cols(q, width):
        return pl.ds(pl.multiple_of(q * width, HEAD), width)

    def ends(n, q):
        return [
            (mix_ref.at[:, cols(q, gate_at)], full_ref.at[me, here, :, :gate_at]),
            (gate_ref.at[:, cols(q, tail_at - gate_at)], full_ref.at[me, here, :, gate_at:tail_at]),
            (tail_ref, full_ref.at[me, here, :, tail_at:]),
            (x_ref, xfull_ref.at[rows(me)]),
            (sides.at[q], stage_ref.at[me]),
        ][n]

    def exchange(n, i):
        q = partner(me, i, size)
        source, target = ends(n, q)
        return pltpu.make_async_remote_copy(
            source, target, seq_send.at[n, i - 1], seq_recv.at[n, i - 1], device_id={"seq": q}, device_id_type=MESH
        )

    def own(n):
        return pltpu.make_async_copy(*ends(n, me), local_sem.at[n])

    def begin(n):
        own(n).start()
        for i in range(1, size):
            exchange(n, i).start()

    def end(n):
        own(n).wait()
        for i in range(1, size):
            exchange(n, i).wait_recv()

    for n in range(3):
        begin(n)
    sides[...] = jnp.zeros_like(sides)
    for q in range(size):
        sides[q, 0, :, :inner] = wg_ref[:, q * inner : (q + 1) * inner]
        sides[q, 1, :, :inner] = wu_ref[:, q * inner : (q + 1) * inner]
    line = Line(
        pieces, [lambda c, i=i: full_ref.at[partner(me, i, size), c] for i in range(size)], line_send, line_recv
    )
    for n in range(3):
        own(n).wait()
    line.own(0)
    for i in range(1, size):
        for n in range(3):
            exchange(n, i).wait_recv()
        line.own(i)
    begin(3)
    begin(4)
    last = xfull_ref.at[pl.ds(size * count - HALO, HALO)]
    passing = pltpu.make_async_remote_copy(
        last, halo_ref, halo_sem.at[0], halo_sem.at[1], device_id={"ctx": here + 1}, device_id_type=MESH
    )
    hops = pieces // 2 - 1
    for distance in range(1, hops):
        line.hop(distance)
    end(3)
    pl.when(here < pieces - 1)(passing.start)

    @pl.when(here == 0)
    def _():
        filling = pltpu.make_async_copy(last, halo_ref, local_sem.at[5])
        filling.start()
        filling.wait()

    line.hop(hops)
    line.finish()
    end(4)
    pl.when(here > 0)(passing.wait_recv)
    pl.when(here < pieces - 1)(passing.wait_send)
    for n in range(5):
        for i in range(1, size):
            exchange(n, i).wait_send()


def start_gather(size, pieces, norm_at, x, mix, gate, scal, norm_a, norm_m, taps, mask, w_gate, w_up):
    anywhere = pl.BlockSpec(memory_space=pl.ANY)
    vmem = pl.BlockSpec(memory_space=pltpu.VMEM)
    out = lambda *dims: jax.ShapeDtypeStruct(dims, BF16)
    dma = pltpu.SemaphoreType.DMA
    held, padded = w_gate.shape[0], lanes_for(w_gate.shape[1] // size)
    width = (mix.shape[1] + gate.shape[1]) // size + HEAD
    return pl.pallas_call(
        functools.partial(start_kernel, size, pieces, norm_at),
        in_specs=[anywhere] * 3 + [vmem] * 7,
        out_specs=[anywhere] * 4,
        out_shape=[
            out(x.shape[0] * size, D), out(HALO, D), out(size, pieces, held, width), out(size, 2, held, padded),
        ],
        scratch_shapes=[
            pltpu.VMEM((held, HEAD), BF16), pltpu.VMEM((size, 2, held, padded), BF16),
            dma((6,)), dma((5, size - 1)), dma((5, size - 1)), dma((size, 3, pieces)), dma((size, pieces)), dma((2,)),
        ],
        compiler_params=pltpu.CompilerParams(
            vmem_limit_bytes=VMEM_LIMIT, collective_id=2, has_side_effects=True
        ),
        name="start_gather",
    )(x, mix, gate, scal, norm_a, norm_m, taps, mask, w_gate, w_up)


def exact(a, b, ca=1, cb=0):
    return lax.dot_general(
        a, b, (((ca,), (cb,)), ((), ())), precision=lax.Precision.HIGHEST, preferred_element_type=F32
    )


def tap_lanes(channels, tap, at):
    lanes = iota((channels, HEAD), 1)
    return (lanes == at + CONV * (iota((channels, HEAD), 0) % (WIDE // HEAD)) + tap).astype(BF16)


def channel_rows(rows, channels):
    return iota((rows, channels), 1) // (WIDE // HEAD) == iota((rows, channels), 0)


def front_body(
    heads, norm_at, rates_ref, x_ref, halo_ref, w_ref, marks_ref,
    proj_ref, normed_ref, gate_ref, tok_ref, slope_ref, col_ref, row_ref, taps_ref, norms_ref,
):
    me = lax.axis_index("seq")
    channels = heads * WIDE
    tail_at = channels + heads * HEAD
    rows = x_ref.shape[0]
    own_rows = D * heads // HEADS

    def dot(a, b, ca=1, cb=0):
        return lax.dot_general(a, b, (((ca,), (cb,)), ((), ())), preferred_element_type=F32)

    pick = (iota((8, HEAD), 1) == norm_at + iota((8, HEAD), 0)).astype(BF16)
    norms_ref[...] = dot(pick, w_ref[:, tail_at:], 1, 1)

    def normal(values):
        values = values.astype(F32)
        scale = lax.rsqrt(jnp.mean(values * values, axis=1, keepdims=True) + NORM_EPS)
        return (values * scale * norms_ref[0:1, :]).astype(BF16)

    early = normal(halo_ref[...])
    normed_ref[...] = normal(x_ref[...])
    proj_ref[:HALO] = dot(early, w_ref[:, :channels]).astype(BF16)
    proj_ref[HALO:] = dot(normed_ref[...], w_ref[:, :channels]).astype(BF16)
    gate_ref[...] = dot(normed_ref[...], w_ref[:, channels:tail_at])
    tail = w_ref[pl.ds(pl.multiple_of(me * own_rows, own_rows), own_rows), tail_at:]
    taps_ref[...] = jnp.zeros_like(taps_ref)
    mine = channel_rows(own_rows, channels)
    for lag in range(CONV):
        spread = dot(tail, tap_lanes(channels, CONV - 1 - lag, norm_at + 3), 1, 1)
        taps_ref[lag : lag + 1] = jnp.sum(jnp.where(mine, spread, 0.0), axis=0, keepdims=True)

    raw = dot(normed_ref[...], w_ref[:, tail_at:]).astype(BF16).astype(F32)
    raw = pltpu.roll(raw, lax.rem(HEAD - me * lane_of(heads, 0), HEAD), 1)
    lane = iota((1, HEAD), 1)
    rate, lift = jnp.zeros((1, HEAD), F32), jnp.zeros((1, HEAD), F32)
    for h in range(heads):
        here = lane == lane_of(h, NH)
        rate = jnp.where(here, -jnp.exp(jnp.zeros((1, HEAD), F32) + rates_ref[0, me * heads + h]), rate)
        lift = jnp.where(here, rates_ref[1, me * heads + h], lift)
    is_log = (lane % (NH + 1) == NH) & (lane < lane_of(heads, 0))
    lifted = raw + lift
    sig = jax.nn.sigmoid(lifted)
    logs = rate * (jnp.maximum(lifted, 0.0) + jnp.log1p(jnp.exp(-jnp.abs(lifted))))
    slope_ref[...] = jnp.where(is_log, rate * sig, sig * (1.0 - sig)) * (lane < HEAD // 2) + pltpu.roll(
        jnp.where(is_log, logs, 0.0), HEAD // 2, 1
    )
    place = (iota((8, HEAD), 1) == LINK + iota((8, HEAD), 0)) & (iota((8, HEAD), 0) < CONV - 1)
    links = dot(marks_ref[...].astype(BF16), place.astype(BF16), 0, 0)
    open_ = column(links, LINK)
    summed = jnp.where(is_log, logs * open_, jnp.where(lane == DOC, 1.0 - open_, 0.0))
    lower = (iota((BLOCK_LEN, BLOCK_LEN), 0) >= iota((BLOCK_LEN, BLOCK_LEN), 1)).astype(F32)
    spread = (iota((ROWS, BLOCK_LEN), 0) // NH == iota((ROWS, BLOCK_LEN), 1)).astype(F32)
    step = iota((ROWS, HEAD), 0) % NH
    for b in range(rows // BLOCK_LEN):
        span = slice(b * BLOCK_LEN, (b + 1) * BLOCK_LEN)
        sums = exact(lower, summed[span])
        tok = jnp.where(is_log | (lane == DOC), sums, jnp.where(lane < DOC, sig[span], links[span]))
        tok_ref[span] = tok
        wide = exact(spread, tok)
        first = wide
        for j in range(1, NH):
            first = jnp.where(step == j, pltpu.roll(wide, HEAD - j, 1), first)
        col = jnp.where(lane % (NH + 1) == 0, jnp.where(lane < lane_of(heads, 0), first, wide), wide)
        col_ref[b * ROWS : (b + 1) * ROWS] = col
        row_ref[b * 8 : (b + 1) * 8] = col.T[:8]


def fwd_kernel(
    heads, pieces, steps, per, span_pieces, norm_at,
    rates_ref, x_ref, halo_ref, full_ref, marks_ref, stage_ref, wo_ref,
    proj_ref, normed_ref, gate_ref, tok_ref, slope_ref, col_ref, row_ref, taps_ref, norms_ref,
    oloc_ref, carr_ref, sin_ref, mapsout_ref, conv_ref, q_ref, k_ref, v_ref, t_ref, kk_ref, at_ref, uw_ref, pl_ref,
    wgfull_ref, wufull_ref, wofull_ref,
    state, weave, maps, wgs, wus, wos, local_sem, line_send, line_recv, map_send, map_recv,
):
    step = pl.program_id(0)
    here = lax.axis_index("ctx")
    weights = Line(
        pieces, [lambda c: wgs.at[:, c], lambda c: wus.at[:, c], lambda c: wos.at[c]], line_send, line_recv
    )
    eye = (iota((HEAD, HEAD), 0) == iota((HEAD, HEAD), 1)).astype(F32)

    @pl.when(step == 0)
    def _():
        owned = [
            pltpu.make_async_copy(source, target, local_sem.at[n])
            for n, (source, target) in enumerate(
                [(stage_ref.at[:, 0], wgs.at[:, here]), (stage_ref.at[:, 1], wus.at[:, here]), (wo_ref, wos.at[here])]
            )
        ]
        for copy in owned:
            copy.start()
        barrier = pltpu.get_barrier_semaphore()
        pl.semaphore_wait(barrier, greet(line_neighbours(pieces), barrier))
        for copy in owned:
            copy.wait()
        weights.own()
        front_body(
            heads, norm_at, rates_ref, x_ref, halo_ref, full_ref, marks_ref,
            proj_ref, normed_ref, gate_ref, tok_ref, slope_ref, col_ref, row_ref, taps_ref, norms_ref,
        )
        for h in range(heads):
            state[h, :, :HEAD] = eye
            state[h, :, HEAD:] = jnp.zeros((HEAD, HEAD), F32)

    hops = [(d * 2 * steps) // (pieces // 2) - 1 for d in range(1, pieces // 2)]
    for distance, at in enumerate(hops, 1):
        if at < steps:
            pl.when(step == at)(lambda distance=distance: weights.hop(distance))

    items = [(j, h) for j in range(per) for h in range(heads)]
    cols = lambda h: slice(h * WIDE, (h + 1) * WIDE)
    span = lambda j, length=BLOCK_LEN: slice(j * length, (j + 1) * length)
    tables = []
    for j in range(per):
        block = step * per + j
        tables.append(
            (
                row_ref[pl.ds(pl.multiple_of(block * 8, 8), 8), :],
                col_ref[pl.ds(pl.multiple_of(block * ROWS, ROWS), ROWS), :],
                tok_ref[pl.ds(pl.multiple_of(block * BLOCK_LEN, BLOCK_LEN), BLOCK_LEN), :],
            )
        )
    acts = []
    for j, h in items:
        base = pl.multiple_of((step * per + j) * BLOCK_LEN, BLOCK_LEN)
        ext = proj_ref[pl.ds(base, BLOCK_LEN + HALO), cols(h)].astype(F32)
        conv = ext[HALO:] * taps_ref[0:1, cols(h)]
        for lag in range(1, CONV):
            conv = conv + column(tables[j][2], LINK + lag - 1) * lag_rows(ext, lag) * taps_ref[lag : lag + 1, cols(h)]
        conv_ref[span(j), cols(h)] = conv
        acts.append(conv * jax.nn.sigmoid(conv))
    queries, keys, values = [], [], []
    for n, act in enumerate(acts):
        unit = []
        for part in range(1 + NH):
            piece = act[:, part * HEAD : (part + 1) * HEAD]
            unit.append(piece * lax.rsqrt(jnp.sum(piece * piece, axis=1, keepdims=True) + NORM_EPS))
        queries.append(unit[0] * (1.0 / math.sqrt(HEAD)))
        for j in range(NH):
            weave[2 * n, pl.ds(j, BLOCK_LEN, NH), :] = unit[1 + j]
            weave[2 * n + 1, pl.ds(j, BLOCK_LEN, NH), :] = act[:, (1 + NH + j) * HEAD : (2 + NH + j) * HEAD]
    for n in range(len(items)):
        keys.append(weave[2 * n])
        values.append(weave[2 * n + 1])
    factors = [decays(*tables[j], h) for j, h in items]
    grams = [mm(jnp.concatenate([q, k], axis=0), k, 1, 1) for q, k in zip(queries, keys)]
    kks = [f[1] * g[BLOCK_LEN:] for f, g in zip(factors, grams)]
    attns = [f[2] * g[:BLOCK_LEN] for f, g in zip(factors, grams)]
    invs = unit_lower_inverses([f[0] * kk for f, kk in zip(factors, kks)])
    uws = [
        mm(inv, jnp.concatenate([f[0] * v, (f[0] * f[3]) * k], axis=1))
        for inv, f, v, k in zip(invs, factors, values, keys)
    ]
    auws = [mm(attn, uw) for attn, uw in zip(attns, uws)]
    nms = [mm(f[5] * k, uw, 0, 0) for f, k, uw in zip(factors, keys, uws)]
    for n, (j, h) in enumerate(items):
        before = state[h]
        f = factors[n]
        both = mm(
            jnp.concatenate([f[4] * queries[n] - auws[n][:, HEAD:], f[6] * eye - nms[n][:, HEAD:]], axis=0), before
        )
        hc = slice(h * HEAD, (h + 1) * HEAD)
        carr_ref[span(j), hc] = both[:BLOCK_LEN, :HEAD]
        oloc_ref[span(j), hc] = both[:BLOCK_LEN, HEAD:] + auws[n][:, :HEAD]
        state[h, :, :HEAD] = both[BLOCK_LEN:, :HEAD]
        state[h, :, HEAD:] = both[BLOCK_LEN:, HEAD:] + nms[n][:, :HEAD]
        q_ref[j, h] = queries[n]
        k_ref[j, h] = keys[n]
        v_ref[j, h] = values[n]
        t_ref[j, h] = invs[n]
        kk_ref[j, h] = kks[n]
        at_ref[j, h] = attns[n]
        uw_ref[j, h] = uws[n]
        pl_ref[j, h] = before

    @pl.when(step == steps - 1)
    def _():
        maps[here] = state[...].astype(BF16)
        line = Line(pieces, [lambda c: maps.at[c]], map_send, map_recv, reach=chips_within(span_pieces, pieces))
        line.own()
        for distance in range(1, line.reach + 1):
            line.hop(distance)
        line.finish()
        for distance in range(1, pieces // 2):
            if hops[distance - 1] >= steps:
                weights.hop(distance)

        def hop(k, states):
            return tuple(
                mm(maps[k, h, :, :HEAD], states[h]) + maps[k, h, :, HEAD:].astype(F32) for h in range(heads)
            )

        states = lax.fori_loop(jnp.maximum(here - span_pieces, 0), here, hop, tuple(jnp.zeros((HEAD, HEAD), F32) for _ in range(heads)))
        for h in range(heads):
            sin_ref[h] = states[h]

        def keep(k, carry):
            mapsout_ref[k] = maps[k, :, :, :HEAD]
            return carry

        lax.fori_loop(
            jnp.maximum(here - span_pieces, 0), jnp.minimum(here + span_pieces + 1, pieces), keep, 0
        )
        weights.finish()
        given = [
            pltpu.make_async_copy(source, target, local_sem.at[n])
            for n, (source, target) in enumerate([(wgs, wgfull_ref), (wus, wufull_ref), (wos, wofull_ref)])
        ]
        for copy in given:
            copy.start()
        for copy in given:
            copy.wait()


def recurrence_forward(heads, pieces, span_pieces, norm_at, rates, x_full, halo, weights, marks, stage, w_out):
    rows = x_full.shape[0]
    blocks = rows // BLOCK_LEN
    per = 2
    size = stage.shape[0]
    whole = lambda *dims: pl.BlockSpec(dims, lambda i: (0,) * len(dims))
    by_block = lambda *dims: pl.BlockSpec((per,) + dims, lambda i: (i,) + (0,) * len(dims))
    token = lambda cols: pl.BlockSpec((per * BLOCK_LEN, cols), lambda i: (i, 0))
    shape = lambda *dims: jax.ShapeDtypeStruct(dims, F32)
    low_shape = lambda *dims: jax.ShapeDtypeStruct(dims, BF16)
    hbm = pl.BlockSpec(memory_space=pltpu.HBM)
    vmem = pl.BlockSpec(memory_space=pltpu.VMEM)
    square = (heads, ROWS, HEAD)
    dma = pltpu.SemaphoreType.DMA
    side = (size, pieces, *stage.shape[2:])
    front = [
        low_shape(rows + HALO, heads * WIDE), low_shape(rows, D), shape(rows, heads * HEAD), shape(rows, HEAD),
        shape(rows, HEAD), shape(blocks * ROWS, HEAD), shape(blocks * 8, ROWS), shape(8, heads * WIDE), shape(8, D),
    ]
    return pl.pallas_call(
        functools.partial(fwd_kernel, heads, pieces, blocks // per, per, span_pieces, norm_at),
        grid=(blocks // per,),
        in_specs=[pl.BlockSpec(memory_space=pltpu.SMEM)] + [vmem] * 4 + [hbm] * 2,
        out_specs=[whole(*f.shape) for f in front] + [
            token(heads * HEAD), token(heads * HEAD), whole(heads, HEAD, HEAD), whole(pieces, heads, HEAD, HEAD),
            token(heads * WIDE),
            by_block(heads, BLOCK_LEN, HEAD), by_block(*square), by_block(*square), by_block(*square),
            by_block(*square), by_block(heads, BLOCK_LEN, ROWS), by_block(heads, ROWS, 2 * HEAD),
            by_block(heads, HEAD, 2 * HEAD), hbm, hbm, hbm,
        ],
        out_shape=front + [
            shape(rows, heads * HEAD), shape(rows, heads * HEAD), shape(heads, HEAD, HEAD),
            low_shape(pieces, heads, HEAD, HEAD), shape(rows, heads * WIDE),
            shape(blocks, heads, BLOCK_LEN, HEAD), shape(blocks, *square), shape(blocks, *square), shape(blocks, *square),
            shape(blocks, *square), shape(blocks, heads, BLOCK_LEN, ROWS), shape(blocks, heads, ROWS, 2 * HEAD),
            shape(blocks, heads, HEAD, 2 * HEAD),
            low_shape(*side), low_shape(*side), low_shape(pieces, *w_out.shape),
        ],
        scratch_shapes=[
            pltpu.VMEM((heads, HEAD, 2 * HEAD), F32), pltpu.VMEM((2 * heads * per, ROWS, HEAD), F32),
            pltpu.VMEM((pieces, heads, HEAD, 2 * HEAD), BF16),
            pltpu.VMEM(side, BF16), pltpu.VMEM(side, BF16), pltpu.VMEM((pieces, *w_out.shape), BF16),
            dma((3,)), dma((3, 3, pieces)), dma((3, pieces)), dma((1, 3, pieces)), dma((1, pieces)),
        ],
        compiler_params=pltpu.CompilerParams(
            vmem_limit_bytes=VMEM_LIMIT, collective_id=3, has_side_effects=True
        ),
        name="recurrence_forward",
    )(rates, x_full, halo, weights, marks, stage, w_out)


def middle_kernel(
    size, heads, token_total,
    x_ref, teach_ref, mask_ref, norms_ref, gain_ref, *streams_and_rest,
):
    streams, rest = streams_and_rest[:8], streams_and_rest[8:]
    middle_body(size, heads, token_total, x_ref, teach_ref, mask_ref, norms_ref, gain_ref, streams, *rest)


def middle_body(
    size, heads, token_total, x_ref, teach_ref, mask_ref, norms_ref, gain_ref, streams,
    final_ref, gmid_ref, ghead_ref, ggate_ref, cot_ref, ggain_ref, gnorm_ref, loss_ref,
    wheld, theld, outg_ref,
    oloc_ref, carr_ref, gate_ref, sin_ref, wout_ref, wg_ref, wu_ref, wd_ref, load_sem, heads_ref, mixed_ref,
    line_send, line_recv, wds, wide_ref, tall_ref, wtheirs, ttheirs, wcame, tcame,
    pair_send, pair_recv, sum_send, sum_recv,
    second, branch, low, sent, got, own, mid, gfin, gates, ups, hidden, ggates, gups, send_sem, recv_sem,
):
    me = lax.axis_index("seq")
    count = x_ref.shape[0]
    loads = [
        pltpu.make_async_copy(source, target, load_sem.at[n])
        for n, (source, target) in enumerate(
            zip(streams, (oloc_ref, carr_ref, gate_ref, sin_ref, wout_ref, wg_ref, wu_ref, wds.at[lax.axis_index("ctx")]))
        )
    ]
    for load in loads:
        load.start()
    pieces = 2 * wide_ref.shape[0]
    barrier = pltpu.get_barrier_semaphore()
    peers = [({"seq": partner(me, i, size)}, me >= 0) for i in range(1, size)]
    pl.semaphore_wait(barrier, greet(peers + line_neighbours(pieces), barrier))
    loads[7].wait()
    line = Line(pieces, [lambda c: wds.at[c]], line_send, line_recv)
    line.own()
    for load in loads[:5]:
        load.wait()
    norm = norms_ref[1:2, :]
    gain = gain_ref[...].astype(F32)

    def dot(a, b, ca=1, cb=0):
        return lax.dot_general(a, b, (((ca,), (cb,)), ((), ())), preferred_element_type=F32)

    def rows(q):
        return pl.ds(pl.multiple_of(q * count, count), count)

    def part_copy(phase, i):
        return pltpu.make_async_remote_copy(
            sent.at[phase, i - 1], got.at[phase, i - 1], send_sem.at[phase, i - 1], recv_sem.at[phase, i - 1],
            device_id={"seq": partner(me, i, size)}, device_id_type=MESH,
        )

    def block_copy(buffer, phase, i, owner):
        return pltpu.make_async_remote_copy(
            buffer.at[rows(owner)], buffer.at[rows(owner)], send_sem.at[phase, i - 1], recv_sem.at[phase, i - 1],
            device_id={"seq": partner(me, i, size)}, device_id_type=MESH,
        )

    def give_part(phase, i, part):
        @pl.when(i > 0)
        def _():
            sent[phase, i - 1] = part.astype(BF16)
            part_copy(phase, i).start()

        @pl.when(i == 0)
        def _():
            own[...] = part

    def take_parts(phase):
        def add(i, total):
            part_copy(phase, i).wait_recv()
            return total + got[phase, i - 1].astype(F32)

        return lax.fori_loop(1, size, add, own[...])

    relayed = size == 4

    def half_copy(buffer, phase, n, owner):
        part = pl.ds(pl.multiple_of(owner * count + (n - 1) * (count // 2), count // 2), count // 2)
        return pltpu.make_async_remote_copy(
            buffer.at[part], buffer.at[part], send_sem.at[phase, 1 + n], recv_sem.at[phase, 1 + n],
            device_id={"seq": partner(me, 3 - n, size)}, device_id_type=MESH,
        )

    def give_block(buffer, phase, value):
        buffer[rows(me)] = value
        for i in range(1, 3 if relayed else size):
            block_copy(buffer, phase, i, me).start()

    def take_block(buffer, phase, i):
        q = partner(me, i, size)
        if relayed:

            @pl.when(i == 1)
            def _():
                for n in (1, 2):
                    block_copy(buffer, phase, n, partner(me, n, size)).wait_recv()
                    half_copy(buffer, phase, n, partner(me, n, size)).start()

            @pl.when(i == 3)
            def _():
                for n in (1, 2):
                    half_copy(buffer, phase, n, q).wait_recv()

        else:
            pl.when(i > 0)(lambda: block_copy(buffer, phase, i, q).wait_recv())
        return q

    def block_left(buffer, phase):
        for i in range(1, 3 if relayed else size):
            block_copy(buffer, phase, i, me).wait_send()
        if relayed:
            for n in (1, 2):
                half_copy(buffer, phase, n, partner(me, n, size)).wait_send()

    def out_part(k, carry):
        i = size - 1 - k
        q = partner(me, i, size)
        for h in range(heads):
            hc = slice(h * HEAD, (h + 1) * HEAD)
            out = (oloc_ref[rows(q), hc] + mm(carr_ref[rows(q), hc], sin_ref[h])).astype(BF16)
            heads_ref[rows(q), hc] = out
            wide = out.astype(F32)
            gate = gate_ref[rows(q), hc]
            scaled = wide * lax.rsqrt(jnp.mean(wide * wide, axis=1, keepdims=True) + NORM_EPS) * gain
            mixed_ref[rows(q), hc] = (scaled * (gate * jax.nn.sigmoid(gate))).astype(BF16)
        give_part(0, i, dot(mixed_ref[rows(q)], wout_ref[...]))
        return carry

    lax.fori_loop(0, size, out_part, 0)
    hops = pieces // 2 - 1
    for distance in range(1, hops // 2 + 1):
        line.hop(distance)
    middle = x_ref[...].astype(F32) + take_parts(0)
    mid[...] = middle
    inv = lax.rsqrt(jnp.mean(middle * middle, axis=1, keepdims=True) + NORM_EPS)
    give_block(second, 3, (middle * inv * norm).astype(BF16))
    for load in loads[5:7]:
        load.wait()
    deep = wds.shape[1]
    for distance in range(hops // 2 + 1, hops):
        line.hop(distance)

    def take_down():
        line.hop(hops)
        line.finish()
        inner = pieces * deep
        wd_ref[inner:] = jnp.zeros((wd_ref.shape[0] - inner, D), BF16)
        for c in range(pieces):
            wd_ref[c * deep : (c + 1) * deep] = wds[c]

    def feed(i, carry):
        q = take_block(second, 3, i)
        here = second[rows(q)]
        gate = dot(here, wg_ref[...])
        up = dot(here, wu_ref[...])
        gates[rows(q)] = gate
        ups[rows(q)] = up
        hid = (gate * jax.nn.sigmoid(gate) * up).astype(BF16)
        hidden[rows(q)] = hid
        pl.when(i == 0)(take_down)
        give_part(1, i, dot(hid, wd_ref[...]))
        return carry

    lax.fori_loop(0, size, feed, 0)
    final = mid[...] + take_parts(1)
    final_ref[...] = final.astype(BF16)
    error = final - teach_ref[...].astype(F32)
    mask = jnp.broadcast_to(mask_ref[...].astype(F32), (count, count)).T[:, :1]
    weighted = mask * error
    loss_ref[...] = jnp.broadcast_to(
        jnp.sum(jnp.sum(weighted * error, axis=1, keepdims=True), axis=0, keepdims=True), loss_ref.shape
    )
    valid = jnp.maximum(jnp.sum(norms_ref[2:3, :], axis=1, keepdims=True), 1.0)
    grad_final = token_total / valid * weighted
    gfin[...] = grad_final
    give_block(branch, 4, grad_final.astype(BF16))

    def feed_back(i, carry):
        q = take_block(branch, 4, i)
        ghid = dot(branch[rows(q)], wd_ref[...], 1, 1)
        gate = gates[rows(q)]
        sig = jax.nn.sigmoid(gate)
        silu = gate * sig
        ggate = (ghid * ups[rows(q)] * (sig + silu * (1.0 - sig))).astype(BF16)
        gup = (ghid * silu).astype(BF16)
        ggates[rows(q)] = ggate
        gups[rows(q)] = gup
        give_part(2, i, dot(ggate, wg_ref[...], 1, 1) + dot(gup, wu_ref[...], 1, 1))
        return carry

    lax.fori_loop(0, size, feed_back, 0)
    held = D // (size * pieces)
    tall_ref[...] = jnp.zeros_like(tall_ref)
    grad = dot(hidden[...], branch[...], 0, 0)
    for c in range(pieces):
        tall_ref[c // 2, c % 2, :deep] = grad[c * deep : (c + 1) * deep].astype(BF16)
    parts = ((tall_ref, ttheirs, theld, tcame), (wide_ref, wtheirs, wheld, wcame))
    pairs = [
        Siblings([part], [theirs], [kept], pair_send.at[n], pair_recv.at[n])
        for n, (part, theirs, kept, _) in enumerate(parts)
    ]
    sums = [LineSum(pieces, [kept], [came], sum_send.at[n], sum_recv.at[n]) for n, (_, _, kept, came) in enumerate(parts)]
    pairs[0].start()
    for n, side in enumerate((ggates, gups)):
        grad = dot(second[...], side[...], 0, 0)
        for c in range(pieces):
            for r in range(size):
                first = (r * pieces + c) * held
                wide_ref[c // 2, c % 2, (n * size + r) * held : (n * size + r + 1) * held] = grad[
                    first : first + held
                ].astype(BF16)
    pairs[1].start()
    for pair, line_sum in zip(pairs, sums):
        pair.add()
        line_sum.round(0)
    gsecond = take_parts(2)
    middle = mid[...]
    inv = lax.rsqrt(jnp.mean(middle * middle, axis=1, keepdims=True) + NORM_EPS)
    unit = middle * inv
    gnorm_ref[...] = jnp.sum(gsecond * unit, axis=0, keepdims=True)
    down = gsecond * norm
    gmid = gfin[...] + inv * (down - unit * jnp.mean(down * unit, axis=1, keepdims=True))
    gmid_ref[...] = gmid
    give_block(low, 5, gmid.astype(BF16))
    ggain_ref[...] = jnp.zeros_like(ggain_ref)
    cot_ref[...] = jnp.zeros_like(cot_ref)

    def out_back(i, carry):
        q = take_block(low, 5, i)
        gmixed = dot(low[rows(q)], wout_ref[...], 1, 1)
        for h in range(heads):
            hc = slice(h * HEAD, (h + 1) * HEAD)
            x = heads_ref[rows(q), hc].astype(F32)
            gate = gate_ref[rows(q), hc]
            grad = gmixed[:, hc]
            inv = lax.rsqrt(jnp.mean(x * x, axis=1, keepdims=True) + NORM_EPS)
            sig = jax.nn.sigmoid(gate)
            silu = gate * sig
            unit = x * inv
            ggate_ref[rows(q), hc] = (grad * unit * gain * (sig + silu * (1.0 - sig))).astype(BF16)
            weighted = grad * silu
            ggain_ref[...] += jnp.sum(weighted * unit, axis=0, keepdims=True)
            down = weighted * gain
            ghead = (inv * (down - unit * jnp.mean(down * unit, axis=1, keepdims=True))).astype(BF16)
            ghead_ref[rows(q), hc] = ghead
            cot_ref[h] += mm(carr_ref[rows(q), hc], ghead, 0, 0)
        return carry

    out_back(0, 0)
    early = max(1, hops - 1)
    for r in range(1, early):
        for line_sum in sums:
            line_sum.round(r)
    lax.fori_loop(1, size, out_back, 0)
    grad = dot(mixed_ref[...], low[...], 0, 0)
    for c in range(pieces):
        outg_ref[c // 2, c % 2] = grad[c * held : (c + 1) * held].astype(BF16)
    for pair, line_sum in zip(pairs, sums):
        line_sum.settle(early)
        pair.left()
        for r in range(early):
            line_sum.left(r)

    for i in range(1, size):
        for phase in range(3):
            part_copy(phase, i).wait_send()
    for buffer, phase in ((second, 3), (branch, 4), (low, 5)):
        block_left(buffer, phase)


def middle_part(
    size, heads, pieces, token_total, x, teacher, mask, norms, gain, oloc, carr, gate_out, state_in, wout, wg, wu, wd
):
    count = x.shape[0]
    rows = count * size
    inner = wg.shape[1]
    held, deep = D // (size * pieces), wd.shape[0]
    chips = pieces // 2
    wide, tall = (2 * size * held, inner), (-(-deep // 16) * 16, D)
    vmem = pl.BlockSpec(memory_space=pltpu.VMEM)
    out = lambda dims, kind: jax.ShapeDtypeStruct(dims, kind)
    low = lambda *dims: pltpu.VMEM(dims, BF16)
    high = lambda *dims: pltpu.VMEM(dims, F32)
    dma = pltpu.SemaphoreType.DMA
    return pl.pallas_call(
        functools.partial(middle_kernel, size, heads, float(token_total)),
        in_specs=[vmem] * 5 + [pl.BlockSpec(memory_space=pltpu.HBM)] * 8,
        out_specs=[vmem] * 11,
        out_shape=[
            out((count, D), BF16), out((count, D), F32),
            out((rows, heads * HEAD), BF16), out((rows, heads * HEAD), BF16), out((heads, HEAD, HEAD), F32),
            out((1, HEAD), F32), out((1, D), F32), out((1, HEAD), F32),
            out((chips, 2 * size * held, inner), BF16), out((chips, -(-deep // 16) * 16, D), BF16),
            out((chips, 2, held, D), BF16),
        ],
        scratch_shapes=[
            high(rows, heads * HEAD), high(rows, heads * HEAD), high(rows, heads * HEAD), high(heads, HEAD, HEAD),
            low(*wout.shape), low(*wg.shape), low(*wu.shape), low(inner, D), dma((8,)),
            low(rows, heads * HEAD), low(rows, heads * HEAD), dma((1, 3, pieces)), dma((1, pieces)), low(pieces, *wd.shape),
            low(chips, 2, *wide), low(chips, 2, *tall), low(chips, *wide), low(chips, *tall), low(2, chips, *wide),
            low(2, chips, *tall), dma((2, 1)), dma((2, 1)), dma((2, 1, chips)), dma((2, 1, 2, chips)),
            low(rows, D), low(rows, D), low(rows, D), low(3, size - 1, count, D), low(3, size - 1, count, D),
            high(count, D), high(count, D), high(count, D), high(rows, inner), high(rows, inner), low(rows, inner),
            low(rows, inner), low(rows, inner), dma((6, size)), dma((6, size)),
        ],
        compiler_params=pltpu.CompilerParams(
            vmem_limit_bytes=VMEM_LIMIT, collective_id=1, has_side_effects=True
        ),
        name="middle_part",
    )(x, teacher, mask, norms, gain, oloc, carr, gate_out, state_in, wout, wg, wu, wd)


def bwd_kernel(
    heads, pieces, steps, per, begun, span_pieces, maps_ref, cot_ref, sin_ref, proj_ref, w_ref, rowp_ref, colp_ref, tokp_ref, slope_ref,
    go_ref, conv_ref, q_ref, k_ref, v_ref, t_ref, kk_ref, at_ref, uw_ref, pl_ref, wide_ref, tall_ref, outg_ref, normed_ref, ggate_ref,
    gproj_ref, fix_ref, gw_ref, gscal_ref, gsum_ref, widesum_ref, tallsum_ref, outsum_ref, gatesum_ref,
    dstate, weave, rim, last, cots, rim_in, wheld, theld, wcame, tcame,
    gateg, otheirs, gtheirs, oheld, gheld, ocame, gcame,
    cot_send, cot_recv, pair_send, pair_recv, early_send, early_recv, line_send, line_recv, rim_sem,
):
    step = pl.program_id(0)
    block = steps - 1 - step
    here = lax.axis_index("ctx")
    core = lax.rem(here, 2)
    early = [
        LineSum(pieces, [kept], [came], early_send.at[n], early_recv.at[n])
        for n, (kept, came) in enumerate(((theld, tcame), (wheld, wcame)))
    ]
    pair = Siblings([outg_ref, gateg], [otheirs, gtheirs], [oheld, gheld], pair_send, pair_recv)
    line = LineSum(pieces, [oheld, gheld], [ocame, gcame], line_send, line_recv)
    rounds = pieces // 2 - 1
    when_round = [min(steps - 1, 1 + (r * steps) // rounds) for r in range(rounds)]

    @pl.when(step == 0)
    def _():
        barrier = pltpu.get_barrier_semaphore()
        side = [({"ctx": here + 1}, (core == 1) & (here < pieces - 1)), ({"ctx": here - 1}, (core == 0) & (here > 0))]
        pl.semaphore_wait(barrier, greet(line_neighbours(pieces) + side, barrier))
        cots[here] = cot_ref[...].astype(BF16)
        spread = Line(
            pieces, [lambda c: cots.at[c]], cot_send, cot_recv, up=False, reach=chips_within(span_pieces, pieces)
        )
        spread.own()
        wheld[...] = wide_ref[...]
        theld[...] = tall_ref[...]
        grad = lax.dot_general(
            normed_ref[...], ggate_ref[...], (((0,), (0,)), ((), ())), preferred_element_type=F32
        )
        held, size = gateg.shape[3], gateg.shape[2]
        for c in range(pieces):
            for r in range(size):
                row = (r * pieces + c) * held
                gateg[c // 2, c % 2, r] = grad[row : row + held].astype(BF16)
        for distance in range(1, spread.reach + 1):
            spread.hop(distance)
        spread.finish()
        for one in early:
            one.launch(begun)
        pair.start()

        farthest = jnp.minimum(here + span_pieces, pieces - 1)

        def hop(i, states):
            k = farthest - i
            return tuple(
                mm(maps_ref[k, h], states[h], 0, 0) + cots[k, h].astype(F32) for h in range(heads)
            )

        found = lax.fori_loop(
            0, farthest - here, hop, tuple(jnp.zeros((HEAD, HEAD), F32) for _ in range(heads))
        )
        for h in range(heads):
            dstate[h] = found[h]
        rim[...] = jnp.zeros_like(rim)
        gw_ref[...] = jnp.zeros_like(gw_ref)
        gsum_ref[...] = jnp.zeros_like(gsum_ref)

    for r in range(begun + 1, rounds):
        at = min(steps - 1, 1 + ((r - begun) * (steps - 1)) // (rounds - begun))
        pl.when(step == at)(lambda r=r: [one.round(r) for one in early] and None)
    pl.when(step == 1)(pair.add)
    for r in range(rounds):
        pl.when(step == when_round[r])(lambda r=r: line.round(r))

    last_row = iota((ROWS, 1), 0) == ROWS - 1
    diagonal = iota((ROWS, ROWS), 0) == iota((ROWS, ROWS), 1)
    first_lane = lax.axis_index("seq") * lane_of(heads, 0)
    gscals = [[] for _ in range(per)]
    dnexts = {(per - 1, h): dstate[h] for h in range(heads)}
    rims = {(per - 1, h): rim[:, h * WIDE : (h + 1) * WIDE] for h in range(heads)}

    def item(j, h):
        n = j * heads + h
        span = slice(j * BLOCK_LEN, (j + 1) * BLOCK_LEN)
        rowp, colp = rowp_ref[j * 8 : (j + 1) * 8], colp_ref[j * ROWS : (j + 1) * ROWS]
        tokp, slope = tokp_ref[span], slope_ref[span]
        cols = slice(h * WIDE, (h + 1) * WIDE)
        hc = slice(h * HEAD, (h + 1) * HEAD)
        beta, decay, qdecay, carry, qcarry, dlast, clast = decays(rowp, colp, tokp, h)
        go = go_ref[span, hc]
        query, keys, values = q_ref[j, h], k_ref[j, h], v_ref[j, h]
        inv, kk, attn, uw = t_ref[j, h], kk_ref[j, h], at_ref[j, h], uw_ref[j, h]
        yield
        state = mm(pl_ref[j, h, :, :HEAD], sin_ref[h]) + pl_ref[j, h, :, HEAD:]
        yield
        both = mm(jnp.concatenate([keys, uw[:, HEAD:]], axis=0), state)
        ks = both[:ROWS]
        upd = uw[:, :HEAD] - both[ROWS:]
        dlocal = mm(attn, go, 0, 0)
        while (j, h) not in dnexts:
            yield
        dnext = dnexts[j, h]
        yield
        dupd = dlocal + dlast * mm(keys, dnext)
        yield
        dx = mm(inv, dupd, 0, 0)
        yield
        dv = beta * dx
        dy = -(carry * dv)
        go32 = go.astype(F32)
        dnexts[j - 1, h] = clast * dnext + mm(
            jnp.concatenate([qcarry * query, keys], axis=0), jnp.concatenate([go32, dy], axis=0), 0, 0
        )
        yield
        outer = mm(jnp.concatenate([go32, dx], axis=0), upd, 1, 1)
        dattn, da = outer[:BLOCK_LEN], -outer[BLOCK_LEN:]
        yield
        dkd = mm(upd, dnext, 1, 1)
        right = mm(jnp.concatenate([go32, dy], axis=0), state, 1, 1)
        gos = right[:BLOCK_LEN]
        yield
        e = beta * da * decay
        f = dattn * qdecay
        ef = jnp.concatenate([f, e], axis=0)
        efk = mm(ef, keys)
        dq = qcarry * gos + efk[:BLOCK_LEN]
        yield
        dk = (
            right[BLOCK_LEN:]
            + dlast * dkd
            + efk[BLOCK_LEN:]
            + mm(ef, jnp.concatenate([query, keys], axis=0), 0, 0)
        )
        weave[3 * n] = dk
        weave[3 * n + 1] = dv
        yield
        dakk = da * kk
        z1 = beta * dakk
        z2 = dattn * attn
        kept = dlast * (dkd * keys)
        below = jnp.sum(z1, axis=0, keepdims=True) + jnp.sum(z2, axis=0, keepdims=True)
        dbeta = jnp.sum(dx * (values - carry * ks) + dakk, axis=1, keepdims=True)
        tail = jnp.sum(
            jnp.sum(kept, axis=0, keepdims=True) + clast * jnp.sum(state * dnext, axis=0, keepdims=True),
            axis=1, keepdims=True,
        )
        dgrow = jnp.sum(z1 + dy * ks - kept - jnp.where(diagonal, below, 0.0), axis=1, keepdims=True)
        dgrow = dgrow + jnp.where(last_row, tail, 0.0)
        lane = iota((ROWS, HEAD), 1)
        weave[3 * n + 2] = jnp.where(lane == 0, dbeta, dgrow)
        yield
        by_step = [weave[3 * n + 2, pl.ds(i, BLOCK_LEN, NH), :] for i in range(NH)]
        dg = sum(x[:, 1:2] for x in by_step) + jnp.sum(z2 + qcarry * (query * gos), axis=1, keepdims=True)
        after = (iota((BLOCK_LEN, BLOCK_LEN), 0) <= iota((BLOCK_LEN, BLOCK_LEN), 1)).astype(BF16)
        dlog = column(tokp, LINK) * mm(after, jnp.broadcast_to(dg, (BLOCK_LEN, HEAD)))[:, :1]
        dscal = [by_step[i][:, 0:1] * column(slope, lane_of(h, i)) for i in range(NH)]
        dscal.append(dlog * column(slope, lane_of(h, NH)))
        lane = iota((BLOCK_LEN, HEAD), 1)
        for i in range(NH + 1):
            gscals[j].append(jnp.where(lane == first_lane + lane_of(h, i), dscal[i], 0.0))
        logs = column(slope, HEAD // 2 + lane_of(h, NH))
        sums = jnp.where(lane == 0, dlog * logs, jnp.where(lane == 1, dscal[NH], 0.0))
        gsum_ref[h : h + 1, :] += jnp.sum(sums, axis=0, keepdims=True)
        yield
        conv = conv_ref[span, cols]
        sig = jax.nn.sigmoid(conv)
        act = conv * sig
        parts = []
        for part in range(1 + NH):
            piece = act[:, part * HEAD : (part + 1) * HEAD]
            scale = lax.rsqrt(jnp.sum(piece * piece, axis=1, keepdims=True) + NORM_EPS)
            if part:
                grad = weave[3 * n, pl.ds(part - 1, BLOCK_LEN, NH), :]
            else:
                grad = dq * (1.0 / math.sqrt(HEAD))
            unit = piece * scale
            parts.append(scale * (grad - unit * jnp.sum(grad * unit, axis=1, keepdims=True)))
        for i in range(NH):
            parts.append(weave[3 * n + 1, pl.ds(i, BLOCK_LEN, NH), :])
        dconv = jnp.concatenate(parts, axis=1) * (sig * (1.0 + conv * (1.0 - sig)))
        yield
        base = pl.multiple_of((block * per + j) * BLOCK_LEN, BLOCK_LEN)
        ext = proj_ref[pl.ds(base, BLOCK_LEN + HALO), cols].astype(F32)
        gw_ref[0:1, cols] += jnp.sum(dconv * ext[HALO:], axis=0, keepdims=True)
        zeros = jnp.zeros((8, WIDE), F32)
        length = BLOCK_LEN + 8
        total = jnp.concatenate([zeros, dconv * w_ref[0:1, cols]], axis=0)
        for lag in range(1, CONV):
            masked = column(tokp, LINK + lag - 1) * dconv
            gw_ref[lag : lag + 1, cols] += jnp.sum(masked * lag_rows(ext, lag), axis=0, keepdims=True)
            total = total + pltpu.roll(
                jnp.concatenate([zeros, masked * w_ref[lag : lag + 1, cols]], axis=0), length - lag, 0
            )
        rims[j - 1, h] = total[:8]
        fixed = total[length - 8 :] + rims[j, h]
        gproj_ref[span, cols] = jnp.concatenate([total[8 : length - 8], fixed], axis=0).astype(BF16)
        if j == per - 1:

            @pl.when(step == 0)
            def _():
                last[:, cols] = fixed

    running = [item(j, h) for j in reversed(range(per)) for h in range(heads)]
    while running:
        running = [one for one in running if next(one, "done") != "done"]
    for h in range(heads):
        dstate[h] = dnexts[-1, h]
        rim[:, h * WIDE : (h + 1) * WIDE] = rims[-1, h]
    for j in range(per):
        gscal_ref[j * BLOCK_LEN : (j + 1) * BLOCK_LEN] = sum(gscals[j]).astype(BF16)

    @pl.when(step == steps - 1)
    def _():
        passing = pltpu.make_async_remote_copy(
            rim, rim_in, rim_sem.at[0], rim_sem.at[1], device_id={"ctx": here - 1}, device_id_type=MESH
        )
        pl.when(here > 0)(passing.start)
        fix_ref[...] = last[...].astype(BF16)

        @pl.when(here < pieces - 1)
        def _():
            passing.wait_recv()
            fix_ref[...] = (last[...] + rim_in[...]).astype(BF16)

        for one in early:
            one.finish()
        line.finish()
        widesum_ref[...] = wheld[here // 2]
        tallsum_ref[...] = theld[here // 2].astype(F32)
        outsum_ref[...] = oheld[here // 2].astype(F32)
        gatesum_ref[...] = gheld[here // 2]
        pair.left()
        for r in range(begun, rounds):
            for one in early:
                one.left(r)
        for r in range(rounds):
            line.left(r)
        pl.when(here > 0)(passing.wait_send)


def recurrence_backward(
    maps, cot, state_in, proj_ext, conv_w, rowp, colp, tokp, slopes, grad_heads, saved, wide, tall, outg, normed, ggate,
    heads, pieces, span_pieces,
):
    rows = tokp.shape[0]
    blocks = rows // BLOCK_LEN
    chips = pieces // 2
    per = 2
    final = blocks // per - 1
    whole = lambda *dims: pl.BlockSpec(dims, lambda i: (0,) * len(dims))
    by_block = lambda *dims: pl.BlockSpec((per,) + dims, lambda i: (final - i,) + (0,) * len(dims))
    token = lambda cols: pl.BlockSpec((per * BLOCK_LEN, cols), lambda i: (final - i, 0))
    shape = lambda *dims: jax.ShapeDtypeStruct(dims, F32)
    low_shape = lambda *dims: jax.ShapeDtypeStruct(dims, BF16)
    vmem = pl.BlockSpec(memory_space=pltpu.VMEM)
    low = lambda *dims: pltpu.VMEM(dims, BF16)
    square = (heads, ROWS, HEAD)
    wide_chunk, tall_chunk, out_chunk = wide.shape[1:], tall.shape[1:], outg.shape[2:]
    gate_chunk = (HEADS // heads, out_chunk[0], ggate.shape[1])
    dma = pltpu.SemaphoreType.DMA
    return pl.pallas_call(
        functools.partial(bwd_kernel, heads, pieces, blocks // per, per, max(1, chips - 2), span_pieces),
        grid=(blocks // per,),
        in_specs=[
            vmem, vmem, vmem, vmem, vmem,
            pl.BlockSpec((per * 8, ROWS), lambda i: (final - i, 0)),
            pl.BlockSpec((per * ROWS, HEAD), lambda i: (final - i, 0)), token(HEAD), token(HEAD),
            token(heads * HEAD), token(heads * WIDE),
            by_block(heads, BLOCK_LEN, HEAD), by_block(*square), by_block(*square), by_block(*square),
            by_block(*square), by_block(heads, BLOCK_LEN, ROWS), by_block(heads, ROWS, 2 * HEAD),
            by_block(heads, HEAD, 2 * HEAD), vmem, vmem, vmem, vmem, vmem,
        ],
        out_specs=[
            token(heads * WIDE), whole(8, heads * WIDE), whole(8, heads * WIDE), token(HEAD), whole(8, HEAD),
            whole(*wide_chunk), whole(*tall_chunk), whole(*out_chunk), whole(*gate_chunk),
        ],
        out_shape=[
            low_shape(rows, heads * WIDE), low_shape(8, heads * WIDE), shape(8, heads * WIDE), low_shape(rows, HEAD),
            shape(8, HEAD), low_shape(*wide_chunk), shape(*tall_chunk), shape(*out_chunk), low_shape(*gate_chunk),
        ],
        scratch_shapes=[
            pltpu.VMEM((heads, HEAD, HEAD), F32), pltpu.VMEM((3 * heads * per, ROWS, HEAD), F32),
            pltpu.VMEM((8, heads * WIDE), F32), pltpu.VMEM((8, heads * WIDE), F32),
            pltpu.VMEM((pieces, heads, HEAD, HEAD), BF16), pltpu.VMEM((8, heads * WIDE), F32),
            low(chips, *wide_chunk), low(chips, *tall_chunk), low(2, chips, *wide_chunk), low(2, chips, *tall_chunk),
            low(chips, 2, *gate_chunk), low(chips, *out_chunk), low(chips, *gate_chunk), low(chips, *out_chunk),
            low(chips, *gate_chunk), low(2, chips, *out_chunk), low(2, chips, *gate_chunk),
            dma((1, 3, pieces)), dma((1, pieces)), dma((2,)), dma((2,)), dma((2, 1, chips)), dma((2, 1, 2, chips)),
            dma((2, chips)), dma((2, 2, chips)), dma((2,)),
        ],
        compiler_params=pltpu.CompilerParams(
            vmem_limit_bytes=VMEM_LIMIT, collective_id=4, has_side_effects=True
        ),
        name="recurrence_backward",
    )(maps, cot, state_in, proj_ext, conv_w, rowp, colp, tokp, slopes, grad_heads, *saved, wide, tall, outg, normed, ggate)


def final_kernel(
    size, pieces, heads, norm_at, inner, gp_any, gg_any, gs_any, w_any, normed_any,
    fix_ref, x_ref, gmid_ref, norms_ref, gw_ref, gain_ref, gsum_ref, loss_ref, gnorm_ref, wide_ref, gatesum_ref,
    ingrad_ref, gmix_ref, ggate_ref, gtail_ref, gwg_ref, gwu_ref, mean_ref, ends_ref, both_ref,
    gp_ref, gg_ref, gs_ref, w_ref, normed_ref, load_sem, wideout_ref, gateout_ref,
    sent, got, whole, turned, *halves_and_rest,
):
    grads, theirs, helds, cames, blocks = [halves_and_rest[2 * n : 2 * n + 2] for n in range(5)]
    around, along, summed, *sems = halves_and_rest[10:]
    final_body(
        size, pieces, heads, norm_at, inner, gp_any, gg_any, gs_any, w_any, normed_any,
        fix_ref, x_ref, gmid_ref, norms_ref, gw_ref, gain_ref, gsum_ref, loss_ref, gnorm_ref, wide_ref, gatesum_ref,
        ingrad_ref, gmix_ref, ggate_ref, gtail_ref, gwg_ref, gwu_ref, mean_ref, ends_ref, both_ref,
        gp_ref, gg_ref, gs_ref, w_ref, normed_ref, load_sem, wideout_ref, gateout_ref,
        sent, got, whole, turned, grads, theirs, helds, cames, blocks, around, along, summed, *sems,
    )


def final_body(
    size, pieces, heads, norm_at, inner, gp_any, gg_any, gs_any, w_any, normed_any,
    fix_ref, x_ref, gmid_ref, norms_ref, gw_ref, gain_ref, gsum_ref, loss_ref, gnorm_ref, wide_ref, gatesum_ref,
    ingrad_ref, gmix_ref, ggate_ref, gtail_ref, gwg_ref, gwu_ref, mean_ref, ends_ref, both_ref,
    gp_ref, gg_ref, gs_ref, w_ref, normed_ref, load_sem, wideout_ref, gateout_ref,
    sent, got, whole, turned, grads, theirs, helds, cames, blocks, around, along, summed,
    local_sem, seq_send, seq_recv, pair_send, pair_recv, line_send, line_recv, ctx_send, ctx_recv,
):
    me, here = lax.axis_index("seq"), lax.axis_index("ctx")
    count = x_ref.shape[0]
    loads = [
        pltpu.make_async_copy(source, target, load_sem.at[n])
        for n, (source, target) in enumerate(
            [(gp_any, gp_ref), (gg_any, gg_ref), (gs_any, gs_ref), (w_any, w_ref), (normed_any, normed_ref)]
        )
    ]
    for load in loads:
        load.start()
    barrier = pltpu.get_barrier_semaphore()
    peers = [({"seq": partner(me, i, size)}, here >= 0) for i in range(1, size)]
    peers += [({"ctx": lax.rem(here + i, pieces)}, here >= 0) for i in range(1, pieces)]
    pl.semaphore_wait(barrier, greet(peers, barrier))

    def dot(a, b, ca=1, cb=0):
        return lax.dot_general(a, b, (((ca,), (cb,)), ((), ())), preferred_element_type=F32)

    def rows(q):
        return pl.ds(pl.multiple_of(q * count, count), count)

    def to_peer(n, i):
        q = partner(me, i, size)
        source, target = [
            (sent.at[i - 1], got.at[i - 1]), (wide_ref.at[:, q], wideout_ref.at[me]),
            (around.at[me], around.at[me]), (helds[0].at[here // 2, q], blocks[0].at[me]),
            (gatesum_ref.at[q], gateout_ref.at[me]), (helds[1].at[here // 2, q], blocks[1].at[me]),
        ][n]
        return pltpu.make_async_remote_copy(
            source, target, seq_send.at[n, i - 1], seq_recv.at[n, i - 1], device_id={"seq": q}, device_id_type=MESH
        )

    def to_piece(i):
        return pltpu.make_async_remote_copy(
            along.at[here], along.at[here], ctx_send.at[i - 1], ctx_recv.at[i - 1],
            device_id={"ctx": lax.rem(here + i, pieces)}, device_id_type=MESH,
        )

    gate_at, tail_at = gp_ref.shape[1], gp_ref.shape[1] + gg_ref.shape[1]
    for load in loads:
        load.wait()
    gp_ref[gp_ref.shape[0] - 8 :] = fix_ref[...]

    def parts():
        for first in range(0, D, 256):
            tile = slice(first, first + 256)
            value = (
                dot(gp_ref[...], w_ref[tile, :gate_at], 1, 1)
                + dot(gg_ref[...], w_ref[tile, gate_at:tail_at], 1, 1)
                + dot(gs_ref[...], w_ref[tile, tail_at:], 1, 1)
            )
            whole[:, tile] = value

        def give(k, carry):
            i = size - 1 - k
            sent[i - 1] = whole[rows(partner(me, i, size))].astype(BF16)
            pltpu.make_async_remote_copy(
                sent.at[i - 1], got.at[i - 1], seq_send.at[0, i - 1], seq_recv.at[0, i - 1],
                device_id={"seq": partner(me, i, size)}, device_id_type=MESH,
            ).start()
            return carry

        lax.fori_loop(0, size - 1, give, 0)

    turned[...] = normed_ref[...].T
    rank_rows = D // (size * pieces)
    pairs = [Siblings([grads[n]], [theirs[n]], [helds[n]], pair_send.at[n], pair_recv.at[n]) for n in range(2)]
    lines = [LineSum(pieces, [helds[n]], [cames[n]], line_send.at[n], line_recv.at[n]) for n in range(2)]
    split = grads[0].shape[4]

    def gradient(source, first, cols, n, at):
        grad = dot(turned[...], source[:, first : first + cols])
        for r in range(size):
            for c in range(pieces):
                row = (r * pieces + c) * rank_rows
                grads[n][c // 2, c % 2, r, :, at : at + cols] = grad[row : row + rank_rows].astype(BF16)

    for first in range(0, split, 256):
        gradient(gp_ref, first, min(256, split - first), 0, first)
    pairs[0].start()
    for first in range(split, gate_at, 256):
        gradient(gp_ref, first, min(256, gate_at - first), 1, first - split)
    gradient(gs_ref, 0, HEAD, 1, gate_at - split)
    channels = gw_ref.shape[1]
    mine = channel_rows(D // size, channels)
    taps = jnp.zeros((D // size, HEAD), F32)
    for lag in range(CONV):
        spread = jnp.where(mine, gw_ref[lag : lag + 1], 0.0).astype(BF16)
        taps = taps + dot(spread, tap_lanes(channels, CONV - 1 - lag, norm_at + 3))
    for c in range(pieces):
        grads[1][c // 2, c % 2, me, :, gate_at - split :] = (
            grads[1][c // 2, c % 2, me, :, gate_at - split :].astype(F32) + taps[c * rank_rows : (c + 1) * rank_rows]
        ).astype(BF16)
    pairs[1].start()
    pairs[0].add()
    lines[0].round(0)
    parts()
    pairs[1].add()
    lines[1].round(0)
    rounds = pieces // 2 - 1
    for r in range(1, rounds - 1):
        for line in lines:
            line.round(r)
    for i in range(1, size):
        to_peer(0, i).wait_recv()
    gnormed = whole[rows(me)]
    for i in range(1, size):
        gnormed = gnormed + got[i - 1].astype(F32)
    x = x_ref[...].astype(F32)
    inv = lax.rsqrt(jnp.mean(x * x, axis=1, keepdims=True) + NORM_EPS)
    unit = x * inv
    down = gnormed * norms_ref[0:1, :]
    ingrad_ref[...] = gmid_ref[...] + inv * (down - unit * jnp.mean(down * unit, axis=1, keepdims=True))
    term = jnp.sum(gnormed * unit, axis=0, keepdims=True)
    lane = iota((1, HEAD), 1)
    ends = jnp.where(lane == 2 * HEADS, loss_ref[...], 0.0)
    for h in range(heads):
        for n in range(2):
            ends = jnp.where(lane == n * HEADS + me * heads + h, gsum_ref[h : h + 1, n : n + 1], ends)
    around[me] = jnp.zeros(around.shape[1:], F32)
    around[me, 0:1] = gain_ref[...]
    around[me, 1:2] = ends
    for j in range(D // HEAD):
        around[me, 8 + j : 9 + j] = term[:, j * HEAD : (j + 1) * HEAD]
        around[me, 8 + D // HEAD + j : 9 + D // HEAD + j] = gnorm_ref[:, j * HEAD : (j + 1) * HEAD]
    for i in range(1, size):
        to_peer(2, i).start()
    kept = [
        pltpu.make_async_copy(wide_ref.at[:, me], wideout_ref.at[me], local_sem.at[0]),
        pltpu.make_async_copy(gatesum_ref.at[me], gateout_ref.at[me], local_sem.at[1]),
    ]
    for copy in kept:
        copy.start()
    for i in reversed(range(1, size)):
        to_peer(1, i).start()
        to_peer(4, i).start()
    for line in lines:
        line.round(rounds - 1)
    for i in range(1, size):
        to_peer(2, i).wait_recv()
    mine = around[0]
    for r in range(1, size):
        mine = mine + around[r]
    along[here] = mine
    for i in range(1, pieces):
        to_piece(i).start()
    for n, phase in ((0, 3), (1, 5)):
        lines[n].finish()
        blocks[n][me] = helds[n][here // 2, me]
        for i in reversed(range(1, size)):
            to_peer(phase, i).start()
    for i in range(1, pieces):
        to_piece(i).wait_recv()
    total = along[0]
    for c in range(1, pieces):
        total = total + along[c]
    ends_ref[...] = total[:2]
    valid = jnp.maximum(jnp.sum(norms_ref[2:3, :], axis=1, keepdims=True), 1.0)
    mean_ref[...] = total[1:2, 2 * HEADS : 2 * HEADS + 1] / (D * valid)
    summed[...] = total
    place = (me * pieces + here) * rank_rows
    for n in range(2):
        row = summed[pl.ds(8 + n * (D // HEAD) + place // HEAD, 1), :]
        both_ref[n : n + 1, :] = pltpu.roll(row, lax.rem(HEAD - lax.rem(place, HEAD), HEAD), 1)
    tail = jnp.zeros((rank_rows, HEAD), F32)
    for copy in kept:
        copy.wait()
    for i in range(1, size):
        for n in (1, 4, 3):
            to_peer(n, i).wait_recv()
    wide_cols = tail_at - gate_at
    for r in range(size):
        gwg_ref[:, r * inner : (r + 1) * inner] = wideout_ref[r, 0, :, :inner].astype(F32)
        gwu_ref[:, r * inner : (r + 1) * inner] = wideout_ref[r, 1, :, :inner].astype(F32)
        ggate_ref[:, r * wide_cols : (r + 1) * wide_cols] = gateout_ref[r].astype(F32)
        gmix_ref[:, r * gate_at : r * gate_at + split] = blocks[0][r].astype(F32)
    for i in range(1, size):
        to_peer(5, i).wait_recv()
    for r in range(size):
        block = blocks[1][r].astype(F32)
        gmix_ref[:, r * gate_at + split : (r + 1) * gate_at] = block[:, : gate_at - split]
        tail = tail + block[:, gate_at - split :]
    gtail_ref[...] = tail
    for pair in pairs:
        pair.left()
    for line in lines:
        for r in range(pieces // 2 - 1):
            line.left(r)
    for i in range(1, size):
        for n in range(6):
            to_peer(n, i).wait_send()
    for i in range(1, pieces):
        to_piece(i).wait_send()


def final_part(
    size, pieces, heads, norm_at, gp, gg, gs, weights, normed, fix, x, gmid, norms, gw, gain, gsum, loss, gnorm, wide,
    gatesum,
):
    count = x.shape[0]
    chips = pieces // 2
    held, inner = D // (size * pieces), FF // size
    split = WIDE if heads > 1 else 3 * HEAD
    widths = (split, gp.shape[1] - split + gs.shape[1])
    small = (8 + 2 * (D // HEAD), HEAD)
    vmem = pl.BlockSpec(memory_space=pltpu.VMEM)
    out = lambda *dims: jax.ShapeDtypeStruct(dims, F32)
    low = lambda *dims: pltpu.VMEM(dims, BF16)
    high = lambda *dims: pltpu.VMEM(dims, F32)
    dma = pltpu.SemaphoreType.DMA
    return pl.pallas_call(
        functools.partial(final_kernel, size, pieces, heads, norm_at, inner),
        in_specs=[pl.BlockSpec(memory_space=pltpu.HBM)] * 5 + [vmem] * 11,
        out_specs=[vmem] * 9,
        out_shape=[
            out(count, D), out(held, size * gp.shape[1]), out(held, size * gg.shape[1]), out(held, HEAD),
            out(held, size * inner), out(held, size * inner), out(1, 1), out(2, HEAD), out(2, HEAD),
        ],
        scratch_shapes=[
            low(*gp.shape), low(*gg.shape), low(*gs.shape), low(*weights.shape), low(*normed.shape), dma((5,)),
            low(size, 2, held, wide.shape[3]), low(*gatesum.shape),
            low(size - 1, count, D), low(size - 1, count, D), high(size * count, D), low(D, normed.shape[0]),
            *[low(chips, 2, size, held, w) for w in widths], *[low(chips, size, held, w) for w in widths],
            *[low(chips, size, held, w) for w in widths], *[low(2, chips, size, held, w) for w in widths],
            *[low(size, held, w) for w in widths], high(size, *small), high(pieces, *small), high(*small),
            dma((2,)), dma((6, size - 1)), dma((6, size - 1)), dma((2, 1)), dma((2, 1)), dma((2, 1, chips)),
            dma((2, 1, 2, chips)),
            dma((pieces - 1,)), dma((pieces - 1,)),
        ],
        compiler_params=pltpu.CompilerParams(
            vmem_limit_bytes=VMEM_LIMIT, collective_id=5, has_side_effects=True
        ),
        name="final_part",
    )(gp, gg, gs, weights, normed, fix, x, gmid, norms, gw, gain, gsum, loss, gnorm, wide, gatesum)


def finish_kernel(
    scal_cols, taps_at, final_ref, ingrad_ref, gmix_ref, ggate_ref, gwg_ref, gwu_ref, tall_ref, outsum_ref,
    tail_ref, ends_ref, both_ref,
    final_out, ingrad_out, gmix_out, ggate_out, gwg_out, gwu_out, gwd_out, gout_out,
    gscal_out, gconv_out, norma_out, normm_out, gain_out, alog_out, dt_out,
):
    for source, target in (
        (final_ref, final_out), (ingrad_ref, ingrad_out), (gmix_ref, gmix_out), (ggate_ref, ggate_out),
        (gwg_ref, gwg_out), (gwu_ref, gwu_out), (outsum_ref, gout_out),
    ):
        target[...] = source[...]
    gwd_out[...] = tall_ref[: gwd_out.shape[0]]
    tail = tail_ref[...]
    rows, channels = tail.shape[0], gconv_out.shape[1]
    square = jnp.concatenate([tail, jnp.zeros((HEAD - rows, HEAD), F32)], axis=0)
    gscal_out[...] = square.T[:scal_cols, :rows]
    mine = channel_rows(rows, channels)
    for tap in range(CONV):
        spread = exact(tail, tap_lanes(channels, tap, taps_at).astype(F32), 1, 1)
        gconv_out[tap : tap + 1] = jnp.sum(jnp.where(mine, spread, 0.0), axis=0, keepdims=True)
    held = norma_out.shape[1]
    norma_out[...] = both_ref[0:1, :held]
    normm_out[...] = both_ref[1:2, :held]
    gain_out[...] = ends_ref[0:1, :]
    alog_out[...] = ends_ref[1:2, :HEADS]
    dt_out[...] = ends_ref[1:2, HEADS : 2 * HEADS]


def finish_part(scal_cols, taps_at, deep, channels, *parts):
    vmem = pl.BlockSpec(memory_space=pltpu.VMEM)
    held = parts[2].shape[0]
    out = lambda dims, kind=F32: jax.ShapeDtypeStruct(dims, kind)
    return pl.pallas_call(
        functools.partial(finish_kernel, scal_cols, taps_at),
        in_specs=[vmem] * 11,
        out_specs=[vmem] * 15,
        out_shape=[out(p.shape, p.dtype) for p in parts[:6]] + [
            out((deep, D)), out(parts[7].shape), out((scal_cols, held)), out((CONV, channels)),
            out((1, held)), out((1, held)), out((1, HEAD)), out((1, HEADS)), out((1, HEADS)),
        ],
        compiler_params=pltpu.CompilerParams(vmem_limit_bytes=VMEM_LIMIT),
        name="finish_part",
    )(*parts)


def local(
    block_input, teacher, valid_mask, segments, mix_proj, scalar_proj, gate_proj, out_proj, conv_weight,
    norm_attn, norm_mlp, head_gain, a_log, dt_bias, w_gate, w_up, w_down,
):
    seq_size, pieces = lax.axis_size("seq"), lax.axis_size("ctx")
    heads = HEADS // seq_size
    rows = block_input.shape[0] * seq_size
    token_total = segments.shape[0]
    seq_length = min(SEQ_LEN, token_total)
    span_pieces = min(pieces, (MOST_DOC.get(token_total, token_total) - 2) // rows + 1)
    index = lax.axis_index("ctx")
    held = mix_proj.shape[0]
    scal_cols = HEADS * (NH + 1)
    norm_at, taps_at = scal_cols, scal_cols + 3

    x_full, halo, gathered, stage = start_gather(
        seq_size, pieces, norm_at, block_input, mix_proj, gate_proj, scalar_proj.T, norm_attn[None, :],
        norm_mlp[None, :], conv_weight.T, valid_mask[None, :], w_gate, w_up,
    )
    weights = gathered.reshape(D, -1)
    piece_start = index * rows
    window = lax.dynamic_slice_in_dim(jnp.pad(segments, (CONV, 0)), piece_start, rows + CONV)
    place_in = (piece_start + jnp.arange(rows, dtype=jnp.int32)) % seq_length
    marks = jnp.stack(
        [
            ((window[CONV - lag : CONV - lag + rows] == window[CONV:]) & (place_in >= lag)).astype(F32)
            if lag < CONV
            else jnp.zeros((rows,), F32)
            for lag in range(1, 9)
        ]
    )
    rates = jnp.stack([a_log.astype(F32), dt_bias.astype(F32)])
    (
        proj_ext, normed, gate_out, tokp, slopes, colp, rowp, conv_w, norms,
        oloc, carr, state_in, maps, *saved, wg_full, wu_full, wo_full,
    ) = recurrence_forward(heads, pieces, span_pieces, norm_at, rates, x_full, halo, weights, marks, stage, out_proj)
    (
        final_out, grad_middle, grad_heads, grad_gate_out, cot, gain_term, norm_mlp_term, loss, wide, tall, outg,
    ) = middle_part(
        seq_size, heads, pieces, token_total, block_input, teacher, valid_mask[None, :], norms, head_gain[None, :],
        oloc, carr, gate_out, state_in, wo_full.reshape(heads * HEAD, D), wg_full.reshape(D, -1),
        wu_full.reshape(D, -1), w_down,
    )
    grad_proj, fixed_rows, gw, grad_scal, gsum, wide_sum, tall_sum, out_sum, gate_sum = recurrence_backward(
        maps, cot, state_in, proj_ext, conv_w, rowp, colp, tokp, slopes, grad_heads, saved, wide, tall, outg, normed,
        grad_gate_out, heads, pieces, span_pieces,
    )
    input_grad, mix_grad, gate_grad, tail_grad, wg_grad, wu_grad, mean_loss, ends, norm_grads = final_part(
        seq_size, pieces, heads, norm_at, grad_proj, grad_gate_out, grad_scal, weights, normed, fixed_rows, block_input,
        grad_middle, norms, gw, gain_term, gsum, loss, norm_mlp_term, wide_sum.reshape(2, seq_size, held, -1),
        gate_sum,
    )
    (
        final_out, input_grad, mix_grad, gate_grad, wg_grad, wu_grad, wd_grad, out_grad,
        scal_grad, conv_grad, norm_a_grad, norm_m_grad, gain_grad, alog_grad, dt_grad,
    ) = finish_part(
        scal_cols, taps_at, w_down.shape[0], conv_weight.shape[0],
        final_out, input_grad, mix_grad, gate_grad, wg_grad, wu_grad, tall_sum, out_sum, tail_grad, ends, norm_grads,
    )
    return (
        final_out, mean_loss[0, 0], input_grad, mix_grad, scal_grad.T, gate_grad, out_grad, conv_grad.T,
        norm_a_grad.reshape(-1), norm_m_grad.reshape(-1), gain_grad.reshape(-1), alog_grad.reshape(-1),
        dt_grad.reshape(-1), wg_grad, wu_grad, wd_grad,
    )


def solution(mesh):
    tokens, vector, matrix = P(("ctx", "seq"), None), P(BOTH), P(BOTH, None)
    in_specs = (
        tokens, tokens, P(("ctx", "seq")), P(), matrix, matrix, matrix, matrix, matrix, vector, vector,
        P(), P(), P(), matrix, matrix, matrix,
    )
    out_specs = (
        tokens, P(), tokens, matrix, matrix, matrix, matrix, matrix, vector, vector, P(), P(), P(),
        matrix, matrix, matrix,
    )
    return jax.shard_map(local, mesh=mesh, in_specs=in_specs, out_specs=out_specs, check_vma=False)
```

```python
import functools
import math

import jax
import jax.numpy as jnp
from jax import lax
from jax.experimental import pallas as pl
from jax.experimental.pallas import tpu as pltpu
from jax.sharding import PartitionSpec as P

D = 1024
HEADS = 8
HEAD = 128
NH = 2
FF = 2816
BLOCK_LEN = 64
ROWS = BLOCK_LEN * NH
CONV = 4
SEQ_LEN = 32768
MOST_DOC = {4096: 2048, 32768: 8192}
WIDE = (1 + 2 * NH) * HEAD
HALO = 16
NORM_EPS = 1e-06
VMEM_LIMIT = 60 << 20
F32 = jnp.float32
BF16 = jnp.bfloat16
BOTH = ("seq", "ctx")
MESH = pl.DeviceIdType.MESH


class Split:
    def __init__(self, x):
        self.high = x.astype(BF16)
        self.low = (x - self.high.astype(F32)).astype(BF16)


def mm(a, b, ca=1, cb=0):
    if not isinstance(a, Split) and a.dtype != BF16:
        a = Split(a)
    if not isinstance(b, Split) and b.dtype != BF16:
        b = Split(b)
    if isinstance(a, Split) and isinstance(b, Split):
        left, right = (a.high, a.high, a.low), (b.high, b.low, b.high)
    elif isinstance(a, Split):
        left, right = (a.high, a.low), (b, b)
    elif isinstance(b, Split):
        left, right = (a, a), (b.high, b.low)
    else:
        left, right = (a,), (b,)
    if len(left) > 1:
        left, right = (jnp.concatenate(left, axis=ca),), (jnp.concatenate(right, axis=cb),)
    return lax.dot_general(left[0], right[0], (((ca,), (cb,)), ((), ())), preferred_element_type=F32)


def lanes_for(columns):
    return -(-columns // HEAD) * HEAD


def iota(shape, axis):
    return lax.broadcasted_iota(jnp.int32, shape, axis)


def unit_lower_inverses(systems):
    n = systems[0].shape[0]
    ri, ci = iota((n, n), 0), iota((n, n), 1)
    pick = (iota((n, 8), 0) % 8 == iota((n, 8), 1)).astype(BF16)
    own = ri // 8 == ci // 8
    eye = (ri == ci).astype(F32).reshape(n // 8, 8, n)
    small = [mm(jnp.where(own, a, 0.0), pick).reshape(n // 8, 8, 8) for a in systems]
    inv = [eye for _ in systems]
    for j in range(7):
        inv = [x - m[:, :, j : j + 1] * x[:, j : j + 1, :] for x, m in zip(inv, small)]
    inv = [x.reshape(n, n) for x in inv]
    size = 8
    while size < n:
        off = (ri // (2 * size) == ci // (2 * size)) & (ri // size != ci // size)
        halves = [Split(x) for x in inv]
        right = [mm(jnp.where(off, a, 0.0), x) for a, x in zip(systems, halves)]
        inv = [x - mm(y, z) for x, y, z in zip(inv, halves, right)]
        size *= 2
    return inv


DOC = 7
LINK = DOC + 1


def lane_of(h, what):
    return h * (NH + 1) + what


def column(table, lane):
    return table[:, lane : lane + 1]


def decays(rowp, colp, tokp, h):
    g = lane_of(h, NH)
    cs_row, g_row = rowp[DOC : DOC + 1, :], rowp[g : g + 1, :]
    cs_col, g_col = column(colp, DOC), column(colp, g)
    cs_tok, g_tok = column(tokp, DOC), column(tokp, g)
    beta = column(colp, lane_of(h, 0))
    ri, ci = iota((ROWS, ROWS), 0), iota((ROWS, ROWS), 1)
    strict = (ri > ci) & (cs_col == cs_row)
    decay = jnp.where(strict, jnp.exp(jnp.where(strict, g_col - g_row, 0.0)), 0.0)
    rt, ct = iota((BLOCK_LEN, ROWS), 0), iota((BLOCK_LEN, ROWS), 1)
    seen = (rt * NH + NH - 1 >= ct) & (cs_tok == cs_row)
    qdecay = jnp.where(seen, jnp.exp(jnp.where(seen, g_tok - g_row, 0.0)), 0.0)
    carry = jnp.where(cs_col == 0.0, jnp.exp(g_col), 0.0)
    qcarry = jnp.where(cs_tok == 0.0, jnp.exp(g_tok), 0.0)
    cs_last, g_last = cs_row[:, ROWS - 1 :], g_row[:, ROWS - 1 :]
    same = cs_col == cs_last
    dlast = jnp.where(same, jnp.exp(jnp.where(same, g_last - g_col, 0.0)), 0.0)
    clast = jnp.where(cs_last == 0.0, jnp.exp(g_last), 0.0)
    return beta, decay, qdecay, carry, qcarry, dlast, clast


def lag_rows(ext, lag):
    moved = pltpu.roll(ext, lag, 0) if lag else ext
    return moved[HALO:]


UP, DOWN, ACROSS = 0, 1, 2


class Line:
    def __init__(self, pieces, parts, send_sem, recv_sem, up=True, down=True, reach=None):
        self.chips = pieces // 2
        self.reach = self.chips - 1 if reach is None else reach
        self.here = lax.axis_index("ctx")
        self.chip = self.here // 2
        self.core = lax.rem(self.here, 2)
        self.other = self.here + 1 - 2 * self.core
        self.parts, self.send_sem, self.recv_sem, self.up, self.down = parts, send_sem, recv_sem, up, down

    def copies(self, chunk, way, only=None):
        target = (self.here + 2, self.here - 2, self.other)[way]
        return [
            pltpu.make_async_remote_copy(
                part(chunk), part(chunk), self.send_sem.at[n, way, chunk], self.recv_sem.at[n, chunk],
                device_id={"ctx": target}, device_id_type=MESH,
            )
            for n, part in enumerate(self.parts)
            if only is None or n == only
        ]

    def start(self, chunk, way, only=None):
        for copy in self.copies(chunk, way, only):
            copy.start()

    def arrived(self, chunk, only=None):
        for copy in self.copies(chunk, ACROSS, only):
            copy.wait_recv()

    def left(self, chunk, way):
        for copy in self.copies(chunk, way):
            copy.wait_send()

    def routes(self, distance, act):
        if distance == 0:
            if self.up and self.reach:
                pl.when(self.chip < self.chips - 1)(lambda: act(self.here, UP))
            if self.down and self.reach:
                pl.when(self.chip > 0)(lambda: act(self.here, DOWN))
            act(self.here, ACROSS)
            return
        below, above = self.here - 2 * distance, self.here + 2 * distance
        onward = distance < self.reach
        if self.up:

            @pl.when(self.chip >= distance)
            def _():
                if onward:
                    pl.when(self.chip < self.chips - 1)(lambda: act(below, UP))
                act(below, ACROSS)

        if self.down:

            @pl.when(self.chip + distance < self.chips)
            def _():
                if onward:
                    pl.when(self.chip > 0)(lambda: act(above, DOWN))
                act(above, ACROSS)

    def own(self, only=None):
        self.routes(0, lambda chunk, way: self.start(chunk, way, only))

    def hop(self, distance):
        for n in range(len(self.parts)):
            if self.up:
                pl.when(self.chip >= distance)(lambda n=n: self.arrived(self.here - 2 * distance, n))
            if self.down:
                pl.when(self.chip + distance < self.chips)(lambda n=n: self.arrived(self.here + 2 * distance, n))
            self.routes(distance, lambda chunk, way, n=n: self.start(chunk, way, n))

    def finish(self):
        for chip in range(self.chips):
            needed = (self.chip <= chip + (self.reach if self.up else 0)) & (
                self.chip >= chip - (self.reach if self.down else 0)
            )
            pl.when(needed)(lambda chip=chip: self.arrived(2 * chip + 1 - self.core))
        for distance in range(self.reach + 1):
            self.routes(distance, self.left)


class LineSum:
    def __init__(self, pieces, held, came, send_sem, recv_sem):
        self.chips = pieces // 2
        self.here = lax.axis_index("ctx")
        self.chip = self.here // 2
        self.held, self.came, self.send_sem, self.recv_sem = held, came, send_sem, recv_sem

    def copies(self, owner, way):
        return [
            pltpu.make_async_remote_copy(
                held.at[owner], came.at[way, owner], self.send_sem.at[n, owner], self.recv_sem.at[n, way, owner],
                device_id={"ctx": self.here + 2 - 4 * way}, device_id_type=MESH,
            )
            for n, (held, came) in enumerate(zip(self.held, self.came))
        ]

    def take(self, owner, way):
        for copy in self.copies(owner, way):
            copy.wait_recv()
        for held, came in zip(self.held, self.came):
            held[owner] = (held[owner].astype(F32) + came[way, owner].astype(F32)).astype(BF16)

    def send(self, owner, way):
        for copy in self.copies(owner, way):
            copy.start()

    def each(self, r, act):
        top = self.chips - 1
        for way, place in ((UP, self.chip), (DOWN, top - self.chip)):
            owner = top - (r - place) if way == UP else r - place
            pl.when((place <= r) & (place < top))(lambda: act(owner, way, place))

    def settle(self, r):
        self.each(r, lambda owner, way, place: pl.when(place > 0)(lambda: self.take(owner, way)))

    def launch(self, r):
        self.each(r, lambda owner, way, place: self.send(owner, way))

    def left(self, r):
        def wait(owner, way, place):
            for copy in self.copies(owner, way):
                copy.wait_send()

        self.each(r, wait)

    def round(self, r):
        self.settle(r)
        self.launch(r)

    def finish(self):
        top = self.chips - 1
        pl.when(self.chip > 0)(lambda: self.take(self.chip, UP))
        pl.when(self.chip < top)(lambda: self.take(self.chip, DOWN))


def early_rounds(pieces):
    rounds = pieces // 2 - 1
    return max(1, rounds - 1), max(1, rounds - 2)


class Siblings:
    def __init__(self, parts, theirs, held, send_sem, recv_sem):
        self.here = lax.axis_index("ctx")
        self.core = lax.rem(self.here, 2)
        self.parts, self.theirs, self.held, self.send_sem, self.recv_sem = parts, theirs, held, send_sem, recv_sem

    def copies(self):
        return [
            pltpu.make_async_remote_copy(
                part.at[:, 1 - self.core], theirs, self.send_sem.at[n], self.recv_sem.at[n],
                device_id={"ctx": self.here + 1 - 2 * self.core}, device_id_type=MESH,
            )
            for n, (part, theirs) in enumerate(zip(self.parts, self.theirs))
        ]

    def start(self):
        for copy in self.copies():
            copy.start()

    def add(self):
        for copy in self.copies():
            copy.wait_recv()
        for part, theirs, held in zip(self.parts, self.theirs, self.held):

            def one(chip, carry, part=part, theirs=theirs, held=held):
                held[chip] = (part[chip, self.core].astype(F32) + theirs[chip].astype(F32)).astype(BF16)
                return carry

            lax.fori_loop(0, part.shape[0], one, 0)

    def left(self):
        for copy in self.copies():
            copy.wait_send()


def partner(me, i, size):
    total, bit = 0, 1
    while bit < size:
        total = total + lax.rem(me // bit + i // bit, 2) * bit
        bit *= 2
    return total


def chips_within(span_pieces, pieces):
    return min(pieces // 2 - 1, (span_pieces + 1) // 2)


def greet(devices, barrier):
    total = 0
    for place, there in devices:
        pl.when(there)(
            lambda place=place: pl.semaphore_signal(barrier, inc=1, device_id=place, device_id_type=MESH)
        )
        total = total + jnp.asarray(there, jnp.int32)
    return total


def line_neighbours(pieces):
    here = lax.axis_index("ctx")
    chip, core = here // 2, lax.rem(here, 2)
    return [
        ({"ctx": here + 2}, chip < pieces // 2 - 1),
        ({"ctx": here - 2}, chip > 0),
        ({"ctx": here + 1 - 2 * core}, here >= 0),
    ]


def start_kernel(
    size, pieces, norm_at, x_ref, mix_ref, gate_ref, scal_ref, norma_ref, normm_ref, taps_ref, mask_ref, wg_ref, wu_ref,
    xfull_ref, halo_ref, full_ref, stage_ref,
    tail_ref, sides, local_sem, seq_send, seq_recv, line_send, line_recv, halo_sem,
):
    me, here = lax.axis_index("seq"), lax.axis_index("ctx")
    count = x_ref.shape[0]
    core = lax.rem(here, 2)
    inner = wg_ref.shape[1] // size
    gate_at = mix_ref.shape[1] // size
    tail_at = gate_at + gate_ref.shape[1] // size

    def placed(rows_, lane):
        at = (iota((rows_.shape[0], HEAD), 1) == lane + iota((rows_.shape[0], HEAD), 0)).astype(BF16)
        return lax.dot_general(rows_, at, (((0,), (0,)), ((), ())), preferred_element_type=F32)

    held, channels = tail_ref.shape[0], taps_ref.shape[1]
    pack = placed(scal_ref[...], 0) + placed(norma_ref[...], norm_at) + placed(normm_ref[...], norm_at + 1)
    valid = jnp.sum(mask_ref[...].astype(F32), axis=1, keepdims=True)
    pack = pack + jnp.where((iota((held, HEAD), 0) == 0) & (iota((held, HEAD), 1) == norm_at + 2), valid, 0.0)
    mine = channel_rows(held, channels)
    for tap in range(CONV):
        spread = jnp.where(mine, taps_ref[tap : tap + 1].astype(F32), 0.0).astype(BF16)
        pack = pack + lax.dot_general(
            spread, tap_lanes(channels, tap, norm_at + 3), (((1,), (0,)), ((), ())), preferred_element_type=F32
        )
    tail_ref[...] = pack.astype(BF16)
    barrier = pltpu.get_barrier_semaphore()
    peers = [({"seq": partner(me, i, size)}, here >= 0) for i in range(1, size)]
    side = [({"ctx": here + 1}, (core == 1) & (here < pieces - 1)), ({"ctx": here - 1}, (core == 0) & (here > 0))]
    total = greet(peers + line_neighbours(pieces) + side, barrier)
    pl.semaphore_wait(barrier, total)

    def rows(q):
        return pl.ds(pl.multiple_of(q * count, count), count)

    def cols(q, width):
        return pl.ds(pl.multiple_of(q * width, HEAD), width)

    def ends(n, q):
        return [
            (mix_ref.at[:, cols(q, gate_at)], full_ref.at[me, here, :, :gate_at]),
            (gate_ref.at[:, cols(q, tail_at - gate_at)], full_ref.at[me, here, :, gate_at:tail_at]),
            (tail_ref, full_ref.at[me, here, :, tail_at:]),
            (x_ref, xfull_ref.at[rows(me)]),
            (sides.at[q], stage_ref.at[me]),
        ][n]

    def exchange(n, i):
        q = partner(me, i, size)
        source, target = ends(n, q)
        return pltpu.make_async_remote_copy(
            source, target, seq_send.at[n, i - 1], seq_recv.at[n, i - 1], device_id={"seq": q}, device_id_type=MESH
        )

    def own(n):
        return pltpu.make_async_copy(*ends(n, me), local_sem.at[n])

    def begin(n):
        own(n).start()
        for i in range(1, size):
            exchange(n, i).start()

    def end(n):
        own(n).wait()
        for i in range(1, size):
            exchange(n, i).wait_recv()

    for n in range(3):
        begin(n)
    sides[...] = jnp.zeros_like(sides)
    for q in range(size):
        sides[q, 0, :, :inner] = wg_ref[:, q * inner : (q + 1) * inner]
        sides[q, 1, :, :inner] = wu_ref[:, q * inner : (q + 1) * inner]
    line = Line(
        pieces, [lambda c, i=i: full_ref.at[partner(me, i, size), c] for i in range(size)], line_send, line_recv
    )
    for n in range(3):
        own(n).wait()
    line.own(0)
    for i in range(1, size):
        for n in range(3):
            exchange(n, i).wait_recv()
        line.own(i)
    begin(3)
    begin(4)
    last = xfull_ref.at[pl.ds(size * count - HALO, HALO)]
    passing = pltpu.make_async_remote_copy(
        last, halo_ref, halo_sem.at[0], halo_sem.at[1], device_id={"ctx": here + 1}, device_id_type=MESH
    )
    hops = pieces // 2 - 1
    for distance in range(1, hops):
        line.hop(distance)
    end(3)
    pl.when(here < pieces - 1)(passing.start)

    @pl.when(here == 0)
    def _():
        filling = pltpu.make_async_copy(last, halo_ref, local_sem.at[5])
        filling.start()
        filling.wait()

    line.hop(hops)
    line.finish()
    end(4)
    pl.when(here > 0)(passing.wait_recv)
    pl.when(here < pieces - 1)(passing.wait_send)
    for n in range(5):
        for i in range(1, size):
            exchange(n, i).wait_send()


def start_gather(size, pieces, norm_at, x, mix, gate, scal, norm_a, norm_m, taps, mask, w_gate, w_up):
    anywhere = pl.BlockSpec(memory_space=pl.ANY)
    vmem = pl.BlockSpec(memory_space=pltpu.VMEM)
    out = lambda *dims: jax.ShapeDtypeStruct(dims, BF16)
    dma = pltpu.SemaphoreType.DMA
    held, padded = w_gate.shape[0], lanes_for(w_gate.shape[1] // size)
    width = (mix.shape[1] + gate.shape[1]) // size + HEAD
    return pl.pallas_call(
        functools.partial(start_kernel, size, pieces, norm_at),
        in_specs=[anywhere] * 3 + [vmem] * 7,
        out_specs=[anywhere] * 4,
        out_shape=[
            out(x.shape[0] * size, D), out(HALO, D), out(size, pieces, held, width), out(size, 2, held, padded),
        ],
        scratch_shapes=[
            pltpu.VMEM((held, HEAD), BF16), pltpu.VMEM((size, 2, held, padded), BF16),
            dma((6,)), dma((5, size - 1)), dma((5, size - 1)), dma((size, 3, pieces)), dma((size, pieces)), dma((2,)),
        ],
        compiler_params=pltpu.CompilerParams(
            vmem_limit_bytes=VMEM_LIMIT, collective_id=2, has_side_effects=True
        ),
        name="start_gather",
    )(x, mix, gate, scal, norm_a, norm_m, taps, mask, w_gate, w_up)


def exact(a, b, ca=1, cb=0):
    return lax.dot_general(
        a, b, (((ca,), (cb,)), ((), ())), precision=lax.Precision.HIGHEST, preferred_element_type=F32
    )


def tap_lanes(channels, tap, at):
    lanes = iota((channels, HEAD), 1)
    return (lanes == at + CONV * (iota((channels, HEAD), 0) % (WIDE // HEAD)) + tap).astype(BF16)


def channel_rows(rows, channels):
    return iota((rows, channels), 1) // (WIDE // HEAD) == iota((rows, channels), 0)


def front_body(
    heads, norm_at, alog_ref, lift_ref, x_ref, halo_ref, w_ref, marks_ref,
    proj_ref, normed_ref, gate_ref, tok_ref, slope_ref, col_ref, row_ref, taps_ref, norms_ref,
):
    me = lax.axis_index("seq")
    channels = heads * WIDE
    tail_at = channels + heads * HEAD
    rows = x_ref.shape[0]
    own_rows = D * heads // HEADS

    def dot(a, b, ca=1, cb=0):
        return lax.dot_general(a, b, (((ca,), (cb,)), ((), ())), preferred_element_type=F32)

    pick = (iota((8, HEAD), 1) == norm_at + iota((8, HEAD), 0)).astype(BF16)
    norms_ref[...] = dot(pick, w_ref[:, tail_at:], 1, 1)

    def normal(values):
        values = values.astype(F32)
        scale = lax.rsqrt(jnp.mean(values * values, axis=1, keepdims=True) + NORM_EPS)
        return (values * scale * norms_ref[0:1, :]).astype(BF16)

    early = normal(halo_ref[...])
    normed_ref[...] = normal(x_ref[...])
    proj_ref[:HALO] = dot(early, w_ref[:, :channels]).astype(BF16)
    proj_ref[HALO:] = dot(normed_ref[...], w_ref[:, :channels]).astype(BF16)
    gate_ref[...] = dot(normed_ref[...], w_ref[:, channels:tail_at])
    tail = w_ref[pl.ds(pl.multiple_of(me * own_rows, own_rows), own_rows), tail_at:]
    taps_ref[...] = jnp.zeros_like(taps_ref)
    mine = channel_rows(own_rows, channels)
    for lag in range(CONV):
        spread = dot(tail, tap_lanes(channels, CONV - 1 - lag, norm_at + 3), 1, 1)
        taps_ref[lag : lag + 1] = jnp.sum(jnp.where(mine, spread, 0.0), axis=0, keepdims=True)

    raw = dot(normed_ref[...], w_ref[:, tail_at:]).astype(BF16).astype(F32)
    raw = pltpu.roll(raw, lax.rem(HEAD - me * lane_of(heads, 0), HEAD), 1)
    lane = iota((1, HEAD), 1)
    rate, lift = jnp.zeros((1, HEAD), F32), jnp.zeros((1, HEAD), F32)
    for h in range(heads):
        here = lane == lane_of(h, NH)
        mine_here = iota((1, HEADS), 1) == me * heads + h
        own = [
            jnp.sum(jnp.where(mine_here, ref[...].astype(F32), 0.0), axis=1, keepdims=True) for ref in (alog_ref, lift_ref)
        ]
        rate = jnp.where(here, -jnp.exp(own[0]), rate)
        lift = jnp.where(here, own[1], lift)
    is_log = (lane % (NH + 1) == NH) & (lane < lane_of(heads, 0))
    lifted = raw + lift
    sig = jax.nn.sigmoid(lifted)
    logs = rate * (jnp.maximum(lifted, 0.0) + jnp.log1p(jnp.exp(-jnp.abs(lifted))))
    slope_ref[...] = jnp.where(is_log, rate * sig, sig * (1.0 - sig)) * (lane < HEAD // 2) + pltpu.roll(
        jnp.where(is_log, logs, 0.0), HEAD // 2, 1
    )
    place = (iota((8, HEAD), 1) == LINK + iota((8, HEAD), 0)) & (iota((8, HEAD), 0) < CONV - 1)
    links = dot(marks_ref[...].astype(BF16), place.astype(BF16), 0, 0)
    open_ = column(links, LINK)
    summed = jnp.where(is_log, logs * open_, jnp.where(lane == DOC, 1.0 - open_, 0.0))
    lower = (iota((BLOCK_LEN, BLOCK_LEN), 0) >= iota((BLOCK_LEN, BLOCK_LEN), 1)).astype(F32)
    spread = (iota((ROWS, BLOCK_LEN), 0) // NH == iota((ROWS, BLOCK_LEN), 1)).astype(F32)
    step = iota((ROWS, HEAD), 0) % NH
    for b in range(rows // BLOCK_LEN):
        span = slice(b * BLOCK_LEN, (b + 1) * BLOCK_LEN)
        sums = exact(lower, summed[span])
        tok = jnp.where(is_log | (lane == DOC), sums, jnp.where(lane < DOC, sig[span], links[span]))
        tok_ref[span] = tok
        wide = exact(spread, tok)
        first = wide
        for j in range(1, NH):
            first = jnp.where(step == j, pltpu.roll(wide, HEAD - j, 1), first)
        col = jnp.where(lane % (NH + 1) == 0, jnp.where(lane < lane_of(heads, 0), first, wide), wide)
        col_ref[b * ROWS : (b + 1) * ROWS] = col
        row_ref[b * 8 : (b + 1) * 8] = col.T[:8]


def fwd_kernel(
    heads, pieces, steps, per, span_pieces, norm_at,
    alog_ref, lift_ref, x_ref, halo_ref, full_ref, marks_ref, stage_ref, wo_ref,
    proj_ref, normed_ref, gate_ref, tok_ref, slope_ref, col_ref, row_ref, taps_ref, norms_ref,
    oloc_ref, carr_ref, sin_ref, mapsout_ref, conv_ref, q_ref, k_ref, v_ref, t_ref, kk_ref, at_ref, uw_ref, pl_ref,
    wgfull_ref, wufull_ref, wofull_ref,
    state, weave, maps, wgs, wus, wos, local_sem, line_send, line_recv, map_send, map_recv,
):
    step = pl.program_id(0)
    here = lax.axis_index("ctx")
    weights = Line(
        pieces, [lambda c: wgs.at[:, c], lambda c: wus.at[:, c], lambda c: wos.at[c]], line_send, line_recv
    )
    eye = (iota((HEAD, HEAD), 0) == iota((HEAD, HEAD), 1)).astype(F32)

    @pl.when(step == 0)
    def _():
        owned = [
            pltpu.make_async_copy(source, target, local_sem.at[n])
            for n, (source, target) in enumerate(
                [(stage_ref.at[:, 0], wgs.at[:, here]), (stage_ref.at[:, 1], wus.at[:, here]), (wo_ref, wos.at[here])]
            )
        ]
        for copy in owned:
            copy.start()
        barrier = pltpu.get_barrier_semaphore()
        pl.semaphore_wait(barrier, greet(line_neighbours(pieces), barrier))
        for copy in owned:
            copy.wait()
        weights.own()
        front_body(
            heads, norm_at, alog_ref, lift_ref, x_ref, halo_ref, full_ref, marks_ref,
            proj_ref, normed_ref, gate_ref, tok_ref, slope_ref, col_ref, row_ref, taps_ref, norms_ref,
        )
        for h in range(heads):
            state[h, :, :HEAD] = eye
            state[h, :, HEAD:] = jnp.zeros((HEAD, HEAD), F32)

    hops = [(d * 2 * steps) // (pieces // 2) - 1 for d in range(1, pieces // 2)]
    for distance, at in enumerate(hops, 1):
        if at < steps:
            pl.when(step == at)(lambda distance=distance: weights.hop(distance))

    items = [(j, h) for j in range(per) for h in range(heads)]
    cols = lambda h: slice(h * WIDE, (h + 1) * WIDE)
    span = lambda j, length=BLOCK_LEN: slice(j * length, (j + 1) * length)
    tables = []
    for j in range(per):
        block = step * per + j
        tables.append(
            (
                row_ref[pl.ds(pl.multiple_of(block * 8, 8), 8), :],
                col_ref[pl.ds(pl.multiple_of(block * ROWS, ROWS), ROWS), :],
                tok_ref[pl.ds(pl.multiple_of(block * BLOCK_LEN, BLOCK_LEN), BLOCK_LEN), :],
            )
        )
    acts = []
    for j, h in items:
        base = pl.multiple_of((step * per + j) * BLOCK_LEN, BLOCK_LEN)
        ext = proj_ref[pl.ds(base, BLOCK_LEN + HALO), cols(h)].astype(F32)
        conv = ext[HALO:] * taps_ref[0:1, cols(h)]
        for lag in range(1, CONV):
            conv = conv + column(tables[j][2], LINK + lag - 1) * lag_rows(ext, lag) * taps_ref[lag : lag + 1, cols(h)]
        conv_ref[span(j), cols(h)] = conv
        acts.append(conv * jax.nn.sigmoid(conv))
    queries, keys, values = [], [], []
    for n, act in enumerate(acts):
        unit = []
        for part in range(1 + NH):
            piece = act[:, part * HEAD : (part + 1) * HEAD]
            unit.append(piece * lax.rsqrt(jnp.sum(piece * piece, axis=1, keepdims=True) + NORM_EPS))
        queries.append(unit[0] * (1.0 / math.sqrt(HEAD)))
        for j in range(NH):
            weave[2 * n, pl.ds(j, BLOCK_LEN, NH), :] = unit[1 + j]
            weave[2 * n + 1, pl.ds(j, BLOCK_LEN, NH), :] = act[:, (1 + NH + j) * HEAD : (2 + NH + j) * HEAD]
    for n in range(len(items)):
        keys.append(weave[2 * n])
        values.append(weave[2 * n + 1])
    factors = [decays(*tables[j], h) for j, h in items]
    grams = [mm(jnp.concatenate([q, k], axis=0), k, 1, 1) for q, k in zip(queries, keys)]
    kks = [f[1] * g[BLOCK_LEN:] for f, g in zip(factors, grams)]
    attns = [f[2] * g[:BLOCK_LEN] for f, g in zip(factors, grams)]
    invs = unit_lower_inverses([f[0] * kk for f, kk in zip(factors, kks)])
    uws = [
        mm(inv, jnp.concatenate([f[0] * v, (f[0] * f[3]) * k], axis=1))
        for inv, f, v, k in zip(invs, factors, values, keys)
    ]
    auws = [mm(attn, uw) for attn, uw in zip(attns, uws)]
    nms = [mm(f[5] * k, uw, 0, 0) for f, k, uw in zip(factors, keys, uws)]
    for n, (j, h) in enumerate(items):
        before = state[h]
        f = factors[n]
        both = mm(
            jnp.concatenate([f[4] * queries[n] - auws[n][:, HEAD:], f[6] * eye - nms[n][:, HEAD:]], axis=0), before
        )
        hc = slice(h * HEAD, (h + 1) * HEAD)
        carr_ref[span(j), hc] = both[:BLOCK_LEN, :HEAD]
        oloc_ref[span(j), hc] = both[:BLOCK_LEN, HEAD:] + auws[n][:, :HEAD]
        state[h, :, :HEAD] = both[BLOCK_LEN:, :HEAD]
        state[h, :, HEAD:] = both[BLOCK_LEN:, HEAD:] + nms[n][:, :HEAD]
        q_ref[j, h] = queries[n]
        k_ref[j, h] = keys[n]
        v_ref[j, h] = values[n]
        t_ref[j, h] = invs[n]
        kk_ref[j, h] = kks[n]
        at_ref[j, h] = attns[n]
        uw_ref[j, h] = uws[n]
        pl_ref[j, h] = before

    @pl.when(step == steps - 1)
    def _():
        maps[here] = state[...].astype(BF16)
        line = Line(pieces, [lambda c: maps.at[c]], map_send, map_recv, reach=chips_within(span_pieces, pieces))
        line.own()
        for distance in range(1, line.reach + 1):
            line.hop(distance)
        line.finish()
        for distance in range(1, pieces // 2):
            if hops[distance - 1] >= steps:
                weights.hop(distance)

        def hop(k, states):
            return tuple(
                mm(maps[k, h, :, :HEAD], states[h]) + maps[k, h, :, HEAD:].astype(F32) for h in range(heads)
            )

        states = lax.fori_loop(jnp.maximum(here - span_pieces, 0), here, hop, tuple(jnp.zeros((HEAD, HEAD), F32) for _ in range(heads)))
        for h in range(heads):
            sin_ref[h] = states[h]

        def keep(k, carry):
            mapsout_ref[k] = maps[k, :, :, :HEAD]
            return carry

        lax.fori_loop(
            jnp.maximum(here - span_pieces, 0), jnp.minimum(here + span_pieces + 1, pieces), keep, 0
        )
        weights.finish()
        given = [
            pltpu.make_async_copy(source, target, local_sem.at[n])
            for n, (source, target) in enumerate([(wgs, wgfull_ref), (wus, wufull_ref), (wos, wofull_ref)])
        ]
        for copy in given:
            copy.start()
        for copy in given:
            copy.wait()


def recurrence_forward(heads, pieces, span_pieces, norm_at, a_log, dt_bias, x_full, halo, weights, marks, stage, w_out):
    rows = x_full.shape[0]
    blocks = rows // BLOCK_LEN
    per = 2
    size = stage.shape[0]
    whole = lambda *dims: pl.BlockSpec(dims, lambda i: (0,) * len(dims))
    by_block = lambda *dims: pl.BlockSpec((per,) + dims, lambda i: (i,) + (0,) * len(dims))
    token = lambda cols: pl.BlockSpec((per * BLOCK_LEN, cols), lambda i: (i, 0))
    shape = lambda *dims: jax.ShapeDtypeStruct(dims, F32)
    low_shape = lambda *dims: jax.ShapeDtypeStruct(dims, BF16)
    hbm = pl.BlockSpec(memory_space=pltpu.HBM)
    vmem = pl.BlockSpec(memory_space=pltpu.VMEM)
    square = (heads, ROWS, HEAD)
    dma = pltpu.SemaphoreType.DMA
    side = (size, pieces, *stage.shape[2:])
    front = [
        low_shape(rows + HALO, heads * WIDE), low_shape(rows, D), shape(rows, heads * HEAD), shape(rows, HEAD),
        shape(rows, HEAD), shape(blocks * ROWS, HEAD), shape(blocks * 8, ROWS), shape(8, heads * WIDE), shape(8, D),
    ]
    return pl.pallas_call(
        functools.partial(fwd_kernel, heads, pieces, blocks // per, per, span_pieces, norm_at),
        grid=(blocks // per,),
        in_specs=[vmem] * 6 + [hbm] * 2,
        out_specs=[whole(*f.shape) for f in front] + [
            token(heads * HEAD), token(heads * HEAD), whole(heads, HEAD, HEAD), whole(pieces, heads, HEAD, HEAD),
            token(heads * WIDE),
            by_block(heads, BLOCK_LEN, HEAD), by_block(*square), by_block(*square), by_block(*square),
            by_block(*square), by_block(heads, BLOCK_LEN, ROWS), by_block(heads, ROWS, 2 * HEAD),
            by_block(heads, HEAD, 2 * HEAD), hbm, hbm, hbm,
        ],
        out_shape=front + [
            shape(rows, heads * HEAD), shape(rows, heads * HEAD), shape(heads, HEAD, HEAD),
            low_shape(pieces, heads, HEAD, HEAD), shape(rows, heads * WIDE),
            shape(blocks, heads, BLOCK_LEN, HEAD), shape(blocks, *square), shape(blocks, *square), shape(blocks, *square),
            shape(blocks, *square), shape(blocks, heads, BLOCK_LEN, ROWS), shape(blocks, heads, ROWS, 2 * HEAD),
            shape(blocks, heads, HEAD, 2 * HEAD),
            low_shape(*side), low_shape(*side), low_shape(pieces, *w_out.shape),
        ],
        scratch_shapes=[
            pltpu.VMEM((heads, HEAD, 2 * HEAD), F32), pltpu.VMEM((2 * heads * per, ROWS, HEAD), F32),
            pltpu.VMEM((pieces, heads, HEAD, 2 * HEAD), BF16),
            pltpu.VMEM(side, BF16), pltpu.VMEM(side, BF16), pltpu.VMEM((pieces, *w_out.shape), BF16),
            dma((3,)), dma((3, 3, pieces)), dma((3, pieces)), dma((1, 3, pieces)), dma((1, pieces)),
        ],
        compiler_params=pltpu.CompilerParams(
            vmem_limit_bytes=VMEM_LIMIT, collective_id=3, has_side_effects=True
        ),
        name="recurrence_forward",
    )(a_log, dt_bias, x_full, halo, weights, marks, stage, w_out)


def middle_kernel(
    size, heads, token_total,
    x_ref, teach_ref, mask_ref, norms_ref, gain_ref, *streams_and_rest,
):
    streams, rest = streams_and_rest[:8], streams_and_rest[8:]
    middle_body(size, heads, token_total, x_ref, teach_ref, mask_ref, norms_ref, gain_ref, streams, *rest)


def middle_body(
    size, heads, token_total, x_ref, teach_ref, mask_ref, norms_ref, gain_ref, streams,
    final_ref, gmid_ref, ghead_ref, ggate_ref, cot_ref, ggain_ref, gnorm_ref, loss_ref,
    wheld, theld, outg_ref,
    oloc_ref, carr_ref, gate_ref, sin_ref, wout_ref, wg_ref, wu_ref, wd_ref, load_sem, heads_ref, mixed_ref,
    line_send, line_recv, wds, wide_ref, tall_ref, wtheirs, ttheirs, wcame, tcame,
    pair_send, pair_recv, sum_send, sum_recv,
    second, branch, low, sent, got, own, mid, gfin, gates, ups, hidden, ggates, gups, send_sem, recv_sem,
):
    me = lax.axis_index("seq")
    count = x_ref.shape[0]
    loads = [
        pltpu.make_async_copy(source, target, load_sem.at[n])
        for n, (source, target) in enumerate(
            zip(streams, (oloc_ref, carr_ref, gate_ref, sin_ref, wout_ref, wg_ref, wu_ref, wds.at[lax.axis_index("ctx")]))
        )
    ]
    for load in loads:
        load.start()
    pieces = 2 * wide_ref.shape[0]
    barrier = pltpu.get_barrier_semaphore()
    peers = [({"seq": partner(me, i, size)}, me >= 0) for i in range(1, size)]
    pl.semaphore_wait(barrier, greet(peers + line_neighbours(pieces), barrier))
    loads[7].wait()
    line = Line(pieces, [lambda c: wds.at[c]], line_send, line_recv)
    line.own()
    for load in loads[:5]:
        load.wait()
    norm = norms_ref[1:2, :]
    gain = gain_ref[...].astype(F32)

    def dot(a, b, ca=1, cb=0):
        return lax.dot_general(a, b, (((ca,), (cb,)), ((), ())), preferred_element_type=F32)

    def rows(q):
        return pl.ds(pl.multiple_of(q * count, count), count)

    def part_copy(phase, i):
        return pltpu.make_async_remote_copy(
            sent.at[phase, i - 1], got.at[phase, i - 1], send_sem.at[phase, i - 1], recv_sem.at[phase, i - 1],
            device_id={"seq": partner(me, i, size)}, device_id_type=MESH,
        )

    def block_copy(buffer, phase, i, owner):
        return pltpu.make_async_remote_copy(
            buffer.at[rows(owner)], buffer.at[rows(owner)], send_sem.at[phase, i - 1], recv_sem.at[phase, i - 1],
            device_id={"seq": partner(me, i, size)}, device_id_type=MESH,
        )

    def give_part(phase, i, part):
        @pl.when(i > 0)
        def _():
            sent[phase, i - 1] = part.astype(BF16)
            part_copy(phase, i).start()

        @pl.when(i == 0)
        def _():
            own[...] = part

    def take_parts(phase):
        def add(i, total):
            part_copy(phase, i).wait_recv()
            return total + got[phase, i - 1].astype(F32)

        return lax.fori_loop(1, size, add, own[...])

    relayed = size == 4

    def half_copy(buffer, phase, n, owner):
        part = pl.ds(pl.multiple_of(owner * count + (n - 1) * (count // 2), count // 2), count // 2)
        return pltpu.make_async_remote_copy(
            buffer.at[part], buffer.at[part], send_sem.at[phase, 1 + n], recv_sem.at[phase, 1 + n],
            device_id={"seq": partner(me, 3 - n, size)}, device_id_type=MESH,
        )

    def give_block(buffer, phase, value):
        buffer[rows(me)] = value
        for i in range(1, 3 if relayed else size):
            block_copy(buffer, phase, i, me).start()

    def take_block(buffer, phase, i):
        q = partner(me, i, size)
        if relayed:

            @pl.when(i == 1)
            def _():
                for n in (1, 2):
                    block_copy(buffer, phase, n, partner(me, n, size)).wait_recv()
                    half_copy(buffer, phase, n, partner(me, n, size)).start()

            @pl.when(i == 3)
            def _():
                for n in (1, 2):
                    half_copy(buffer, phase, n, q).wait_recv()

        else:
            pl.when(i > 0)(lambda: block_copy(buffer, phase, i, q).wait_recv())
        return q

    def block_left(buffer, phase):
        for i in range(1, 3 if relayed else size):
            block_copy(buffer, phase, i, me).wait_send()
        if relayed:
            for n in (1, 2):
                half_copy(buffer, phase, n, partner(me, n, size)).wait_send()

    def out_part(k, carry):
        i = size - 1 - k
        q = partner(me, i, size)
        for h in range(heads):
            hc = slice(h * HEAD, (h + 1) * HEAD)
            out = (oloc_ref[rows(q), hc] + mm(carr_ref[rows(q), hc], sin_ref[h])).astype(BF16)
            heads_ref[rows(q), hc] = out
            wide = out.astype(F32)
            gate = gate_ref[rows(q), hc]
            scaled = wide * lax.rsqrt(jnp.mean(wide * wide, axis=1, keepdims=True) + NORM_EPS) * gain
            mixed_ref[rows(q), hc] = (scaled * (gate * jax.nn.sigmoid(gate))).astype(BF16)
        give_part(0, i, dot(mixed_ref[rows(q)], wout_ref[...]))
        return carry

    lax.fori_loop(0, size, out_part, 0)
    hops = pieces // 2 - 1
    for distance in range(1, hops // 2 + 1):
        line.hop(distance)
    middle = x_ref[...].astype(F32) + take_parts(0)
    mid[...] = middle
    inv = lax.rsqrt(jnp.mean(middle * middle, axis=1, keepdims=True) + NORM_EPS)
    give_block(second, 3, (middle * inv * norm).astype(BF16))
    for load in loads[5:7]:
        load.wait()
    deep = wds.shape[1]
    for distance in range(hops // 2 + 1, hops):
        line.hop(distance)

    def take_down():
        line.hop(hops)
        line.finish()
        inner = pieces * deep
        wd_ref[inner:] = jnp.zeros((wd_ref.shape[0] - inner, D), BF16)
        for c in range(pieces):
            wd_ref[c * deep : (c + 1) * deep] = wds[c]

    def feed(i, carry):
        q = take_block(second, 3, i)
        here = second[rows(q)]
        gate = dot(here, wg_ref[...])
        up = dot(here, wu_ref[...])
        gates[rows(q)] = gate
        ups[rows(q)] = up
        hid = (gate * jax.nn.sigmoid(gate) * up).astype(BF16)
        hidden[rows(q)] = hid
        pl.when(i == 0)(take_down)
        give_part(1, i, dot(hid, wd_ref[...]))
        return carry

    lax.fori_loop(0, size, feed, 0)
    final = mid[...] + take_parts(1)
    final_ref[...] = final.astype(BF16)
    error = final - teach_ref[...].astype(F32)
    mask = jnp.broadcast_to(mask_ref[...].astype(F32), (count, count)).T[:, :1]
    weighted = mask * error
    loss_ref[...] = jnp.broadcast_to(
        jnp.sum(jnp.sum(weighted * error, axis=1, keepdims=True), axis=0, keepdims=True), loss_ref.shape
    )
    valid = jnp.maximum(jnp.sum(norms_ref[2:3, :], axis=1, keepdims=True), 1.0)
    grad_final = token_total / valid * weighted
    gfin[...] = grad_final
    give_block(branch, 4, grad_final.astype(BF16))

    def feed_back(i, carry):
        q = take_block(branch, 4, i)
        ghid = dot(branch[rows(q)], wd_ref[...], 1, 1)
        gate = gates[rows(q)]
        sig = jax.nn.sigmoid(gate)
        silu = gate * sig
        ggate = (ghid * ups[rows(q)] * (sig + silu * (1.0 - sig))).astype(BF16)
        gup = (ghid * silu).astype(BF16)
        ggates[rows(q)] = ggate
        gups[rows(q)] = gup
        give_part(2, i, dot(ggate, wg_ref[...], 1, 1) + dot(gup, wu_ref[...], 1, 1))
        return carry

    lax.fori_loop(0, size, feed_back, 0)
    held = D // (size * pieces)
    tall_ref[...] = jnp.zeros_like(tall_ref)
    grad = dot(hidden[...], branch[...], 0, 0)
    for c in range(pieces):
        tall_ref[c // 2, c % 2, :deep] = grad[c * deep : (c + 1) * deep].astype(BF16)
    parts = ((tall_ref, ttheirs, theld, tcame), (wide_ref, wtheirs, wheld, wcame))
    pairs = [
        Siblings([part], [theirs], [kept], pair_send.at[n], pair_recv.at[n])
        for n, (part, theirs, kept, _) in enumerate(parts)
    ]
    sums = [LineSum(pieces, [kept], [came], sum_send.at[n], sum_recv.at[n]) for n, (_, _, kept, came) in enumerate(parts)]
    pairs[0].start()
    for n, side in enumerate((ggates, gups)):
        grad = dot(second[...], side[...], 0, 0)
        for c in range(pieces):
            for r in range(size):
                first = (r * pieces + c) * held
                wide_ref[c // 2, c % 2, (n * size + r) * held : (n * size + r + 1) * held] = grad[
                    first : first + held
                ].astype(BF16)
    pairs[1].start()
    for pair, line_sum in zip(pairs, sums):
        pair.add()
        line_sum.round(0)
    gsecond = take_parts(2)
    middle = mid[...]
    inv = lax.rsqrt(jnp.mean(middle * middle, axis=1, keepdims=True) + NORM_EPS)
    unit = middle * inv
    gnorm_ref[...] = jnp.sum(gsecond * unit, axis=0, keepdims=True)
    down = gsecond * norm
    gmid = gfin[...] + inv * (down - unit * jnp.mean(down * unit, axis=1, keepdims=True))
    gmid_ref[...] = gmid
    give_block(low, 5, gmid.astype(BF16))
    ggain_ref[...] = jnp.zeros_like(ggain_ref)
    cot_ref[...] = jnp.zeros_like(cot_ref)

    def out_back(i, carry):
        q = take_block(low, 5, i)
        gmixed = dot(low[rows(q)], wout_ref[...], 1, 1)
        for h in range(heads):
            hc = slice(h * HEAD, (h + 1) * HEAD)
            x = heads_ref[rows(q), hc].astype(F32)
            gate = gate_ref[rows(q), hc]
            grad = gmixed[:, hc]
            inv = lax.rsqrt(jnp.mean(x * x, axis=1, keepdims=True) + NORM_EPS)
            sig = jax.nn.sigmoid(gate)
            silu = gate * sig
            unit = x * inv
            ggate_ref[rows(q), hc] = (grad * unit * gain * (sig + silu * (1.0 - sig))).astype(BF16)
            weighted = grad * silu
            ggain_ref[...] += jnp.sum(weighted * unit, axis=0, keepdims=True)
            down = weighted * gain
            ghead = (inv * (down - unit * jnp.mean(down * unit, axis=1, keepdims=True))).astype(BF16)
            ghead_ref[rows(q), hc] = ghead
            cot_ref[h] += mm(carr_ref[rows(q), hc], ghead, 0, 0)
        return carry

    out_back(0, 0)
    early = early_rounds(pieces)
    for line_sum, ended in zip(sums, early):
        for r in range(1, ended):
            line_sum.round(r)
    lax.fori_loop(1, size, out_back, 0)
    grad = dot(mixed_ref[...], low[...], 0, 0)
    for c in range(pieces):
        outg_ref[c // 2, c % 2] = grad[c * held : (c + 1) * held].astype(BF16)
    for pair, line_sum, ended in zip(pairs, sums, early):
        line_sum.settle(ended)
        pair.left()
        for r in range(ended):
            line_sum.left(r)

    for i in range(1, size):
        for phase in range(3):
            part_copy(phase, i).wait_send()
    for buffer, phase in ((second, 3), (branch, 4), (low, 5)):
        block_left(buffer, phase)


def middle_part(
    size, heads, pieces, token_total, x, teacher, mask, norms, gain, oloc, carr, gate_out, state_in, wout, wg, wu, wd
):
    count = x.shape[0]
    rows = count * size
    inner = wg.shape[1]
    held, deep = D // (size * pieces), wd.shape[0]
    chips = pieces // 2
    wide, tall = (2 * size * held, inner), (-(-deep // 16) * 16, D)
    vmem = pl.BlockSpec(memory_space=pltpu.VMEM)
    out = lambda dims, kind: jax.ShapeDtypeStruct(dims, kind)
    low = lambda *dims: pltpu.VMEM(dims, BF16)
    high = lambda *dims: pltpu.VMEM(dims, F32)
    dma = pltpu.SemaphoreType.DMA
    return pl.pallas_call(
        functools.partial(middle_kernel, size, heads, float(token_total)),
        in_specs=[vmem] * 5 + [pl.BlockSpec(memory_space=pltpu.HBM)] * 8,
        out_specs=[vmem] * 11,
        out_shape=[
            out((count, D), BF16), out((count, D), F32),
            out((rows, heads * HEAD), BF16), out((rows, heads * HEAD), BF16), out((heads, HEAD, HEAD), F32),
            out((1, HEAD), F32), out((1, D), F32), out((1, HEAD), F32),
            out((chips, 2 * size * held, inner), BF16), out((chips, -(-deep // 16) * 16, D), BF16),
            out((chips, 2, held, D), BF16),
        ],
        scratch_shapes=[
            high(rows, heads * HEAD), high(rows, heads * HEAD), high(rows, heads * HEAD), high(heads, HEAD, HEAD),
            low(*wout.shape), low(*wg.shape), low(*wu.shape), low(inner, D), dma((8,)),
            low(rows, heads * HEAD), low(rows, heads * HEAD), dma((1, 3, pieces)), dma((1, pieces)), low(pieces, *wd.shape),
            low(chips, 2, *wide), low(chips, 2, *tall), low(chips, *wide), low(chips, *tall), low(2, chips, *wide),
            low(2, chips, *tall), dma((2, 1)), dma((2, 1)), dma((2, 1, chips)), dma((2, 1, 2, chips)),
            low(rows, D), low(rows, D), low(rows, D), low(3, size - 1, count, D), low(3, size - 1, count, D),
            high(count, D), high(count, D), high(count, D), high(rows, inner), high(rows, inner), low(rows, inner),
            low(rows, inner), low(rows, inner), dma((6, size)), dma((6, size)),
        ],
        compiler_params=pltpu.CompilerParams(
            vmem_limit_bytes=VMEM_LIMIT, collective_id=1, has_side_effects=True
        ),
        name="middle_part",
    )(x, teacher, mask, norms, gain, oloc, carr, gate_out, state_in, wout, wg, wu, wd)


def bwd_kernel(
    heads, pieces, steps, per, begun, span_pieces, maps_ref, cot_ref, sin_ref, proj_ref, w_ref, rowp_ref, colp_ref, tokp_ref, slope_ref,
    go_ref, conv_ref, q_ref, k_ref, v_ref, t_ref, kk_ref, at_ref, uw_ref, pl_ref, wide_ref, tall_ref, outg_ref, normed_ref, ggate_ref,
    gproj_ref, fix_ref, gw_ref, gscal_ref, gsum_ref, widesum_ref, tallsum_ref, outsum_ref, gatesum_ref,
    dstate, weave, rim, last, cots, rim_in, wheld, theld, wcame, tcame,
    gateg, otheirs, gtheirs, oheld, gheld, ocame, gcame,
    cot_send, cot_recv, pair_send, pair_recv, early_send, early_recv, line_send, line_recv, rim_sem,
):
    step = pl.program_id(0)
    block = steps - 1 - step
    here = lax.axis_index("ctx")
    core = lax.rem(here, 2)
    early = [
        LineSum(pieces, [kept], [came], early_send.at[n], early_recv.at[n])
        for n, (kept, came) in enumerate(((theld, tcame), (wheld, wcame)))
    ]
    pair = Siblings([outg_ref, gateg], [otheirs, gtheirs], [oheld, gheld], pair_send, pair_recv)
    line = LineSum(pieces, [oheld, gheld], [ocame, gcame], line_send, line_recv)
    rounds = pieces // 2 - 1
    when_round = [min(steps - 1, 1 + (r * steps) // rounds) for r in range(rounds)]

    @pl.when(step == 0)
    def _():
        barrier = pltpu.get_barrier_semaphore()
        side = [({"ctx": here + 1}, (core == 1) & (here < pieces - 1)), ({"ctx": here - 1}, (core == 0) & (here > 0))]
        pl.semaphore_wait(barrier, greet(line_neighbours(pieces) + side, barrier))
        cots[here] = cot_ref[...].astype(BF16)
        spread = Line(
            pieces, [lambda c: cots.at[c]], cot_send, cot_recv, up=False, reach=chips_within(span_pieces, pieces)
        )
        spread.own()
        wheld[...] = wide_ref[...]
        theld[...] = tall_ref[...]
        grad = lax.dot_general(
            normed_ref[...], ggate_ref[...], (((0,), (0,)), ((), ())), preferred_element_type=F32
        )
        held, size = gateg.shape[3], gateg.shape[2]
        for c in range(pieces):
            for r in range(size):
                row = (r * pieces + c) * held
                gateg[c // 2, c % 2, r] = grad[row : row + held].astype(BF16)
        for distance in range(1, spread.reach + 1):
            spread.hop(distance)
        spread.finish()
        for one, first in zip(early, begun):
            one.launch(first)
        pair.start()

        farthest = jnp.minimum(here + span_pieces, pieces - 1)

        def hop(i, states):
            k = farthest - i
            return tuple(
                mm(maps_ref[k, h], states[h], 0, 0) + cots[k, h].astype(F32) for h in range(heads)
            )

        found = lax.fori_loop(
            0, farthest - here, hop, tuple(jnp.zeros((HEAD, HEAD), F32) for _ in range(heads))
        )
        for h in range(heads):
            dstate[h] = found[h]
        rim[...] = jnp.zeros_like(rim)
        gw_ref[...] = jnp.zeros_like(gw_ref)
        gsum_ref[...] = jnp.zeros_like(gsum_ref)

    for one, first in zip(early, begun):
        for r in range(first + 1, rounds):
            at = min(steps - 1, 1 + ((r - first) * (steps - 1)) // (rounds - first))
            pl.when(step == at)(lambda one=one, r=r: one.round(r))
    pl.when(step == 1)(pair.add)
    for r in range(rounds):
        pl.when(step == when_round[r])(lambda r=r: line.round(r))

    last_row = iota((ROWS, 1), 0) == ROWS - 1
    diagonal = iota((ROWS, ROWS), 0) == iota((ROWS, ROWS), 1)
    first_lane = lax.axis_index("seq") * lane_of(heads, 0)
    gscals = [[] for _ in range(per)]
    dnexts = {(per - 1, h): dstate[h] for h in range(heads)}
    rims = {(per - 1, h): rim[:, h * WIDE : (h + 1) * WIDE] for h in range(heads)}

    def item(j, h):
        n = j * heads + h
        span = slice(j * BLOCK_LEN, (j + 1) * BLOCK_LEN)
        rowp, colp = rowp_ref[j * 8 : (j + 1) * 8], colp_ref[j * ROWS : (j + 1) * ROWS]
        tokp, slope = tokp_ref[span], slope_ref[span]
        cols = slice(h * WIDE, (h + 1) * WIDE)
        hc = slice(h * HEAD, (h + 1) * HEAD)
        beta, decay, qdecay, carry, qcarry, dlast, clast = decays(rowp, colp, tokp, h)
        go = go_ref[span, hc]
        query, keys, values = q_ref[j, h], k_ref[j, h], v_ref[j, h]
        inv, kk, attn, uw = t_ref[j, h], kk_ref[j, h], at_ref[j, h], uw_ref[j, h]
        yield
        state = mm(pl_ref[j, h, :, :HEAD], sin_ref[h]) + pl_ref[j, h, :, HEAD:]
        yield
        both = mm(jnp.concatenate([keys, uw[:, HEAD:]], axis=0), state)
        ks = both[:ROWS]
        upd = uw[:, :HEAD] - both[ROWS:]
        dlocal = mm(attn, go, 0, 0)
        while (j, h) not in dnexts:
            yield
        dnext = dnexts[j, h]
        yield
        dupd = dlocal + dlast * mm(keys, dnext)
        yield
        dx = mm(inv, dupd, 0, 0)
        yield
        dv = beta * dx
        dy = -(carry * dv)
        go32 = go.astype(F32)
        dnexts[j - 1, h] = clast * dnext + mm(
            jnp.concatenate([qcarry * query, keys], axis=0), jnp.concatenate([go32, dy], axis=0), 0, 0
        )
        yield
        outer = mm(jnp.concatenate([go32, dx], axis=0), upd, 1, 1)
        dattn, da = outer[:BLOCK_LEN], -outer[BLOCK_LEN:]
        yield
        dkd = mm(upd, dnext, 1, 1)
        right = mm(jnp.concatenate([go32, dy], axis=0), state, 1, 1)
        gos = right[:BLOCK_LEN]
        yield
        e = beta * da * decay
        f = dattn * qdecay
        ef = jnp.concatenate([f, e], axis=0)
        efk = mm(ef, keys)
        dq = qcarry * gos + efk[:BLOCK_LEN]
        yield
        dk = (
            right[BLOCK_LEN:]
            + dlast * dkd
            + efk[BLOCK_LEN:]
            + mm(ef, jnp.concatenate([query, keys], axis=0), 0, 0)
        )
        weave[3 * n] = dk
        weave[3 * n + 1] = dv
        yield
        dakk = da * kk
        z1 = beta * dakk
        z2 = dattn * attn
        kept = dlast * (dkd * keys)
        below = jnp.sum(z1, axis=0, keepdims=True) + jnp.sum(z2, axis=0, keepdims=True)
        dbeta = jnp.sum(dx * (values - carry * ks) + dakk, axis=1, keepdims=True)
        tail = jnp.sum(
            jnp.sum(kept, axis=0, keepdims=True) + clast * jnp.sum(state * dnext, axis=0, keepdims=True),
            axis=1, keepdims=True,
        )
        dgrow = jnp.sum(z1 + dy * ks - kept - jnp.where(diagonal, below, 0.0), axis=1, keepdims=True)
        dgrow = dgrow + jnp.where(last_row, tail, 0.0)
        lane = iota((ROWS, HEAD), 1)
        weave[3 * n + 2] = jnp.where(lane == 0, dbeta, dgrow)
        yield
        by_step = [weave[3 * n + 2, pl.ds(i, BLOCK_LEN, NH), :] for i in range(NH)]
        dg = sum(x[:, 1:2] for x in by_step) + jnp.sum(z2 + qcarry * (query * gos), axis=1, keepdims=True)
        after = (iota((BLOCK_LEN, BLOCK_LEN), 0) <= iota((BLOCK_LEN, BLOCK_LEN), 1)).astype(BF16)
        dlog = column(tokp, LINK) * mm(after, jnp.broadcast_to(dg, (BLOCK_LEN, HEAD)))[:, :1]
        dscal = [by_step[i][:, 0:1] * column(slope, lane_of(h, i)) for i in range(NH)]
        dscal.append(dlog * column(slope, lane_of(h, NH)))
        lane = iota((BLOCK_LEN, HEAD), 1)
        for i in range(NH + 1):
            gscals[j].append(jnp.where(lane == first_lane + lane_of(h, i), dscal[i], 0.0))
        logs = column(slope, HEAD // 2 + lane_of(h, NH))
        sums = jnp.where(lane == 0, dlog * logs, jnp.where(lane == 1, dscal[NH], 0.0))
        gsum_ref[h : h + 1, :] += jnp.sum(sums, axis=0, keepdims=True)
        yield
        conv = conv_ref[span, cols]
        sig = jax.nn.sigmoid(conv)
        act = conv * sig
        parts = []
        for part in range(1 + NH):
            piece = act[:, part * HEAD : (part + 1) * HEAD]
            scale = lax.rsqrt(jnp.sum(piece * piece, axis=1, keepdims=True) + NORM_EPS)
            if part:
                grad = weave[3 * n, pl.ds(part - 1, BLOCK_LEN, NH), :]
            else:
                grad = dq * (1.0 / math.sqrt(HEAD))
            unit = piece * scale
            parts.append(scale * (grad - unit * jnp.sum(grad * unit, axis=1, keepdims=True)))
        for i in range(NH):
            parts.append(weave[3 * n + 1, pl.ds(i, BLOCK_LEN, NH), :])
        dconv = jnp.concatenate(parts, axis=1) * (sig * (1.0 + conv * (1.0 - sig)))
        yield
        base = pl.multiple_of((block * per + j) * BLOCK_LEN, BLOCK_LEN)
        ext = proj_ref[pl.ds(base, BLOCK_LEN + HALO), cols].astype(F32)
        gw_ref[0:1, cols] += jnp.sum(dconv * ext[HALO:], axis=0, keepdims=True)
        zeros = jnp.zeros((8, WIDE), F32)
        length = BLOCK_LEN + 8
        total = jnp.concatenate([zeros, dconv * w_ref[0:1, cols]], axis=0)
        for lag in range(1, CONV):
            masked = column(tokp, LINK + lag - 1) * dconv
            gw_ref[lag : lag + 1, cols] += jnp.sum(masked * lag_rows(ext, lag), axis=0, keepdims=True)
            total = total + pltpu.roll(
                jnp.concatenate([zeros, masked * w_ref[lag : lag + 1, cols]], axis=0), length - lag, 0
            )
        rims[j - 1, h] = total[:8]
        fixed = total[length - 8 :] + rims[j, h]
        gproj_ref[span, cols] = jnp.concatenate([total[8 : length - 8], fixed], axis=0).astype(BF16)
        if j == per - 1:

            @pl.when(step == 0)
            def _():
                last[:, cols] = fixed

    running = [item(j, h) for j in reversed(range(per)) for h in range(heads)]
    while running:
        running = [one for one in running if next(one, "done") != "done"]
    for h in range(heads):
        dstate[h] = dnexts[-1, h]
        rim[:, h * WIDE : (h + 1) * WIDE] = rims[-1, h]
    for j in range(per):
        gscal_ref[j * BLOCK_LEN : (j + 1) * BLOCK_LEN] = sum(gscals[j]).astype(BF16)

    @pl.when(step == steps - 1)
    def _():
        passing = pltpu.make_async_remote_copy(
            rim, rim_in, rim_sem.at[0], rim_sem.at[1], device_id={"ctx": here - 1}, device_id_type=MESH
        )
        pl.when(here > 0)(passing.start)
        fix_ref[...] = last[...].astype(BF16)

        @pl.when(here < pieces - 1)
        def _():
            passing.wait_recv()
            fix_ref[...] = (last[...] + rim_in[...]).astype(BF16)

        for one in early:
            one.finish()
        line.finish()
        widesum_ref[...] = wheld[here // 2]
        tallsum_ref[...] = theld[here // 2].astype(F32)
        outsum_ref[...] = oheld[here // 2].astype(F32)
        gatesum_ref[...] = gheld[here // 2]
        pair.left()
        for one, first in zip(early, begun):
            for r in range(first, rounds):
                one.left(r)
        for r in range(rounds):
            line.left(r)
        pl.when(here > 0)(passing.wait_send)


def recurrence_backward(
    maps, cot, state_in, proj_ext, conv_w, rowp, colp, tokp, slopes, grad_heads, saved, wide, tall, outg, normed, ggate,
    heads, pieces, span_pieces,
):
    rows = tokp.shape[0]
    blocks = rows // BLOCK_LEN
    chips = pieces // 2
    per = 2
    final = blocks // per - 1
    whole = lambda *dims: pl.BlockSpec(dims, lambda i: (0,) * len(dims))
    by_block = lambda *dims: pl.BlockSpec((per,) + dims, lambda i: (final - i,) + (0,) * len(dims))
    token = lambda cols: pl.BlockSpec((per * BLOCK_LEN, cols), lambda i: (final - i, 0))
    shape = lambda *dims: jax.ShapeDtypeStruct(dims, F32)
    low_shape = lambda *dims: jax.ShapeDtypeStruct(dims, BF16)
    vmem = pl.BlockSpec(memory_space=pltpu.VMEM)
    low = lambda *dims: pltpu.VMEM(dims, BF16)
    square = (heads, ROWS, HEAD)
    wide_chunk, tall_chunk, out_chunk = wide.shape[1:], tall.shape[1:], outg.shape[2:]
    gate_chunk = (HEADS // heads, out_chunk[0], ggate.shape[1])
    dma = pltpu.SemaphoreType.DMA
    return pl.pallas_call(
        functools.partial(bwd_kernel, heads, pieces, blocks // per, per, early_rounds(pieces), span_pieces),
        grid=(blocks // per,),
        in_specs=[
            vmem, vmem, vmem, vmem, vmem,
            pl.BlockSpec((per * 8, ROWS), lambda i: (final - i, 0)),
            pl.BlockSpec((per * ROWS, HEAD), lambda i: (final - i, 0)), token(HEAD), token(HEAD),
            token(heads * HEAD), token(heads * WIDE),
            by_block(heads, BLOCK_LEN, HEAD), by_block(*square), by_block(*square), by_block(*square),
            by_block(*square), by_block(heads, BLOCK_LEN, ROWS), by_block(heads, ROWS, 2 * HEAD),
            by_block(heads, HEAD, 2 * HEAD), vmem, vmem, vmem, vmem, vmem,
        ],
        out_specs=[
            token(heads * WIDE), whole(8, heads * WIDE), whole(8, heads * WIDE), token(HEAD), whole(8, HEAD),
            whole(*wide_chunk), whole(*tall_chunk), whole(*out_chunk), whole(*gate_chunk),
        ],
        out_shape=[
            low_shape(rows, heads * WIDE), low_shape(8, heads * WIDE), shape(8, heads * WIDE), low_shape(rows, HEAD),
            shape(8, HEAD), low_shape(*wide_chunk), shape(*tall_chunk), shape(*out_chunk), low_shape(*gate_chunk),
        ],
        scratch_shapes=[
            pltpu.VMEM((heads, HEAD, HEAD), F32), pltpu.VMEM((3 * heads * per, ROWS, HEAD), F32),
            pltpu.VMEM((8, heads * WIDE), F32), pltpu.VMEM((8, heads * WIDE), F32),
            pltpu.VMEM((pieces, heads, HEAD, HEAD), BF16), pltpu.VMEM((8, heads * WIDE), F32),
            low(chips, *wide_chunk), low(chips, *tall_chunk), low(2, chips, *wide_chunk), low(2, chips, *tall_chunk),
            low(chips, 2, *gate_chunk), low(chips, *out_chunk), low(chips, *gate_chunk), low(chips, *out_chunk),
            low(chips, *gate_chunk), low(2, chips, *out_chunk), low(2, chips, *gate_chunk),
            dma((1, 3, pieces)), dma((1, pieces)), dma((2,)), dma((2,)), dma((2, 1, chips)), dma((2, 1, 2, chips)),
            dma((2, chips)), dma((2, 2, chips)), dma((2,)),
        ],
        compiler_params=pltpu.CompilerParams(
            vmem_limit_bytes=VMEM_LIMIT, collective_id=4, has_side_effects=True
        ),
        name="recurrence_backward",
    )(maps, cot, state_in, proj_ext, conv_w, rowp, colp, tokp, slopes, grad_heads, *saved, wide, tall, outg, normed, ggate)


def final_kernel(
    size, pieces, heads, norm_at, inner, gp_any, gg_any, gs_any, w_any, normed_any,
    fix_ref, x_ref, gmid_ref, norms_ref, gw_ref, gain_ref, gsum_ref, loss_ref, gnorm_ref, wide_ref, gatesum_ref,
    ingrad_ref, gmix_ref, ggate_ref, gtail_ref, gwg_ref, gwu_ref, mean_ref, ends_ref, both_ref,
    gp_ref, gg_ref, gs_ref, w_ref, normed_ref, load_sem, wideout_ref, gateout_ref,
    sent, got, whole, turned, *halves_and_rest,
):
    grads, theirs, helds, cames, blocks = [halves_and_rest[2 * n : 2 * n + 2] for n in range(5)]
    around, along, summed, *sems = halves_and_rest[10:]
    final_body(
        size, pieces, heads, norm_at, inner, gp_any, gg_any, gs_any, w_any, normed_any,
        fix_ref, x_ref, gmid_ref, norms_ref, gw_ref, gain_ref, gsum_ref, loss_ref, gnorm_ref, wide_ref, gatesum_ref,
        ingrad_ref, gmix_ref, ggate_ref, gtail_ref, gwg_ref, gwu_ref, mean_ref, ends_ref, both_ref,
        gp_ref, gg_ref, gs_ref, w_ref, normed_ref, load_sem, wideout_ref, gateout_ref,
        sent, got, whole, turned, grads, theirs, helds, cames, blocks, around, along, summed, *sems,
    )


def final_body(
    size, pieces, heads, norm_at, inner, gp_any, gg_any, gs_any, w_any, normed_any,
    fix_ref, x_ref, gmid_ref, norms_ref, gw_ref, gain_ref, gsum_ref, loss_ref, gnorm_ref, wide_ref, gatesum_ref,
    ingrad_ref, gmix_ref, ggate_ref, gtail_ref, gwg_ref, gwu_ref, mean_ref, ends_ref, both_ref,
    gp_ref, gg_ref, gs_ref, w_ref, normed_ref, load_sem, wideout_ref, gateout_ref,
    sent, got, whole, turned, grads, theirs, helds, cames, blocks, around, along, summed,
    local_sem, seq_send, seq_recv, pair_send, pair_recv, line_send, line_recv, ctx_send, ctx_recv,
):
    me, here = lax.axis_index("seq"), lax.axis_index("ctx")
    count = x_ref.shape[0]
    loads = [
        pltpu.make_async_copy(source, target, load_sem.at[n])
        for n, (source, target) in enumerate(
            [(gp_any, gp_ref), (gg_any, gg_ref), (gs_any, gs_ref), (w_any, w_ref), (normed_any, normed_ref)]
        )
    ]
    for load in loads:
        load.start()
    barrier = pltpu.get_barrier_semaphore()
    peers = [({"seq": partner(me, i, size)}, here >= 0) for i in range(1, size)]
    peers += [({"ctx": lax.rem(here + i, pieces)}, here >= 0) for i in range(1, pieces)]
    pl.semaphore_wait(barrier, greet(peers, barrier))

    def dot(a, b, ca=1, cb=0):
        return lax.dot_general(a, b, (((ca,), (cb,)), ((), ())), preferred_element_type=F32)

    def rows(q):
        return pl.ds(pl.multiple_of(q * count, count), count)

    def to_peer(n, i):
        q = partner(me, i, size)
        source, target = [
            (sent.at[i - 1], got.at[i - 1]), (wide_ref.at[:, q], wideout_ref.at[me]),
            (around.at[me], around.at[me]), (helds[0].at[here // 2, q], blocks[0].at[me]),
            (gatesum_ref.at[q], gateout_ref.at[me]), (helds[1].at[here // 2, q], blocks[1].at[me]),
        ][n]
        return pltpu.make_async_remote_copy(
            source, target, seq_send.at[n, i - 1], seq_recv.at[n, i - 1], device_id={"seq": q}, device_id_type=MESH
        )

    def to_piece(i):
        return pltpu.make_async_remote_copy(
            along.at[here], along.at[here], ctx_send.at[i - 1], ctx_recv.at[i - 1],
            device_id={"ctx": lax.rem(here + i, pieces)}, device_id_type=MESH,
        )

    gate_at, tail_at = gp_ref.shape[1], gp_ref.shape[1] + gg_ref.shape[1]
    for load in loads:
        load.wait()
    gp_ref[gp_ref.shape[0] - 8 :] = fix_ref[...]

    def parts():
        for first in range(0, D, 256):
            tile = slice(first, first + 256)
            value = (
                dot(gp_ref[...], w_ref[tile, :gate_at], 1, 1)
                + dot(gg_ref[...], w_ref[tile, gate_at:tail_at], 1, 1)
                + dot(gs_ref[...], w_ref[tile, tail_at:], 1, 1)
            )
            whole[:, tile] = value

        def give(k, carry):
            i = size - 1 - k
            sent[i - 1] = whole[rows(partner(me, i, size))].astype(BF16)
            pltpu.make_async_remote_copy(
                sent.at[i - 1], got.at[i - 1], seq_send.at[0, i - 1], seq_recv.at[0, i - 1],
                device_id={"seq": partner(me, i, size)}, device_id_type=MESH,
            ).start()
            return carry

        lax.fori_loop(0, size - 1, give, 0)

    turned[...] = normed_ref[...].T
    rank_rows = D // (size * pieces)
    pairs = [Siblings([grads[n]], [theirs[n]], [helds[n]], pair_send.at[n], pair_recv.at[n]) for n in range(2)]
    lines = [LineSum(pieces, [helds[n]], [cames[n]], line_send.at[n], line_recv.at[n]) for n in range(2)]
    split = grads[0].shape[4]

    def gradient(source, first, cols, n, at):
        grad = dot(turned[...], source[:, first : first + cols])
        for r in range(size):
            for c in range(pieces):
                row = (r * pieces + c) * rank_rows
                grads[n][c // 2, c % 2, r, :, at : at + cols] = grad[row : row + rank_rows].astype(BF16)

    for first in range(0, split, 256):
        gradient(gp_ref, first, min(256, split - first), 0, first)
    pairs[0].start()
    for first in range(split, gate_at, 256):
        gradient(gp_ref, first, min(256, gate_at - first), 1, first - split)
    gradient(gs_ref, 0, HEAD, 1, gate_at - split)
    channels = gw_ref.shape[1]
    mine = channel_rows(D // size, channels)
    taps = jnp.zeros((D // size, HEAD), F32)
    for lag in range(CONV):
        spread = jnp.where(mine, gw_ref[lag : lag + 1], 0.0).astype(BF16)
        taps = taps + dot(spread, tap_lanes(channels, CONV - 1 - lag, norm_at + 3))
    for c in range(pieces):
        grads[1][c // 2, c % 2, me, :, gate_at - split :] = (
            grads[1][c // 2, c % 2, me, :, gate_at - split :].astype(F32) + taps[c * rank_rows : (c + 1) * rank_rows]
        ).astype(BF16)
    pairs[1].start()
    pairs[0].add()
    lines[0].round(0)
    parts()
    pairs[1].add()
    lines[1].round(0)
    rounds = pieces // 2 - 1
    for r in range(1, rounds - 1):
        for line in lines:
            line.round(r)
    for i in range(1, size):
        to_peer(0, i).wait_recv()
    gnormed = whole[rows(me)]
    for i in range(1, size):
        gnormed = gnormed + got[i - 1].astype(F32)
    x = x_ref[...].astype(F32)
    inv = lax.rsqrt(jnp.mean(x * x, axis=1, keepdims=True) + NORM_EPS)
    unit = x * inv
    down = gnormed * norms_ref[0:1, :]
    ingrad_ref[...] = gmid_ref[...] + inv * (down - unit * jnp.mean(down * unit, axis=1, keepdims=True))
    term = jnp.sum(gnormed * unit, axis=0, keepdims=True)
    lane = iota((1, HEAD), 1)
    ends = jnp.where(lane == 2 * HEADS, loss_ref[...], 0.0)
    for h in range(heads):
        for n in range(2):
            ends = jnp.where(lane == n * HEADS + me * heads + h, gsum_ref[h : h + 1, n : n + 1], ends)
    around[me] = jnp.zeros(around.shape[1:], F32)
    around[me, 0:1] = gain_ref[...]
    around[me, 1:2] = ends
    for j in range(D // HEAD):
        around[me, 8 + j : 9 + j] = term[:, j * HEAD : (j + 1) * HEAD]
        around[me, 8 + D // HEAD + j : 9 + D // HEAD + j] = gnorm_ref[:, j * HEAD : (j + 1) * HEAD]
    for i in range(1, size):
        to_peer(2, i).start()
    kept = [
        pltpu.make_async_copy(wide_ref.at[:, me], wideout_ref.at[me], local_sem.at[0]),
        pltpu.make_async_copy(gatesum_ref.at[me], gateout_ref.at[me], local_sem.at[1]),
    ]
    for copy in kept:
        copy.start()
    for i in reversed(range(1, size)):
        to_peer(1, i).start()
        to_peer(4, i).start()
    for line in lines:
        line.round(rounds - 1)
    for i in range(1, size):
        to_peer(2, i).wait_recv()
    mine = around[0]
    for r in range(1, size):
        mine = mine + around[r]
    along[here] = mine
    for i in range(1, pieces):
        to_piece(i).start()
    for n, phase in ((0, 3), (1, 5)):
        lines[n].finish()
        blocks[n][me] = helds[n][here // 2, me]
        for i in reversed(range(1, size)):
            to_peer(phase, i).start()
    for i in range(1, pieces):
        to_piece(i).wait_recv()
    total = along[0]
    for c in range(1, pieces):
        total = total + along[c]
    ends_ref[...] = total[:2]
    valid = jnp.maximum(jnp.sum(norms_ref[2:3, :], axis=1, keepdims=True), 1.0)
    mean_ref[...] = total[1:2, 2 * HEADS : 2 * HEADS + 1] / (D * valid)
    summed[...] = total
    place = (me * pieces + here) * rank_rows
    for n in range(2):
        row = summed[pl.ds(8 + n * (D // HEAD) + place // HEAD, 1), :]
        both_ref[n : n + 1, :] = pltpu.roll(row, lax.rem(HEAD - lax.rem(place, HEAD), HEAD), 1)
    tail = jnp.zeros((rank_rows, HEAD), F32)
    for copy in kept:
        copy.wait()
    for i in range(1, size):
        for n in (1, 4, 3):
            to_peer(n, i).wait_recv()
    wide_cols = tail_at - gate_at
    for r in range(size):
        gwg_ref[:, r * inner : (r + 1) * inner] = wideout_ref[r, 0, :, :inner].astype(F32)
        gwu_ref[:, r * inner : (r + 1) * inner] = wideout_ref[r, 1, :, :inner].astype(F32)
        ggate_ref[:, r * wide_cols : (r + 1) * wide_cols] = gateout_ref[r].astype(F32)
        gmix_ref[:, r * gate_at : r * gate_at + split] = blocks[0][r].astype(F32)
    for i in range(1, size):
        to_peer(5, i).wait_recv()
    for r in range(size):
        block = blocks[1][r].astype(F32)
        gmix_ref[:, r * gate_at + split : (r + 1) * gate_at] = block[:, : gate_at - split]
        tail = tail + block[:, gate_at - split :]
    gtail_ref[...] = tail
    for pair in pairs:
        pair.left()
    for line in lines:
        for r in range(pieces // 2 - 1):
            line.left(r)
    for i in range(1, size):
        for n in range(6):
            to_peer(n, i).wait_send()
    for i in range(1, pieces):
        to_piece(i).wait_send()


def final_part(
    size, pieces, heads, norm_at, gp, gg, gs, weights, normed, fix, x, gmid, norms, gw, gain, gsum, loss, gnorm, wide,
    gatesum,
):
    count = x.shape[0]
    chips = pieces // 2
    held, inner = D // (size * pieces), FF // size
    split = WIDE if heads > 1 else 3 * HEAD
    widths = (split, gp.shape[1] - split + gs.shape[1])
    small = (8 + 2 * (D // HEAD), HEAD)
    vmem = pl.BlockSpec(memory_space=pltpu.VMEM)
    out = lambda *dims: jax.ShapeDtypeStruct(dims, F32)
    low = lambda *dims: pltpu.VMEM(dims, BF16)
    high = lambda *dims: pltpu.VMEM(dims, F32)
    dma = pltpu.SemaphoreType.DMA
    return pl.pallas_call(
        functools.partial(final_kernel, size, pieces, heads, norm_at, inner),
        in_specs=[pl.BlockSpec(memory_space=pltpu.HBM)] * 5 + [vmem] * 11,
        out_specs=[vmem] * 9,
        out_shape=[
            out(count, D), out(held, size * gp.shape[1]), out(held, size * gg.shape[1]), out(held, HEAD),
            out(held, size * inner), out(held, size * inner), out(1, 1), out(2, HEAD), out(2, HEAD),
        ],
        scratch_shapes=[
            low(*gp.shape), low(*gg.shape), low(*gs.shape), low(*weights.shape), low(*normed.shape), dma((5,)),
            low(size, 2, held, wide.shape[3]), low(*gatesum.shape),
            low(size - 1, count, D), low(size - 1, count, D), high(size * count, D), low(D, normed.shape[0]),
            *[low(chips, 2, size, held, w) for w in widths], *[low(chips, size, held, w) for w in widths],
            *[low(chips, size, held, w) for w in widths], *[low(2, chips, size, held, w) for w in widths],
            *[low(size, held, w) for w in widths], high(size, *small), high(pieces, *small), high(*small),
            dma((2,)), dma((6, size - 1)), dma((6, size - 1)), dma((2, 1)), dma((2, 1)), dma((2, 1, chips)),
            dma((2, 1, 2, chips)),
            dma((pieces - 1,)), dma((pieces - 1,)),
        ],
        compiler_params=pltpu.CompilerParams(
            vmem_limit_bytes=VMEM_LIMIT, collective_id=5, has_side_effects=True
        ),
        name="final_part",
    )(gp, gg, gs, weights, normed, fix, x, gmid, norms, gw, gain, gsum, loss, gnorm, wide, gatesum)


def finish_kernel(
    scal_cols, taps_at, final_ref, ingrad_ref, gmix_ref, ggate_ref, gwg_ref, gwu_ref, tall_ref, outsum_ref,
    tail_ref, ends_ref, both_ref,
    final_out, ingrad_out, gmix_out, ggate_out, gwg_out, gwu_out, gwd_out, gout_out,
    gscal_out, gconv_out, norma_out, normm_out, gain_out, alog_out, dt_out,
):
    for source, target in (
        (final_ref, final_out), (ingrad_ref, ingrad_out), (gmix_ref, gmix_out), (ggate_ref, ggate_out),
        (gwg_ref, gwg_out), (gwu_ref, gwu_out), (outsum_ref, gout_out),
    ):
        target[...] = source[...]
    gwd_out[...] = tall_ref[: gwd_out.shape[0]]
    tail = tail_ref[...]
    rows, channels = tail.shape[0], gconv_out.shape[1]
    square = jnp.concatenate([tail, jnp.zeros((HEAD - rows, HEAD), F32)], axis=0)
    gscal_out[...] = square.T[:scal_cols, :rows]
    mine = channel_rows(rows, channels)
    for tap in range(CONV):
        spread = exact(tail, tap_lanes(channels, tap, taps_at).astype(F32), 1, 1)
        gconv_out[tap : tap + 1] = jnp.sum(jnp.where(mine, spread, 0.0), axis=0, keepdims=True)
    held = norma_out.shape[1]
    norma_out[...] = both_ref[0:1, :held]
    normm_out[...] = both_ref[1:2, :held]
    gain_out[...] = ends_ref[0:1, :]
    alog_out[...] = ends_ref[1:2, :HEADS]
    dt_out[...] = ends_ref[1:2, HEADS : 2 * HEADS]


def finish_part(scal_cols, taps_at, deep, channels, *parts):
    vmem = pl.BlockSpec(memory_space=pltpu.VMEM)
    held = parts[2].shape[0]
    out = lambda dims, kind=F32: jax.ShapeDtypeStruct(dims, kind)
    return pl.pallas_call(
        functools.partial(finish_kernel, scal_cols, taps_at),
        in_specs=[vmem] * 11,
        out_specs=[vmem] * 15,
        out_shape=[out(p.shape, p.dtype) for p in parts[:6]] + [
            out((deep, D)), out(parts[7].shape), out((scal_cols, held)), out((CONV, channels)),
            out((1, held)), out((1, held)), out((1, HEAD)), out((1, HEADS)), out((1, HEADS)),
        ],
        compiler_params=pltpu.CompilerParams(vmem_limit_bytes=VMEM_LIMIT),
        name="finish_part",
    )(*parts)


def local(
    block_input, teacher, valid_mask, segments, mix_proj, scalar_proj, gate_proj, out_proj, conv_weight,
    norm_attn, norm_mlp, head_gain, a_log, dt_bias, w_gate, w_up, w_down,
):
    seq_size, pieces = lax.axis_size("seq"), lax.axis_size("ctx")
    heads = HEADS // seq_size
    rows = block_input.shape[0] * seq_size
    token_total = segments.shape[0]
    seq_length = min(SEQ_LEN, token_total)
    span_pieces = min(pieces, (MOST_DOC.get(token_total, token_total) - 2) // rows + 1)
    index = lax.axis_index("ctx")
    held = mix_proj.shape[0]
    scal_cols = HEADS * (NH + 1)
    norm_at, taps_at = scal_cols, scal_cols + 3

    x_full, halo, gathered, stage = start_gather(
        seq_size, pieces, norm_at, block_input, mix_proj, gate_proj, scalar_proj.T, norm_attn[None, :],
        norm_mlp[None, :], conv_weight.T, valid_mask[None, :], w_gate, w_up,
    )
    weights = gathered.reshape(D, -1)
    piece_start = index * rows
    window = lax.dynamic_slice_in_dim(jnp.pad(segments, (CONV, 0)), piece_start, rows + CONV)
    place_in = (piece_start + jnp.arange(rows, dtype=jnp.int32)) % seq_length
    marks = jnp.stack(
        [
            ((window[CONV - lag : CONV - lag + rows] == window[CONV:]) & (place_in >= lag)).astype(F32)
            if lag < CONV
            else jnp.zeros((rows,), F32)
            for lag in range(1, 9)
        ]
    )
    (
        proj_ext, normed, gate_out, tokp, slopes, colp, rowp, conv_w, norms,
        oloc, carr, state_in, maps, *saved, wg_full, wu_full, wo_full,
    ) = recurrence_forward(heads, pieces, span_pieces, norm_at, a_log[None, :], dt_bias[None, :], x_full, halo, weights, marks, stage, out_proj)
    (
        final_out, grad_middle, grad_heads, grad_gate_out, cot, gain_term, norm_mlp_term, loss, wide, tall, outg,
    ) = middle_part(
        seq_size, heads, pieces, token_total, block_input, teacher, valid_mask[None, :], norms, head_gain[None, :],
        oloc, carr, gate_out, state_in, wo_full.reshape(heads * HEAD, D), wg_full.reshape(D, -1),
        wu_full.reshape(D, -1), w_down,
    )
    grad_proj, fixed_rows, gw, grad_scal, gsum, wide_sum, tall_sum, out_sum, gate_sum = recurrence_backward(
        maps, cot, state_in, proj_ext, conv_w, rowp, colp, tokp, slopes, grad_heads, saved, wide, tall, outg, normed,
        grad_gate_out, heads, pieces, span_pieces,
    )
    input_grad, mix_grad, gate_grad, tail_grad, wg_grad, wu_grad, mean_loss, ends, norm_grads = final_part(
        seq_size, pieces, heads, norm_at, grad_proj, grad_gate_out, grad_scal, weights, normed, fixed_rows, block_input,
        grad_middle, norms, gw, gain_term, gsum, loss, norm_mlp_term, wide_sum.reshape(2, seq_size, held, -1),
        gate_sum,
    )
    (
        final_out, input_grad, mix_grad, gate_grad, wg_grad, wu_grad, wd_grad, out_grad,
        scal_grad, conv_grad, norm_a_grad, norm_m_grad, gain_grad, alog_grad, dt_grad,
    ) = finish_part(
        scal_cols, taps_at, w_down.shape[0], conv_weight.shape[0],
        final_out, input_grad, mix_grad, gate_grad, wg_grad, wu_grad, tall_sum, out_sum, tail_grad, ends, norm_grads,
    )
    return (
        final_out, mean_loss[0, 0], input_grad, mix_grad, scal_grad.T, gate_grad, out_grad, conv_grad.T,
        norm_a_grad.reshape(-1), norm_m_grad.reshape(-1), gain_grad.reshape(-1), alog_grad.reshape(-1),
        dt_grad.reshape(-1), wg_grad, wu_grad, wd_grad,
    )


def solution(mesh):
    tokens, vector, matrix = P(("ctx", "seq"), None), P(BOTH), P(BOTH, None)
    in_specs = (
        tokens, tokens, P(("ctx", "seq")), P(), matrix, matrix, matrix, matrix, matrix, vector, vector,
        P(), P(), P(), matrix, matrix, matrix,
    )
    out_specs = (
        tokens, P(), tokens, matrix, matrix, matrix, matrix, matrix, vector, vector, P(), P(), P(),
        matrix, matrix, matrix,
    )
    return jax.shard_map(local, mesh=mesh, in_specs=in_specs, out_specs=out_specs, check_vma=False)
```

```python
import functools
import math

import jax
import jax.numpy as jnp
from jax import lax
from jax.experimental import pallas as pl
from jax.experimental.pallas import tpu as pltpu
from jax.sharding import PartitionSpec as P

D = 1024
HEADS = 8
HEAD = 128
NH = 2
FF = 2816
BLOCK_LEN = 64
ROWS = BLOCK_LEN * NH
CONV = 4
SEQ_LEN = 32768
MOST_DOC = {4096: 2048, 32768: 8192}
WIDE = (1 + 2 * NH) * HEAD
HALO = 16
NORM_EPS = 1e-06
VMEM_LIMIT = 60 << 20
F32 = jnp.float32
BF16 = jnp.bfloat16
BOTH = ("seq", "ctx")
MESH = pl.DeviceIdType.MESH


class Split:
    def __init__(self, x):
        self.high = x.astype(BF16)
        self.low = (x - self.high.astype(F32)).astype(BF16)


def mm(a, b, ca=1, cb=0):
    if not isinstance(a, Split) and a.dtype != BF16:
        a = Split(a)
    if not isinstance(b, Split) and b.dtype != BF16:
        b = Split(b)
    if isinstance(a, Split) and isinstance(b, Split):
        left, right = (a.high, a.high, a.low), (b.high, b.low, b.high)
    elif isinstance(a, Split):
        left, right = (a.high, a.low), (b, b)
    elif isinstance(b, Split):
        left, right = (a, a), (b.high, b.low)
    else:
        left, right = (a,), (b,)
    if len(left) > 1:
        left, right = (jnp.concatenate(left, axis=ca),), (jnp.concatenate(right, axis=cb),)
    return lax.dot_general(left[0], right[0], (((ca,), (cb,)), ((), ())), preferred_element_type=F32)


def lanes_for(columns):
    return -(-columns // HEAD) * HEAD


def iota(shape, axis):
    return lax.broadcasted_iota(jnp.int32, shape, axis)


def unit_lower_inverses(systems):
    n = systems[0].shape[0]
    ri, ci = iota((n, n), 0), iota((n, n), 1)
    pick = (iota((n, 8), 0) % 8 == iota((n, 8), 1)).astype(BF16)
    own = ri // 8 == ci // 8
    eye = (ri == ci).astype(F32).reshape(n // 8, 8, n)
    small = [mm(jnp.where(own, a, 0.0), pick).reshape(n // 8, 8, 8) for a in systems]
    inv = [eye for _ in systems]
    for j in range(7):
        inv = [x - m[:, :, j : j + 1] * x[:, j : j + 1, :] for x, m in zip(inv, small)]
    inv = [x.reshape(n, n) for x in inv]
    size = 8
    while size < n:
        off = (ri // (2 * size) == ci // (2 * size)) & (ri // size != ci // size)
        halves = [Split(x) for x in inv]
        right = [mm(jnp.where(off, a, 0.0), x) for a, x in zip(systems, halves)]
        inv = [x - mm(y, z) for x, y, z in zip(inv, halves, right)]
        size *= 2
    return inv


DOC = 7
LINK = DOC + 1


def lane_of(h, what):
    return h * (NH + 1) + what


def column(table, lane):
    return table[:, lane : lane + 1]


def decays(rowp, colp, tokp, h):
    g = lane_of(h, NH)
    cs_row, g_row = rowp[DOC : DOC + 1, :], rowp[g : g + 1, :]
    cs_col, g_col = column(colp, DOC), column(colp, g)
    cs_tok, g_tok = column(tokp, DOC), column(tokp, g)
    beta = column(colp, lane_of(h, 0))
    ri, ci = iota((ROWS, ROWS), 0), iota((ROWS, ROWS), 1)
    strict = (ri > ci) & (cs_col == cs_row)
    decay = jnp.where(strict, jnp.exp(jnp.where(strict, g_col - g_row, 0.0)), 0.0)
    rt, ct = iota((BLOCK_LEN, ROWS), 0), iota((BLOCK_LEN, ROWS), 1)
    seen = (rt * NH + NH - 1 >= ct) & (cs_tok == cs_row)
    qdecay = jnp.where(seen, jnp.exp(jnp.where(seen, g_tok - g_row, 0.0)), 0.0)
    carry = jnp.where(cs_col == 0.0, jnp.exp(g_col), 0.0)
    qcarry = jnp.where(cs_tok == 0.0, jnp.exp(g_tok), 0.0)
    cs_last, g_last = cs_row[:, ROWS - 1 :], g_row[:, ROWS - 1 :]
    same = cs_col == cs_last
    dlast = jnp.where(same, jnp.exp(jnp.where(same, g_last - g_col, 0.0)), 0.0)
    clast = jnp.where(cs_last == 0.0, jnp.exp(g_last), 0.0)
    return beta, decay, qdecay, carry, qcarry, dlast, clast


def lag_rows(ext, lag):
    moved = pltpu.roll(ext, lag, 0) if lag else ext
    return moved[HALO:]


UP, DOWN, ACROSS = 0, 1, 2


class Line:
    def __init__(self, pieces, parts, send_sem, recv_sem, up=True, down=True, reach=None):
        self.chips = pieces // 2
        self.reach = self.chips - 1 if reach is None else reach
        self.here = lax.axis_index("ctx")
        self.chip = self.here // 2
        self.core = lax.rem(self.here, 2)
        self.other = self.here + 1 - 2 * self.core
        self.parts, self.send_sem, self.recv_sem, self.up, self.down = parts, send_sem, recv_sem, up, down

    def copies(self, chunk, way, only=None):
        target = (self.here + 2, self.here - 2, self.other)[way]
        return [
            pltpu.make_async_remote_copy(
                part(chunk), part(chunk), self.send_sem.at[n, way, chunk], self.recv_sem.at[n, chunk],
                device_id={"ctx": target}, device_id_type=MESH,
            )
            for n, part in enumerate(self.parts)
            if only is None or n == only
        ]

    def start(self, chunk, way, only=None):
        for copy in self.copies(chunk, way, only):
            copy.start()

    def arrived(self, chunk, only=None):
        for copy in self.copies(chunk, ACROSS, only):
            copy.wait_recv()

    def left(self, chunk, way):
        for copy in self.copies(chunk, way):
            copy.wait_send()

    def routes(self, distance, act):
        if distance == 0:
            if self.up and self.reach:
                pl.when(self.chip < self.chips - 1)(lambda: act(self.here, UP))
            if self.down and self.reach:
                pl.when(self.chip > 0)(lambda: act(self.here, DOWN))
            act(self.here, ACROSS)
            return
        below, above = self.here - 2 * distance, self.here + 2 * distance
        onward = distance < self.reach
        if self.up:

            @pl.when(self.chip >= distance)
            def _():
                if onward:
                    pl.when(self.chip < self.chips - 1)(lambda: act(below, UP))
                act(below, ACROSS)

        if self.down:

            @pl.when(self.chip + distance < self.chips)
            def _():
                if onward:
                    pl.when(self.chip > 0)(lambda: act(above, DOWN))
                act(above, ACROSS)

    def own(self, only=None):
        self.routes(0, lambda chunk, way: self.start(chunk, way, only))

    def hop(self, distance):
        for n in range(len(self.parts)):
            if self.up:
                pl.when(self.chip >= distance)(lambda n=n: self.arrived(self.here - 2 * distance, n))
            if self.down:
                pl.when(self.chip + distance < self.chips)(lambda n=n: self.arrived(self.here + 2 * distance, n))
            self.routes(distance, lambda chunk, way, n=n: self.start(chunk, way, n))

    def finish(self):
        for chip in range(self.chips):
            needed = (self.chip <= chip + (self.reach if self.up else 0)) & (
                self.chip >= chip - (self.reach if self.down else 0)
            )
            pl.when(needed)(lambda chip=chip: self.arrived(2 * chip + 1 - self.core))
        for distance in range(self.reach + 1):
            self.routes(distance, self.left)


class LineSum:
    def __init__(self, pieces, held, came, send_sem, recv_sem):
        self.chips = pieces // 2
        self.here = lax.axis_index("ctx")
        self.chip = self.here // 2
        self.held, self.came, self.send_sem, self.recv_sem = held, came, send_sem, recv_sem

    def copies(self, owner, way):
        return [
            pltpu.make_async_remote_copy(
                held.at[owner], came.at[way, owner], self.send_sem.at[n, owner], self.recv_sem.at[n, way, owner],
                device_id={"ctx": self.here + 2 - 4 * way}, device_id_type=MESH,
            )
            for n, (held, came) in enumerate(zip(self.held, self.came))
        ]

    def take(self, owner, way):
        for copy in self.copies(owner, way):
            copy.wait_recv()
        for held, came in zip(self.held, self.came):
            held[owner] = (held[owner].astype(F32) + came[way, owner].astype(F32)).astype(BF16)

    def send(self, owner, way):
        for copy in self.copies(owner, way):
            copy.start()

    def each(self, r, act):
        top = self.chips - 1
        for way, place in ((UP, self.chip), (DOWN, top - self.chip)):
            owner = top - (r - place) if way == UP else r - place
            pl.when((place <= r) & (place < top))(lambda: act(owner, way, place))

    def settle(self, r):
        self.each(r, lambda owner, way, place: pl.when(place > 0)(lambda: self.take(owner, way)))

    def launch(self, r):
        self.each(r, lambda owner, way, place: self.send(owner, way))

    def left(self, r):
        def wait(owner, way, place):
            for copy in self.copies(owner, way):
                copy.wait_send()

        self.each(r, wait)

    def round(self, r):
        self.settle(r)
        self.launch(r)

    def finish(self):
        top = self.chips - 1
        pl.when(self.chip > 0)(lambda: self.take(self.chip, UP))
        pl.when(self.chip < top)(lambda: self.take(self.chip, DOWN))


def early_rounds(pieces):
    rounds = pieces // 2 - 1
    return max(1, rounds - 1), max(1, rounds - 2)


class Siblings:
    def __init__(self, parts, theirs, held, send_sem, recv_sem):
        self.here = lax.axis_index("ctx")
        self.core = lax.rem(self.here, 2)
        self.parts, self.theirs, self.held, self.send_sem, self.recv_sem = parts, theirs, held, send_sem, recv_sem

    def copies(self):
        return [
            pltpu.make_async_remote_copy(
                part.at[:, 1 - self.core], theirs, self.send_sem.at[n], self.recv_sem.at[n],
                device_id={"ctx": self.here + 1 - 2 * self.core}, device_id_type=MESH,
            )
            for n, (part, theirs) in enumerate(zip(self.parts, self.theirs))
        ]

    def start(self):
        for copy in self.copies():
            copy.start()

    def add(self):
        for copy in self.copies():
            copy.wait_recv()
        for part, theirs, held in zip(self.parts, self.theirs, self.held):

            def one(chip, carry, part=part, theirs=theirs, held=held):
                held[chip] = (part[chip, self.core].astype(F32) + theirs[chip].astype(F32)).astype(BF16)
                return carry

            lax.fori_loop(0, part.shape[0], one, 0)

    def left(self):
        for copy in self.copies():
            copy.wait_send()


def partner(me, i, size):
    total, bit = 0, 1
    while bit < size:
        total = total + lax.rem(me // bit + i // bit, 2) * bit
        bit *= 2
    return total


def chips_within(span_pieces, pieces):
    return min(pieces // 2 - 1, (span_pieces + 1) // 2)


def greet(devices, barrier):
    total = 0
    for place, there in devices:
        pl.when(there)(
            lambda place=place: pl.semaphore_signal(barrier, inc=1, device_id=place, device_id_type=MESH)
        )
        total = total + jnp.asarray(there, jnp.int32)
    return total


def line_neighbours(pieces):
    here = lax.axis_index("ctx")
    chip, core = here // 2, lax.rem(here, 2)
    return [
        ({"ctx": here + 2}, chip < pieces // 2 - 1),
        ({"ctx": here - 2}, chip > 0),
        ({"ctx": here + 1 - 2 * core}, here >= 0),
    ]


def start_kernel(
    size, pieces, norm_at, x_ref, mix_ref, gate_ref, scal_ref, norma_ref, normm_ref, taps_ref, mask_ref, wg_ref, wu_ref,
    xfull_ref, halo_ref, full_ref, stage_ref,
    tail_ref, sides, local_sem, seq_send, seq_recv, line_send, line_recv, halo_sem,
):
    me, here = lax.axis_index("seq"), lax.axis_index("ctx")
    count = x_ref.shape[0]
    core = lax.rem(here, 2)
    inner = wg_ref.shape[1] // size
    gate_at = mix_ref.shape[1] // size
    tail_at = gate_at + gate_ref.shape[1] // size

    def placed(rows_, lane):
        at = (iota((rows_.shape[0], HEAD), 1) == lane + iota((rows_.shape[0], HEAD), 0)).astype(BF16)
        return lax.dot_general(rows_, at, (((0,), (0,)), ((), ())), preferred_element_type=F32)

    held, channels = tail_ref.shape[0], taps_ref.shape[1]
    pack = placed(scal_ref[...], 0) + placed(norma_ref[...], norm_at) + placed(normm_ref[...], norm_at + 1)
    valid = jnp.sum(mask_ref[...].astype(F32), axis=1, keepdims=True)
    pack = pack + jnp.where((iota((held, HEAD), 0) == 0) & (iota((held, HEAD), 1) == norm_at + 2), valid, 0.0)
    mine = channel_rows(held, channels)
    for tap in range(CONV):
        spread = jnp.where(mine, taps_ref[tap : tap + 1].astype(F32), 0.0).astype(BF16)
        pack = pack + lax.dot_general(
            spread, tap_lanes(channels, tap, norm_at + 3), (((1,), (0,)), ((), ())), preferred_element_type=F32
        )
    tail_ref[...] = pack.astype(BF16)
    barrier = pltpu.get_barrier_semaphore()
    peers = [({"seq": partner(me, i, size)}, here >= 0) for i in range(1, size)]
    side = [({"ctx": here + 1}, (core == 1) & (here < pieces - 1)), ({"ctx": here - 1}, (core == 0) & (here > 0))]
    total = greet(peers + line_neighbours(pieces) + side, barrier)
    pl.semaphore_wait(barrier, total)

    def rows(q):
        return pl.ds(pl.multiple_of(q * count, count), count)

    def cols(q, width):
        return pl.ds(pl.multiple_of(q * width, HEAD), width)

    def ends(n, q):
        return [
            (mix_ref.at[:, cols(q, gate_at)], full_ref.at[me, here, :, :gate_at]),
            (gate_ref.at[:, cols(q, tail_at - gate_at)], full_ref.at[me, here, :, gate_at:tail_at]),
            (tail_ref, full_ref.at[me, here, :, tail_at:]),
            (x_ref, xfull_ref.at[rows(me)]),
            (sides.at[q], stage_ref.at[me]),
        ][n]

    def exchange(n, i):
        q = partner(me, i, size)
        source, target = ends(n, q)
        return pltpu.make_async_remote_copy(
            source, target, seq_send.at[n, i - 1], seq_recv.at[n, i - 1], device_id={"seq": q}, device_id_type=MESH
        )

    def own(n):
        return pltpu.make_async_copy(*ends(n, me), local_sem.at[n])

    def begin(n):
        own(n).start()
        for i in range(1, size):
            exchange(n, i).start()

    def end(n):
        own(n).wait()
        for i in range(1, size):
            exchange(n, i).wait_recv()

    for n in range(3):
        begin(n)
    sides[...] = jnp.zeros_like(sides)
    for q in range(size):
        sides[q, 0, :, :inner] = wg_ref[:, q * inner : (q + 1) * inner]
        sides[q, 1, :, :inner] = wu_ref[:, q * inner : (q + 1) * inner]
    line = Line(
        pieces, [lambda c, i=i: full_ref.at[partner(me, i, size), c] for i in range(size)], line_send, line_recv
    )
    for n in range(3):
        own(n).wait()
    line.own(0)
    for i in range(1, size):
        for n in range(3):
            exchange(n, i).wait_recv()
        line.own(i)
    begin(3)
    begin(4)
    last = xfull_ref.at[pl.ds(size * count - HALO, HALO)]
    passing = pltpu.make_async_remote_copy(
        last, halo_ref, halo_sem.at[0], halo_sem.at[1], device_id={"ctx": here + 1}, device_id_type=MESH
    )
    hops = pieces // 2 - 1
    for distance in range(1, hops):
        line.hop(distance)
    end(3)
    pl.when(here < pieces - 1)(passing.start)

    @pl.when(here == 0)
    def _():
        filling = pltpu.make_async_copy(last, halo_ref, local_sem.at[5])
        filling.start()
        filling.wait()

    line.hop(hops)
    line.finish()
    end(4)
    pl.when(here > 0)(passing.wait_recv)
    pl.when(here < pieces - 1)(passing.wait_send)
    for n in range(5):
        for i in range(1, size):
            exchange(n, i).wait_send()


def start_gather(size, pieces, norm_at, x, mix, gate, scal, norm_a, norm_m, taps, mask, w_gate, w_up):
    anywhere = pl.BlockSpec(memory_space=pl.ANY)
    vmem = pl.BlockSpec(memory_space=pltpu.VMEM)
    out = lambda *dims: jax.ShapeDtypeStruct(dims, BF16)
    dma = pltpu.SemaphoreType.DMA
    held, padded = w_gate.shape[0], lanes_for(w_gate.shape[1] // size)
    width = (mix.shape[1] + gate.shape[1]) // size + HEAD
    return pl.pallas_call(
        functools.partial(start_kernel, size, pieces, norm_at),
        in_specs=[anywhere] * 3 + [vmem] * 7,
        out_specs=[anywhere] * 4,
        out_shape=[
            out(x.shape[0] * size, D), out(HALO, D), out(size, pieces, held, width), out(size, 2, held, padded),
        ],
        scratch_shapes=[
            pltpu.VMEM((held, HEAD), BF16), pltpu.VMEM((size, 2, held, padded), BF16),
            dma((6,)), dma((5, size - 1)), dma((5, size - 1)), dma((size, 3, pieces)), dma((size, pieces)), dma((2,)),
        ],
        compiler_params=pltpu.CompilerParams(
            vmem_limit_bytes=VMEM_LIMIT, collective_id=2, has_side_effects=True
        ),
        name="start_gather",
    )(x, mix, gate, scal, norm_a, norm_m, taps, mask, w_gate, w_up)


def exact(a, b, ca=1, cb=0):
    return lax.dot_general(
        a, b, (((ca,), (cb,)), ((), ())), precision=lax.Precision.HIGHEST, preferred_element_type=F32
    )


def tap_lanes(channels, tap, at):
    lanes = iota((channels, HEAD), 1)
    return (lanes == at + CONV * (iota((channels, HEAD), 0) % (WIDE // HEAD)) + tap).astype(BF16)


def channel_rows(rows, channels):
    return iota((rows, channels), 1) // (WIDE // HEAD) == iota((rows, channels), 0)


def front_body(
    heads, norm_at, alog_ref, lift_ref, x_ref, halo_ref, w_ref, marks_ref,
    proj_ref, normed_ref, gate_ref, tok_ref, slope_ref, col_ref, row_ref, taps_ref, norms_ref,
):
    me = lax.axis_index("seq")
    channels = heads * WIDE
    tail_at = channels + heads * HEAD
    rows = x_ref.shape[0]
    own_rows = D * heads // HEADS

    def dot(a, b, ca=1, cb=0):
        return lax.dot_general(a, b, (((ca,), (cb,)), ((), ())), preferred_element_type=F32)

    pick = (iota((8, HEAD), 1) == norm_at + iota((8, HEAD), 0)).astype(BF16)
    norms_ref[...] = dot(pick, w_ref[:, tail_at:], 1, 1)

    def normal(values):
        values = values.astype(F32)
        scale = lax.rsqrt(jnp.mean(values * values, axis=1, keepdims=True) + NORM_EPS)
        return (values * scale * norms_ref[0:1, :]).astype(BF16)

    early = normal(halo_ref[...])
    normed_ref[...] = normal(x_ref[...])
    proj_ref[:HALO] = dot(early, w_ref[:, :channels]).astype(BF16)
    proj_ref[HALO:] = dot(normed_ref[...], w_ref[:, :channels]).astype(BF16)
    gate_ref[...] = dot(normed_ref[...], w_ref[:, channels:tail_at])
    tail = w_ref[pl.ds(pl.multiple_of(me * own_rows, own_rows), own_rows), tail_at:]
    taps_ref[...] = jnp.zeros_like(taps_ref)
    mine = channel_rows(own_rows, channels)
    for lag in range(CONV):
        spread = dot(tail, tap_lanes(channels, CONV - 1 - lag, norm_at + 3), 1, 1)
        taps_ref[lag : lag + 1] = jnp.sum(jnp.where(mine, spread, 0.0), axis=0, keepdims=True)

    raw = dot(normed_ref[...], w_ref[:, tail_at:]).astype(BF16).astype(F32)
    raw = pltpu.roll(raw, lax.rem(HEAD - me * lane_of(heads, 0), HEAD), 1)
    lane = iota((1, HEAD), 1)
    rate, lift = jnp.zeros((1, HEAD), F32), jnp.zeros((1, HEAD), F32)
    for h in range(heads):
        here = lane == lane_of(h, NH)
        mine_here = iota((1, HEADS), 1) == me * heads + h
        own = [
            jnp.sum(jnp.where(mine_here, ref[...].astype(F32), 0.0), axis=1, keepdims=True) for ref in (alog_ref, lift_ref)
        ]
        rate = jnp.where(here, -jnp.exp(own[0]), rate)
        lift = jnp.where(here, own[1], lift)
    is_log = (lane % (NH + 1) == NH) & (lane < lane_of(heads, 0))
    lifted = raw + lift
    sig = jax.nn.sigmoid(lifted)
    logs = rate * (jnp.maximum(lifted, 0.0) + jnp.log1p(jnp.exp(-jnp.abs(lifted))))
    slope_ref[...] = jnp.where(is_log, rate * sig, sig * (1.0 - sig)) * (lane < HEAD // 2) + pltpu.roll(
        jnp.where(is_log, logs, 0.0), HEAD // 2, 1
    )
    place = (iota((8, HEAD), 1) == LINK + iota((8, HEAD), 0)) & (iota((8, HEAD), 0) < CONV - 1)
    links = dot(marks_ref[...].astype(BF16), place.astype(BF16), 0, 0)
    open_ = column(links, LINK)
    summed = jnp.where(is_log, logs * open_, jnp.where(lane == DOC, 1.0 - open_, 0.0))
    lower = (iota((BLOCK_LEN, BLOCK_LEN), 0) >= iota((BLOCK_LEN, BLOCK_LEN), 1)).astype(F32)
    spread = (iota((ROWS, BLOCK_LEN), 0) // NH == iota((ROWS, BLOCK_LEN), 1)).astype(F32)
    step = iota((ROWS, HEAD), 0) % NH
    for b in range(rows // BLOCK_LEN):
        span = slice(b * BLOCK_LEN, (b + 1) * BLOCK_LEN)
        sums = exact(lower, summed[span])
        tok = jnp.where(is_log | (lane == DOC), sums, jnp.where(lane < DOC, sig[span], links[span]))
        tok_ref[span] = tok
        wide = exact(spread, tok)
        first = wide
        for j in range(1, NH):
            first = jnp.where(step == j, pltpu.roll(wide, HEAD - j, 1), first)
        col = jnp.where(lane % (NH + 1) == 0, jnp.where(lane < lane_of(heads, 0), first, wide), wide)
        col_ref[b * ROWS : (b + 1) * ROWS] = col
        row_ref[b * 8 : (b + 1) * 8] = col.T[:8]


def fwd_kernel(
    heads, pieces, steps, per, span_pieces, norm_at,
    alog_ref, lift_ref, x_ref, halo_ref, full_ref, marks_ref, stage_ref, wo_ref,
    proj_ref, normed_ref, gate_ref, tok_ref, slope_ref, col_ref, row_ref, taps_ref, norms_ref,
    oloc_ref, carr_ref, sin_ref, mapsout_ref, conv_ref, q_ref, k_ref, v_ref, t_ref, kk_ref, at_ref, uw_ref, pl_ref,
    wgfull_ref, wufull_ref, wofull_ref,
    state, weave, maps, wgs, wus, wos, local_sem, line_send, line_recv, map_send, map_recv,
):
    step = pl.program_id(0)
    here = lax.axis_index("ctx")
    weights = Line(
        pieces, [lambda c: wgs.at[:, c], lambda c: wus.at[:, c], lambda c: wos.at[c]], line_send, line_recv
    )
    eye = (iota((HEAD, HEAD), 0) == iota((HEAD, HEAD), 1)).astype(F32)

    @pl.when(step == 0)
    def _():
        owned = [
            pltpu.make_async_copy(source, target, local_sem.at[n])
            for n, (source, target) in enumerate(
                [(stage_ref.at[:, 0], wgs.at[:, here]), (stage_ref.at[:, 1], wus.at[:, here]), (wo_ref, wos.at[here])]
            )
        ]
        for copy in owned:
            copy.start()
        barrier = pltpu.get_barrier_semaphore()
        pl.semaphore_wait(barrier, greet(line_neighbours(pieces), barrier))
        for copy in owned:
            copy.wait()
        weights.own()
        front_body(
            heads, norm_at, alog_ref, lift_ref, x_ref, halo_ref, full_ref, marks_ref,
            proj_ref, normed_ref, gate_ref, tok_ref, slope_ref, col_ref, row_ref, taps_ref, norms_ref,
        )
        for h in range(heads):
            state[h, :, :HEAD] = eye
            state[h, :, HEAD:] = jnp.zeros((HEAD, HEAD), F32)

    hops = [(d * 2 * steps) // (pieces // 2) - 1 for d in range(1, pieces // 2)]
    for distance, at in enumerate(hops, 1):
        if at < steps:
            pl.when(step == at)(lambda distance=distance: weights.hop(distance))

    items = [(j, h) for j in range(per) for h in range(heads)]
    cols = lambda h: slice(h * WIDE, (h + 1) * WIDE)
    span = lambda j, length=BLOCK_LEN: slice(j * length, (j + 1) * length)
    tables = []
    for j in range(per):
        block = step * per + j
        tables.append(
            (
                row_ref[pl.ds(pl.multiple_of(block * 8, 8), 8), :],
                col_ref[pl.ds(pl.multiple_of(block * ROWS, ROWS), ROWS), :],
                tok_ref[pl.ds(pl.multiple_of(block * BLOCK_LEN, BLOCK_LEN), BLOCK_LEN), :],
            )
        )
    acts = []
    for j, h in items:
        base = pl.multiple_of((step * per + j) * BLOCK_LEN, BLOCK_LEN)
        ext = proj_ref[pl.ds(base, BLOCK_LEN + HALO), cols(h)].astype(F32)
        conv = ext[HALO:] * taps_ref[0:1, cols(h)]
        for lag in range(1, CONV):
            conv = conv + column(tables[j][2], LINK + lag - 1) * lag_rows(ext, lag) * taps_ref[lag : lag + 1, cols(h)]
        conv_ref[span(j), cols(h)] = conv
        acts.append(conv * jax.nn.sigmoid(conv))
    queries, keys, values = [], [], []
    for n, act in enumerate(acts):
        unit = []
        for part in range(1 + NH):
            piece = act[:, part * HEAD : (part + 1) * HEAD]
            unit.append(piece * lax.rsqrt(jnp.sum(piece * piece, axis=1, keepdims=True) + NORM_EPS))
        queries.append(unit[0] * (1.0 / math.sqrt(HEAD)))
        for j in range(NH):
            weave[2 * n, pl.ds(j, BLOCK_LEN, NH), :] = unit[1 + j]
            weave[2 * n + 1, pl.ds(j, BLOCK_LEN, NH), :] = act[:, (1 + NH + j) * HEAD : (2 + NH + j) * HEAD]
    for n in range(len(items)):
        keys.append(weave[2 * n])
        values.append(weave[2 * n + 1])
    factors = [decays(*tables[j], h) for j, h in items]
    grams = [mm(jnp.concatenate([q, k], axis=0), k, 1, 1) for q, k in zip(queries, keys)]
    kks = [f[1] * g[BLOCK_LEN:] for f, g in zip(factors, grams)]
    attns = [f[2] * g[:BLOCK_LEN] for f, g in zip(factors, grams)]
    invs = unit_lower_inverses([f[0] * kk for f, kk in zip(factors, kks)])
    uws = [
        mm(inv, jnp.concatenate([f[0] * v, (f[0] * f[3]) * k], axis=1))
        for inv, f, v, k in zip(invs, factors, values, keys)
    ]
    auws = [mm(attn, uw) for attn, uw in zip(attns, uws)]
    nms = [mm(f[5] * k, uw, 0, 0) for f, k, uw in zip(factors, keys, uws)]
    for n, (j, h) in enumerate(items):
        before = state[h]
        f = factors[n]
        both = mm(
            jnp.concatenate([f[4] * queries[n] - auws[n][:, HEAD:], f[6] * eye - nms[n][:, HEAD:]], axis=0), before
        )
        hc = slice(h * HEAD, (h + 1) * HEAD)
        carr_ref[span(j), hc] = both[:BLOCK_LEN, :HEAD]
        oloc_ref[span(j), hc] = both[:BLOCK_LEN, HEAD:] + auws[n][:, :HEAD]
        state[h, :, :HEAD] = both[BLOCK_LEN:, :HEAD]
        state[h, :, HEAD:] = both[BLOCK_LEN:, HEAD:] + nms[n][:, :HEAD]
        q_ref[j, h] = queries[n]
        k_ref[j, h] = keys[n]
        v_ref[j, h] = values[n]
        t_ref[j, h] = invs[n]
        kk_ref[j, h] = kks[n]
        at_ref[j, h] = attns[n]
        uw_ref[j, h] = uws[n]
        pl_ref[j, h] = before

    @pl.when(step == steps - 1)
    def _():
        maps[here] = state[...].astype(BF16)
        line = Line(pieces, [lambda c: maps.at[c]], map_send, map_recv, reach=chips_within(span_pieces, pieces))
        line.own()
        for distance in range(1, line.reach + 1):
            line.hop(distance)
        line.finish()
        for distance in range(1, pieces // 2):
            if hops[distance - 1] >= steps:
                weights.hop(distance)

        def hop(k, states):
            return tuple(
                mm(maps[k, h, :, :HEAD], states[h]) + maps[k, h, :, HEAD:].astype(F32) for h in range(heads)
            )

        states = lax.fori_loop(jnp.maximum(here - span_pieces, 0), here, hop, tuple(jnp.zeros((HEAD, HEAD), F32) for _ in range(heads)))
        for h in range(heads):
            sin_ref[h] = states[h]

        def keep(k, carry):
            mapsout_ref[k] = maps[k, :, :, :HEAD]
            return carry

        lax.fori_loop(
            jnp.maximum(here - span_pieces, 0), jnp.minimum(here + span_pieces + 1, pieces), keep, 0
        )
        weights.finish()
        given = [
            pltpu.make_async_copy(source, target, local_sem.at[n])
            for n, (source, target) in enumerate([(wgs, wgfull_ref), (wus, wufull_ref), (wos, wofull_ref)])
        ]
        for copy in given:
            copy.start()
        for copy in given:
            copy.wait()


def recurrence_forward(heads, pieces, span_pieces, norm_at, a_log, dt_bias, x_full, halo, weights, marks, stage, w_out):
    rows = x_full.shape[0]
    blocks = rows // BLOCK_LEN
    per = 2
    size = stage.shape[0]
    whole = lambda *dims: pl.BlockSpec(dims, lambda i: (0,) * len(dims))
    by_block = lambda *dims: pl.BlockSpec((per,) + dims, lambda i: (i,) + (0,) * len(dims))
    token = lambda cols: pl.BlockSpec((per * BLOCK_LEN, cols), lambda i: (i, 0))
    shape = lambda *dims: jax.ShapeDtypeStruct(dims, F32)
    low_shape = lambda *dims: jax.ShapeDtypeStruct(dims, BF16)
    hbm = pl.BlockSpec(memory_space=pltpu.HBM)
    vmem = pl.BlockSpec(memory_space=pltpu.VMEM)
    square = (heads, ROWS, HEAD)
    dma = pltpu.SemaphoreType.DMA
    side = (size, pieces, *stage.shape[2:])
    front = [
        low_shape(rows + HALO, heads * WIDE), low_shape(rows, D), shape(rows, heads * HEAD), shape(rows, HEAD),
        shape(rows, HEAD), shape(blocks * ROWS, HEAD), shape(blocks * 8, ROWS), shape(8, heads * WIDE), shape(8, D),
    ]
    return pl.pallas_call(
        functools.partial(fwd_kernel, heads, pieces, blocks // per, per, span_pieces, norm_at),
        grid=(blocks // per,),
        in_specs=[vmem] * 6 + [hbm] * 2,
        out_specs=[whole(*f.shape) for f in front] + [
            token(heads * HEAD), token(heads * HEAD), whole(heads, HEAD, HEAD), whole(pieces, heads, HEAD, HEAD),
            token(heads * WIDE),
            by_block(heads, BLOCK_LEN, HEAD), by_block(*square), by_block(*square), by_block(*square),
            by_block(*square), by_block(heads, BLOCK_LEN, ROWS), by_block(heads, ROWS, 2 * HEAD),
            by_block(heads, HEAD, 2 * HEAD), hbm, hbm, hbm,
        ],
        out_shape=front + [
            shape(rows, heads * HEAD), shape(rows, heads * HEAD), shape(heads, HEAD, HEAD),
            low_shape(pieces, heads, HEAD, HEAD), shape(rows, heads * WIDE),
            shape(blocks, heads, BLOCK_LEN, HEAD), shape(blocks, *square), shape(blocks, *square), shape(blocks, *square),
            shape(blocks, *square), shape(blocks, heads, BLOCK_LEN, ROWS), shape(blocks, heads, ROWS, 2 * HEAD),
            shape(blocks, heads, HEAD, 2 * HEAD),
            low_shape(*side), low_shape(*side), low_shape(pieces, *w_out.shape),
        ],
        scratch_shapes=[
            pltpu.VMEM((heads, HEAD, 2 * HEAD), F32), pltpu.VMEM((2 * heads * per, ROWS, HEAD), F32),
            pltpu.VMEM((pieces, heads, HEAD, 2 * HEAD), BF16),
            pltpu.VMEM(side, BF16), pltpu.VMEM(side, BF16), pltpu.VMEM((pieces, *w_out.shape), BF16),
            dma((3,)), dma((3, 3, pieces)), dma((3, pieces)), dma((1, 3, pieces)), dma((1, pieces)),
        ],
        compiler_params=pltpu.CompilerParams(
            vmem_limit_bytes=VMEM_LIMIT, collective_id=3, has_side_effects=True
        ),
        name="recurrence_forward",
    )(a_log, dt_bias, x_full, halo, weights, marks, stage, w_out)


def middle_kernel(
    size, heads, token_total,
    x_ref, teach_ref, mask_ref, norms_ref, gain_ref, *streams_and_rest,
):
    streams, rest = streams_and_rest[:8], streams_and_rest[8:]
    middle_body(size, heads, token_total, x_ref, teach_ref, mask_ref, norms_ref, gain_ref, streams, *rest)


def middle_body(
    size, heads, token_total, x_ref, teach_ref, mask_ref, norms_ref, gain_ref, streams,
    final_ref, gmid_ref, ghead_ref, ggate_ref, cot_ref, ggain_ref, gnorm_ref, loss_ref,
    wheld, theld, outg_ref,
    oloc_ref, carr_ref, gate_ref, sin_ref, wout_ref, wg_ref, wu_ref, wd_ref, load_sem, heads_ref, mixed_ref,
    line_send, line_recv, wds, wide_ref, tall_ref, wtheirs, ttheirs, wcame, tcame,
    pair_send, pair_recv, sum_send, sum_recv,
    second, branch, low, sent, got, own, mid, gfin, gates, ups, hidden, ggates, gups, send_sem, recv_sem,
):
    me = lax.axis_index("seq")
    count = x_ref.shape[0]
    loads = [
        pltpu.make_async_copy(source, target, load_sem.at[n])
        for n, (source, target) in enumerate(
            zip(streams, (oloc_ref, carr_ref, gate_ref, sin_ref, wout_ref, wg_ref, wu_ref, wds.at[lax.axis_index("ctx")]))
        )
    ]
    for load in loads:
        load.start()
    pieces = 2 * wide_ref.shape[0]
    barrier = pltpu.get_barrier_semaphore()
    peers = [({"seq": partner(me, i, size)}, me >= 0) for i in range(1, size)]
    pl.semaphore_wait(barrier, greet(peers + line_neighbours(pieces), barrier))
    loads[7].wait()
    line = Line(pieces, [lambda c: wds.at[c]], line_send, line_recv)
    line.own()
    for load in loads[:5]:
        load.wait()
    norm = norms_ref[1:2, :]
    gain = gain_ref[...].astype(F32)

    def dot(a, b, ca=1, cb=0):
        return lax.dot_general(a, b, (((ca,), (cb,)), ((), ())), preferred_element_type=F32)

    def rows(q):
        return pl.ds(pl.multiple_of(q * count, count), count)

    def part_copy(phase, i):
        return pltpu.make_async_remote_copy(
            sent.at[phase, i - 1], got.at[phase, i - 1], send_sem.at[phase, i - 1], recv_sem.at[phase, i - 1],
            device_id={"seq": partner(me, i, size)}, device_id_type=MESH,
        )

    def block_copy(buffer, phase, i, owner):
        return pltpu.make_async_remote_copy(
            buffer.at[rows(owner)], buffer.at[rows(owner)], send_sem.at[phase, i - 1], recv_sem.at[phase, i - 1],
            device_id={"seq": partner(me, i, size)}, device_id_type=MESH,
        )

    def give_part(phase, i, part):
        @pl.when(i > 0)
        def _():
            sent[phase, i - 1] = part.astype(BF16)
            part_copy(phase, i).start()

        @pl.when(i == 0)
        def _():
            own[...] = part

    def take_parts(phase):
        def add(i, total):
            part_copy(phase, i).wait_recv()
            return total + got[phase, i - 1].astype(F32)

        return lax.fori_loop(1, size, add, own[...])

    relayed = size == 4

    def half_copy(buffer, phase, n, owner):
        part = pl.ds(pl.multiple_of(owner * count + (n - 1) * (count // 2), count // 2), count // 2)
        return pltpu.make_async_remote_copy(
            buffer.at[part], buffer.at[part], send_sem.at[phase, 1 + n], recv_sem.at[phase, 1 + n],
            device_id={"seq": partner(me, 3 - n, size)}, device_id_type=MESH,
        )

    def give_block(buffer, phase, value):
        buffer[rows(me)] = value
        for i in range(1, 3 if relayed else size):
            block_copy(buffer, phase, i, me).start()

    def take_block(buffer, phase, i):
        q = partner(me, i, size)
        if relayed:

            @pl.when(i == 1)
            def _():
                for n in (1, 2):
                    block_copy(buffer, phase, n, partner(me, n, size)).wait_recv()
                    half_copy(buffer, phase, n, partner(me, n, size)).start()

            @pl.when(i == 3)
            def _():
                for n in (1, 2):
                    half_copy(buffer, phase, n, q).wait_recv()

        else:
            pl.when(i > 0)(lambda: block_copy(buffer, phase, i, q).wait_recv())
        return q

    def block_left(buffer, phase):
        for i in range(1, 3 if relayed else size):
            block_copy(buffer, phase, i, me).wait_send()
        if relayed:
            for n in (1, 2):
                half_copy(buffer, phase, n, partner(me, n, size)).wait_send()

    def out_part(k, carry):
        i = size - 1 - k
        q = partner(me, i, size)
        for h in range(heads):
            hc = slice(h * HEAD, (h + 1) * HEAD)
            out = (oloc_ref[rows(q), hc] + mm(carr_ref[rows(q), hc], sin_ref[h])).astype(BF16)
            heads_ref[rows(q), hc] = out
            wide = out.astype(F32)
            gate = gate_ref[rows(q), hc]
            scaled = wide * lax.rsqrt(jnp.mean(wide * wide, axis=1, keepdims=True) + NORM_EPS) * gain
            mixed_ref[rows(q), hc] = (scaled * (gate * jax.nn.sigmoid(gate))).astype(BF16)
        give_part(0, i, dot(mixed_ref[rows(q)], wout_ref[...]))
        return carry

    lax.fori_loop(0, size, out_part, 0)
    hops = pieces // 2 - 1
    for distance in range(1, hops // 2 + 1):
        line.hop(distance)
    middle = x_ref[...].astype(F32) + take_parts(0)
    mid[...] = middle
    inv = lax.rsqrt(jnp.mean(middle * middle, axis=1, keepdims=True) + NORM_EPS)
    give_block(second, 3, (middle * inv * norm).astype(BF16))
    for load in loads[5:7]:
        load.wait()
    deep = wds.shape[1]
    for distance in range(hops // 2 + 1, hops):
        line.hop(distance)

    def take_down():
        line.hop(hops)
        line.finish()
        inner = pieces * deep
        wd_ref[inner:] = jnp.zeros((wd_ref.shape[0] - inner, D), BF16)
        for c in range(pieces):
            wd_ref[c * deep : (c + 1) * deep] = wds[c]

    def feed(i, carry):
        q = take_block(second, 3, i)
        here = second[rows(q)]
        gate = dot(here, wg_ref[...])
        up = dot(here, wu_ref[...])
        gates[rows(q)] = gate
        ups[rows(q)] = up
        hid = (gate * jax.nn.sigmoid(gate) * up).astype(BF16)
        hidden[rows(q)] = hid
        pl.when(i == 0)(take_down)
        give_part(1, i, dot(hid, wd_ref[...]))
        return carry

    lax.fori_loop(0, size, feed, 0)
    final = mid[...] + take_parts(1)
    final_ref[...] = final.astype(BF16)
    error = final - teach_ref[...].astype(F32)
    mask = jnp.broadcast_to(mask_ref[...].astype(F32), (count, count)).T[:, :1]
    weighted = mask * error
    loss_ref[...] = jnp.broadcast_to(
        jnp.sum(jnp.sum(weighted * error, axis=1, keepdims=True), axis=0, keepdims=True), loss_ref.shape
    )
    valid = jnp.maximum(jnp.sum(norms_ref[2:3, :], axis=1, keepdims=True), 1.0)
    grad_final = token_total / valid * weighted
    gfin[...] = grad_final
    give_block(branch, 4, grad_final.astype(BF16))

    def feed_back(i, carry):
        q = take_block(branch, 4, i)
        ghid = dot(branch[rows(q)], wd_ref[...], 1, 1)
        gate = gates[rows(q)]
        sig = jax.nn.sigmoid(gate)
        silu = gate * sig
        ggate = (ghid * ups[rows(q)] * (sig + silu * (1.0 - sig))).astype(BF16)
        gup = (ghid * silu).astype(BF16)
        ggates[rows(q)] = ggate
        gups[rows(q)] = gup
        give_part(2, i, dot(ggate, wg_ref[...], 1, 1) + dot(gup, wu_ref[...], 1, 1))
        return carry

    lax.fori_loop(0, size, feed_back, 0)
    held = D // (size * pieces)
    tall_ref[...] = jnp.zeros_like(tall_ref)
    grad = dot(hidden[...], branch[...], 0, 0)
    for c in range(pieces):
        tall_ref[c // 2, c % 2, :deep] = grad[c * deep : (c + 1) * deep].astype(BF16)
    parts = ((tall_ref, ttheirs, theld, tcame), (wide_ref, wtheirs, wheld, wcame))
    pairs = [
        Siblings([part], [theirs], [kept], pair_send.at[n], pair_recv.at[n])
        for n, (part, theirs, kept, _) in enumerate(parts)
    ]
    sums = [LineSum(pieces, [kept], [came], sum_send.at[n], sum_recv.at[n]) for n, (_, _, kept, came) in enumerate(parts)]
    pairs[0].start()
    for n, side in enumerate((ggates, gups)):
        grad = dot(second[...], side[...], 0, 0)
        for c in range(pieces):
            for r in range(size):
                first = (r * pieces + c) * held
                wide_ref[c // 2, c % 2, (n * size + r) * held : (n * size + r + 1) * held] = grad[
                    first : first + held
                ].astype(BF16)
    pairs[1].start()
    for pair, line_sum in zip(pairs, sums):
        pair.add()
        line_sum.round(0)
    gsecond = take_parts(2)
    middle = mid[...]
    inv = lax.rsqrt(jnp.mean(middle * middle, axis=1, keepdims=True) + NORM_EPS)
    unit = middle * inv
    gnorm_ref[...] = jnp.sum(gsecond * unit, axis=0, keepdims=True)
    down = gsecond * norm
    gmid = gfin[...] + inv * (down - unit * jnp.mean(down * unit, axis=1, keepdims=True))
    gmid_ref[...] = gmid
    give_block(low, 5, gmid.astype(BF16))
    ggain_ref[...] = jnp.zeros_like(ggain_ref)
    cot_ref[...] = jnp.zeros_like(cot_ref)

    def out_back(i, carry):
        q = take_block(low, 5, i)
        gmixed = dot(low[rows(q)], wout_ref[...], 1, 1)
        for h in range(heads):
            hc = slice(h * HEAD, (h + 1) * HEAD)
            x = heads_ref[rows(q), hc].astype(F32)
            gate = gate_ref[rows(q), hc]
            grad = gmixed[:, hc]
            inv = lax.rsqrt(jnp.mean(x * x, axis=1, keepdims=True) + NORM_EPS)
            sig = jax.nn.sigmoid(gate)
            silu = gate * sig
            unit = x * inv
            ggate_ref[rows(q), hc] = (grad * unit * gain * (sig + silu * (1.0 - sig))).astype(BF16)
            weighted = grad * silu
            ggain_ref[...] += jnp.sum(weighted * unit, axis=0, keepdims=True)
            down = weighted * gain
            ghead = (inv * (down - unit * jnp.mean(down * unit, axis=1, keepdims=True))).astype(BF16)
            ghead_ref[rows(q), hc] = ghead
            cot_ref[h] += mm(carr_ref[rows(q), hc], ghead, 0, 0)
        return carry

    out_back(0, 0)
    early = early_rounds(pieces)
    for line_sum, ended in zip(sums, early):
        for r in range(1, ended):
            line_sum.round(r)
    lax.fori_loop(1, size, out_back, 0)
    grad = dot(mixed_ref[...], low[...], 0, 0)
    for c in range(pieces):
        outg_ref[c // 2, c % 2] = grad[c * held : (c + 1) * held].astype(BF16)
    for pair, line_sum, ended in zip(pairs, sums, early):
        line_sum.settle(ended)
        pair.left()
        for r in range(ended):
            line_sum.left(r)

    for i in range(1, size):
        for phase in range(3):
            part_copy(phase, i).wait_send()
    for buffer, phase in ((second, 3), (branch, 4), (low, 5)):
        block_left(buffer, phase)


def middle_part(
    size, heads, pieces, token_total, x, teacher, mask, norms, gain, oloc, carr, gate_out, state_in, wout, wg, wu, wd
):
    count = x.shape[0]
    rows = count * size
    inner = wg.shape[1]
    held, deep = D // (size * pieces), wd.shape[0]
    chips = pieces // 2
    wide, tall = (2 * size * held, inner), (-(-deep // 16) * 16, D)
    vmem = pl.BlockSpec(memory_space=pltpu.VMEM)
    out = lambda dims, kind: jax.ShapeDtypeStruct(dims, kind)
    low = lambda *dims: pltpu.VMEM(dims, BF16)
    high = lambda *dims: pltpu.VMEM(dims, F32)
    dma = pltpu.SemaphoreType.DMA
    return pl.pallas_call(
        functools.partial(middle_kernel, size, heads, float(token_total)),
        in_specs=[vmem] * 5 + [pl.BlockSpec(memory_space=pltpu.HBM)] * 8,
        out_specs=[vmem] * 11,
        out_shape=[
            out((count, D), BF16), out((count, D), F32),
            out((rows, heads * HEAD), BF16), out((rows, heads * HEAD), BF16), out((heads, HEAD, HEAD), F32),
            out((1, HEAD), F32), out((1, D), F32), out((1, HEAD), F32),
            out((chips, 2 * size * held, inner), BF16), out((chips, -(-deep // 16) * 16, D), BF16),
            out((chips, 2, held, D), BF16),
        ],
        scratch_shapes=[
            high(rows, heads * HEAD), high(rows, heads * HEAD), high(rows, heads * HEAD), high(heads, HEAD, HEAD),
            low(*wout.shape), low(*wg.shape), low(*wu.shape), low(inner, D), dma((8,)),
            low(rows, heads * HEAD), low(rows, heads * HEAD), dma((1, 3, pieces)), dma((1, pieces)), low(pieces, *wd.shape),
            low(chips, 2, *wide), low(chips, 2, *tall), low(chips, *wide), low(chips, *tall), low(2, chips, *wide),
            low(2, chips, *tall), dma((2, 1)), dma((2, 1)), dma((2, 1, chips)), dma((2, 1, 2, chips)),
            low(rows, D), low(rows, D), low(rows, D), low(3, size - 1, count, D), low(3, size - 1, count, D),
            high(count, D), high(count, D), high(count, D), high(rows, inner), high(rows, inner), low(rows, inner),
            low(rows, inner), low(rows, inner), dma((6, size)), dma((6, size)),
        ],
        compiler_params=pltpu.CompilerParams(
            vmem_limit_bytes=VMEM_LIMIT, collective_id=1, has_side_effects=True
        ),
        name="middle_part",
    )(x, teacher, mask, norms, gain, oloc, carr, gate_out, state_in, wout, wg, wu, wd)


def bwd_kernel(
    heads, pieces, steps, per, begun, span_pieces, maps_ref, cot_ref, sin_ref, proj_ref, w_ref, rowp_ref, colp_ref, tokp_ref, slope_ref,
    go_ref, conv_ref, q_ref, k_ref, v_ref, t_ref, kk_ref, at_ref, uw_ref, pl_ref, wide_ref, tall_ref, outg_ref, normed_ref, ggate_ref,
    gproj_ref, fix_ref, gw_ref, gscal_ref, gsum_ref, widesum_ref, tallsum_ref, outsum_ref, gatesum_ref,
    dstate, weave, rim, last, cots, rim_in, wheld, theld, wcame, tcame,
    gateg, otheirs, gtheirs, oheld, gheld, ocame, gcame,
    cot_send, cot_recv, pair_send, pair_recv, early_send, early_recv, line_send, line_recv, rim_sem,
):
    step = pl.program_id(0)
    block = steps - 1 - step
    here = lax.axis_index("ctx")
    core = lax.rem(here, 2)
    early = [
        LineSum(pieces, [kept], [came], early_send.at[n], early_recv.at[n])
        for n, (kept, came) in enumerate(((theld, tcame), (wheld, wcame)))
    ]
    pair = Siblings([outg_ref, gateg], [otheirs, gtheirs], [oheld, gheld], pair_send, pair_recv)
    line = LineSum(pieces, [oheld, gheld], [ocame, gcame], line_send, line_recv)
    rounds = pieces // 2 - 1
    when_round = [min(steps - 1, 1 + (r * steps) // rounds) for r in range(rounds)]

    @pl.when(step == 0)
    def _():
        barrier = pltpu.get_barrier_semaphore()
        side = [({"ctx": here + 1}, (core == 1) & (here < pieces - 1)), ({"ctx": here - 1}, (core == 0) & (here > 0))]
        pl.semaphore_wait(barrier, greet(line_neighbours(pieces) + side, barrier))
        cots[here] = cot_ref[...].astype(BF16)
        spread = Line(
            pieces, [lambda c: cots.at[c]], cot_send, cot_recv, up=False, reach=chips_within(span_pieces, pieces)
        )
        spread.own()
        wheld[...] = wide_ref[...]
        theld[...] = tall_ref[...]
        grad = lax.dot_general(
            normed_ref[...], ggate_ref[...], (((0,), (0,)), ((), ())), preferred_element_type=F32
        )
        held, size = gateg.shape[3], gateg.shape[2]
        for c in range(pieces):
            for r in range(size):
                row = (r * pieces + c) * held
                gateg[c // 2, c % 2, r] = grad[row : row + held].astype(BF16)
        for distance in range(1, spread.reach + 1):
            spread.hop(distance)
        spread.finish()
        for one, first in zip(early, begun):
            one.launch(first)
        pair.start()

        farthest = jnp.minimum(here + span_pieces, pieces - 1)

        def hop(i, states):
            k = farthest - i
            return tuple(
                mm(maps_ref[k, h], states[h], 0, 0) + cots[k, h].astype(F32) for h in range(heads)
            )

        found = lax.fori_loop(
            0, farthest - here, hop, tuple(jnp.zeros((HEAD, HEAD), F32) for _ in range(heads))
        )
        for h in range(heads):
            dstate[h] = found[h]
        rim[...] = jnp.zeros_like(rim)
        gw_ref[...] = jnp.zeros_like(gw_ref)
        gsum_ref[...] = jnp.zeros_like(gsum_ref)

    for one, first in zip(early, begun):
        for r in range(first + 1, rounds):
            at = steps - 1
            pl.when(step == at)(lambda one=one, r=r: one.round(r))
    pl.when(step == 1)(pair.add)
    for r in range(rounds):
        pl.when(step == when_round[r])(lambda r=r: line.round(r))

    last_row = iota((ROWS, 1), 0) == ROWS - 1
    diagonal = iota((ROWS, ROWS), 0) == iota((ROWS, ROWS), 1)
    first_lane = lax.axis_index("seq") * lane_of(heads, 0)
    gscals = [[] for _ in range(per)]
    dnexts = {(per - 1, h): dstate[h] for h in range(heads)}
    rims = {(per - 1, h): rim[:, h * WIDE : (h + 1) * WIDE] for h in range(heads)}

    def item(j, h):
        n = j * heads + h
        span = slice(j * BLOCK_LEN, (j + 1) * BLOCK_LEN)
        rowp, colp = rowp_ref[j * 8 : (j + 1) * 8], colp_ref[j * ROWS : (j + 1) * ROWS]
        tokp, slope = tokp_ref[span], slope_ref[span]
        cols = slice(h * WIDE, (h + 1) * WIDE)
        hc = slice(h * HEAD, (h + 1) * HEAD)
        beta, decay, qdecay, carry, qcarry, dlast, clast = decays(rowp, colp, tokp, h)
        go = go_ref[span, hc]
        query, keys, values = q_ref[j, h], k_ref[j, h], v_ref[j, h]
        inv, kk, attn, uw = t_ref[j, h], kk_ref[j, h], at_ref[j, h], uw_ref[j, h]
        yield
        state = mm(pl_ref[j, h, :, :HEAD], sin_ref[h]) + pl_ref[j, h, :, HEAD:]
        yield
        both = mm(jnp.concatenate([keys, uw[:, HEAD:]], axis=0), state)
        ks = both[:ROWS]
        upd = uw[:, :HEAD] - both[ROWS:]
        dlocal = mm(attn, go, 0, 0)
        while (j, h) not in dnexts:
            yield
        dnext = dnexts[j, h]
        yield
        dupd = dlocal + dlast * mm(keys, dnext)
        yield
        dx = mm(inv, dupd, 0, 0)
        yield
        dv = beta * dx
        dy = -(carry * dv)
        go32 = go.astype(F32)
        dnexts[j - 1, h] = clast * dnext + mm(
            jnp.concatenate([qcarry * query, keys], axis=0), jnp.concatenate([go32, dy], axis=0), 0, 0
        )
        yield
        outer = mm(jnp.concatenate([go32, dx], axis=0), upd, 1, 1)
        dattn, da = outer[:BLOCK_LEN], -outer[BLOCK_LEN:]
        yield
        dkd = mm(upd, dnext, 1, 1)
        right = mm(jnp.concatenate([go32, dy], axis=0), state, 1, 1)
        gos = right[:BLOCK_LEN]
        yield
        e = beta * da * decay
        f = dattn * qdecay
        ef = jnp.concatenate([f, e], axis=0)
        efk = mm(ef, keys)
        dq = qcarry * gos + efk[:BLOCK_LEN]
        yield
        dk = (
            right[BLOCK_LEN:]
            + dlast * dkd
            + efk[BLOCK_LEN:]
            + mm(ef, jnp.concatenate([query, keys], axis=0), 0, 0)
        )
        weave[3 * n] = dk
        weave[3 * n + 1] = dv
        yield
        dakk = da * kk
        z1 = beta * dakk
        z2 = dattn * attn
        kept = dlast * (dkd * keys)
        below = jnp.sum(z1, axis=0, keepdims=True) + jnp.sum(z2, axis=0, keepdims=True)
        dbeta = jnp.sum(dx * (values - carry * ks) + dakk, axis=1, keepdims=True)
        tail = jnp.sum(
            jnp.sum(kept, axis=0, keepdims=True) + clast * jnp.sum(state * dnext, axis=0, keepdims=True),
            axis=1, keepdims=True,
        )
        dgrow = jnp.sum(z1 + dy * ks - kept - jnp.where(diagonal, below, 0.0), axis=1, keepdims=True)
        dgrow = dgrow + jnp.where(last_row, tail, 0.0)
        lane = iota((ROWS, HEAD), 1)
        weave[3 * n + 2] = jnp.where(lane == 0, dbeta, dgrow)
        yield
        by_step = [weave[3 * n + 2, pl.ds(i, BLOCK_LEN, NH), :] for i in range(NH)]
        dg = sum(x[:, 1:2] for x in by_step) + jnp.sum(z2 + qcarry * (query * gos), axis=1, keepdims=True)
        after = (iota((BLOCK_LEN, BLOCK_LEN), 0) <= iota((BLOCK_LEN, BLOCK_LEN), 1)).astype(BF16)
        dlog = column(tokp, LINK) * mm(after, jnp.broadcast_to(dg, (BLOCK_LEN, HEAD)))[:, :1]
        dscal = [by_step[i][:, 0:1] * column(slope, lane_of(h, i)) for i in range(NH)]
        dscal.append(dlog * column(slope, lane_of(h, NH)))
        lane = iota((BLOCK_LEN, HEAD), 1)
        for i in range(NH + 1):
            gscals[j].append(jnp.where(lane == first_lane + lane_of(h, i), dscal[i], 0.0))
        logs = column(slope, HEAD // 2 + lane_of(h, NH))
        sums = jnp.where(lane == 0, dlog * logs, jnp.where(lane == 1, dscal[NH], 0.0))
        gsum_ref[h : h + 1, :] += jnp.sum(sums, axis=0, keepdims=True)
        yield
        conv = conv_ref[span, cols]
        sig = jax.nn.sigmoid(conv)
        act = conv * sig
        parts = []
        for part in range(1 + NH):
            piece = act[:, part * HEAD : (part + 1) * HEAD]
            scale = lax.rsqrt(jnp.sum(piece * piece, axis=1, keepdims=True) + NORM_EPS)
            if part:
                grad = weave[3 * n, pl.ds(part - 1, BLOCK_LEN, NH), :]
            else:
                grad = dq * (1.0 / math.sqrt(HEAD))
            unit = piece * scale
            parts.append(scale * (grad - unit * jnp.sum(grad * unit, axis=1, keepdims=True)))
        for i in range(NH):
            parts.append(weave[3 * n + 1, pl.ds(i, BLOCK_LEN, NH), :])
        dconv = jnp.concatenate(parts, axis=1) * (sig * (1.0 + conv * (1.0 - sig)))
        yield
        base = pl.multiple_of((block * per + j) * BLOCK_LEN, BLOCK_LEN)
        ext = proj_ref[pl.ds(base, BLOCK_LEN + HALO), cols].astype(F32)
        gw_ref[0:1, cols] += jnp.sum(dconv * ext[HALO:], axis=0, keepdims=True)
        zeros = jnp.zeros((8, WIDE), F32)
        length = BLOCK_LEN + 8
        total = jnp.concatenate([zeros, dconv * w_ref[0:1, cols]], axis=0)
        for lag in range(1, CONV):
            masked = column(tokp, LINK + lag - 1) * dconv
            gw_ref[lag : lag + 1, cols] += jnp.sum(masked * lag_rows(ext, lag), axis=0, keepdims=True)
            total = total + pltpu.roll(
                jnp.concatenate([zeros, masked * w_ref[lag : lag + 1, cols]], axis=0), length - lag, 0
            )
        rims[j - 1, h] = total[:8]
        fixed = total[length - 8 :] + rims[j, h]
        gproj_ref[span, cols] = jnp.concatenate([total[8 : length - 8], fixed], axis=0).astype(BF16)
        if j == per - 1:

            @pl.when(step == 0)
            def _():
                last[:, cols] = fixed

    running = [item(j, h) for j in reversed(range(per)) for h in range(heads)]
    while running:
        running = [one for one in running if next(one, "done") != "done"]
    for h in range(heads):
        dstate[h] = dnexts[-1, h]
        rim[:, h * WIDE : (h + 1) * WIDE] = rims[-1, h]
    for j in range(per):
        gscal_ref[j * BLOCK_LEN : (j + 1) * BLOCK_LEN] = sum(gscals[j]).astype(BF16)

    @pl.when(step == steps - 1)
    def _():
        passing = pltpu.make_async_remote_copy(
            rim, rim_in, rim_sem.at[0], rim_sem.at[1], device_id={"ctx": here - 1}, device_id_type=MESH
        )
        pl.when(here > 0)(passing.start)
        fix_ref[...] = last[...].astype(BF16)

        @pl.when(here < pieces - 1)
        def _():
            passing.wait_recv()
            fix_ref[...] = (last[...] + rim_in[...]).astype(BF16)

        for one in early:
            one.finish()
        line.finish()
        widesum_ref[...] = wheld[here // 2]
        tallsum_ref[...] = theld[here // 2].astype(F32)
        outsum_ref[...] = oheld[here // 2].astype(F32)
        gatesum_ref[...] = gheld[here // 2]
        pair.left()
        for one, first in zip(early, begun):
            for r in range(first, rounds):
                one.left(r)
        for r in range(rounds):
            line.left(r)
        pl.when(here > 0)(passing.wait_send)


def recurrence_backward(
    maps, cot, state_in, proj_ext, conv_w, rowp, colp, tokp, slopes, grad_heads, saved, wide, tall, outg, normed, ggate,
    heads, pieces, span_pieces,
):
    rows = tokp.shape[0]
    blocks = rows // BLOCK_LEN
    chips = pieces // 2
    per = 2
    final = blocks // per - 1
    whole = lambda *dims: pl.BlockSpec(dims, lambda i: (0,) * len(dims))
    by_block = lambda *dims: pl.BlockSpec((per,) + dims, lambda i: (final - i,) + (0,) * len(dims))
    token = lambda cols: pl.BlockSpec((per * BLOCK_LEN, cols), lambda i: (final - i, 0))
    shape = lambda *dims: jax.ShapeDtypeStruct(dims, F32)
    low_shape = lambda *dims: jax.ShapeDtypeStruct(dims, BF16)
    vmem = pl.BlockSpec(memory_space=pltpu.VMEM)
    low = lambda *dims: pltpu.VMEM(dims, BF16)
    square = (heads, ROWS, HEAD)
    wide_chunk, tall_chunk, out_chunk = wide.shape[1:], tall.shape[1:], outg.shape[2:]
    gate_chunk = (HEADS // heads, out_chunk[0], ggate.shape[1])
    dma = pltpu.SemaphoreType.DMA
    return pl.pallas_call(
        functools.partial(bwd_kernel, heads, pieces, blocks // per, per, early_rounds(pieces), span_pieces),
        grid=(blocks // per,),
        in_specs=[
            vmem, vmem, vmem, vmem, vmem,
            pl.BlockSpec((per * 8, ROWS), lambda i: (final - i, 0)),
            pl.BlockSpec((per * ROWS, HEAD), lambda i: (final - i, 0)), token(HEAD), token(HEAD),
            token(heads * HEAD), token(heads * WIDE),
            by_block(heads, BLOCK_LEN, HEAD), by_block(*square), by_block(*square), by_block(*square),
            by_block(*square), by_block(heads, BLOCK_LEN, ROWS), by_block(heads, ROWS, 2 * HEAD),
            by_block(heads, HEAD, 2 * HEAD), vmem, vmem, vmem, vmem, vmem,
        ],
        out_specs=[
            token(heads * WIDE), whole(8, heads * WIDE), whole(8, heads * WIDE), token(HEAD), whole(8, HEAD),
            whole(*wide_chunk), whole(*tall_chunk), whole(*out_chunk), whole(*gate_chunk),
        ],
        out_shape=[
            low_shape(rows, heads * WIDE), low_shape(8, heads * WIDE), shape(8, heads * WIDE), low_shape(rows, HEAD),
            shape(8, HEAD), low_shape(*wide_chunk), shape(*tall_chunk), shape(*out_chunk), low_shape(*gate_chunk),
        ],
        scratch_shapes=[
            pltpu.VMEM((heads, HEAD, HEAD), F32), pltpu.VMEM((3 * heads * per, ROWS, HEAD), F32),
            pltpu.VMEM((8, heads * WIDE), F32), pltpu.VMEM((8, heads * WIDE), F32),
            pltpu.VMEM((pieces, heads, HEAD, HEAD), BF16), pltpu.VMEM((8, heads * WIDE), F32),
            low(chips, *wide_chunk), low(chips, *tall_chunk), low(2, chips, *wide_chunk), low(2, chips, *tall_chunk),
            low(chips, 2, *gate_chunk), low(chips, *out_chunk), low(chips, *gate_chunk), low(chips, *out_chunk),
            low(chips, *gate_chunk), low(2, chips, *out_chunk), low(2, chips, *gate_chunk),
            dma((1, 3, pieces)), dma((1, pieces)), dma((2,)), dma((2,)), dma((2, 1, chips)), dma((2, 1, 2, chips)),
            dma((2, chips)), dma((2, 2, chips)), dma((2,)),
        ],
        compiler_params=pltpu.CompilerParams(
            vmem_limit_bytes=VMEM_LIMIT, collective_id=4, has_side_effects=True
        ),
        name="recurrence_backward",
    )(maps, cot, state_in, proj_ext, conv_w, rowp, colp, tokp, slopes, grad_heads, *saved, wide, tall, outg, normed, ggate)


def final_kernel(
    size, pieces, heads, norm_at, inner, gp_any, gg_any, gs_any, w_any, normed_any,
    fix_ref, x_ref, gmid_ref, norms_ref, gw_ref, gain_ref, gsum_ref, loss_ref, gnorm_ref, wide_ref, gatesum_ref,
    ingrad_ref, gmix_ref, ggate_ref, gtail_ref, gwg_ref, gwu_ref, mean_ref, ends_ref, both_ref,
    gp_ref, gg_ref, gs_ref, w_ref, normed_ref, load_sem, wideout_ref, gateout_ref,
    sent, got, whole, turned, *halves_and_rest,
):
    grads, theirs, helds, cames, blocks = [halves_and_rest[2 * n : 2 * n + 2] for n in range(5)]
    around, along, summed, *sems = halves_and_rest[10:]
    final_body(
        size, pieces, heads, norm_at, inner, gp_any, gg_any, gs_any, w_any, normed_any,
        fix_ref, x_ref, gmid_ref, norms_ref, gw_ref, gain_ref, gsum_ref, loss_ref, gnorm_ref, wide_ref, gatesum_ref,
        ingrad_ref, gmix_ref, ggate_ref, gtail_ref, gwg_ref, gwu_ref, mean_ref, ends_ref, both_ref,
        gp_ref, gg_ref, gs_ref, w_ref, normed_ref, load_sem, wideout_ref, gateout_ref,
        sent, got, whole, turned, grads, theirs, helds, cames, blocks, around, along, summed, *sems,
    )


def final_body(
    size, pieces, heads, norm_at, inner, gp_any, gg_any, gs_any, w_any, normed_any,
    fix_ref, x_ref, gmid_ref, norms_ref, gw_ref, gain_ref, gsum_ref, loss_ref, gnorm_ref, wide_ref, gatesum_ref,
    ingrad_ref, gmix_ref, ggate_ref, gtail_ref, gwg_ref, gwu_ref, mean_ref, ends_ref, both_ref,
    gp_ref, gg_ref, gs_ref, w_ref, normed_ref, load_sem, wideout_ref, gateout_ref,
    sent, got, whole, turned, grads, theirs, helds, cames, blocks, around, along, summed,
    local_sem, seq_send, seq_recv, pair_send, pair_recv, line_send, line_recv, ctx_send, ctx_recv,
):
    me, here = lax.axis_index("seq"), lax.axis_index("ctx")
    count = x_ref.shape[0]
    loads = [
        pltpu.make_async_copy(source, target, load_sem.at[n])
        for n, (source, target) in enumerate(
            [(gp_any, gp_ref), (gg_any, gg_ref), (gs_any, gs_ref), (w_any, w_ref), (normed_any, normed_ref)]
        )
    ]
    for load in loads:
        load.start()
    barrier = pltpu.get_barrier_semaphore()
    peers = [({"seq": partner(me, i, size)}, here >= 0) for i in range(1, size)]
    peers += [({"ctx": lax.rem(here + i, pieces)}, here >= 0) for i in range(1, pieces)]
    pl.semaphore_wait(barrier, greet(peers, barrier))

    def dot(a, b, ca=1, cb=0):
        return lax.dot_general(a, b, (((ca,), (cb,)), ((), ())), preferred_element_type=F32)

    def rows(q):
        return pl.ds(pl.multiple_of(q * count, count), count)

    def to_peer(n, i):
        q = partner(me, i, size)
        source, target = [
            (sent.at[i - 1], got.at[i - 1]), (wide_ref.at[:, q], wideout_ref.at[me]),
            (around.at[me], around.at[me]), (helds[0].at[here // 2, q], blocks[0].at[me]),
            (gatesum_ref.at[q], gateout_ref.at[me]), (helds[1].at[here // 2, q], blocks[1].at[me]),
        ][n]
        return pltpu.make_async_remote_copy(
            source, target, seq_send.at[n, i - 1], seq_recv.at[n, i - 1], device_id={"seq": q}, device_id_type=MESH
        )

    def to_piece(i):
        return pltpu.make_async_remote_copy(
            along.at[here], along.at[here], ctx_send.at[i - 1], ctx_recv.at[i - 1],
            device_id={"ctx": lax.rem(here + i, pieces)}, device_id_type=MESH,
        )

    gate_at, tail_at = gp_ref.shape[1], gp_ref.shape[1] + gg_ref.shape[1]
    for load in loads:
        load.wait()
    gp_ref[gp_ref.shape[0] - 8 :] = fix_ref[...]

    def parts():
        for first in range(0, D, 256):
            tile = slice(first, first + 256)
            value = (
                dot(gp_ref[...], w_ref[tile, :gate_at], 1, 1)
                + dot(gg_ref[...], w_ref[tile, gate_at:tail_at], 1, 1)
                + dot(gs_ref[...], w_ref[tile, tail_at:], 1, 1)
            )
            whole[:, tile] = value

        def give(k, carry):
            i = size - 1 - k
            sent[i - 1] = whole[rows(partner(me, i, size))].astype(BF16)
            pltpu.make_async_remote_copy(
                sent.at[i - 1], got.at[i - 1], seq_send.at[0, i - 1], seq_recv.at[0, i - 1],
                device_id={"seq": partner(me, i, size)}, device_id_type=MESH,
            ).start()
            return carry

        lax.fori_loop(0, size - 1, give, 0)

    turned[...] = normed_ref[...].T
    rank_rows = D // (size * pieces)
    pairs = [Siblings([grads[n]], [theirs[n]], [helds[n]], pair_send.at[n], pair_recv.at[n]) for n in range(2)]
    lines = [LineSum(pieces, [helds[n]], [cames[n]], line_send.at[n], line_recv.at[n]) for n in range(2)]
    split = grads[0].shape[4]

    def gradient(source, first, cols, n, at):
        grad = dot(turned[...], source[:, first : first + cols])
        for r in range(size):
            for c in range(pieces):
                row = (r * pieces + c) * rank_rows
                grads[n][c // 2, c % 2, r, :, at : at + cols] = grad[row : row + rank_rows].astype(BF16)

    for first in range(0, split, 256):
        gradient(gp_ref, first, min(256, split - first), 0, first)
    pairs[0].start()
    for first in range(split, gate_at, 256):
        gradient(gp_ref, first, min(256, gate_at - first), 1, first - split)
    gradient(gs_ref, 0, HEAD, 1, gate_at - split)
    channels = gw_ref.shape[1]
    mine = channel_rows(D // size, channels)
    taps = jnp.zeros((D // size, HEAD), F32)
    for lag in range(CONV):
        spread = jnp.where(mine, gw_ref[lag : lag + 1], 0.0).astype(BF16)
        taps = taps + dot(spread, tap_lanes(channels, CONV - 1 - lag, norm_at + 3))
    for c in range(pieces):
        grads[1][c // 2, c % 2, me, :, gate_at - split :] = (
            grads[1][c // 2, c % 2, me, :, gate_at - split :].astype(F32) + taps[c * rank_rows : (c + 1) * rank_rows]
        ).astype(BF16)
    pairs[1].start()
    pairs[0].add()
    lines[0].round(0)
    parts()
    pairs[1].add()
    lines[1].round(0)
    rounds = pieces // 2 - 1
    for r in range(1, rounds - 1):
        for line in lines:
            line.round(r)
    for i in range(1, size):
        to_peer(0, i).wait_recv()
    gnormed = whole[rows(me)]
    for i in range(1, size):
        gnormed = gnormed + got[i - 1].astype(F32)
    x = x_ref[...].astype(F32)
    inv = lax.rsqrt(jnp.mean(x * x, axis=1, keepdims=True) + NORM_EPS)
    unit = x * inv
    down = gnormed * norms_ref[0:1, :]
    ingrad_ref[...] = gmid_ref[...] + inv * (down - unit * jnp.mean(down * unit, axis=1, keepdims=True))
    term = jnp.sum(gnormed * unit, axis=0, keepdims=True)
    lane = iota((1, HEAD), 1)
    ends = jnp.where(lane == 2 * HEADS, loss_ref[...], 0.0)
    for h in range(heads):
        for n in range(2):
            ends = jnp.where(lane == n * HEADS + me * heads + h, gsum_ref[h : h + 1, n : n + 1], ends)
    around[me] = jnp.zeros(around.shape[1:], F32)
    around[me, 0:1] = gain_ref[...]
    around[me, 1:2] = ends
    for j in range(D // HEAD):
        around[me, 8 + j : 9 + j] = term[:, j * HEAD : (j + 1) * HEAD]
        around[me, 8 + D // HEAD + j : 9 + D // HEAD + j] = gnorm_ref[:, j * HEAD : (j + 1) * HEAD]
    for i in range(1, size):
        to_peer(2, i).start()
    kept = [
        pltpu.make_async_copy(wide_ref.at[:, me], wideout_ref.at[me], local_sem.at[0]),
        pltpu.make_async_copy(gatesum_ref.at[me], gateout_ref.at[me], local_sem.at[1]),
    ]
    for copy in kept:
        copy.start()
    for i in reversed(range(1, size)):
        to_peer(1, i).start()
        to_peer(4, i).start()
    for line in lines:
        line.round(rounds - 1)
    for i in range(1, size):
        to_peer(2, i).wait_recv()
    mine = around[0]
    for r in range(1, size):
        mine = mine + around[r]
    along[here] = mine
    for i in range(1, pieces):
        to_piece(i).start()
    for n, phase in ((0, 3), (1, 5)):
        lines[n].finish()
        blocks[n][me] = helds[n][here // 2, me]
        for i in reversed(range(1, size)):
            to_peer(phase, i).start()
    for i in range(1, pieces):
        to_piece(i).wait_recv()
    total = along[0]
    for c in range(1, pieces):
        total = total + along[c]
    ends_ref[...] = total[:2]
    valid = jnp.maximum(jnp.sum(norms_ref[2:3, :], axis=1, keepdims=True), 1.0)
    mean_ref[...] = total[1:2, 2 * HEADS : 2 * HEADS + 1] / (D * valid)
    summed[...] = total
    place = (me * pieces + here) * rank_rows
    for n in range(2):
        row = summed[pl.ds(8 + n * (D // HEAD) + place // HEAD, 1), :]
        both_ref[n : n + 1, :] = pltpu.roll(row, lax.rem(HEAD - lax.rem(place, HEAD), HEAD), 1)
    tail = jnp.zeros((rank_rows, HEAD), F32)
    for copy in kept:
        copy.wait()
    for i in range(1, size):
        for n in (1, 4, 3):
            to_peer(n, i).wait_recv()
    wide_cols = tail_at - gate_at
    for r in range(size):
        gwg_ref[:, r * inner : (r + 1) * inner] = wideout_ref[r, 0, :, :inner].astype(F32)
        gwu_ref[:, r * inner : (r + 1) * inner] = wideout_ref[r, 1, :, :inner].astype(F32)
        ggate_ref[:, r * wide_cols : (r + 1) * wide_cols] = gateout_ref[r].astype(F32)
        gmix_ref[:, r * gate_at : r * gate_at + split] = blocks[0][r].astype(F32)
    for i in range(1, size):
        to_peer(5, i).wait_recv()
    for r in range(size):
        block = blocks[1][r].astype(F32)
        gmix_ref[:, r * gate_at + split : (r + 1) * gate_at] = block[:, : gate_at - split]
        tail = tail + block[:, gate_at - split :]
    gtail_ref[...] = tail
    for pair in pairs:
        pair.left()
    for line in lines:
        for r in range(pieces // 2 - 1):
            line.left(r)
    for i in range(1, size):
        for n in range(6):
            to_peer(n, i).wait_send()
    for i in range(1, pieces):
        to_piece(i).wait_send()


def final_part(
    size, pieces, heads, norm_at, gp, gg, gs, weights, normed, fix, x, gmid, norms, gw, gain, gsum, loss, gnorm, wide,
    gatesum,
):
    count = x.shape[0]
    chips = pieces // 2
    held, inner = D // (size * pieces), FF // size
    split = WIDE if heads > 1 else 3 * HEAD
    widths = (split, gp.shape[1] - split + gs.shape[1])
    small = (8 + 2 * (D // HEAD), HEAD)
    vmem = pl.BlockSpec(memory_space=pltpu.VMEM)
    out = lambda *dims: jax.ShapeDtypeStruct(dims, F32)
    low = lambda *dims: pltpu.VMEM(dims, BF16)
    high = lambda *dims: pltpu.VMEM(dims, F32)
    dma = pltpu.SemaphoreType.DMA
    return pl.pallas_call(
        functools.partial(final_kernel, size, pieces, heads, norm_at, inner),
        in_specs=[pl.BlockSpec(memory_space=pltpu.HBM)] * 5 + [vmem] * 11,
        out_specs=[vmem] * 9,
        out_shape=[
            out(count, D), out(held, size * gp.shape[1]), out(held, size * gg.shape[1]), out(held, HEAD),
            out(held, size * inner), out(held, size * inner), out(1, 1), out(2, HEAD), out(2, HEAD),
        ],
        scratch_shapes=[
            low(*gp.shape), low(*gg.shape), low(*gs.shape), low(*weights.shape), low(*normed.shape), dma((5,)),
            low(size, 2, held, wide.shape[3]), low(*gatesum.shape),
            low(size - 1, count, D), low(size - 1, count, D), high(size * count, D), low(D, normed.shape[0]),
            *[low(chips, 2, size, held, w) for w in widths], *[low(chips, size, held, w) for w in widths],
            *[low(chips, size, held, w) for w in widths], *[low(2, chips, size, held, w) for w in widths],
            *[low(size, held, w) for w in widths], high(size, *small), high(pieces, *small), high(*small),
            dma((2,)), dma((6, size - 1)), dma((6, size - 1)), dma((2, 1)), dma((2, 1)), dma((2, 1, chips)),
            dma((2, 1, 2, chips)),
            dma((pieces - 1,)), dma((pieces - 1,)),
        ],
        compiler_params=pltpu.CompilerParams(
            vmem_limit_bytes=VMEM_LIMIT, collective_id=5, has_side_effects=True
        ),
        name="final_part",
    )(gp, gg, gs, weights, normed, fix, x, gmid, norms, gw, gain, gsum, loss, gnorm, wide, gatesum)


def finish_kernel(
    scal_cols, taps_at, final_ref, ingrad_ref, gmix_ref, ggate_ref, gwg_ref, gwu_ref, tall_ref, outsum_ref,
    tail_ref, ends_ref, both_ref,
    final_out, ingrad_out, gmix_out, ggate_out, gwg_out, gwu_out, gwd_out, gout_out,
    gscal_out, gconv_out, norma_out, normm_out, gain_out, alog_out, dt_out,
):
    for source, target in (
        (final_ref, final_out), (ingrad_ref, ingrad_out), (gmix_ref, gmix_out), (ggate_ref, ggate_out),
        (gwg_ref, gwg_out), (gwu_ref, gwu_out), (outsum_ref, gout_out),
    ):
        target[...] = source[...]
    gwd_out[...] = tall_ref[: gwd_out.shape[0]]
    tail = tail_ref[...]
    rows, channels = tail.shape[0], gconv_out.shape[1]
    square = jnp.concatenate([tail, jnp.zeros((HEAD - rows, HEAD), F32)], axis=0)
    gscal_out[...] = square.T[:scal_cols, :rows]
    mine = channel_rows(rows, channels)
    for tap in range(CONV):
        spread = exact(tail, tap_lanes(channels, tap, taps_at).astype(F32), 1, 1)
        gconv_out[tap : tap + 1] = jnp.sum(jnp.where(mine, spread, 0.0), axis=0, keepdims=True)
    held = norma_out.shape[1]
    norma_out[...] = both_ref[0:1, :held]
    normm_out[...] = both_ref[1:2, :held]
    gain_out[...] = ends_ref[0:1, :]
    alog_out[...] = ends_ref[1:2, :HEADS]
    dt_out[...] = ends_ref[1:2, HEADS : 2 * HEADS]


def finish_part(scal_cols, taps_at, deep, channels, *parts):
    vmem = pl.BlockSpec(memory_space=pltpu.VMEM)
    held = parts[2].shape[0]
    out = lambda dims, kind=F32: jax.ShapeDtypeStruct(dims, kind)
    return pl.pallas_call(
        functools.partial(finish_kernel, scal_cols, taps_at),
        in_specs=[vmem] * 11,
        out_specs=[vmem] * 15,
        out_shape=[out(p.shape, p.dtype) for p in parts[:6]] + [
            out((deep, D)), out(parts[7].shape), out((scal_cols, held)), out((CONV, channels)),
            out((1, held)), out((1, held)), out((1, HEAD)), out((1, HEADS)), out((1, HEADS)),
        ],
        compiler_params=pltpu.CompilerParams(vmem_limit_bytes=VMEM_LIMIT),
        name="finish_part",
    )(*parts)


def local(
    block_input, teacher, valid_mask, segments, mix_proj, scalar_proj, gate_proj, out_proj, conv_weight,
    norm_attn, norm_mlp, head_gain, a_log, dt_bias, w_gate, w_up, w_down,
):
    seq_size, pieces = lax.axis_size("seq"), lax.axis_size("ctx")
    heads = HEADS // seq_size
    rows = block_input.shape[0] * seq_size
    token_total = segments.shape[0]
    seq_length = min(SEQ_LEN, token_total)
    span_pieces = min(pieces, (MOST_DOC.get(token_total, token_total) - 2) // rows + 1)
    index = lax.axis_index("ctx")
    held = mix_proj.shape[0]
    scal_cols = HEADS * (NH + 1)
    norm_at, taps_at = scal_cols, scal_cols + 3

    x_full, halo, gathered, stage = start_gather(
        seq_size, pieces, norm_at, block_input, mix_proj, gate_proj, scalar_proj.T, norm_attn[None, :],
        norm_mlp[None, :], conv_weight.T, valid_mask[None, :], w_gate, w_up,
    )
    weights = gathered.reshape(D, -1)
    piece_start = index * rows
    window = lax.dynamic_slice_in_dim(jnp.pad(segments, (CONV, 0)), piece_start, rows + CONV)
    place_in = (piece_start + jnp.arange(rows, dtype=jnp.int32)) % seq_length
    marks = jnp.stack(
        [
            ((window[CONV - lag : CONV - lag + rows] == window[CONV:]) & (place_in >= lag)).astype(F32)
            if lag < CONV
            else jnp.zeros((rows,), F32)
            for lag in range(1, 9)
        ]
    )
    (
        proj_ext, normed, gate_out, tokp, slopes, colp, rowp, conv_w, norms,
        oloc, carr, state_in, maps, *saved, wg_full, wu_full, wo_full,
    ) = recurrence_forward(heads, pieces, span_pieces, norm_at, a_log[None, :], dt_bias[None, :], x_full, halo, weights, marks, stage, out_proj)
    (
        final_out, grad_middle, grad_heads, grad_gate_out, cot, gain_term, norm_mlp_term, loss, wide, tall, outg,
    ) = middle_part(
        seq_size, heads, pieces, token_total, block_input, teacher, valid_mask[None, :], norms, head_gain[None, :],
        oloc, carr, gate_out, state_in, wo_full.reshape(heads * HEAD, D), wg_full.reshape(D, -1),
        wu_full.reshape(D, -1), w_down,
    )
    grad_proj, fixed_rows, gw, grad_scal, gsum, wide_sum, tall_sum, out_sum, gate_sum = recurrence_backward(
        maps, cot, state_in, proj_ext, conv_w, rowp, colp, tokp, slopes, grad_heads, saved, wide, tall, outg, normed,
        grad_gate_out, heads, pieces, span_pieces,
    )
    input_grad, mix_grad, gate_grad, tail_grad, wg_grad, wu_grad, mean_loss, ends, norm_grads = final_part(
        seq_size, pieces, heads, norm_at, grad_proj, grad_gate_out, grad_scal, weights, normed, fixed_rows, block_input,
        grad_middle, norms, gw, gain_term, gsum, loss, norm_mlp_term, wide_sum.reshape(2, seq_size, held, -1),
        gate_sum,
    )
    (
        final_out, input_grad, mix_grad, gate_grad, wg_grad, wu_grad, wd_grad, out_grad,
        scal_grad, conv_grad, norm_a_grad, norm_m_grad, gain_grad, alog_grad, dt_grad,
    ) = finish_part(
        scal_cols, taps_at, w_down.shape[0], conv_weight.shape[0],
        final_out, input_grad, mix_grad, gate_grad, wg_grad, wu_grad, tall_sum, out_sum, tail_grad, ends, norm_grads,
    )
    return (
        final_out, mean_loss[0, 0], input_grad, mix_grad, scal_grad.T, gate_grad, out_grad, conv_grad.T,
        norm_a_grad.reshape(-1), norm_m_grad.reshape(-1), gain_grad.reshape(-1), alog_grad.reshape(-1),
        dt_grad.reshape(-1), wg_grad, wu_grad, wd_grad,
    )


def solution(mesh):
    tokens, vector, matrix = P(("ctx", "seq"), None), P(BOTH), P(BOTH, None)
    in_specs = (
        tokens, tokens, P(("ctx", "seq")), P(), matrix, matrix, matrix, matrix, matrix, vector, vector,
        P(), P(), P(), matrix, matrix, matrix,
    )
    out_specs = (
        tokens, P(), tokens, matrix, matrix, matrix, matrix, matrix, vector, vector, P(), P(), P(),
        matrix, matrix, matrix,
    )
    return jax.shard_map(local, mesh=mesh, in_specs=in_specs, out_specs=out_specs, check_vma=False)
```
